32 devices in a mesh: dp: 8 (over y, x, core), tensor: 4 (over z).
Axes of the slice: x: 2, y: 2, z: 4, core: 2. Of those that a mesh axis runs over, the one named last changes fastest.
Arguments:
- tokens: bfloat16 [32, 1024, 512], P(('dp', 'tensor')), may hold values from -6 to 6
- timestep: int32 [32], P(('dp', 'tensor')), may hold values from 0 to 999
- segment_ids: int32 [32, 1024], P('dp'), may hold values from 0 to 7, never falling along the last dimension, each value on 1 to 512 neighbouring positions
- span_lengths: int32 [32], P('dp'), may hold values from 512 to 1024
- w_qkv: float32 [3, 512, 512], P(None, 'dp', 'tensor'), may hold values from -0.25 to 0.25
- w_out_t: float32 [512, 512], P('dp', 'tensor'), may hold values from -1.5 to 1.5
- w_up: float32 [512, 2048], P('dp', 'tensor'), may hold values from -0.25 to 0.25
- w_down_t: float32 [512, 2048], P('dp', 'tensor'), may hold values from -0.125 to 0.125
- w_time: float32 [512, 512], replicated, may hold values from -0.25 to 0.25
- b_time: float32 [512], replicated, may hold values from -3 to 3
- ln1_gain: float32 [512], replicated, may hold values from 0.1 to 1.9
- ln1_bias: float32 [512], replicated, may hold values from -3 to 3
- ln2_gain: float32 [512], replicated, may hold values from 0.1 to 1.9
- ln2_bias: float32 [512], replicated, may hold values from -3 to 3
- b_up: float32 [2048], replicated, may hold values from -3 to 3
- b_down: float32 [512], replicated, may hold values from -3 to 3
- cotangent: bfloat16 [32, 1024, 512], P(('dp', 'tensor')), may hold values from -6 to 6
Outputs:
- layer_out: bfloat16 [32, 1024, 512], P(('dp', 'tensor'))
- grad_tokens: float32 [32, 1024, 512], P(('dp', 'tensor'))
- grad_w_qkv: float32 [3, 512, 512], P(None, 'dp', 'tensor')
- grad_w_out_t: float32 [512, 512], P('dp', 'tensor')
- grad_w_up: float32 [512, 2048], P('dp', 'tensor')
- grad_w_down_t: float32 [512, 2048], P('dp', 'tensor')
- grad_w_time: float32 [512, 512], replicated
- grad_b_time: float32 [512], replicated
- grad_ln1_gain: float32 [512], replicated
- grad_ln1_bias: float32 [512], replicated
- grad_ln2_gain: float32 [512], replicated
- grad_ln2_bias: float32 [512], replicated
- grad_b_up: float32 [2048], replicated
- grad_b_down: float32 [512], replicated
The draws below stay inside these ranges and needn't reach their ends.
Inputs may be any that keep to these rules, and one draw needn't show every extreme that they name: `segment_ids`: never falls along a row; each document has 1 to 512 positions and one has exactly that many.
All inputs are finite; a program needn't handle non-finite values.
Results may differ from the reference program's by a relative error of at most 0.013.
Values may be sent and summed in bfloat16 or wider, within the bound.
A program may use at most 192 MiB of HBM per device.

```python
import math
import jax
import jax.numpy as jnp
import numpy as np
from jax import lax

D = 512
H = 8
HS = 64
FF = 2048
SEQ = 1024
HD = 512
ROWS = 32


def draw_span_lengths(key, part):
    lengths = jax.random.randint(key, (ROWS,), SEQ // 2, SEQ + 1, dtype=jnp.int32)
    lengths = lengths.at[0].set(SEQ)
    return lengths.at[1].set(SEQ // 2)


def with_ends(array, own_key, least, largest):
    extent = array.shape
    index_at = [jax.random.randint(jax.random.fold_in(own_key, axis), (), 0, extent[axis]) for axis in range(len(extent))]
    array = array.at[tuple(index_at)].set(least)
    longest = extent.index(max(extent))
    index_at[longest] = (index_at[longest] + 1) % extent[longest]
    return array.at[tuple(index_at)].set(largest)


def levels(rng, extent, cuts, least, high):
    factor_of, own = 1.0, jax.random.fold_in(rng, 6)
    for dim, parts in cuts:
        heights = jnp.exp(jax.random.uniform(jax.random.fold_in(own, dim), (parts,), jnp.float32, least / len(cuts), high / len(cuts)))
        factor_of = factor_of * jnp.repeat(heights, extent[dim] // parts).reshape([-1 if axis == dim else 1 for axis in range(len(extent))])
    return factor_of


def profile(amount, total, most, lean):
    weights = [(1 << 20) // math.isqrt(grade ** lean) + 1 for grade in range(2, amount + 1)]
    rest, counts = total - most - (amount - 1), [1] * (amount - 1)
    while rest > 0:
        candidates = [i for i in range(amount - 1) if counts[i] < most]
        mass, budget = sum([weights[i] for i in candidates]), rest
        for i in candidates:
            addition = min(most - counts[i], max(1, budget * weights[i] // mass), rest)
            counts[i] = counts[i] + addition
            rest = rest - addition
    return np.array([most] + counts)


def uneven(stream_key, number_of, total, limit, slope):
    if number_of == 2:
        one = jax.random.randint(stream_key, (), max(1, total - limit), min(limit, total - 1) + 1)
        return jnp.stack([one, total - one])
    tallies = jnp.asarray(profile(number_of, total, limit, slope), jnp.int32)
    couples = (number_of - 1) // 2
    donor, taker = tallies[1:1 + 2 * couples:2], tallies[2:2 + 2 * couples:2]
    slack = jnp.minimum(donor - 1, limit - taker)
    shifted = jax.random.randint(jax.random.fold_in(stream_key, 1), (couples,), 0, 1 << 20) % (slack + 1)
    tallies = tallies.at[1:1 + 2 * couples:2].set(donor - shifted).at[2:2 + 2 * couples:2].set(taker + shifted)
    return tallies[jax.random.permutation(jax.random.fold_in(stream_key, 2), number_of)]


def noise(rng, extent, spread, reach, cuts=(), held_as=jnp.bfloat16):
    drawn = spread * jax.random.normal(rng, extent, jnp.float32)
    if cuts:
        drawn = drawn * levels(rng, extent, cuts, -0.22, 0.18)
    return jnp.clip(drawn, -reach, reach).astype(held_as)


def setup_inputs(seed: int = 0) -> dict:
    key_list = jax.random.split(jax.random.key(seed), 18)
    return {
        "tokens": noise(key_list[0], (ROWS, SEQ, D), 1.0, 6.0, ((0, 32),)),
        "timestep": with_ends(jax.random.randint(key_list[1], (ROWS,), 0, 1000), jax.random.fold_in(key_list[1], 1), 0, 999).astype(jnp.int32),
        "segment_ids": jax.vmap(lambda own: jnp.searchsorted(jnp.cumsum(uneven(own, max(SEQ // 128, 4), SEQ, SEQ // 2, 0)), jnp.arange(SEQ), side="right"))(jax.random.split(key_list[2], ROWS)).reshape((ROWS, SEQ)).astype(jnp.int32),
        "span_lengths": draw_span_lengths(jax.random.fold_in(key_list[17], 71), 0),
        "w_qkv": noise(key_list[4], (3, D, HD), D ** -0.5, 0.25, ((1, 8), (2, 4)), jnp.float32),
        "w_out_t": noise(key_list[5], (D, HD), (HD // 32) ** -0.5, 1.5, ((0, 8), (1, 4)), jnp.float32),
        "w_up": noise(key_list[6], (D, FF), D ** -0.5, 0.25, ((0, 8), (1, 4)), jnp.float32),
        "w_down_t": noise(key_list[7], (D, FF), FF ** -0.5, 0.125, ((0, 8), (1, 4)), jnp.float32),
        "w_time": noise(key_list[8], (D, D), D ** -0.5, 0.25, (), jnp.float32),
        "b_time": noise(key_list[9], (D,), 0.5, 3.0, (), jnp.float32),
        "ln1_gain": jnp.clip(1.0 + 0.18 * jax.random.normal(key_list[10], (D,), jnp.float32), 0.1, 1.9),
        "ln1_bias": noise(key_list[11], (D,), 0.5, 3.0, (), jnp.float32),
        "ln2_gain": jnp.clip(1.0 + 0.18 * jax.random.normal(key_list[12], (D,), jnp.float32), 0.1, 1.9),
        "ln2_bias": noise(key_list[13], (D,), 0.5, 3.0, (), jnp.float32),
        "b_up": noise(key_list[14], (FF,), 0.5, 3.0, (), jnp.float32),
        "b_down": noise(key_list[15], (D,), 0.5, 3.0, (), jnp.float32),
        "cotangent": noise(key_list[16], (ROWS, SEQ, D), 1.0, 6.0, ((0, 32),)),
    }


highest = lax.Precision.HIGHEST
epsilon = 1e-05
masked_score = -1e+30

@jax.custom_vjp
def low(v):
    return lax.optimization_barrier(v.astype(jnp.bfloat16)).astype(jnp.float32)

@jax.custom_vjp
def low_back(v):
    return v

def low_keep(v):
    return (low(v), None)

def low_pass(kept, grad):
    return (grad,)

def back_keep(v):
    return (v, None)

def back_low(kept, grad):
    return (low(grad),)
low.defvjp(low_keep, low_pass)
low_back.defvjp(back_keep, back_low)

def norm_layer(values, gain_vec, shift_vec):
    row_mean = lax.optimization_barrier(jnp.mean(values, axis=-1, keepdims=True))
    centred = values - row_mean
    variance = lax.optimization_barrier(jnp.mean(centred * centred, axis=-1, keepdims=True))
    return centred * lax.rsqrt(variance + epsilon) * gain_vec + shift_vec

def time_features(timestep, features):
    half_width = features // 2
    frequency = jnp.exp(-math.log(10000.0) * jnp.arange(half_width, dtype=jnp.float32) / half_width)
    angles = timestep.astype(jnp.float32)[:, None] * frequency[None, :]
    return jnp.concatenate([jnp.sin(angles), jnp.cos(angles)], axis=1)

def allowed_keys(segment, length):
    places = jnp.arange(segment.shape[0], dtype=jnp.int32)
    same_doc = segment[:, None] == segment[None, :]
    is_valid = (places < length)[None, :] | (places[:, None] == places[None, :])
    return same_doc & is_valid

def attend(packed):
    queries, key_rows, values, segment, length = packed
    seq_len = queries.shape[0]
    query_heads = queries.reshape(seq_len, H, HS)
    key_heads = key_rows.reshape(seq_len, H, HS)
    value_heads = values.reshape(seq_len, H, HS)
    scores = low_back(jnp.einsum('qhe,khe->hqk', query_heads, key_heads, precision=highest) * (1.0 / math.sqrt(HS)))
    scores = jnp.where(allowed_keys(segment, length)[None], scores, masked_score)
    probs_low = low(jax.nn.softmax(scores, axis=-1))
    mixed = jnp.einsum('hqk,khe->qhe', probs_low, value_heads, precision=highest)
    return low_back(low(mixed.reshape(seq_len, H * HS)))

def reference(tokens, timestep, segment_ids, span_lengths, w_qkv, w_out_t, w_up, w_down_t, w_time, b_time, ln1_gain, ln1_bias, ln2_gain, ln2_bias, b_up, b_down, cotangent):

    def forward(start_tokens, wq_master, wo_master, wu_master, wd_master, wt_weight, bt_bias, gain_one, bias_one, gain_two, bias_two, bias_up, bias_down):
        time_emb = time_features(timestep, start_tokens.shape[2])
        time_proj = jnp.dot(time_emb, wt_weight, precision=highest) + bt_bias
        start = start_tokens + time_proj[:, None, :]
        normed_one = low(norm_layer(start, gain_one, bias_one))
        qkv_act = low_back(low(jnp.einsum('nsd,cde->cnse', normed_one, low(wq_master), precision=highest)))
        mixed = lax.map(jax.checkpoint(attend), (qkv_act[0], qkv_act[1], qkv_act[2], segment_ids, span_lengths))
        attn_out = low_back(jnp.einsum('nse,de->nsd', mixed, low(wo_master), precision=highest))
        middle = start + attn_out
        normed_two = low(norm_layer(middle, gain_two, bias_two))
        upper = low_back(jnp.einsum('nsd,df->nsf', normed_two, low(wu_master), precision=highest) + bias_up)
        activated = low(jax.nn.gelu(upper, approximate=True))
        ffn_out = low_back(jnp.einsum('nsf,df->nsd', activated, low(wd_master), precision=highest))
        return middle + ffn_out + bias_down
    result, pull_back = jax.vjp(forward, tokens.astype(jnp.float32), w_qkv, w_out_t, w_up, w_down_t, w_time, b_time, ln1_gain, ln1_bias, ln2_gain, ln2_bias, b_up, b_down)
    grads = pull_back(cotangent.astype(jnp.float32))
    return (result.astype(jnp.bfloat16), grads[0], grads[1], grads[2], grads[3], grads[4], grads[5], grads[6], grads[7], grads[8], grads[9], grads[10], grads[11], grads[12])
```

```python
import math

import jax
import jax.numpy as jnp
from jax import lax
from jax.sharding import PartitionSpec as P

HS = 64
FF = 2048


highest = lax.Precision.HIGHEST
epsilon = 1e-05
masked_score = -1e30


def split_up(value, dim, count):
    before, after = (value.shape[:dim], value.shape[dim + 1 :])
    return jnp.moveaxis(value.reshape(*before, count, -1, *after), dim, 0)


def sent_and_summed(value, axis, dim):
    count = lax.axis_size(axis)
    parts = lax.all_to_all(split_up(value, dim, count), axis, 0, 0, tiled=True)
    return jnp.sum(parts.astype(jnp.float32), axis=0)


def side_by_side(arrays, axis, dim, along):
    ends, at = ([], 0)
    for a in arrays[:-1]:
        at += a.shape[along]
        ends.append(at)
    both = jnp.concatenate(arrays, axis=along)
    return tuple(jnp.split(sent_and_summed(both, axis, dim), ends, axis=along))


def norm_layer(values, gain_vec, shift_vec):
    row_mean = jnp.mean(values, axis=-1, keepdims=True)
    centred = values - row_mean
    variance = jnp.mean(centred * centred, axis=-1, keepdims=True)
    return centred * lax.rsqrt(variance + epsilon) * gain_vec + shift_vec


def time_features(timestep, features):
    half_width = features // 2
    frequency = jnp.exp(-math.log(10000.0) * jnp.arange(half_width, dtype=jnp.float32) / half_width)
    angles = timestep.astype(jnp.float32)[:, None] * frequency[None, :]
    return jnp.concatenate([jnp.sin(angles), jnp.cos(angles)], axis=1)


def allowed_keys(segment, length):
    places = jnp.arange(segment.shape[0], dtype=jnp.int32)
    same_doc = segment[:, None] == segment[None, :]
    is_valid = (places < length)[None, :] | (places[:, None] == places[None, :])
    return same_doc & is_valid


def gelu_tanh(values):
    return jax.nn.gelu(values, approximate=True)


def split_heads(values):
    return values.reshape(values.shape[0], values.shape[1] // HS, HS)


def head_scores(query_heads, key_heads, allowed):
    scores = jnp.einsum(
        "qhe,khe->hqk", query_heads, key_heads, preferred_element_type=jnp.float32
    ) * (1.0 / math.sqrt(HS))
    return jnp.where(allowed[None], scores, masked_score)


def attend_forward(packed):
    query_heads = split_heads(packed[0])
    key_heads = split_heads(packed[1])
    value_heads = split_heads(packed[2])
    scores = head_scores(query_heads, key_heads, allowed_keys(packed[3], packed[4]))
    row_max = jnp.max(scores, axis=-1, keepdims=True)
    raised = jnp.exp(scores - row_max)
    row_total = jnp.sum(raised, axis=-1, keepdims=True)
    probs_low = (raised / row_total).astype(jnp.bfloat16)
    mixed = jnp.einsum("hqk,khe->qhe", probs_low, value_heads, preferred_element_type=jnp.float32)
    return (mixed.reshape(packed[0].shape).astype(jnp.bfloat16), row_max + jnp.log(row_total))


def attend_backward(packed):
    query_heads = split_heads(packed[0])
    key_heads = split_heads(packed[1])
    value_heads = split_heads(packed[2])
    grad_heads = split_heads(packed[3])
    scores = head_scores(query_heads, key_heads, allowed_keys(packed[5], packed[6]))
    attn_probs = jnp.exp(scores - packed[4])
    probs_low = attn_probs.astype(jnp.bfloat16)
    grad_values = jnp.einsum(
        "hqk,qhe->khe", probs_low, grad_heads, preferred_element_type=jnp.float32
    )
    grad_probs = jnp.einsum(
        "qhe,khe->hqk", grad_heads, value_heads, preferred_element_type=jnp.float32
    )
    row_delta = jnp.sum(attn_probs * grad_probs, axis=-1, keepdims=True)
    grad_scores = (attn_probs * (grad_probs - row_delta)).astype(jnp.bfloat16)
    score_scale = 1.0 / math.sqrt(HS)
    grad_queries = (
        jnp.einsum("hqk,khe->qhe", grad_scores, key_heads, preferred_element_type=jnp.float32)
        * score_scale
    )
    grad_keys = (
        jnp.einsum("hqk,qhe->khe", grad_scores, query_heads, preferred_element_type=jnp.float32)
        * score_scale
    )
    shape_rows = packed[0].shape
    return jnp.stack(
        [
            grad_queries.reshape(shape_rows),
            grad_keys.reshape(shape_rows),
            grad_values.reshape(shape_rows),
        ]
    ).astype(jnp.bfloat16)


def shards(
    tokens,
    timestep,
    segment_ids,
    span_lengths,
    w_qkv,
    w_out_t,
    w_up,
    w_down_t,
    w_time,
    b_time,
    ln1_gain,
    ln1_bias,
    ln2_gain,
    ln2_bias,
    b_up,
    b_down,
    cotangent,
):
    def whole(w, dim):
        w = lax.all_gather(w.astype(jnp.bfloat16), "tensor", axis=dim + 1, tiled=True)
        return lax.all_gather(w, "dp", axis=dim, tiled=True)

    def part(g, dim):
        g = lax.psum_scatter(g.astype(jnp.bfloat16), "dp", scatter_dimension=dim, tiled=True)
        return lax.psum_scatter(g, "tensor", scatter_dimension=dim + 1, tiled=True).astype(jnp.float32)

    qkv_copy, out_copy, up_copy, down_copy = (
        whole(w_qkv, 1), whole(w_out_t, 0), whole(w_up, 0), whole(w_down_t, 0),
    )
    row = lax.axis_index("tensor")
    rows = tokens.shape[0]
    own_ids = lax.dynamic_slice_in_dim(segment_ids, row * rows, rows, 0)
    own_len = lax.dynamic_slice_in_dim(span_lengths, row * rows, rows, 0)
    time_emb = time_features(timestep, tokens.shape[2])
    time_proj = jnp.dot(time_emb, w_time, precision=highest) + b_time
    start = tokens.astype(jnp.float32) + time_proj[:, None, :]
    normed_one = norm_layer(start, ln1_gain, ln1_bias).astype(jnp.bfloat16)
    qkv_act = jnp.einsum(
        "nsd,cde->cnse", normed_one, qkv_copy, preferred_element_type=jnp.float32
    ).astype(jnp.bfloat16)
    mixed, log_total = lax.map(
        attend_forward, (qkv_act[0], qkv_act[1], qkv_act[2], own_ids, own_len)
    )
    attn_out = jnp.einsum("nse,de->nsd", mixed, out_copy, preferred_element_type=jnp.float32)
    middle = start + attn_out
    normed_two = norm_layer(middle, ln2_gain, ln2_bias).astype(jnp.bfloat16)
    upper = (
        jnp.einsum("nsd,df->nsf", normed_two, up_copy, preferred_element_type=jnp.float32)
        + b_up
    )
    activated = gelu_tanh(upper).astype(jnp.bfloat16)
    ffn_out = jnp.einsum("nsf,df->nsd", activated, down_copy, preferred_element_type=jnp.float32)
    layer_out = (middle + ffn_out + b_down).astype(jnp.bfloat16)
    grad_b_down = jnp.sum(cotangent.astype(jnp.float32), axis=(0, 1))
    grad_down = jnp.einsum("nsd,nsf->df", cotangent, activated, preferred_element_type=jnp.float32)
    grad_act = jnp.einsum("nsd,df->nsf", cotangent, down_copy, preferred_element_type=jnp.float32)
    gelu_value, gelu_pull = jax.vjp(gelu_tanh, upper)
    grad_upper = gelu_pull(grad_act)[0].astype(jnp.bfloat16)
    grad_bias_up = jnp.sum(grad_upper.astype(jnp.float32), axis=(0, 1))
    grad_up = jnp.einsum("nsd,nsf->df", normed_two, grad_upper, preferred_element_type=jnp.float32)
    grad_normed_two = jnp.einsum("nsf,df->nsd", grad_upper, up_copy, preferred_element_type=jnp.float32)
    norm_two_value, norm_two_pull = jax.vjp(norm_layer, middle, ln2_gain, ln2_bias)
    grad_middle_norm, grad_gain_two, grad_bias_two = norm_two_pull(grad_normed_two)
    grad_middle = cotangent.astype(jnp.float32) + grad_middle_norm
    grad_attn = grad_middle.astype(jnp.bfloat16)
    grad_out_w = jnp.einsum("nsd,nse->de", grad_attn, mixed, preferred_element_type=jnp.float32)
    grad_mixed = jnp.einsum(
        "nsd,de->nse", grad_attn, out_copy, preferred_element_type=jnp.float32
    ).astype(jnp.bfloat16)
    grad_qkv_act = lax.map(
        attend_backward,
        (qkv_act[0], qkv_act[1], qkv_act[2], grad_mixed, log_total, own_ids, own_len),
    )
    grad_qkv_w = jnp.einsum(
        "nsd,ncse->cde", normed_one, grad_qkv_act, preferred_element_type=jnp.float32
    )
    grad_normed_one = jnp.einsum(
        "ncse,cde->nsd", grad_qkv_act, qkv_copy, preferred_element_type=jnp.float32
    )
    norm_one_value, norm_one_pull = jax.vjp(norm_layer, start, ln1_gain, ln1_bias)
    grad_start_norm, grad_gain_one, grad_bias_one = norm_one_pull(grad_normed_one)
    grad_tokens = grad_middle + grad_start_norm
    grad_time_rows = jnp.sum(grad_tokens, axis=1)
    lines = jnp.concatenate([time_emb, grad_time_rows], axis=1)
    lines = lax.all_gather(lines, ("dp", "tensor"), axis=0, tiled=True)
    all_emb, all_grad = lines[:, : time_emb.shape[1]], lines[:, time_emb.shape[1] :]
    grad_time_w = jnp.dot(all_emb.T, all_grad, precision=highest)
    grad_time_bias = jnp.sum(all_grad, axis=0)
    small = jnp.concatenate(
        [grad_gain_one, grad_bias_one, grad_gain_two, grad_bias_two, grad_b_down, grad_bias_up]
    )
    small = lax.psum(small, ("dp", "tensor"))
    cuts = jnp.split(small, [tokens.shape[2] * k for k in range(1, 6)])
    return (
        layer_out,
        grad_tokens,
        part(grad_qkv_w, 1),
        part(grad_out_w, 0),
        part(grad_up, 0),
        part(grad_down, 0),
        grad_time_w,
        grad_time_bias,
        cuts[0],
        cuts[1],
        cuts[2],
        cuts[3],
        cuts[5],
        cuts[4],
    )


def solution(mesh):
    return jax.shard_map(
        shards,
        mesh=mesh,
        in_specs=(
            P(("dp", "tensor"), None, None),
            P(("dp", "tensor")),
            P("dp", None),
            P("dp"),
            P(None, "dp", "tensor"),
            P("dp", "tensor"),
            P("dp", "tensor"),
            P("dp", "tensor"),
            P(),
            P(),
            P(),
            P(),
            P(),
            P(),
            P(),
            P(),
            P(("dp", "tensor"), None, None),
        ),
        out_specs=(
            P(("dp", "tensor"), None, None),
            P(("dp", "tensor"), None, None),
            P(None, "dp", "tensor"),
            P("dp", "tensor"),
            P("dp", "tensor"),
            P("dp", "tensor"),
            P(),
            P(),
            P(),
            P(),
            P(),
            P(),
            P(),
            P(),
        ),
        check_vma=False,
    )
```

```python
import functools
import math

import jax
import jax.numpy as jnp
from jax import lax
from jax.experimental import pallas as pl
from jax.experimental.pallas import tpu as pltpu
from jax.sharding import PartitionSpec as P_

f32, bf16 = jnp.float32, jnp.bfloat16
HS = 64
TR = 256
BIG = 1e30
EPS = 1e-5
LOG2E = math.log2(math.e)
LN2 = math.log(2.0)
SCALE = 1.0 / math.sqrt(HS)


def nt_dot(a, b):
    return lax.dot_general(a, b, (((1,), (1,)), ((), ())), preferred_element_type=f32)


def tn_dot(a, b):
    return lax.dot_general(a, b, (((0,), (0,)), ((), ())), preferred_element_type=f32)


def nn_dot(a, b):
    return jnp.dot(a, b, preferred_element_type=f32)


def lane(shape):
    return lax.broadcasted_iota(jnp.int32, shape, len(shape) - 1)


def rows_of(i, n=TR):
    return pl.ds(pl.multiple_of(i * n, n), n)


def normed(x):
    mean = jnp.mean(x, axis=-1, keepdims=True)
    c = x - mean
    var = jnp.mean(c * c, axis=-1, keepdims=True)
    r = lax.rsqrt(var + EPS)
    return c * r, r


def norm_back(xhat, r, gain, gy):
    gh = gy * gain
    a = jnp.mean(gh, axis=-1, keepdims=True)
    b = jnp.mean(gh * xhat, axis=-1, keepdims=True)
    return r * (gh - a - xhat * b)


def colsum(x):
    return jnp.sum(x, axis=0, keepdims=True)


def halves(prod):
    low = lane(prod.shape) < HS
    s0 = jnp.sum(jnp.where(low, prod, 0.0), axis=-1, keepdims=True)
    s1 = jnp.sum(jnp.where(low, 0.0, prod), axis=-1, keepdims=True)
    return s0, s1


def split3(x):
    hi = x.astype(bf16)
    rest = x - hi.astype(f32)
    mid = rest.astype(bf16)
    lo = (rest - mid.astype(f32)).astype(bf16)
    return hi, mid, lo


def window(i, seq, most):
    lo = max(0, (i * TR - most + 1) // 128 * 128)
    hi = min(seq, -(-(i * TR + TR - 1 + most) // 128) * 128)
    return lo, hi


def attend_fwd(seq, most, length, qkv, qaug, kaug, mixed, lse, qq, kk, vv, hp):
    n = seq // TR
    def prep(i, _):
        r = rows_of(i)
        low = lane((TR, 128)) < HS
        q, k, v = (qkv[hp, r, 128 * c:128 * c + 128] for c in range(3))
        qa, ka = qaug[r, :], kaug[r, :]
        one = jnp.ones_like(v)
        qq[0, r, :] = jnp.where(low, q, qa)
        qq[1, r, :] = jnp.where(low, qa, q)
        kk[0, r, :] = jnp.where(low, k, ka)
        kk[1, r, :] = jnp.where(low, ka, k)
        vv[0, r, :] = jnp.where(low, v, one)
        vv[1, r, :] = jnp.where(low, one, v)
        return 0
    lax.fori_loop(0, n, prep, 0)
    for i in range(n):
        lo, hi = window(i, seq, most)
        r = slice(i * TR, i * TR + TR)
        low = lane((TR, 128)) < HS
        q, k, v = (qkv[hp, r, 128 * c:128 * c + 128].astype(f32) for c in range(3))
        own = halves(q * k)
        pad = (lax.broadcasted_iota(jnp.int32, (TR, 1), 0) + i * TR) >= length
        tops, outs = [], []
        for h in range(2):
            s = nt_dot(qq[h, r, :], kk[h, lo:hi, :])
            m = jnp.max(s, axis=-1, keepdims=True)
            m = jnp.where(pad, jnp.maximum(m, own[h]), m)
            p = jnp.exp2(s - m).astype(bf16)
            outs.append(nn_dot(p, vv[h, lo:hi, :]))
            tops.append(m)
        padf = pad.astype(f32)
        e0 = jnp.exp2(jnp.minimum(own[0] - tops[0], 0.0)).astype(bf16).astype(f32) * padf
        e1 = jnp.exp2(jnp.minimum(own[1] - tops[1], 0.0)).astype(bf16).astype(f32) * padf
        num = jnp.where(low, outs[0], outs[1]) + jnp.where(low, e0, e1) * v
        den_x = jnp.where(low, outs[1], outs[0]) + jnp.where(low, e1, e0)
        den = pltpu.roll(den_x, HS, 1)
        mixed[hp, r, :] = (num / den).astype(bf16)
        lse[hp, r, :] = jnp.where(low, tops[1], tops[0]) + jnp.log2(den_x)


def attend_bwd(seq, most, length, qkv, qaug, kaug, mixed, lse, gm, qq, kk, vv, oo, dq, dkv, dqkv, hp):
    n = seq // TR
    def prep(i, _):
        r = rows_of(i)
        low = lane((TR, 128)) < HS
        spot = lane((TR, 128)) % HS
        q, k, v = (qkv[hp, r, 128 * c:128 * c + 128] for c in range(3))
        g = gm[hp, r, :]
        d0, d1 = halves(g.astype(f32) * mixed[hp, r, :].astype(f32))
        dx = jnp.where(low, d1, d0)
        def put(base, x):
            hi, mid, lo = split3(x)
            z = jnp.where(spot == 8, hi, base)
            z = jnp.where(spot == 9, mid, z)
            return jnp.where(spot == 10, lo, z)
        zero = jnp.zeros((TR, 128), bf16)
        qa = put(qaug[r, :], lse[hp, r, :])
        oa = put(zero, dx)
        ka = kaug[r, :]
        va = jnp.where((spot >= 8) & (spot < 11), -jnp.ones_like(zero), zero)
        for ref, x, a in ((qq, q, qa), (kk, k, ka), (vv, v, va), (oo, g, oa)):
            ref[0, r, :] = jnp.where(low, x, a)
            ref[1, r, :] = jnp.where(low, a, x)
        return 0
    lax.fori_loop(0, n, prep, 0)
    for h in range(2):
        dq[h] = jnp.zeros(dq.shape[1:], f32)
    for i in range(n):
        lo, hi = window(i, seq, most)
        r = slice(i * TR, i * TR + TR)
        for h in range(2):
            st = nt_dot(kk[h, r, :], qq[h, lo:hi, :])
            pt = jnp.exp2(st)
            dpt = nt_dot(vv[h, r, :], oo[h, lo:hi, :])
            dst = (pt * dpt).astype(bf16)
            dkv[h, 0, r, :] = nn_dot(dst, qq[h, lo:hi, :])
            dkv[h, 1, r, :] = nn_dot(pt.astype(bf16), oo[h, lo:hi, :])
            dq[h, lo:hi, :] += tn_dot(dst, kk[h, r, :])
    def post(i, _):
        r = rows_of(i)
        low = lane((TR, 128)) < HS
        q, k, v = (qkv[hp, r, 128 * c:128 * c + 128].astype(f32) for c in range(3))
        g = gm[hp, r, :].astype(f32)
        pad = (lax.broadcasted_iota(jnp.int32, (TR, 1), 0) + i * TR) >= length
        padf = pad.astype(f32)
        s0, s1 = halves(q * k)
        p0, p1 = halves(g * v)
        d0, d1 = halves(g * mixed[hp, r, :].astype(f32))
        ls = pltpu.roll(lse[hp, r, :], HS, 1)
        pf = jnp.exp2(jnp.minimum(jnp.where(low, s0, s1) - ls, 1.0)) * padf
        ds = (pf * (jnp.where(low, p0, p1) - jnp.where(low, d0, d1))).astype(bf16).astype(f32)
        pf = pf.astype(bf16).astype(f32)
        gq = jnp.where(low, dq[0, r, :], dq[1, r, :]) + ds * k
        gk = jnp.where(low, dkv[0, 0, r, :], dkv[1, 0, r, :]) + ds * q
        gv = jnp.where(low, dkv[0, 1, r, :], dkv[1, 1, r, :]) + pf * g
        dqkv[r, 0:128] = (gq * SCALE).astype(bf16)
        dqkv[r, 128:256] = (gk * LN2).astype(bf16)
        dqkv[r, 256:384] = gv.astype(bf16)
        return 0
    lax.fori_loop(0, n, post, 0)


def gelu_parts(u):
    c0, c1 = 0.7978845608028654, 0.044715
    u2 = u * u
    th = jnp.tanh(u * (c0 + (c0 * c1) * u2))
    half = 0.5 + 0.5 * th
    act = u * half
    grad = half + (0.5 * u) * (1.0 - th * th) * (c0 + (3.0 * c0 * c1) * u2)
    return act, grad


def transpose_into(dst, src, seq):
    def step(i, _):
        r = rows_of(i)
        dst[:, r] = src[r, :].T
        return 0
    for i in range(seq // TR):
        r = slice(i * TR, i * TR + TR)
        dst[:, r] = src[r, :].T


def kernel(T, most, len_ref, ts_ref, tok, cot, seg, wq, wo, wu, wd, wt, btime, g1, b1, g2, b2, bdown, bup,
           out, gtok, dwq, dwo, dwu, dwd, vec,
           tp, n1, qkv, qaug, kaug, mixed, lse, qq, kk, vv, oo, dq, dkv, dqkv, mid, n2, ffn, gn, act, gu, gm, xT, xT2):
    seq, D = tok.shape
    P = wq.shape[0]
    n = seq // TR
    length = len_ref[T()]
    t = ts_ref[0].astype(f32)
    half = D // 2
    ang = t * jnp.exp(-math.log(10000.0) * lax.broadcasted_iota(jnp.int32, (8, half), 1).astype(f32) / half)
    emb = jnp.concatenate([jnp.sin(ang), jnp.cos(ang)], axis=1)
    vec[0:1, :] = emb[0:1, :]
    proj = jnp.dot(emb, wt[...], precision=lax.Precision.HIGHEST, preferred_element_type=f32)[0:1, :] + btime[...]
    tp[...] = proj
    def ln1(i, _):
        r = rows_of(i)
        xh, _r = normed(tok[r, :].astype(f32) + tp[...])
        n1[r, :] = (xh * g1[...] + b1[...]).astype(bf16)
        return 0
    lax.fori_loop(0, n, ln1, 0)
    srow = seg[pl.ds(T(), 1), :].astype(f32)
    for b in range(seq // 128):
        col = jnp.broadcast_to(srow[:, 128 * b:128 * b + 128], (128, 128)).T
        spot = lane((128, 128)) % HS
        pos = lax.broadcasted_iota(jnp.int32, (128, 128), 0) + 128 * b
        same = col == spot.astype(f32)
        r = slice(128 * b, 128 * b + 128)
        qaug[r, :] = jnp.where(same & (spot < 8), 1.0, 0.0).astype(bf16)
        ka = jnp.where(same & (pos < length), 0.0, -BIG)
        kaug[r, :] = jnp.where(spot < 8, ka, jnp.where(spot < 11, -1.0, 0.0)).astype(bf16)
    def pair_fwd(hp, _):
        def proj(i, _):
            r = rows_of(i)
            x = nn_dot(n1[r, :], wq[hp])
            s = jnp.where(lane((1, 384)) < 128, SCALE * LOG2E, 1.0)
            qkv[hp, r, :] = (x * s).astype(bf16)
            return 0
        lax.fori_loop(0, n, proj, 0)
        attend_fwd(seq, most, length, qkv, qaug, kaug, mixed, lse, qq, kk, vv, hp)
        return 0
    lax.fori_loop(0, P, pair_fwd, 0)
    def ln2(i, _):
        r = rows_of(i)
        mx = jnp.concatenate([mixed[p, r, :] for p in range(P)], axis=1)
        w = jnp.concatenate([wo[p] for p in range(P)], axis=1)
        x = tok[r, :].astype(f32) + tp[...] + nt_dot(mx, w)
        mid[r, :] = x
        xh, _r = normed(x)
        n2[r, :] = (xh * g2[...] + b2[...]).astype(bf16)
        return 0
    lax.fori_loop(0, n, ln2, 0)
    transpose_into(xT, cot, seq)
    transpose_into(xT2, n2, seq)
    for f in range(wu.shape[0]):
        F = wu.shape[2]
        def tile(i, acc):
            r = rows_of(i)
            u = nn_dot(n2[r, :], wu[f]) + bup[:, f * F:f * F + F]
            a, ga = gelu_parts(u)
            a = a.astype(bf16)
            g = (nn_dot(cot[r, :], wd[f]) * ga).astype(bf16)
            act[r, :] = a
            gu[r, :] = g
            fo = nt_dot(a, wd[f])
            go = nt_dot(g, wu[f])
            if f == 0:
                ffn[r, :] = fo
                gn[r, :] = go
            else:
                ffn[r, :] += fo
                gn[r, :] += go
            return acc + colsum(g.astype(f32))
        acc = lax.fori_loop(0, n, tile, jnp.zeros((1, F), f32))
        vec[7 + f:8 + f, :] = acc
        def wgrad(i, _):
            r = rows_of(i)
            dwd[f, r, :] = nn_dot(xT[r, :], act[...]).astype(bf16)
            dwu[f, r, :] = nn_dot(xT2[r, :], gu[...]).astype(bf16)
            return 0
        lax.fori_loop(0, D // TR, wgrad, 0)
    def ln2b(i, acc):
        r = rows_of(i)
        c = cot[r, :].astype(f32)
        x = mid[r, :]
        out[r, :] = (x + ffn[r, :] + bdown[...]).astype(bf16)
        xh, rr = normed(x)
        gy = gn[r, :]
        gmid = c + norm_back(xh, rr, g2[...], gy)
        mid[r, :] = gmid
        n2[r, :] = gmid.astype(bf16)
        return acc[0] + colsum(gy * xh), acc[1] + colsum(gy), acc[2] + colsum(c)
    z = jnp.zeros((1, D), f32)
    a = lax.fori_loop(0, n, ln2b, (z, z, z))
    vec[4:5, :], vec[5:6, :], vec[6:7, :] = a
    transpose_into(xT2, n2, seq)
    def gmix(i, _):
        r = rows_of(i)
        w = jnp.concatenate([wo[p] for p in range(P)], axis=1)
        x = nn_dot(n2[r, :], w).astype(bf16)
        for p in range(P):
            gm[p, r, :] = x[:, 128 * p:128 * p + 128]
        return 0
    lax.fori_loop(0, n, gmix, 0)
    def gwo(i, _):
        r = rows_of(i)
        m = jnp.concatenate([mixed[p] for p in range(P)], axis=1)
        x = nn_dot(xT2[r, :], m).astype(bf16)
        for p in range(P):
            dwo[p, r, :] = x[:, 128 * p:128 * p + 128]
        return 0
    lax.fori_loop(0, D // TR, gwo, 0)
    transpose_into(xT, n1, seq)
    gn[...] = jnp.zeros(gn.shape, f32)
    def pair_bwd(hp, _):
        attend_bwd(seq, most, length, qkv, qaug, kaug, mixed, lse, gm, qq, kk, vv, oo, dq, dkv, dqkv, hp)
        def wgrad(i, _):
            r = rows_of(i)
            dwq[hp, r, :] = nn_dot(xT[r, :], dqkv[...]).astype(bf16)
            return 0
        lax.fori_loop(0, D // TR, wgrad, 0)
        def back(i, _):
            r = rows_of(i)
            gn[r, :] += nt_dot(dqkv[r, :], wq[hp])
            return 0
        lax.fori_loop(0, n, back, 0)
        return 0
    lax.fori_loop(0, P, pair_bwd, 0)
    def ln1b(i, acc):
        r = rows_of(i)
        xh, rr = normed(tok[r, :].astype(f32) + tp[...])
        gy = gn[r, :]
        gt = mid[r, :] + norm_back(xh, rr, g1[...], gy)
        gtok[r, :] = gt
        return acc[0] + colsum(gt), acc[1] + colsum(gy * xh), acc[2] + colsum(gy)
    a = lax.fori_loop(0, n, ln1b, (z, z, z))
    vec[1:2, :], vec[2:3, :], vec[3:4, :] = a


def run(T, most, length, ts, tok, cot, seg, wq, wo, wu, wd, wt, btime, g1, b1, g2, b2, bdown, bup):
    seq, D = tok.shape
    P, NF, F = wq.shape[0], wu.shape[0], wu.shape[2]
    V = pltpu.VMEM
    S = jax.ShapeDtypeStruct
    scratch = [V((1, D), f32), V((seq, D), bf16), V((P, seq, 384), bf16), V((seq, 128), bf16), V((seq, 128), bf16),
        V((P, seq, 128), bf16), V((P, seq, 128), f32)] + [V((2, seq, 128), bf16)] * 4 + [V((2, seq, 128), f32),
        V((2, 2, seq, 128), f32), V((seq, 384), bf16), V((seq, D), f32), V((seq, D), bf16), V((seq, D), f32), V((seq, D), f32),
        V((seq, F), bf16), V((seq, F), bf16), V((P, seq, 128), bf16), V((D, seq), bf16), V((D, seq), bf16)]
    vm = pl.BlockSpec(memory_space=pltpu.VMEM)
    sm = pl.BlockSpec(memory_space=pltpu.SMEM)
    return pl.pallas_call(
        functools.partial(kernel, T, most),
        out_shape=(S((seq, D), bf16), S((seq, D), f32), S(wq.shape, bf16), S(wo.shape, bf16), S(wu.shape, bf16), S(wd.shape, bf16), S((16, D), f32)),
        in_specs=[sm, sm] + [vm] * 15, out_specs=[vm] * 7,
        scratch_shapes=scratch,
        compiler_params=pltpu.CompilerParams(vmem_limit_bytes=62 << 20),
    )(length, ts, tok, cot, seg, wq, wo, wu, wd, wt, btime[None], g1[None], b1[None], g2[None], b2[None], bdown[None], bup[None])


def shards(
    tokens,
    timestep,
    segment_ids,
    span_lengths,
    w_qkv,
    w_out_t,
    w_up,
    w_down_t,
    w_time,
    b_time,
    ln1_gain,
    ln1_bias,
    ln2_gain,
    ln2_bias,
    b_up,
    b_down,
    cotangent,
):
    b = lambda w: w.astype(bf16)
    rows, seq, D = tokens.shape
    HB = w_qkv.shape[2]

    def whole(w):
        return lax.all_gather(lax.all_gather(b(w), "dp", axis=0, tiled=True), "tensor", axis=0)

    def part(g):
        g = lax.psum_scatter(g, "dp", scatter_dimension=1, tiled=True)
        return lax.psum_scatter(g, "tensor", scatter_dimension=0, tiled=True)[0].astype(f32)

    wq = whole(jnp.transpose(w_qkv, (1, 0, 2)).reshape(w_qkv.shape[1], 3 * HB))
    wo, wu, wd = whole(w_out_t), whole(w_up), whole(w_down_t)
    out, gtok, dwq, dwo, dwu, dwd, vec = run(
        lambda: lax.axis_index("tensor"), seq // 2, span_lengths, timestep, tokens[0], cotangent[0], segment_ids,
        wq, wo, wu, wd, w_time, b_time, ln1_gain, ln1_bias, ln2_gain, ln2_bias, b_down, b_up)
    lines = lax.all_gather(vec[:2], ("dp", "tensor"), axis=1, tiled=False)
    gwt = jnp.dot(lines[0].T, lines[1], precision=lax.Precision.HIGHEST)
    small = lax.psum(vec[1:], ("dp", "tensor"))
    gq = part(dwq)
    return (
        out[None], gtok[None], jnp.transpose(gq.reshape(gq.shape[0], 3, HB), (1, 0, 2)), part(dwo), part(dwu), part(dwd),
        gwt, small[0], small[1], small[2], small[3], small[4], small[6:10].reshape(-1), small[5])


def solution(mesh):
    return jax.shard_map(
        shards,
        mesh=mesh,
        in_specs=(
            P_(("dp", "tensor"), None, None),
            P_(("dp", "tensor")),
            P_("dp", None),
            P_("dp"),
            P_(None, "dp", "tensor"),
            P_("dp", "tensor"),
            P_("dp", "tensor"),
            P_("dp", "tensor"),
            P_(),
            P_(),
            P_(),
            P_(),
            P_(),
            P_(),
            P_(),
            P_(),
            P_(("dp", "tensor"), None, None),
        ),
        out_specs=(
            P_(("dp", "tensor"), None, None),
            P_(("dp", "tensor"), None, None),
            P_(None, "dp", "tensor"),
            P_("dp", "tensor"),
            P_("dp", "tensor"),
            P_("dp", "tensor"),
            P_(),
            P_(),
            P_(),
            P_(),
            P_(),
            P_(),
            P_(),
            P_(),
        ),
        check_vma=False,
    )
```

```python
import functools
import math

import jax
import jax.numpy as jnp
from jax import lax
from jax.experimental import pallas as pl
from jax.experimental.pallas import tpu as pltpu
from jax.sharding import PartitionSpec as P_

f32, bf16 = jnp.float32, jnp.bfloat16
HS = 64
TR = 256
BIG = 1e30
EPS = 1e-5
DOC = 512
LOG2E = math.log2(math.e)
LN2 = math.log(2.0)
SCALE = 1.0 / math.sqrt(HS)


def nt_dot(a, b):
    return lax.dot_general(a, b, (((1,), (1,)), ((), ())), preferred_element_type=f32)


def tn_dot(a, b):
    return lax.dot_general(a, b, (((0,), (0,)), ((), ())), preferred_element_type=f32)


def nn_dot(a, b):
    return jnp.dot(a, b, preferred_element_type=f32)


def lane(shape):
    return lax.broadcasted_iota(jnp.int32, shape, len(shape) - 1)


def rows_of(i, n=TR):
    return pl.ds(pl.multiple_of(i * n, n), n)


def normed(x):
    mean = jnp.mean(x, axis=-1, keepdims=True)
    c = x - mean
    var = jnp.mean(c * c, axis=-1, keepdims=True)
    r = lax.rsqrt(var + EPS)
    return c * r, r


def norm_back(xhat, r, gain, gy):
    gh = gy * gain
    a = jnp.mean(gh, axis=-1, keepdims=True)
    b = jnp.mean(gh * xhat, axis=-1, keepdims=True)
    return r * (gh - a - xhat * b)


def colsum(x):
    return jnp.sum(x, axis=0, keepdims=True)


def halves(prod):
    low = lane(prod.shape) < HS
    s0 = jnp.sum(jnp.where(low, prod, 0.0), axis=-1, keepdims=True)
    s1 = jnp.sum(jnp.where(low, 0.0, prod), axis=-1, keepdims=True)
    return s0, s1


def split3(x):
    hi = x.astype(bf16)
    rest = x - hi.astype(f32)
    mid = rest.astype(bf16)
    lo = (rest - mid.astype(f32)).astype(bf16)
    return hi, mid, lo


def window(i, seq, most):
    lo = max(0, (i * TR - most + 1) // 128 * 128)
    hi = min(seq, -(-(i * TR + TR - 1 + most) // 128) * 128)
    return lo, hi


def attend_fwd(seq, most, length, qkv, qaug, kaug, mixed, lse, qq, kk, vv, hp):
    n = seq // TR
    def prep(i, _):
        r = rows_of(i)
        low = lane((TR, 128)) < HS
        q, k, v = (qkv[hp, r, 128 * c:128 * c + 128] for c in range(3))
        qa, ka = qaug[r, :], kaug[r, :]
        one = jnp.ones_like(v)
        qq[0, r, :] = jnp.where(low, q, qa)
        qq[1, r, :] = jnp.where(low, qa, q)
        kk[0, r, :] = jnp.where(low, k, ka)
        kk[1, r, :] = jnp.where(low, ka, k)
        vv[0, r, :] = jnp.where(low, v, one)
        vv[1, r, :] = jnp.where(low, one, v)
        return 0
    lax.fori_loop(0, n, prep, 0)
    for i in range(n):
        lo, hi = window(i, seq, most)
        r = slice(i * TR, i * TR + TR)
        low = lane((TR, 128)) < HS
        q, k, v = (qkv[hp, r, 128 * c:128 * c + 128].astype(f32) for c in range(3))
        own = halves(q * k)
        pad = (lax.broadcasted_iota(jnp.int32, (TR, 1), 0) + i * TR) >= length
        tops, outs = [], []
        for h in range(2):
            s = nt_dot(qq[h, r, :], kk[h, lo:hi, :])
            m = jnp.max(s, axis=-1, keepdims=True)
            m = jnp.where(pad, jnp.maximum(m, own[h]), m)
            p = jnp.exp2(s - m).astype(bf16)
            outs.append(nn_dot(p, vv[h, lo:hi, :]))
            tops.append(m)
        padf = pad.astype(f32)
        e0 = jnp.exp2(jnp.minimum(own[0] - tops[0], 0.0)).astype(bf16).astype(f32) * padf
        e1 = jnp.exp2(jnp.minimum(own[1] - tops[1], 0.0)).astype(bf16).astype(f32) * padf
        num = jnp.where(low, outs[0], outs[1]) + jnp.where(low, e0, e1) * v
        den_x = jnp.where(low, outs[1], outs[0]) + jnp.where(low, e1, e0)
        den = pltpu.roll(den_x, HS, 1)
        mixed[hp, r, :] = (num / den).astype(bf16)
        lse[hp, r, :] = jnp.where(low, tops[1], tops[0]) + jnp.log2(den_x)


def attend_bwd(seq, most, length, qkv, qaug, kaug, mixed, lse, gm, qq, kk, vv, oo, dq, dkv, dqkv, hp):
    n = seq // TR
    def prep(i, _):
        r = rows_of(i)
        low = lane((TR, 128)) < HS
        spot = lane((TR, 128)) % HS
        q, k, v = (qkv[hp, r, 128 * c:128 * c + 128] for c in range(3))
        g = gm[hp, r, :]
        d0, d1 = halves(g.astype(f32) * mixed[hp, r, :].astype(f32))
        dx = jnp.where(low, d1, d0)
        def put(base, x):
            hi, mid, lo = split3(x)
            z = jnp.where(spot == 8, hi, base)
            z = jnp.where(spot == 9, mid, z)
            return jnp.where(spot == 10, lo, z)
        zero = jnp.zeros((TR, 128), bf16)
        qa = put(qaug[r, :], lse[hp, r, :])
        oa = put(zero, dx)
        ka = kaug[r, :]
        va = jnp.where((spot >= 8) & (spot < 11), -jnp.ones_like(zero), zero)
        for ref, x, a in ((qq, q, qa), (kk, k, ka), (vv, v, va), (oo, g, oa)):
            ref[0, r, :] = jnp.where(low, x, a)
            ref[1, r, :] = jnp.where(low, a, x)
        return 0
    lax.fori_loop(0, n, prep, 0)
    for h in range(2):
        dq[h] = jnp.zeros(dq.shape[1:], f32)
    for i in range(n):
        lo, hi = window(i, seq, most)
        r = slice(i * TR, i * TR + TR)
        for h in range(2):
            st = nt_dot(kk[h, r, :], qq[h, lo:hi, :])
            pt = jnp.exp2(st)
            dpt = nt_dot(vv[h, r, :], oo[h, lo:hi, :])
            dst = (pt * dpt).astype(bf16)
            dkv[h, 0, r, :] = nn_dot(dst, qq[h, lo:hi, :])
            dkv[h, 1, r, :] = nn_dot(pt.astype(bf16), oo[h, lo:hi, :])
            dq[h, lo:hi, :] += tn_dot(dst, kk[h, r, :])
    def post(i, _):
        r = rows_of(i)
        low = lane((TR, 128)) < HS
        q, k, v = (qkv[hp, r, 128 * c:128 * c + 128].astype(f32) for c in range(3))
        g = gm[hp, r, :].astype(f32)
        pad = (lax.broadcasted_iota(jnp.int32, (TR, 1), 0) + i * TR) >= length
        padf = pad.astype(f32)
        s0, s1 = halves(q * k)
        p0, p1 = halves(g * v)
        d0, d1 = halves(g * mixed[hp, r, :].astype(f32))
        ls = pltpu.roll(lse[hp, r, :], HS, 1)
        pf = jnp.exp2(jnp.minimum(jnp.where(low, s0, s1) - ls, 1.0)) * padf
        ds = (pf * (jnp.where(low, p0, p1) - jnp.where(low, d0, d1))).astype(bf16).astype(f32)
        pf = pf.astype(bf16).astype(f32)
        gq = jnp.where(low, dq[0, r, :], dq[1, r, :]) + ds * k
        gk = jnp.where(low, dkv[0, 0, r, :], dkv[1, 0, r, :]) + ds * q
        gv = jnp.where(low, dkv[0, 1, r, :], dkv[1, 1, r, :]) + pf * g
        dqkv[r, 0:128] = (gq * SCALE).astype(bf16)
        dqkv[r, 128:256] = (gk * LN2).astype(bf16)
        dqkv[r, 256:384] = gv.astype(bf16)
        return 0
    lax.fori_loop(0, n, post, 0)


def gelu_parts(u):
    c0, c1 = 0.7978845608028654, 0.044715
    u2 = u * u
    th = jnp.tanh(u * (c0 + (c0 * c1) * u2))
    half = 0.5 + 0.5 * th
    act = u * half
    grad = half + (0.5 * u) * (1.0 - th * th) * (c0 + (3.0 * c0 * c1) * u2)
    return act, grad


def transpose_into(dst, src, seq):
    def step(i, _):
        r = rows_of(i)
        dst[:, r] = src[r, :].T
        return 0
    for i in range(seq // TR):
        r = slice(i * TR, i * TR + TR)
        dst[:, r] = src[r, :].T


MESH = pl.DeviceIdType.MESH


class Plain:
    def __init__(self, wq, wo, w2, dwq, dwo, dw2, vec):
        self.wq, self.wo, self.w2 = wq, wo, w2
        self.dwq, self.dwo, self.dw2, self.vec = dwq, dwo, dw2, vec

    def getq(self, p):
        return self.wq[p]

    def geto(self):
        return jnp.concatenate([self.wo[p] for p in range(self.wo.shape[0])], axis=1)

    def getu(self, f):
        return self.w2[f, 0]

    def getd(self, f):
        return self.w2[f, 1]

    def putq(self, p, i, x):
        self.dwq[p, rows_of(i), :] = x

    def puto(self, p, i, x):
        self.dwo[p, rows_of(i), :] = x

    def put2(self, f, k, i, x):
        self.dw2[f, k, rows_of(i), :] = x

    def order(self, j):
        return j

    def order_back(self, j):
        return j

    def hook(self, *_):
        pass

    def early(self, rows):
        for k, x in enumerate(rows):
            self.vec[k:k + 1, :] = x

    def late(self, rows):
        for k, x in enumerate(rows):
            self.vec[8 + k:9 + k, :] = x


class Linked:
    def __init__(self, ng, nt, bufs, sems):
        self.ng, self.nt = ng, nt
        self.__dict__.update(bufs)
        self.sem = sems
        d, self.t = lax.axis_index("dp"), lax.axis_index("tensor")
        self.d, self.g, self.c = d, d // 2, d % 2
        self.sent = []

    def dev(self, kind, k):
        if kind == "core":
            return (2 * self.g + 1 - self.c, self.t)
        if kind == "plane":
            return (2 * (self.g ^ k) + self.c, self.t)
        return (self.d, self.t ^ k)

    def copy(self, name, at, kind, k, src, dst):
        s, r = self.sem[name]
        for i in at:
            s, r = s.at[i], r.at[i]
        return pltpu.make_async_remote_copy(
            src_ref=src, dst_ref=dst, send_sem=s, recv_sem=r,
            device_id=self.dev(kind, k), device_id_type=MESH)

    def getq(self, p):
        x = self.WQ[p]
        return x.reshape(-1, x.shape[-1])

    def geto(self):
        return jnp.concatenate([self.WO[p].reshape(-1, 128) for p in range(self.nt)], axis=1)

    def getu(self, f):
        x = self.W2[f, 0]
        return x.reshape(-1, x.shape[-1])

    def getd(self, f):
        x = self.W2[f, 1]
        return x.reshape(-1, x.shape[-1])

    def blocks(self, ref, i):
        rows = ref.shape[-2]
        m = TR // (2 * rows)
        return pl.ds(i * m, m), (m, 2, rows, ref.shape[-1])

    def putq(self, p, i, x):
        b, shape = self.blocks(self.DQ, i)
        self.DQ[p, b] = x.reshape(shape)

    def puto(self, p, i, x):
        b, shape = self.blocks(self.DO, i)
        self.DO[p, b] = x.reshape(shape)

    def put2(self, f, k, i, x):
        b, shape = self.blocks(self.D2, i)
        self.D2[f, k, b] = x.reshape(shape)

    def order(self, j):
        return self.t ^ j

    def order_back(self, j):
        return self.t ^ (self.nt - 1 - j)

    def enter(self):
        bar = pltpu.get_barrier_semaphore()
        peers = [("core", 0)] + [("plane", k) for k in range(1, self.ng)] + [("z", k) for k in range(1, self.nt)]
        for kind, k in peers:
            pl.semaphore_signal(bar, inc=1, device_id=self.dev(kind, k), device_id_type=MESH)
        pl.semaphore_wait(bar, len(peers))

    def q_plane(self, k):
        g, c, t = self.g, self.c, self.t
        return self.copy("gq_plane", (k,), "plane", k, self.WQ.at[t, g, c], self.WQ.at[t, g, c])

    def q_plane_in(self, k):
        g, c, t = self.g, self.c, self.t
        return self.copy("gq_plane", (k,), "plane", k, self.WQ.at[t, g, c], self.WQ.at[t, g ^ k, c])

    def q_z(self, k):
        c, t = self.c, self.t
        return self.copy("gq_z", (k,), "z", k, self.WQ.at[t, :, c], self.WQ.at[t, :, c])

    def q_z_in(self, k):
        c, t = self.c, self.t
        return self.copy("gq_z", (k,), "z", k, self.WQ.at[t, :, c], self.WQ.at[t ^ k, :, c])

    def q_core(self, k):
        c, t = self.c, self.t
        return self.copy("gq_core", (k,), "core", 0, self.WQ.at[t ^ k, :, c], self.WQ.at[t ^ k, :, c])

    def q_core_in(self, k):
        c, t = self.c, self.t
        return self.copy("gq_core", (k,), "core", 0, self.WQ.at[t ^ k, :, c], self.WQ.at[t ^ k, :, 1 - c])

    def r_z(self, k, into=None):
        g, c, t = self.g, self.c, self.t
        u = t if into is None else into
        return [self.copy("go_z", (k,), "z", k, self.WO.at[t, g, c], self.WO.at[u, g, c]),
                self.copy("g2_z", (k,), "z", k, self.W2.at[t, :, g, c], self.W2.at[u, :, g, c])]

    def o_plane(self, k, incoming=False):
        g, c = self.g, self.c
        return self.copy("go_plane", (k,), "plane", k, self.WO.at[:, g, c], self.WO.at[:, g ^ k if incoming else g, c])

    def o_core(self, incoming=False):
        c = self.c
        return self.copy("go_core", (), "core", 0, self.WO.at[:, :, c], self.WO.at[:, :, 1 - c if incoming else c])

    def f_plane(self, j, k, incoming=False):
        g, c, f = self.g, self.c, self.t ^ j
        return self.copy("g2_plane", (j, k), "plane", k, self.W2.at[f, :, g, c], self.W2.at[f, :, g ^ k if incoming else g, c])

    def f_core(self, j, incoming=False):
        c, f = self.c, self.t ^ j
        return self.copy("g2_core", (j,), "core", 0, self.W2.at[f, :, :, c], self.W2.at[f, :, :, 1 - c if incoming else c])

    def rq(self, stage, x, k=0, incoming=False):
        g, c, p = self.g, self.c, self.t ^ x
        if stage == "core":
            return self.copy("rq_core", (x,), "core", 0, self.DQ.at[p, :, 1 - c], self.CQ.at[x])
        if stage == "plane":
            return self.copy("rq_plane", (x, k), "plane", k, self.DQ.at[p, g ^ k, c], self.XQ.at[x, k])
        return self.copy("rq_z", (x,), "z", x, self.DQ.at[p, g, c], self.ZQ.at[x])

    def r2(self, stage, x, k=0):
        g, c, p = self.g, self.c, self.t ^ x
        if stage == "core":
            return self.copy("r2_core", (x,), "core", 0, self.D2.at[p, :, :, 1 - c], self.C2.at[x])
        if stage == "plane":
            return self.copy("r2_plane", (x, k), "plane", k, self.D2.at[p, :, g ^ k, c], self.X2.at[x, k])
        return self.copy("r2_z", (x,), "z", x, self.D2.at[p, :, g, c], self.Z2.at[x])

    def ro(self, stage, k=0):
        g, c, t = self.g, self.c, self.t
        if stage == "core":
            return self.copy("ro_core", (), "core", 0, self.DO.at[:, :, 1 - c], self.CO)
        if stage == "plane":
            return self.copy("ro_plane", (k,), "plane", k, self.DO.at[:, g ^ k, c], self.XO.at[k])
        return self.copy("ro_z", (k,), "z", k, self.DO.at[t ^ k, g, c], self.ZO.at[k])

    def q_after_core(self, x):
        p, c = self.t ^ x, self.c
        self.rq("core", x).wait_recv()
        self.DQ[p, :, c] = (self.DQ[p, :, c].astype(f32) + self.CQ[x].astype(f32)).astype(bf16)
        for k in range(1, self.ng):
            self.rq("plane", x, k).start()

    def q_after_plane(self, x):
        p, c, g = self.t ^ x, self.c, self.g
        acc = self.DQ[p, g, c].astype(f32)
        for k in range(1, self.ng):
            self.rq("plane", x, k).wait_recv()
            acc = acc + self.XQ[x, k].astype(f32)
        self.DQ[p, g, c] = acc.astype(bf16)

    def f_after_core(self, x):
        p, c = self.t ^ x, self.c
        self.r2("core", x).wait_recv()
        for u in range(2):
            def step(i, _):
                self.D2[p, u, i, c] = (self.D2[p, u, i, c].astype(f32) + self.C2[x, u, i].astype(f32)).astype(bf16)
                return 0
            lax.fori_loop(0, self.ng, step, 0)
        for k in range(1, self.ng):
            self.r2("plane", x, k).start()

    def f_after_plane(self, x):
        p, c, g = self.t ^ x, self.c, self.g
        for k in range(1, self.ng):
            self.r2("plane", x, k).wait_recv()
        for u in range(2):
            acc = self.D2[p, u, g, c].astype(f32)
            for k in range(1, self.ng):
                acc = acc + self.X2[x, k, u].astype(f32)
            self.D2[p, u, g, c] = acc.astype(bf16)

    def hook(self, place, j=None):
        ng, nt, t, g, c = self.ng, self.nt, self.t, self.g, self.c
        if place == "start":
            rq = self.w_qkv.shape[1]
            for k in range(3):
                self.WQ[t, g, c, :, 128 * k:128 * k + 128] = self.w_qkv[k].astype(bf16)
            self.WO[t, g, c] = self.w_out[...].astype(bf16)
            self.W2[t, 0, g, c] = self.w_up[...].astype(bf16)
            self.W2[t, 1, g, c] = self.w_down[...].astype(bf16)
            self.enter()
            for k in range(1, ng):
                self.q_plane(k).start()
        elif place == "normed":
            for k in range(1, ng):
                self.q_plane_in(k).wait_recv()
            self.q_core(0).start()
            for k in range(1, nt):
                self.q_z(k).start()
            for k in range(1, nt):
                for x in self.r_z(k):
                    x.start()
        elif place == "pair":
            self.q_core_in(j).wait_recv()
        elif place == "pair_mid":
            @pl.when(j < nt - 1)
            def _():
                self.q_z_in(j + 1).wait_recv()
                self.q_core(j + 1).start()
            @pl.when(j == nt // 2)
            def _():
                for k in range(1, nt):
                    for x in self.r_z(k, t ^ k):
                        x.wait_recv()
                for k in range(1, ng):
                    self.o_plane(k).start()
                for x in range(nt):
                    for k in range(1, ng):
                        self.f_plane(x, k).start()
        elif place == "mixed":
            for k in range(1, ng):
                self.o_plane(k, True).wait_recv()
            self.o_core().start()
            for k in range(1, ng):
                self.f_plane(0, k, True).wait_recv()
            self.f_core(0).start()
            self.o_core(True).wait_recv()
        elif place == "chunk":
            self.f_core(j, True).wait_recv()
        elif place == "chunk_mid":
            @pl.when(j < nt - 1)
            def _():
                for k in range(1, ng):
                    self.f_plane(j + 1, k, True).wait_recv()
                self.f_core(j + 1).start()
            @pl.when(j >= 1)
            def _():
                self.f_after_core(j - 1)
            @pl.when(j >= 2)
            def _():
                self.f_after_plane(j - 2)
                @pl.when(j >= 3)
                def _():
                    self.r2("z", j - 2).start()
        elif place == "chunk_end":
            self.r2("core", j).start()
        elif place == "ffn_done":
            self.f_after_core(nt - 1)
            self.f_after_plane(nt - 2)
            self.r2("z", nt - 2).start()
        elif place == "out_grad":
            self.ro("core").start()
        elif place == "back_mid":
            @pl.when(j == 0)
            def _():
                self.f_after_plane(nt - 1)
                self.r2("z", nt - 1).start()
                self.ro("core").wait_recv()
                for p in range(nt):
                    self.DO[p, :, c] = (self.DO[p, :, c].astype(f32) + self.CO[p].astype(f32)).astype(bf16)
                for k in range(1, ng):
                    self.ro("plane", k).start()
            @pl.when(j == 1)
            def _():
                for k in range(1, ng):
                    self.ro("plane", k).wait_recv()
                for p in range(nt):
                    acc = self.DO[p, g, c].astype(f32)
                    for k in range(1, ng):
                        acc = acc + self.XO[k, p].astype(f32)
                    self.DO[p, g, c] = acc.astype(bf16)
                for k in range(1, nt):
                    self.ro("z", k).start()
            @pl.when(j >= 1)
            def _():
                self.q_after_core(nt - j)
            @pl.when(j >= 2)
            def _():
                self.q_after_plane(nt - j + 1)
                self.rq("z", nt - j + 1).start()
        elif place == "back_end":
            self.rq("core", nt - 1 - j).start()
        elif place == "back_done":
            self.q_after_core(0)
            self.q_after_plane(1)
            self.rq("z", 1).start()
        elif place == "finish":
            for x in range(1, nt):
                self.r2("z", x).wait_recv()
                self.ro("z", x).wait_recv()
            for u, o in enumerate((self.o_up, self.o_down)):
                acc = self.D2[t, u, g, c].astype(f32)
                for x in range(1, nt):
                    acc = acc + self.Z2[x, u].astype(f32)
                o[...] = acc
            acc = self.DO[t, g, c].astype(f32)
            for x in range(1, nt):
                acc = acc + self.ZO[x].astype(f32)
            self.o_out[...] = acc
            acc = self.DQ[t, g, c].astype(f32)
            for k in range(1, ng):
                self.rq("plane", 0, k).wait_recv()
                acc = acc + self.XQ[0, k].astype(f32)
            for x in range(1, nt):
                self.rq("z", x).wait_recv()
                acc = acc + self.ZQ[x].astype(f32)
            for k in range(3):
                self.o_qkv[k] = acc[:, 128 * k:128 * k + 128]
        elif place == "leave":
            for k in range(1, ng):
                self.q_plane(k).wait_send()
                self.o_plane(k).wait_send()
                self.ro("plane", k).wait_send()
                for x in range(nt):
                    self.f_plane(x, k).wait_send()
                    self.r2("plane", x, k).wait_send()
                    self.rq("plane", x, k).wait_send()
            for k in range(nt):
                self.q_core(k).wait_send()
                self.f_core(k).wait_send()
                self.r2("core", k).wait_send()
                self.rq("core", k).wait_send()
            self.o_core().wait_send()
            self.ro("core").wait_send()
            for k in range(1, nt):
                self.q_z(k).wait_send()
                for x in self.r_z(k):
                    x.wait_send()
                self.r2("z", k).wait_send()
                self.rq("z", k).wait_send()
                self.ro("z", k).wait_send()

    def v(self, name, stage, k):
        B = getattr(self, name)
        Z, X, C = B
        if stage == "z":
            return self.copy(name + "_z", (k,), "z", k, Z.at[self.t], Z.at[self.t])
        if stage == "plane":
            return self.copy(name + "_plane", (k,), "plane", k, X.at[self.g], X.at[self.g])
        return self.copy(name + "_core", (), "core", 0, C.at[self.c], C.at[self.c])

    def v_in(self, name, stage, k):
        Z, X, C = getattr(self, name)
        if stage == "z":
            return self.copy(name + "_z", (k,), "z", k, Z.at[self.t], Z.at[self.t ^ k])
        if stage == "plane":
            return self.copy(name + "_plane", (k,), "plane", k, X.at[self.g], X.at[self.g ^ k])
        return self.copy(name + "_core", (), "core", 0, C.at[self.c], C.at[1 - self.c])

    def v_start(self, name, rows):
        Z = getattr(self, name)[0]
        for k, x in enumerate(rows):
            Z[self.t, k:k + 1, :] = x
        for k in range(1, self.nt):
            self.v(name, "z", k).start()

    def v_mid(self, name, m):
        Z, X, C = getattr(self, name)
        nt = self.nt
        for k in range(1, nt):
            self.v_in(name, "z", k).wait_recv()
        for k in range(nt):
            X[self.g, k:k + 1, :] = Z[k, 0:1, :]
        s = Z[0, 1:m, :]
        for k in range(1, nt):
            s = s + Z[k, 1:m, :]
        X[self.g, 8:8 + m - 1, :] = s
        for k in range(1, self.ng):
            self.v(name, "plane", k).start()

    def v_last(self, name, m):
        Z, X, C = getattr(self, name)
        nt, ng = self.nt, self.ng
        for k in range(1, ng):
            self.v_in(name, "plane", k).wait_recv()
        for k in range(ng):
            C[self.c, k * nt:k * nt + nt, :] = X[k, 0:nt, :]
        s = X[0, 8:8 + m - 1, :]
        for k in range(1, ng):
            s = s + X[k, 8:8 + m - 1, :]
        C[self.c, ng * nt:ng * nt + m - 1, :] = s
        self.v(name, "core", 0).start()

    def v_done(self, name, m):
        C = getattr(self, name)[2]
        n = self.nt * self.ng
        self.v_in(name, "core", 0).wait_recv()
        kept = jnp.concatenate([C[0, 0:n, :], C[1, 0:n, :]], axis=0)
        return kept, C[0, n:n + m - 1, :] + C[1, n:n + m - 1, :]

    def v_leave(self, name):
        for k in range(1, self.nt):
            self.v(name, "z", k).wait_send()
        for k in range(1, self.ng):
            self.v(name, "plane", k).wait_send()
        self.v(name, "core", 0).wait_send()


def layer(cm, T, most, length, t, tok, cot, seg, wt, btime, g1, b1, g2, b2, bdown, bup, out, gtok, sc):
    tp, n1, qkv, qaug, kaug, mixed, lse, qq, kk, vv, oo, dq, dkv, dqkv, mid, n2, ffn, gn, act, gu, gm, xT, xT2, bsum = sc
    seq, D = tok.shape
    P = qkv.shape[0]
    NF, F = bsum.shape[0], bsum.shape[2]
    n = seq // TR
    cm.hook("start")
    half = D // 2
    ang = t * jnp.exp(-math.log(10000.0) * lax.broadcasted_iota(jnp.int32, (8, half), 1).astype(f32) / half)
    emb = jnp.concatenate([jnp.sin(ang), jnp.cos(ang)], axis=1)
    tp[...] = jnp.dot(emb, wt[...], precision=lax.Precision.HIGHEST, preferred_element_type=f32)[0:1, :] + btime[...]

    def ln1(i, _):
        r = rows_of(i)
        xh, _r = normed(tok[r, :].astype(f32) + tp[...])
        n1[r, :] = (xh * g1[...] + b1[...]).astype(bf16)
        return 0

    lax.fori_loop(0, n, ln1, 0)
    cm.hook("normed")
    srow = seg[pl.ds(T, 1), :].astype(f32)
    for b in range(seq // 128):
        col = jnp.broadcast_to(srow[:, 128 * b:128 * b + 128], (128, 128)).T
        spot = lane((128, 128)) % HS
        pos = lax.broadcasted_iota(jnp.int32, (128, 128), 0) + 128 * b
        same = col == spot.astype(f32)
        r = slice(128 * b, 128 * b + 128)
        qaug[r, :] = jnp.where(same & (spot < 8), 1.0, 0.0).astype(bf16)
        ka = jnp.where(same & (pos < length), 0.0, -BIG)
        kaug[r, :] = jnp.where(spot < 8, ka, jnp.where(spot < 11, -1.0, 0.0)).astype(bf16)

    def pair_fwd(j, _):
        hp = cm.order(j)
        cm.hook("pair", j)

        def proj(i, _):
            r = rows_of(i)
            x = nn_dot(n1[r, :], cm.getq(hp))
            s = jnp.where(lane((1, 384)) < 128, SCALE * LOG2E, 1.0)
            qkv[hp, r, :] = (x * s).astype(bf16)
            return 0

        lax.fori_loop(0, n, proj, 0)
        attend_fwd(seq, most, length, qkv, qaug, kaug, mixed, lse, qq, kk, vv, hp)
        cm.hook("pair_mid", j)
        return 0

    lax.fori_loop(0, P, pair_fwd, 0)
    cm.hook("mixed")

    def ln2(i, _):
        r = rows_of(i)
        mx = jnp.concatenate([mixed[p, r, :] for p in range(P)], axis=1)
        x = tok[r, :].astype(f32) + tp[...] + nt_dot(mx, cm.geto())
        mid[r, :] = x
        xh, _r = normed(x)
        n2[r, :] = (xh * g2[...] + b2[...]).astype(bf16)
        ffn[r, :] = jnp.zeros((TR, D), f32)
        gn[r, :] = jnp.zeros((TR, D), f32)
        return 0

    lax.fori_loop(0, n, ln2, 0)
    transpose_into(xT, cot, seq)
    transpose_into(xT2, n2, seq)

    def chunk(j, _):
        f = cm.order(j)
        cm.hook("chunk", j)

        def tile(i, acc):
            r = rows_of(i)
            u = nn_dot(n2[r, :], cm.getu(f)) + bup[f]
            a, ga = gelu_parts(u)
            a = a.astype(bf16)
            g = (nn_dot(cot[r, :], cm.getd(f)) * ga).astype(bf16)
            act[r, :] = a
            gu[r, :] = g
            ffn[r, :] += nt_dot(a, cm.getd(f))
            gn[r, :] += nt_dot(g, cm.getu(f))
            return acc + colsum(g.astype(f32))

        bsum[f] = lax.fori_loop(0, n, tile, jnp.zeros((1, F), f32))
        cm.hook("chunk_mid", j)

        def wgrad(i, _):
            r = rows_of(i)
            cm.put2(f, 1, i, nn_dot(xT[r, :], act[...]).astype(bf16))
            cm.put2(f, 0, i, nn_dot(xT2[r, :], gu[...]).astype(bf16))
            return 0

        lax.fori_loop(0, D // TR, wgrad, 0)
        cm.hook("chunk_end", j)
        return 0

    lax.fori_loop(0, NF, chunk, 0)

    def ln2b(i, acc):
        r = rows_of(i)
        c = cot[r, :].astype(f32)
        x = mid[r, :]
        out[r, :] = (x + ffn[r, :] + bdown[...]).astype(bf16)
        xh, rr = normed(x)
        gy = gn[r, :]
        gmid = c + norm_back(xh, rr, g2[...], gy)
        mid[r, :] = gmid
        n2[r, :] = gmid.astype(bf16)
        gn[r, :] = jnp.zeros((TR, D), f32)
        return acc[0] + colsum(gy * xh), acc[1] + colsum(gy), acc[2] + colsum(c)

    z = jnp.zeros((1, D), f32)
    a = lax.fori_loop(0, n, ln2b, (z, z, z))
    cm.early([emb[0:1, :], *a] + [bsum[f] for f in range(NF)])
    cm.hook("ffn_done")
    transpose_into(xT2, n2, seq)

    def gmix(i, _):
        r = rows_of(i)
        x = nn_dot(n2[r, :], cm.geto()).astype(bf16)
        for p in range(P):
            gm[p, r, :] = x[:, 128 * p:128 * p + 128]
        return 0

    lax.fori_loop(0, n, gmix, 0)

    def gwo(i, _):
        r = rows_of(i)
        m = jnp.concatenate([mixed[p] for p in range(P)], axis=1)
        x = nn_dot(xT2[r, :], m).astype(bf16)
        for p in range(P):
            cm.puto(p, i, x[:, 128 * p:128 * p + 128])
        return 0

    lax.fori_loop(0, D // TR, gwo, 0)
    cm.hook("out_grad")
    transpose_into(xT, n1, seq)

    def pair_bwd(j, _):
        hp = cm.order_back(j)
        attend_bwd(seq, most, length, qkv, qaug, kaug, mixed, lse, gm, qq, kk, vv, oo, dq, dkv, dqkv, hp)
        cm.hook("back_mid", j)

        def wgrad(i, _):
            cm.putq(hp, i, nn_dot(xT[rows_of(i), :], dqkv[...]).astype(bf16))
            return 0

        lax.fori_loop(0, D // TR, wgrad, 0)
        cm.hook("back_end", j)

        def back(i, _):
            r = rows_of(i)
            gn[r, :] += nt_dot(dqkv[r, :], cm.getq(hp))
            return 0

        lax.fori_loop(0, n, back, 0)
        return 0

    lax.fori_loop(0, P, pair_bwd, 0)
    cm.hook("back_done")

    def ln1b(i, acc):
        r = rows_of(i)
        xh, rr = normed(tok[r, :].astype(f32) + tp[...])
        gy = gn[r, :]
        gt = mid[r, :] + norm_back(xh, rr, g1[...], gy)
        gtok[r, :] = gt
        return acc[0] + colsum(gt), acc[1] + colsum(gy * xh), acc[2] + colsum(gy)

    a = lax.fori_loop(0, n, ln1b, (z, z, z))
    cm.late(list(a))


def layer_scratch(seq, D, P, NF, F):
    V = pltpu.VMEM
    return [V((1, D), f32), V((seq, D), bf16), V((P, seq, 384), bf16), V((seq, 128), bf16), V((seq, 128), bf16),
        V((P, seq, 128), bf16), V((P, seq, 128), f32)] + [V((2, seq, 128), bf16)] * 4 + [V((2, seq, 128), f32),
        V((2, 2, seq, 128), f32), V((seq, 384), bf16), V((seq, D), f32), V((seq, D), bf16), V((seq, D), f32), V((seq, D), f32),
        V((seq, F), bf16), V((seq, F), bf16), V((P, seq, 128), bf16), V((D, seq), bf16), V((D, seq), bf16), V((NF, 1, F), f32)]


def plain_kernel(most, n_sc, *refs):
    len_ref, ts_ref, tok, cot, seg, wq, wo, w2, wt, btime, g1, b1, g2, b2, bdown, bup, out, gtok, dwq, dwo, dw2, vec = refs[:22]
    T = lax.axis_index("tensor")
    cm = Plain(wq, wo, w2, dwq, dwo, dw2, vec)
    layer(cm, T, most, len_ref[T], ts_ref[0].astype(f32), tok, cot, seg, wt, btime, g1, b1, g2, b2, bdown, bup, out, gtok, refs[22:])


def run_plain(most, length, ts, tok, cot, seg, wq, wo, w2, wt, vecs, bup):
    seq, D = tok.shape
    P, NF, F = wq.shape[0], w2.shape[0], w2.shape[-1]
    S = jax.ShapeDtypeStruct
    vm = pl.BlockSpec(memory_space=pltpu.VMEM)
    sm = pl.BlockSpec(memory_space=pltpu.SMEM)
    return pl.pallas_call(
        functools.partial(plain_kernel, most, 0),
        out_shape=(S((seq, D), bf16), S((seq, D), f32), S(wq.shape, bf16), S(wo.shape, bf16), S(w2.shape, bf16), S((16, D), f32)),
        in_specs=[sm, sm] + [vm] * 14, out_specs=[vm] * 6,
        scratch_shapes=layer_scratch(seq, D, P, NF, F),
        compiler_params=pltpu.CompilerParams(vmem_limit_bytes=60 << 20),
    )(length, ts, tok, cot, seg, wq, wo, w2, wt, *[v[None] for v in vecs], bup)


def linked_kernel(most, ng, nt, names, semnames, n_layer, *refs):
    len_ref, ts_ref, tok, cot, seg, w_qkv, w_out, w_up, w_down, wt, btime, g1, b1, g2, b2, bdown, bup = refs[:17]
    out, gtok, o_qkv, o_out, o_up, o_down, gwt, vec = refs[17:25]
    sc = refs[25:25 + n_layer]
    rest = refs[25 + n_layer:]
    bufs = dict(zip(names, rest[:len(names)]))
    sr = rest[len(names):]
    sems = {nm: (sr[2 * i], sr[2 * i + 1]) for i, nm in enumerate(semnames)}
    bufs.update(w_qkv=w_qkv, w_out=w_out, w_up=w_up, w_down=w_down, o_qkv=o_qkv, o_out=o_out, o_up=o_up, o_down=o_down)
    bufs["E"] = tuple(bufs.pop(k) for k in ("EZ", "EX", "EC"))
    bufs["L"] = tuple(bufs.pop(k) for k in ("LZ", "LX", "LC"))
    cm = Linked(ng, nt, bufs, sems)
    T = cm.t
    NE = 4 + bup.shape[0]
    cm.early = lambda rows: cm.v_start("E", rows)
    cm.late = lambda rows: cm.v_start("L", rows)
    plain_hook = cm.hook

    def hook(place, j=None):
        plain_hook(place, j)
        if place == "back_mid":
            @pl.when(j == 0)
            def _():
                cm.v_mid("E", NE)
            @pl.when(j == 1)
            def _():
                cm.v_last("E", NE)

    cm.hook = hook
    layer(cm, T, most, len_ref[T], ts_ref[0].astype(f32), tok, cot, seg, wt, btime, g1, b1, g2, b2, bdown, bup, out, gtok, sc)
    cm.v_mid("L", 3)
    embs, sums = cm.v_done("E", NE)
    vec[4:4 + NE - 1, :] = sums
    cm.v_last("L", 3)
    cm.hook("finish")
    grads, late = cm.v_done("L", 3)
    vec[2:4, :] = late
    vec[1:2, :] = colsum(grads)
    gwt[...] = lax.dot_general(embs, grads, (((0,), (0,)), ((), ())), precision=lax.Precision.HIGHEST, preferred_element_type=f32)
    cm.hook("leave")
    cm.v_leave("E")
    cm.v_leave("L")


def run_linked(most, nd, nt, length, ts, tok, cot, seg, w_qkv, w_out, w_up, w_down, wt, vecs, bup):
    seq, D = tok.shape
    ng = nd // 2
    r, F = w_up.shape
    P, NF = nt, nt
    S, V = jax.ShapeDtypeStruct, pltpu.VMEM
    DMA = pltpu.SemaphoreType.DMA
    bufs = dict(
        WQ=V((nt, ng, 2, r, 384), bf16), WO=V((nt, ng, 2, r, 128), bf16), W2=V((nt, 2, ng, 2, r, F), bf16),
        DQ=V((nt, ng, 2, r, 384), bf16), DO=V((nt, ng, 2, r, 128), bf16), D2=V((nt, 2, ng, 2, r, F), bf16),
        CQ=V((nt, ng, r, 384), bf16), XQ=V((nt, ng, r, 384), bf16), ZQ=V((nt, r, 384), bf16),
        CO=V((nt, ng, r, 128), bf16), XO=V((ng, nt, r, 128), bf16), ZO=V((nt, r, 128), bf16),
        C2=V((nt, 2, ng, r, F), bf16), X2=V((nt, ng, 2, r, F), bf16), Z2=V((nt, 2, r, F), bf16),
        EZ=V((nt, 8, D), f32), EX=V((ng, 16, D), f32), EC=V((2, nt * ng + 8, D), f32),
        LZ=V((nt, 8, D), f32), LX=V((ng, 16, D), f32), LC=V((2, nt * ng + 8, D), f32),
    )
    sems = dict(gq_plane=(ng,), gq_z=(nt,), gq_core=(nt,), go_z=(nt,), g2_z=(nt,), go_plane=(ng,), go_core=(), g2_plane=(nt, ng), g2_core=(nt,),
        rq_core=(nt,), rq_plane=(nt, ng), rq_z=(nt,), r2_core=(nt,), r2_plane=(nt, ng), r2_z=(nt,), ro_core=(), ro_plane=(ng,), ro_z=(nt,),
        E_z=(nt,), E_plane=(ng,), E_core=(), L_z=(nt,), L_plane=(ng,), L_core=())
    ls = layer_scratch(seq, D, P, NF, F)
    scratch = ls + list(bufs.values())
    for s in sems.values():
        scratch += [DMA(s), DMA(s)]
    vm = pl.BlockSpec(memory_space=pltpu.VMEM)
    sm = pl.BlockSpec(memory_space=pltpu.SMEM)
    return pl.pallas_call(
        functools.partial(linked_kernel, most, ng, nt, tuple(bufs), tuple(sems), len(ls)),
        out_shape=(S((seq, D), bf16), S((seq, D), f32), S(w_qkv.shape, f32), S(w_out.shape, f32), S(w_up.shape, f32), S(w_down.shape, f32), S((D, D), f32), S((16, D), f32)),
        in_specs=[sm, sm] + [vm] * 15, out_specs=[vm] * 8,
        scratch_shapes=scratch,
        compiler_params=pltpu.CompilerParams(vmem_limit_bytes=62 << 20, collective_id=0, has_side_effects=True),
    )(length, ts, tok, cot, seg, w_qkv, w_out, w_up, w_down, wt, *[v[None] for v in vecs], bup)


def shards(
    tokens,
    timestep,
    segment_ids,
    span_lengths,
    w_qkv,
    w_out_t,
    w_up,
    w_down_t,
    w_time,
    b_time,
    ln1_gain,
    ln1_bias,
    ln2_gain,
    ln2_bias,
    b_up,
    b_down,
    cotangent,
):
    seq, D = tokens.shape[1:]
    nd, nt = lax.axis_size("dp"), lax.axis_size("tensor")
    vecs = (b_time, ln1_gain, ln1_bias, ln2_gain, ln2_bias, b_down)
    F = w_up.shape[1]
    bup = b_up.reshape(nt, 1, F)
    if w_up.shape[0] % 16 == 0:
        out, gtok, gq, go, gu, gd, gwt, vec = run_linked(
            DOC, nd, nt, span_lengths, timestep, tokens[0], cotangent[0], segment_ids,
            w_qkv, w_out_t, w_up, w_down_t, w_time, vecs, bup)
        return (out[None], gtok[None], gq, go, gu, gd, gwt, vec[1], vec[2], vec[3], vec[4], vec[5],
                vec[7:7 + nt].reshape(-1), vec[6])
    HB = w_qkv.shape[2]

    def whole(w):
        return lax.all_gather(lax.all_gather(w.astype(bf16), "dp", axis=w.ndim - 2, tiled=True), "tensor", axis=0)

    def part(g, dim):
        g = lax.psum_scatter(g, "dp", scatter_dimension=dim, tiled=True)
        return lax.psum_scatter(g, "tensor", scatter_dimension=0, tiled=True)[0].astype(f32)

    wq = whole(jnp.transpose(w_qkv, (1, 0, 2)).reshape(w_qkv.shape[1], 3 * HB))
    out, gtok, dwq, dwo, dw2, vec = run_plain(
        DOC, span_lengths, timestep, tokens[0], cotangent[0], segment_ids,
        wq, whole(w_out_t), whole(jnp.stack([w_up, w_down_t])), w_time, vecs, bup)
    lines = lax.all_gather(jnp.stack([vec[0], vec[8]]), ("dp", "tensor"), axis=1, tiled=False)
    gwt = jnp.dot(lines[0].T, lines[1], precision=lax.Precision.HIGHEST)
    small = lax.psum(vec, ("dp", "tensor"))
    gq, g2 = part(dwq, 1), part(dw2, 2)
    return (
        out[None], gtok[None], jnp.transpose(gq.reshape(gq.shape[0], 3, HB), (1, 0, 2)), part(dwo, 1), g2[0], g2[1],
        gwt, small[8], small[9], small[10], small[1], small[2], small[4:4 + nt].reshape(-1), small[3])


def solution(mesh):
    return jax.shard_map(
        shards,
        mesh=mesh,
        in_specs=(
            P_(("dp", "tensor"), None, None),
            P_(("dp", "tensor")),
            P_("dp", None),
            P_("dp"),
            P_(None, "dp", "tensor"),
            P_("dp", "tensor"),
            P_("dp", "tensor"),
            P_("dp", "tensor"),
            P_(),
            P_(),
            P_(),
            P_(),
            P_(),
            P_(),
            P_(),
            P_(),
            P_(("dp", "tensor"), None, None),
        ),
        out_specs=(
            P_(("dp", "tensor"), None, None),
            P_(("dp", "tensor"), None, None),
            P_(None, "dp", "tensor"),
            P_("dp", "tensor"),
            P_("dp", "tensor"),
            P_("dp", "tensor"),
            P_(),
            P_(),
            P_(),
            P_(),
            P_(),
            P_(),
            P_(),
            P_(),
        ),
        check_vma=False,
    )
```

```python
import functools
import math

import jax
import jax.numpy as jnp
from jax import lax
from jax.experimental import pallas as pl
from jax.experimental.pallas import tpu as pltpu
from jax.sharding import PartitionSpec as P_

f32, bf16 = jnp.float32, jnp.bfloat16
HS = 64
TR = 256
BIG = 1e30
EPS = 1e-5
DOC = 512
LOG2E = math.log2(math.e)
LN2 = math.log(2.0)
SCALE = 1.0 / math.sqrt(HS)


def nt_dot(a, b):
    return lax.dot_general(a, b, (((1,), (1,)), ((), ())), preferred_element_type=f32)


def tn_dot(a, b):
    return lax.dot_general(a, b, (((0,), (0,)), ((), ())), preferred_element_type=f32)


def nn_dot(a, b):
    return jnp.dot(a, b, preferred_element_type=f32)


def lane(shape):
    return lax.broadcasted_iota(jnp.int32, shape, len(shape) - 1)


def rows_of(i, n=TR):
    return pl.ds(pl.multiple_of(i * n, n), n)


def normed(x):
    mean = jnp.mean(x, axis=-1, keepdims=True)
    c = x - mean
    var = jnp.mean(c * c, axis=-1, keepdims=True)
    r = lax.rsqrt(var + EPS)
    return c * r, r


def norm_back(xhat, r, gain, gy):
    gh = gy * gain
    a = jnp.mean(gh, axis=-1, keepdims=True)
    b = jnp.mean(gh * xhat, axis=-1, keepdims=True)
    return r * (gh - a - xhat * b)


def colsum(x):
    return jnp.sum(x, axis=0, keepdims=True)


def halves(prod):
    low = lane(prod.shape) < HS
    s0 = jnp.sum(jnp.where(low, prod, 0.0), axis=-1, keepdims=True)
    s1 = jnp.sum(jnp.where(low, 0.0, prod), axis=-1, keepdims=True)
    return s0, s1


def split3(x):
    hi = x.astype(bf16)
    rest = x - hi.astype(f32)
    mid = rest.astype(bf16)
    lo = (rest - mid.astype(f32)).astype(bf16)
    return hi, mid, lo


def window(i, seq, most):
    lo = max(0, (i * TR - most + 1) // 128 * 128)
    hi = min(seq, -(-(i * TR + TR - 1 + most) // 128) * 128)
    return lo, hi


def attend_fwd(seq, most, length, qkv, qaug, kaug, mixed, lse, qq, kk, vv, hp, half):
    n = seq // TR
    def prep(i, _):
        r = rows_of(i)
        low = lane((TR, 128)) < HS
        q, k, v = (qkv[hp, r, 128 * c:128 * c + 128] for c in range(3))
        qa, ka = qaug[r, :], kaug[r, :]
        one = jnp.ones_like(v)
        qq[0, r, :] = jnp.where(low, q, qa)
        qq[1, r, :] = jnp.where(low, qa, q)
        kk[0, r, :] = jnp.where(low, k, ka)
        kk[1, r, :] = jnp.where(low, ka, k)
        vv[0, r, :] = jnp.where(low, v, one)
        vv[1, r, :] = jnp.where(low, one, v)
        return 0
    lax.fori_loop(0, n, prep, 0)
    for i in range(n):
        if i == n // 2:
            half()
        lo, hi = window(i, seq, most)
        r = slice(i * TR, i * TR + TR)
        low = lane((TR, 128)) < HS
        q, k, v = (qkv[hp, r, 128 * c:128 * c + 128].astype(f32) for c in range(3))
        own = halves(q * k)
        pad = (lax.broadcasted_iota(jnp.int32, (TR, 1), 0) + i * TR) >= length
        tops, outs = [], []
        for h in range(2):
            s = nt_dot(qq[h, r, :], kk[h, lo:hi, :])
            m = jnp.max(s, axis=-1, keepdims=True)
            m = jnp.where(pad, jnp.maximum(m, own[h]), m)
            p = jnp.exp2(s - m).astype(bf16)
            outs.append(nn_dot(p, vv[h, lo:hi, :]))
            tops.append(m)
        padf = pad.astype(f32)
        e0 = jnp.exp2(jnp.minimum(own[0] - tops[0], 0.0)).astype(bf16).astype(f32) * padf
        e1 = jnp.exp2(jnp.minimum(own[1] - tops[1], 0.0)).astype(bf16).astype(f32) * padf
        num = jnp.where(low, outs[0], outs[1]) + jnp.where(low, e0, e1) * v
        den_x = jnp.where(low, outs[1], outs[0]) + jnp.where(low, e1, e0)
        den = pltpu.roll(den_x, HS, 1)
        mixed[hp, r, :] = (num / den).astype(bf16)
        lse[hp, r, :] = jnp.where(low, tops[1], tops[0]) + jnp.log2(den_x)


def attend_bwd(seq, most, length, qkv, qaug, kaug, mixed, lse, gm, qq, kk, vv, oo, dq, dkv, dqkv, hp):
    n = seq // TR
    def prep(i, _):
        r = rows_of(i)
        low = lane((TR, 128)) < HS
        spot = lane((TR, 128)) % HS
        q, k, v = (qkv[hp, r, 128 * c:128 * c + 128] for c in range(3))
        g = gm[hp, r, :]
        d0, d1 = halves(g.astype(f32) * mixed[hp, r, :].astype(f32))
        dx = jnp.where(low, d1, d0)
        def put(base, x):
            hi, mid, lo = split3(x)
            z = jnp.where(spot == 8, hi, base)
            z = jnp.where(spot == 9, mid, z)
            return jnp.where(spot == 10, lo, z)
        zero = jnp.zeros((TR, 128), bf16)
        qa = put(qaug[r, :], lse[hp, r, :])
        oa = put(zero, dx)
        ka = kaug[r, :]
        va = jnp.where((spot >= 8) & (spot < 11), -jnp.ones_like(zero), zero)
        for ref, x, a in ((qq, q, qa), (kk, k, ka), (vv, v, va), (oo, g, oa)):
            ref[0, r, :] = jnp.where(low, x, a)
            ref[1, r, :] = jnp.where(low, a, x)
        return 0
    lax.fori_loop(0, n, prep, 0)
    for h in range(2):
        dq[h] = jnp.zeros(dq.shape[1:], f32)
    for i in range(n):
        lo, hi = window(i, seq, most)
        r = slice(i * TR, i * TR + TR)
        for h in range(2):
            st = nt_dot(kk[h, r, :], qq[h, lo:hi, :])
            pt = jnp.exp2(st)
            dpt = nt_dot(vv[h, r, :], oo[h, lo:hi, :])
            dst = (pt * dpt).astype(bf16)
            dkv[h, 0, r, :] = nn_dot(dst, qq[h, lo:hi, :])
            dkv[h, 1, r, :] = nn_dot(pt.astype(bf16), oo[h, lo:hi, :])
            dq[h, lo:hi, :] += tn_dot(dst, kk[h, r, :])
    def post(i, _):
        r = rows_of(i)
        low = lane((TR, 128)) < HS
        q, k, v = (qkv[hp, r, 128 * c:128 * c + 128].astype(f32) for c in range(3))
        g = gm[hp, r, :].astype(f32)
        pad = (lax.broadcasted_iota(jnp.int32, (TR, 1), 0) + i * TR) >= length
        padf = pad.astype(f32)
        s0, s1 = halves(q * k)
        p0, p1 = halves(g * v)
        d0, d1 = halves(g * mixed[hp, r, :].astype(f32))
        ls = pltpu.roll(lse[hp, r, :], HS, 1)
        pf = jnp.exp2(jnp.minimum(jnp.where(low, s0, s1) - ls, 1.0)) * padf
        ds = (pf * (jnp.where(low, p0, p1) - jnp.where(low, d0, d1))).astype(bf16).astype(f32)
        pf = pf.astype(bf16).astype(f32)
        gq = jnp.where(low, dq[0, r, :], dq[1, r, :]) + ds * k
        gk = jnp.where(low, dkv[0, 0, r, :], dkv[1, 0, r, :]) + ds * q
        gv = jnp.where(low, dkv[0, 1, r, :], dkv[1, 1, r, :]) + pf * g
        dqkv[r, 0:128] = (gq * SCALE).astype(bf16)
        dqkv[r, 128:256] = (gk * LN2).astype(bf16)
        dqkv[r, 256:384] = gv.astype(bf16)
        return 0
    lax.fori_loop(0, n, post, 0)


def gelu_parts(u):
    c0, c1 = 0.7978845608028654, 0.044715
    u2 = u * u
    th = jnp.tanh(u * (c0 + (c0 * c1) * u2))
    half = 0.5 + 0.5 * th
    act = u * half
    grad = half + (0.5 * u) * (1.0 - th * th) * (c0 + (3.0 * c0 * c1) * u2)
    return act, grad


def transpose_into(dst, src, seq):
    def step(i, _):
        r = rows_of(i)
        dst[:, r] = src[r, :].T
        return 0
    for i in range(seq // TR):
        r = slice(i * TR, i * TR + TR)
        dst[:, r] = src[r, :].T


MESH = pl.DeviceIdType.MESH


class Plain:
    def __init__(self, wq, wo, w2, dwq, dwo, dw2, vec):
        self.wq, self.wo, self.w2 = wq, wo, w2
        self.dwq, self.dwo, self.dw2, self.vec = dwq, dwo, dw2, vec

    def getq(self, p):
        return self.wq[p]

    def geto(self):
        return jnp.concatenate([self.wo[p] for p in range(self.wo.shape[0])], axis=1)

    def getu(self, f):
        return self.w2[f, 0]

    def getd(self, f):
        return self.w2[f, 1]

    def putq(self, p, i, x):
        self.dwq[p, i, :] = x

    def puto(self, p, i, x):
        self.dwo[p, i, :] = x

    def put2(self, f, k, i, x):
        self.dw2[f, k, i, :] = x

    def order(self, j):
        return j

    def order_back(self, j):
        return j

    def hook(self, *_):
        pass

    def early(self, rows):
        for k, x in enumerate(rows):
            self.vec[k:k + 1, :] = x

    def late(self, rows):
        for k, x in enumerate(rows):
            self.vec[8 + k:9 + k, :] = x


class Linked:
    def __init__(self, ng, nt, bufs, sems):
        self.ng, self.nt = ng, nt
        self.__dict__.update(bufs)
        self.sem = sems
        d, self.t = lax.axis_index("dp"), lax.axis_index("tensor")
        self.d, self.g, self.c = d, d // 2, d % 2
        self.sent = []

    def dev(self, kind, k):
        if kind == "core":
            return (2 * self.g + 1 - self.c, self.t)
        if kind == "plane":
            return (2 * (self.g ^ k) + self.c, self.t)
        return (self.d, self.t ^ k)

    def copy(self, name, at, kind, k, src, dst):
        s, r = self.sem[name]
        for i in at:
            s, r = s.at[i], r.at[i]
        return pltpu.make_async_remote_copy(
            src_ref=src, dst_ref=dst, send_sem=s, recv_sem=r,
            device_id=self.dev(kind, k), device_id_type=MESH)

    def getq(self, p):
        x = self.WQ[p]
        return x.reshape(-1, x.shape[-1])

    def geto(self):
        return jnp.concatenate([self.WO[p].reshape(-1, 128) for p in range(self.nt)], axis=1)

    def getu(self, f):
        x = self.W2[f, 0]
        return x.reshape(-1, x.shape[-1])

    def getd(self, f):
        x = self.W2[f, 1]
        return x.reshape(-1, x.shape[-1])

    def blocks(self, ref, i):
        rows = ref.shape[-2]
        m = (i.stop - i.start) // (2 * rows)
        return slice(i.start // (2 * rows), i.stop // (2 * rows)), (m, 2, rows, ref.shape[-1])

    def putq(self, p, i, x):
        b, shape = self.blocks(self.DQ, i)
        self.DQ[p, b] = x.reshape(shape)

    def puto(self, p, i, x):
        b, shape = self.blocks(self.DO, i)
        self.DO[p, b] = x.reshape(shape)

    def put2(self, f, k, i, x):
        b, shape = self.blocks(self.D2, i)
        self.D2[f, k, b] = x.reshape(shape)

    def order(self, j):
        return self.t ^ j

    def order_back(self, j):
        return self.t ^ (self.nt - 1 - j)

    def enter(self):
        bar = pltpu.get_barrier_semaphore()
        peers = [("core", 0)] + [("plane", k) for k in range(1, self.ng)] + [("z", k) for k in range(1, self.nt)]
        for kind, k in peers:
            pl.semaphore_signal(bar, inc=1, device_id=self.dev(kind, k), device_id_type=MESH)
        pl.semaphore_wait(bar, len(peers))

    def q_plane(self, x, k, incoming=False):
        g, c, p = self.g, self.c, self.t ^ x
        return self.copy("gq_plane", (x, k), "plane", k, self.WQ.at[p, g, c], self.WQ.at[p, g ^ k if incoming else g, c])

    def q_z(self, k, incoming=False):
        g, c, t = self.g, self.c, self.t
        return self.copy("gq_z", (k,), "z", k, self.WQ.at[t, g, c], self.WQ.at[t ^ k if incoming else t, g, c])

    def q_core(self, k):
        c, t = self.c, self.t
        return self.copy("gq_core", (k,), "core", 0, self.WQ.at[t ^ k, :, c], self.WQ.at[t ^ k, :, c])

    def q_core_in(self, k):
        c, t = self.c, self.t
        return self.copy("gq_core", (k,), "core", 0, self.WQ.at[t ^ k, :, c], self.WQ.at[t ^ k, :, 1 - c])

    def r_z(self, k, into=None):
        g, c, t = self.g, self.c, self.t
        u = t if into is None else into
        return [self.copy("go_z", (k,), "z", k, self.WO.at[t, g, c], self.WO.at[u, g, c]),
                self.copy("g2_z", (k,), "z", k, self.W2.at[t, :, g, c], self.W2.at[u, :, g, c])]

    def o_plane(self, k, incoming=False):
        g, c = self.g, self.c
        return self.copy("go_plane", (k,), "plane", k, self.WO.at[:, g, c], self.WO.at[:, g ^ k if incoming else g, c])

    def o_core(self, incoming=False):
        c = self.c
        return self.copy("go_core", (), "core", 0, self.WO.at[:, :, c], self.WO.at[:, :, 1 - c if incoming else c])

    def f_plane(self, j, k, incoming=False):
        g, c, f = self.g, self.c, self.t ^ j
        return self.copy("g2_plane", (j, k), "plane", k, self.W2.at[f, :, g, c], self.W2.at[f, :, g ^ k if incoming else g, c])

    def f_core(self, j, incoming=False):
        c, f = self.c, self.t ^ j
        return self.copy("g2_core", (j,), "core", 0, self.W2.at[f, :, :, c], self.W2.at[f, :, :, 1 - c if incoming else c])

    def rq(self, stage, x, k=0, incoming=False):
        g, c, p = self.g, self.c, self.t ^ x
        if stage == "core":
            return self.copy("rq_core", (x,), "core", 0, self.DQ.at[p, :, 1 - c], self.CQ.at[x])
        if stage == "plane":
            return self.copy("rq_plane", (x, k), "plane", k, self.DQ.at[p, g ^ k, c], self.XQ.at[x, k])
        return self.copy("rq_z", (x,), "z", x, self.DQ.at[p, g, c], self.ZQ.at[x])

    def r2(self, stage, x, k=0):
        g, c, p = self.g, self.c, self.t ^ x
        if stage == "core":
            return self.copy("r2_core", (x,), "core", 0, self.D2.at[p, :, :, 1 - c], self.C2.at[x])
        if stage == "plane":
            return self.copy("r2_plane", (x, k), "plane", k, self.D2.at[p, :, g ^ k, c], self.X2.at[x, k])
        return self.copy("r2_z", (x,), "z", x, self.D2.at[p, :, g, c], self.Z2.at[x])

    def ro(self, stage, k=0):
        g, c, t = self.g, self.c, self.t
        if stage == "core":
            return self.copy("ro_core", (), "core", 0, self.DO.at[:, :, 1 - c], self.CO)
        if stage == "plane":
            return self.copy("ro_plane", (k,), "plane", k, self.DO.at[:, g ^ k, c], self.XO.at[k])
        return self.copy("ro_z", (k,), "z", k, self.DO.at[t ^ k, g, c], self.ZO.at[k])

    def q_after_core(self, x):
        p, c = self.t ^ x, self.c
        self.rq("core", x).wait_recv()
        self.DQ[p, :, c] = (self.DQ[p, :, c].astype(f32) + self.CQ[x].astype(f32)).astype(bf16)
        for k in range(1, self.ng):
            self.rq("plane", x, k).start()

    def q_after_plane(self, x):
        p, c, g = self.t ^ x, self.c, self.g
        acc = self.DQ[p, g, c].astype(f32)
        for k in range(1, self.ng):
            self.rq("plane", x, k).wait_recv()
            acc = acc + self.XQ[x, k].astype(f32)
        self.DQ[p, g, c] = acc.astype(bf16)

    def f_after_core(self, x):
        p, c = self.t ^ x, self.c
        self.r2("core", x).wait_recv()
        for u in range(2):
            def step(i, _):
                self.D2[p, u, i, c] = (self.D2[p, u, i, c].astype(f32) + self.C2[x, u, i].astype(f32)).astype(bf16)
                return 0
            lax.fori_loop(0, self.ng, step, 0)
        for k in range(1, self.ng):
            self.r2("plane", x, k).start()

    def f_after_plane(self, x):
        p, c, g = self.t ^ x, self.c, self.g
        for k in range(1, self.ng):
            self.r2("plane", x, k).wait_recv()
        for u in range(2):
            acc = self.D2[p, u, g, c].astype(f32)
            for k in range(1, self.ng):
                acc = acc + self.X2[x, k, u].astype(f32)
            self.D2[p, u, g, c] = acc.astype(bf16)

    def hook(self, place, j=None):
        ng, nt, t, g, c = self.ng, self.nt, self.t, self.g, self.c
        if place == "start":
            rq = self.w_qkv.shape[1]
            for k in range(3):
                self.WQ[t, g, c, :, 128 * k:128 * k + 128] = self.w_qkv[k].astype(bf16)
            self.WO[t, g, c] = self.w_out[...].astype(bf16)
            self.W2[t, 0, g, c] = self.w_up[...].astype(bf16)
            self.W2[t, 1, g, c] = self.w_down[...].astype(bf16)
            self.enter()
            for k in range(1, ng):
                self.q_plane(0, k).start()
            for k in range(1, nt):
                self.q_z(k).start()
        elif place == "normed":
            for k in range(1, ng):
                self.q_plane(0, k, True).wait_recv()
            self.q_core(0).start()
            for k in range(1, nt):
                for x in self.r_z(k):
                    x.start()
        elif place == "masked":
            for x in range(1, nt):
                self.q_z(x, True).wait_recv()
                for k in range(1, ng):
                    self.q_plane(x, k).start()
        elif place == "pair":
            self.q_core_in(j).wait_recv()
        elif place == "pair_half":
            @pl.when(j < nt - 1)
            def _():
                for k in range(1, ng):
                    self.q_plane(j + 1, k, True).wait_recv()
                self.q_core(j + 1).start()
            @pl.when(j == nt - 2)
            def _():
                for k in range(1, ng):
                    self.o_plane(k, True).wait_recv()
                self.o_core().start()
            @pl.when(j == nt - 1)
            def _():
                for k in range(1, ng):
                    self.f_plane(0, k, True).wait_recv()
                self.f_core(0).start()
        elif place == "pair_mid":
            @pl.when(j == 0)
            def _():
                for k in range(1, nt):
                    for x in self.r_z(k, t ^ k):
                        x.wait_recv()
                for k in range(1, ng):
                    self.o_plane(k).start()
            for k in range(1, ng):
                self.f_plane(j, k).start()
        elif place == "mixed":
            self.o_core(True).wait_recv()
        elif place == "chunk":
            self.f_core(j, True).wait_recv()
        elif place == "chunk_mid":
            @pl.when(j < nt - 1)
            def _():
                for k in range(1, ng):
                    self.f_plane(j + 1, k, True).wait_recv()
                self.f_core(j + 1).start()
            @pl.when(j >= 1)
            def _():
                self.f_after_core(j - 1)
            @pl.when(j >= 2)
            def _():
                self.f_after_plane(j - 2)
                @pl.when(j >= 3)
                def _():
                    self.r2("z", j - 2).start()
        elif place == "chunk_end":
            self.r2("core", j).start()
        elif place == "ffn_done":
            self.f_after_core(nt - 1)
            self.f_after_plane(nt - 2)
            self.r2("z", nt - 2).start()
        elif place == "out_grad":
            self.ro("core").start()
        elif place == "back_mid":
            @pl.when(j == 0)
            def _():
                self.f_after_plane(nt - 1)
                self.r2("z", nt - 1).start()
                self.ro("core").wait_recv()
                for p in range(nt):
                    self.DO[p, :, c] = (self.DO[p, :, c].astype(f32) + self.CO[p].astype(f32)).astype(bf16)
                for k in range(1, ng):
                    self.ro("plane", k).start()
            @pl.when(j == 1)
            def _():
                for k in range(1, ng):
                    self.ro("plane", k).wait_recv()
                for p in range(nt):
                    acc = self.DO[p, g, c].astype(f32)
                    for k in range(1, ng):
                        acc = acc + self.XO[k, p].astype(f32)
                    self.DO[p, g, c] = acc.astype(bf16)
                for k in range(1, nt):
                    self.ro("z", k).start()
            @pl.when(j >= 1)
            def _():
                self.q_after_core(nt - j)
            @pl.when(j >= 2)
            def _():
                self.q_after_plane(nt - j + 1)
                self.rq("z", nt - j + 1).start()
        elif place == "back_end":
            self.rq("core", nt - 1 - j).start()
        elif place == "back_done":
            self.q_after_core(0)
            self.q_after_plane(1)
            self.rq("z", 1).start()
        elif place == "finish":
            for x in range(1, nt):
                self.r2("z", x).wait_recv()
                self.ro("z", x).wait_recv()
            for u, o in enumerate((self.o_up, self.o_down)):
                acc = self.D2[t, u, g, c].astype(f32)
                for x in range(1, nt):
                    acc = acc + self.Z2[x, u].astype(f32)
                o[...] = acc
            acc = self.DO[t, g, c].astype(f32)
            for x in range(1, nt):
                acc = acc + self.ZO[x].astype(f32)
            self.o_out[...] = acc
            acc = self.DQ[t, g, c].astype(f32)
            for k in range(1, ng):
                self.rq("plane", 0, k).wait_recv()
                acc = acc + self.XQ[0, k].astype(f32)
            for x in range(1, nt):
                self.rq("z", x).wait_recv()
                acc = acc + self.ZQ[x].astype(f32)
            for k in range(3):
                self.o_qkv[k] = acc[:, 128 * k:128 * k + 128]
        elif place == "leave":
            for k in range(1, ng):
                self.o_plane(k).wait_send()
                self.ro("plane", k).wait_send()
                for x in range(nt):
                    self.q_plane(x, k).wait_send()
                    self.f_plane(x, k).wait_send()
                    self.r2("plane", x, k).wait_send()
                    self.rq("plane", x, k).wait_send()
            for k in range(nt):
                self.q_core(k).wait_send()
                self.f_core(k).wait_send()
                self.r2("core", k).wait_send()
                self.rq("core", k).wait_send()
            self.o_core().wait_send()
            self.ro("core").wait_send()
            for k in range(1, nt):
                self.q_z(k).wait_send()
                for x in self.r_z(k):
                    x.wait_send()
                self.r2("z", k).wait_send()
                self.rq("z", k).wait_send()
                self.ro("z", k).wait_send()

    def v(self, name, stage, k):
        B = getattr(self, name)
        Z, X, C = B
        if stage == "z":
            return self.copy(name + "_z", (k,), "z", k, Z.at[self.t], Z.at[self.t])
        if stage == "plane":
            return self.copy(name + "_plane", (k,), "plane", k, X.at[self.g], X.at[self.g])
        return self.copy(name + "_core", (), "core", 0, C.at[self.c], C.at[self.c])

    def v_in(self, name, stage, k):
        Z, X, C = getattr(self, name)
        if stage == "z":
            return self.copy(name + "_z", (k,), "z", k, Z.at[self.t], Z.at[self.t ^ k])
        if stage == "plane":
            return self.copy(name + "_plane", (k,), "plane", k, X.at[self.g], X.at[self.g ^ k])
        return self.copy(name + "_core", (), "core", 0, C.at[self.c], C.at[1 - self.c])

    def v_start(self, name, rows):
        Z = getattr(self, name)[0]
        for k, x in enumerate(rows):
            Z[self.t, k:k + 1, :] = x
        for k in range(1, self.nt):
            self.v(name, "z", k).start()

    def v_mid(self, name, m):
        Z, X, C = getattr(self, name)
        nt = self.nt
        for k in range(1, nt):
            self.v_in(name, "z", k).wait_recv()
        for k in range(nt):
            X[self.g, k:k + 1, :] = Z[k, 0:1, :]
        s = Z[0, 1:m, :]
        for k in range(1, nt):
            s = s + Z[k, 1:m, :]
        X[self.g, 8:8 + m - 1, :] = s
        for k in range(1, self.ng):
            self.v(name, "plane", k).start()

    def v_last(self, name, m):
        Z, X, C = getattr(self, name)
        nt, ng = self.nt, self.ng
        for k in range(1, ng):
            self.v_in(name, "plane", k).wait_recv()
        for k in range(ng):
            C[self.c, k * nt:k * nt + nt, :] = X[k, 0:nt, :]
        s = X[0, 8:8 + m - 1, :]
        for k in range(1, ng):
            s = s + X[k, 8:8 + m - 1, :]
        C[self.c, ng * nt:ng * nt + m - 1, :] = s
        self.v(name, "core", 0).start()

    def v_done(self, name, m):
        C = getattr(self, name)[2]
        n = self.nt * self.ng
        self.v_in(name, "core", 0).wait_recv()
        kept = jnp.concatenate([C[0, 0:n, :], C[1, 0:n, :]], axis=0)
        return kept, C[0, n:n + m - 1, :] + C[1, n:n + m - 1, :]

    def v_leave(self, name):
        for k in range(1, self.nt):
            self.v(name, "z", k).wait_send()
        for k in range(1, self.ng):
            self.v(name, "plane", k).wait_send()
        self.v(name, "core", 0).wait_send()


TILE = dict(ln1=256, proj=1024, ln2=512, tile=512, wgrad=512, ln2b=256, gmix=1024, gwo=512, qgrad=512, back=1024, ln1b=256)
UNROLL = {"proj", "ln2", "tile", "wgrad", "gmix", "gwo", "qgrad", "back"}


def loop(name, total, body, init):
    n = TILE[name]
    if name in UNROLL or total == n:
        for i in range(total // n):
            init = body(slice(i * n, i * n + n), init)
        return init
    return lax.fori_loop(0, total // n, lambda i, x: body(pl.ds(pl.multiple_of(i * n, n), n), x), init)


def layer(cm, T, most, length, t, tok, cot, seg, wt, btime, g1, b1, g2, b2, bdown, bup, out, gtok, sc):
    tp, n1, qkv, qaug, kaug, mixed, lse, qq, kk, vv, oo, dq, dkv, dqkv, mid, n2, ffn, gn, act, gu, gm, xT, xT2, bsum = sc
    seq, D = tok.shape
    P = qkv.shape[0]
    NF, F = bsum.shape[0], bsum.shape[2]
    n = seq // TR
    cm.hook("start")
    half = D // 2
    ang = t * jnp.exp(-math.log(10000.0) * lax.broadcasted_iota(jnp.int32, (8, half), 1).astype(f32) / half)
    emb = jnp.concatenate([jnp.sin(ang), jnp.cos(ang)], axis=1)
    tp[...] = jnp.dot(emb, wt[...], precision=lax.Precision.HIGHEST, preferred_element_type=f32)[0:1, :] + btime[...]

    def ln1(r, _):
        xh, _r = normed(tok[r, :].astype(f32) + tp[...])
        n1[r, :] = (xh * g1[...] + b1[...]).astype(bf16)
        return 0

    loop("ln1", seq, ln1, 0)
    cm.hook("normed")
    srow = seg[pl.ds(T, 1), :].astype(f32)
    for b in range(seq // 128):
        col = jnp.broadcast_to(srow[:, 128 * b:128 * b + 128], (128, 128)).T
        spot = lane((128, 128)) % HS
        pos = lax.broadcasted_iota(jnp.int32, (128, 128), 0) + 128 * b
        same = col == spot.astype(f32)
        r = slice(128 * b, 128 * b + 128)
        qaug[r, :] = jnp.where(same & (spot < 8), 1.0, 0.0).astype(bf16)
        ka = jnp.where(same & (pos < length), 0.0, -BIG)
        kaug[r, :] = jnp.where(spot < 8, ka, jnp.where(spot < 11, -1.0, 0.0)).astype(bf16)

    cm.hook("masked")

    def pair_fwd(j, _):
        hp = cm.order(j)
        cm.hook("pair", j)

        def proj(r, _):
            x = nn_dot(n1[r, :], cm.getq(hp))
            s = jnp.where(lane((1, 384)) < 128, SCALE * LOG2E, 1.0)
            qkv[hp, r, :] = (x * s).astype(bf16)
            return 0

        loop("proj", seq, proj, 0)
        attend_fwd(seq, most, length, qkv, qaug, kaug, mixed, lse, qq, kk, vv, hp, lambda: cm.hook("pair_half", j))
        cm.hook("pair_mid", j)
        return 0

    lax.fori_loop(0, P, pair_fwd, 0)
    cm.hook("mixed")

    def ln2(r, _):
        mx = jnp.concatenate([mixed[p, r, :] for p in range(P)], axis=1)
        x = tok[r, :].astype(f32) + tp[...] + nt_dot(mx, cm.geto())
        mid[r, :] = x
        xh, _r = normed(x)
        n2[r, :] = (xh * g2[...] + b2[...]).astype(bf16)
        ffn[r, :] = jnp.zeros((TILE["ln2"], D), f32)
        gn[r, :] = jnp.zeros((TILE["ln2"], D), f32)
        return 0

    loop("ln2", seq, ln2, 0)
    transpose_into(xT, cot, seq)
    transpose_into(xT2, n2, seq)

    def chunk(j, _):
        f = cm.order(j)
        cm.hook("chunk", j)

        def tile(r, acc):
            u = nn_dot(n2[r, :], cm.getu(f)) + bup[f]
            a, ga = gelu_parts(u)
            a = a.astype(bf16)
            g = (nn_dot(cot[r, :], cm.getd(f)) * ga).astype(bf16)
            act[r, :] = a
            gu[r, :] = g
            ffn[r, :] += nt_dot(a, cm.getd(f))
            gn[r, :] += nt_dot(g, cm.getu(f))
            return acc + colsum(g.astype(f32))

        bsum[f] = loop("tile", seq, tile, jnp.zeros((1, F), f32))
        cm.hook("chunk_mid", j)

        def wgrad(r, _):
            cm.put2(f, 1, r, nn_dot(xT[r, :], act[...]).astype(bf16))
            cm.put2(f, 0, r, nn_dot(xT2[r, :], gu[...]).astype(bf16))
            return 0

        loop("wgrad", D, wgrad, 0)
        cm.hook("chunk_end", j)
        return 0

    lax.fori_loop(0, NF, chunk, 0)

    def ln2b(r, acc):
        c = cot[r, :].astype(f32)
        x = mid[r, :]
        out[r, :] = (x + ffn[r, :] + bdown[...]).astype(bf16)
        xh, rr = normed(x)
        gy = gn[r, :]
        gmid = c + norm_back(xh, rr, g2[...], gy)
        mid[r, :] = gmid
        n2[r, :] = gmid.astype(bf16)
        gn[r, :] = jnp.zeros((TILE["ln2b"], D), f32)
        return acc[0] + colsum(gy * xh), acc[1] + colsum(gy), acc[2] + colsum(c)

    z = jnp.zeros((1, D), f32)
    a = loop("ln2b", seq, ln2b, (z, z, z))
    cm.early([emb[0:1, :], *a] + [bsum[f] for f in range(NF)])
    cm.hook("ffn_done")
    transpose_into(xT2, n2, seq)

    def gmix(r, _):
        x = nn_dot(n2[r, :], cm.geto()).astype(bf16)
        for p in range(P):
            gm[p, r, :] = x[:, 128 * p:128 * p + 128]
        return 0

    loop("gmix", seq, gmix, 0)

    def gwo(r, _):
        m = jnp.concatenate([mixed[p] for p in range(P)], axis=1)
        x = nn_dot(xT2[r, :], m).astype(bf16)
        for p in range(P):
            cm.puto(p, r, x[:, 128 * p:128 * p + 128])
        return 0

    loop("gwo", D, gwo, 0)
    cm.hook("out_grad")
    transpose_into(xT, n1, seq)

    def pair_bwd(j, _):
        hp = cm.order_back(j)
        attend_bwd(seq, most, length, qkv, qaug, kaug, mixed, lse, gm, qq, kk, vv, oo, dq, dkv, dqkv, hp)
        cm.hook("back_mid", j)

        def wgrad(r, _):
            cm.putq(hp, r, nn_dot(xT[r, :], dqkv[...]).astype(bf16))
            return 0

        loop("qgrad", D, wgrad, 0)
        cm.hook("back_end", j)

        def back(r, _):
            gn[r, :] += nt_dot(dqkv[r, :], cm.getq(hp))
            return 0

        loop("back", seq, back, 0)
        return 0

    lax.fori_loop(0, P, pair_bwd, 0)
    cm.hook("back_done")

    def ln1b(r, acc):
        xh, rr = normed(tok[r, :].astype(f32) + tp[...])
        gy = gn[r, :]
        gt = mid[r, :] + norm_back(xh, rr, g1[...], gy)
        gtok[r, :] = gt
        return acc[0] + colsum(gt), acc[1] + colsum(gy * xh), acc[2] + colsum(gy)

    a = loop("ln1b", seq, ln1b, (z, z, z))
    cm.late(list(a))


def layer_scratch(seq, D, P, NF, F):
    V = pltpu.VMEM
    return [V((1, D), f32), V((seq, D), bf16), V((P, seq, 384), bf16), V((seq, 128), bf16), V((seq, 128), bf16),
        V((P, seq, 128), bf16), V((P, seq, 128), f32)] + [V((2, seq, 128), bf16)] * 4 + [V((2, seq, 128), f32),
        V((2, 2, seq, 128), f32), V((seq, 384), bf16), V((seq, D), f32), V((seq, D), bf16), V((seq, D), f32), V((seq, D), f32),
        V((seq, F), bf16), V((seq, F), bf16), V((P, seq, 128), bf16), V((D, seq), bf16), V((D, seq), bf16), V((NF, 1, F), f32)]


def plain_kernel(most, n_sc, *refs):
    len_ref, ts_ref, tok, cot, seg, wq, wo, w2, wt, btime, g1, b1, g2, b2, bdown, bup, out, gtok, dwq, dwo, dw2, vec = refs[:22]
    T = lax.axis_index("tensor")
    cm = Plain(wq, wo, w2, dwq, dwo, dw2, vec)
    layer(cm, T, most, len_ref[T], ts_ref[0].astype(f32), tok, cot, seg, wt, btime, g1, b1, g2, b2, bdown, bup, out, gtok, refs[22:])


def run_plain(most, length, ts, tok, cot, seg, wq, wo, w2, wt, vecs, bup):
    seq, D = tok.shape
    P, NF, F = wq.shape[0], w2.shape[0], w2.shape[-1]
    S = jax.ShapeDtypeStruct
    vm = pl.BlockSpec(memory_space=pltpu.VMEM)
    sm = pl.BlockSpec(memory_space=pltpu.SMEM)
    return pl.pallas_call(
        functools.partial(plain_kernel, most, 0),
        out_shape=(S((seq, D), bf16), S((seq, D), f32), S(wq.shape, bf16), S(wo.shape, bf16), S(w2.shape, bf16), S((16, D), f32)),
        in_specs=[sm, sm] + [vm] * 14, out_specs=[vm] * 6,
        scratch_shapes=layer_scratch(seq, D, P, NF, F),
        compiler_params=pltpu.CompilerParams(vmem_limit_bytes=60 << 20),
    )(length, ts, tok, cot, seg, wq, wo, w2, wt, *[v[None] for v in vecs], bup)


def linked_kernel(most, ng, nt, names, semnames, n_layer, *refs):
    len_ref, ts_ref, tok, cot, seg, w_qkv, w_out, w_up, w_down, wt, btime, g1, b1, g2, b2, bdown, bup = refs[:17]
    out, gtok, o_qkv, o_out, o_up, o_down, gwt, vec = refs[17:25]
    sc = refs[25:25 + n_layer]
    rest = refs[25 + n_layer:]
    bufs = dict(zip(names, rest[:len(names)]))
    sr = rest[len(names):]
    sems = {nm: (sr[2 * i], sr[2 * i + 1]) for i, nm in enumerate(semnames)}
    bufs.update(w_qkv=w_qkv, w_out=w_out, w_up=w_up, w_down=w_down, o_qkv=o_qkv, o_out=o_out, o_up=o_up, o_down=o_down)
    bufs["E"] = tuple(bufs.pop(k) for k in ("EZ", "EX", "EC"))
    bufs["L"] = tuple(bufs.pop(k) for k in ("LZ", "LX", "LC"))
    cm = Linked(ng, nt, bufs, sems)
    T = cm.t
    NE = 4 + bup.shape[0]
    cm.early = lambda rows: cm.v_start("E", rows)
    cm.late = lambda rows: cm.v_start("L", rows)
    plain_hook = cm.hook

    def hook(place, j=None):
        plain_hook(place, j)
        if place == "back_mid":
            @pl.when(j == 0)
            def _():
                cm.v_mid("E", NE)
            @pl.when(j == 1)
            def _():
                cm.v_last("E", NE)

    cm.hook = hook
    layer(cm, T, most, len_ref[T], ts_ref[0].astype(f32), tok, cot, seg, wt, btime, g1, b1, g2, b2, bdown, bup, out, gtok, sc)
    cm.v_mid("L", 3)
    embs, sums = cm.v_done("E", NE)
    vec[4:4 + NE - 1, :] = sums
    cm.v_last("L", 3)
    cm.hook("finish")
    grads, late = cm.v_done("L", 3)
    vec[2:4, :] = late
    vec[1:2, :] = colsum(grads)
    gwt[...] = lax.dot_general(embs, grads, (((0,), (0,)), ((), ())), precision=lax.Precision.HIGHEST, preferred_element_type=f32)
    cm.hook("leave")
    cm.v_leave("E")
    cm.v_leave("L")


def run_linked(most, nd, nt, length, ts, tok, cot, seg, w_qkv, w_out, w_up, w_down, wt, vecs, bup):
    seq, D = tok.shape
    ng = nd // 2
    r, F = w_up.shape
    P, NF = nt, nt
    S, V = jax.ShapeDtypeStruct, pltpu.VMEM
    DMA = pltpu.SemaphoreType.DMA
    bufs = dict(
        WQ=V((nt, ng, 2, r, 384), bf16), WO=V((nt, ng, 2, r, 128), bf16), W2=V((nt, 2, ng, 2, r, F), bf16),
        DQ=V((nt, ng, 2, r, 384), bf16), DO=V((nt, ng, 2, r, 128), bf16), D2=V((nt, 2, ng, 2, r, F), bf16),
        CQ=V((nt, ng, r, 384), bf16), XQ=V((nt, ng, r, 384), bf16), ZQ=V((nt, r, 384), bf16),
        CO=V((nt, ng, r, 128), bf16), XO=V((ng, nt, r, 128), bf16), ZO=V((nt, r, 128), bf16),
        C2=V((nt, 2, ng, r, F), bf16), X2=V((nt, ng, 2, r, F), bf16), Z2=V((nt, 2, r, F), bf16),
        EZ=V((nt, 8, D), f32), EX=V((ng, 16, D), f32), EC=V((2, nt * ng + 8, D), f32),
        LZ=V((nt, 8, D), f32), LX=V((ng, 16, D), f32), LC=V((2, nt * ng + 8, D), f32),
    )
    sems = dict(gq_plane=(nt, ng), gq_z=(nt,), gq_core=(nt,), go_z=(nt,), g2_z=(nt,), go_plane=(ng,), go_core=(), g2_plane=(nt, ng), g2_core=(nt,),
        rq_core=(nt,), rq_plane=(nt, ng), rq_z=(nt,), r2_core=(nt,), r2_plane=(nt, ng), r2_z=(nt,), ro_core=(), ro_plane=(ng,), ro_z=(nt,),
        E_z=(nt,), E_plane=(ng,), E_core=(), L_z=(nt,), L_plane=(ng,), L_core=())
    ls = layer_scratch(seq, D, P, NF, F)
    scratch = ls + list(bufs.values())
    for s in sems.values():
        scratch += [DMA(s), DMA(s)]
    vm = pl.BlockSpec(memory_space=pltpu.VMEM)
    sm = pl.BlockSpec(memory_space=pltpu.SMEM)
    return pl.pallas_call(
        functools.partial(linked_kernel, most, ng, nt, tuple(bufs), tuple(sems), len(ls)),
        out_shape=(S((seq, D), bf16), S((seq, D), f32), S(w_qkv.shape, f32), S(w_out.shape, f32), S(w_up.shape, f32), S(w_down.shape, f32), S((D, D), f32), S((16, D), f32)),
        in_specs=[sm, sm] + [vm] * 15, out_specs=[vm] * 8,
        scratch_shapes=scratch,
        compiler_params=pltpu.CompilerParams(vmem_limit_bytes=62 << 20, collective_id=0, has_side_effects=True),
    )(length, ts, tok, cot, seg, w_qkv, w_out, w_up, w_down, wt, *[v[None] for v in vecs], bup)


def emit_kernel(nb, *refs):
    big, outs, small, bufs = refs[:8], refs[8:15], refs[15:22], refs[22:30]
    sem_in, sem_out = refs[30:]
    ins = [pltpu.make_async_copy(a, b, sem_in.at[i]) for i, (a, b) in enumerate(zip(big, bufs))]
    ups = [pltpu.make_async_copy(a, b, sem_out.at[i]) for i, (a, b) in enumerate(zip(bufs, outs))]
    for x in ins:
        x.start()
    for x, y in zip(ins, ups):
        x.wait()
        y.start()
    ins[7].wait()
    vec = bufs[7]
    for k, o in enumerate(small[:-1]):
        o[...] = vec[1 + k, :]
    n = vec.shape[1]
    for k in range(nb):
        small[-1][pl.ds(k * n, n)] = vec[7 + k, :]
    for y in ups:
        y.wait()


def emit(nb, *big):
    S = jax.ShapeDtypeStruct
    D = big[-1].shape[1]
    vm = pl.BlockSpec(memory_space=pltpu.VMEM)
    hb = pl.BlockSpec(memory_space=pltpu.HBM)
    return pl.pallas_call(
        functools.partial(emit_kernel, nb),
        out_shape=tuple(S(x.shape, x.dtype) for x in big[:-1]) + tuple(S((D,), f32) for _ in range(6)) + (S((nb * D,), f32),),
        in_specs=[hb] * 8, out_specs=[hb] * 7 + [vm] * 7,
        scratch_shapes=[pltpu.VMEM(x.shape, x.dtype) for x in big] + [pltpu.SemaphoreType.DMA((8,)), pltpu.SemaphoreType.DMA((7,))],
        compiler_params=pltpu.CompilerParams(vmem_limit_bytes=60 << 20),
    )(*big)


def shards(
    tokens,
    timestep,
    segment_ids,
    span_lengths,
    w_qkv,
    w_out_t,
    w_up,
    w_down_t,
    w_time,
    b_time,
    ln1_gain,
    ln1_bias,
    ln2_gain,
    ln2_bias,
    b_up,
    b_down,
    cotangent,
):
    seq, D = tokens.shape[1:]
    nd, nt = lax.axis_size("dp"), lax.axis_size("tensor")
    vecs = (b_time, ln1_gain, ln1_bias, ln2_gain, ln2_bias, b_down)
    F = w_up.shape[1]
    bup = b_up.reshape(nt, 1, F)
    if w_up.shape[0] % 16 == 0:
        out, gtok, gq, go, gu, gd, gwt, vec = run_linked(
            DOC, nd, nt, span_lengths, timestep, tokens[0], cotangent[0], segment_ids,
            w_qkv, w_out_t, w_up, w_down_t, w_time, vecs, bup)
        gq, go, gu, gd, out, gwt, gtok, *v = emit(nt, gq, go, gu, gd, out, gwt, gtok, vec)
        return (out[None], gtok[None], gq, go, gu, gd, gwt, v[0], v[1], v[2], v[3], v[4], v[6], v[5])
    HB = w_qkv.shape[2]

    def whole(w):
        return lax.all_gather(lax.all_gather(w.astype(bf16), "dp", axis=w.ndim - 2, tiled=True), "tensor", axis=0)

    def part(g, dim):
        g = lax.psum_scatter(g, "dp", scatter_dimension=dim, tiled=True)
        return lax.psum_scatter(g, "tensor", scatter_dimension=0, tiled=True)[0].astype(f32)

    wq = whole(jnp.transpose(w_qkv, (1, 0, 2)).reshape(w_qkv.shape[1], 3 * HB))
    out, gtok, dwq, dwo, dw2, vec = run_plain(
        DOC, span_lengths, timestep, tokens[0], cotangent[0], segment_ids,
        wq, whole(w_out_t), whole(jnp.stack([w_up, w_down_t])), w_time, vecs, bup)
    lines = lax.all_gather(jnp.stack([vec[0], vec[8]]), ("dp", "tensor"), axis=1, tiled=False)
    gwt = jnp.dot(lines[0].T, lines[1], precision=lax.Precision.HIGHEST)
    small = lax.psum(vec, ("dp", "tensor"))
    gq, g2 = part(dwq, 1), part(dw2, 2)
    return (
        out[None], gtok[None], jnp.transpose(gq.reshape(gq.shape[0], 3, HB), (1, 0, 2)), part(dwo, 1), g2[0], g2[1],
        gwt, small[8], small[9], small[10], small[1], small[2], small[4:4 + nt].reshape(-1), small[3])


def solution(mesh):
    return jax.shard_map(
        shards,
        mesh=mesh,
        in_specs=(
            P_(("dp", "tensor"), None, None),
            P_(("dp", "tensor")),
            P_("dp", None),
            P_("dp"),
            P_(None, "dp", "tensor"),
            P_("dp", "tensor"),
            P_("dp", "tensor"),
            P_("dp", "tensor"),
            P_(),
            P_(),
            P_(),
            P_(),
            P_(),
            P_(),
            P_(),
            P_(),
            P_(("dp", "tensor"), None, None),
        ),
        out_specs=(
            P_(("dp", "tensor"), None, None),
            P_(("dp", "tensor"), None, None),
            P_(None, "dp", "tensor"),
            P_("dp", "tensor"),
            P_("dp", "tensor"),
            P_("dp", "tensor"),
            P_(),
            P_(),
            P_(),
            P_(),
            P_(),
            P_(),
            P_(),
            P_(),
        ),
        check_vma=False,
    )
```

```python
import functools
import math

import jax
import jax.numpy as jnp
from jax import lax
from jax.experimental import pallas as pl
from jax.experimental.pallas import tpu as pltpu
from jax.sharding import PartitionSpec as P_

f32, bf16 = jnp.float32, jnp.bfloat16
HS = 64
TR = 256
BIG = 1e30
EPS = 1e-5
DOC = 512
LEAST = 512
LOG2E = math.log2(math.e)
LN2 = math.log(2.0)
SCALE = 1.0 / math.sqrt(HS)


def nt_dot(a, b):
    return lax.dot_general(a, b, (((1,), (1,)), ((), ())), preferred_element_type=f32)


def tn_dot(a, b):
    return lax.dot_general(a, b, (((0,), (0,)), ((), ())), preferred_element_type=f32)


def nn_dot(a, b):
    return jnp.dot(a, b, preferred_element_type=f32)


def lane(shape):
    return lax.broadcasted_iota(jnp.int32, shape, len(shape) - 1)


def rows_of(i, n=TR):
    return pl.ds(pl.multiple_of(i * n, n), n)


def normed(x):
    mean = jnp.mean(x, axis=-1, keepdims=True)
    c = x - mean
    var = jnp.mean(c * c, axis=-1, keepdims=True)
    r = lax.rsqrt(var + EPS)
    return c * r, r


def norm_back(xhat, r, gain, gy):
    gh = gy * gain
    a = jnp.mean(gh, axis=-1, keepdims=True)
    b = jnp.mean(gh * xhat, axis=-1, keepdims=True)
    return r * (gh - a - xhat * b)


def colsum(x):
    return jnp.sum(x, axis=0, keepdims=True)


def halves(prod):
    low = lane(prod.shape) < HS
    s0 = jnp.sum(jnp.where(low, prod, 0.0), axis=-1, keepdims=True)
    s1 = jnp.sum(jnp.where(low, 0.0, prod), axis=-1, keepdims=True)
    return s0, s1


def split3(x):
    hi = x.astype(bf16)
    rest = x - hi.astype(f32)
    mid = rest.astype(bf16)
    lo = (rest - mid.astype(f32)).astype(bf16)
    return hi, mid, lo


def window(i, seq, most):
    lo = max(0, (i * TR - most + 1) // 128 * 128)
    hi = min(seq, -(-(i * TR + TR - 1 + most) // 128) * 128)
    return lo, hi


def gelu_parts(u):
    c0, c1 = 0.7978845608028654, 0.044715
    u2 = u * u
    th = jnp.tanh(u * (c0 + (c0 * c1) * u2))
    half = 0.5 + 0.5 * th
    act = u * half
    grad = half + (0.5 * u) * (1.0 - th * th) * (c0 + (3.0 * c0 * c1) * u2)
    return act, grad


def transpose_into(dst, src, seq):
    def step(i, _):
        r = rows_of(i)
        dst[:, r] = src[r, :].T
        return 0
    for i in range(seq // TR):
        r = slice(i * TR, i * TR + TR)
        dst[:, r] = src[r, :].T


def half_sums(prod, swap=False):
    hi = prod.astype(bf16)
    lo = (prod - hi.astype(f32)).astype(bf16)
    a = lax.broadcasted_iota(jnp.int32, (256, 128), 0) // HS % 2
    b = lax.broadcasted_iota(jnp.int32, (256, 128), 1) // HS
    w = jnp.where((a != b) if swap else (a == b), 1.0, 0.0).astype(bf16)
    return nn_dot(jnp.concatenate([hi, lo], axis=1), w)


def attend_fwd(seq, most, length, qkv, qaug, kaug, mixed, lse, qq, kk, vv, hp, half):
    n = seq // TR
    def prep(i, _):
        r = rows_of(i)
        low = lane((TR, 128)) < HS
        q, k, v = (qkv[hp, r, 128 * c:128 * c + 128] for c in range(3))
        qa, ka = qaug[r, :], kaug[r, :]
        one = jnp.ones_like(v)
        qq[0, r, :] = jnp.where(low, q, qa)
        qq[1, r, :] = jnp.where(low, qa, q)
        kk[0, r, :] = jnp.where(low, k, ka)
        kk[1, r, :] = jnp.where(low, ka, k)
        vv[0, r, :] = jnp.where(low, v, one)
        vv[1, r, :] = jnp.where(low, one, v)
        return 0
    for i in range(n):
        prep(i, 0)

    def score(i, h):
        lo, hi = window(i, seq, most)
        return nt_dot(qq[h, i * TR:i * TR + TR, :], kk[h, lo:hi, :])

    def soft(i, s, own):
        m = jnp.max(s, axis=-1, keepdims=True)
        if own is not None:
            pad = (lax.broadcasted_iota(jnp.int32, (TR, 1), 0) + i * TR) >= length
            m = jnp.where(pad, jnp.maximum(m, own), m)
        return m, jnp.exp2(s - m).astype(bf16)

    def finish(i, own, tops, outs):
        r = slice(i * TR, i * TR + TR)
        low = lane((TR, 128)) < HS
        num = jnp.where(low, outs[0], outs[1])
        den_x = jnp.where(low, outs[1], outs[0])
        if own[0] is not None:
            padf = ((lax.broadcasted_iota(jnp.int32, (TR, 1), 0) + i * TR) >= length).astype(f32)
            e0 = jnp.exp2(jnp.minimum(own[0] - tops[0], 0.0)).astype(bf16).astype(f32) * padf
            e1 = jnp.exp2(jnp.minimum(own[1] - tops[1], 0.0)).astype(bf16).astype(f32) * padf
            num = num + jnp.where(low, e0, e1) * qkv[hp, r, 256:384].astype(f32)
            den_x = den_x + jnp.where(low, e1, e0)
        mixed[hp, r, :] = (num / pltpu.roll(den_x, HS, 1)).astype(bf16)
        lse[hp, r, :] = jnp.where(low, tops[1], tops[0]) + jnp.log2(den_x)

    def selfs(i):
        if (i + 1) * TR <= LEAST:
            return (None, None)
        r = slice(i * TR, i * TR + TR)
        return halves(qkv[hp, r, 0:128].astype(f32) * qkv[hp, r, 128:256].astype(f32))

    units = [(i, h) for i in range(n) for h in range(2)]
    s = score(*units[0])
    tops, outs = [], []
    for u, (i, h) in enumerate(units):
        if (i, h) == (n // 2, 0):
            half()
        nxt = score(*units[u + 1]) if u + 1 < len(units) else None
        if h == 0:
            own = selfs(i)
        lo, hi = window(i, seq, most)
        m, p = soft(i, s, own[h])
        tops.append(m)
        outs.append(nn_dot(p, vv[h, lo:hi, :]))
        if h == 1:
            finish(i, own, tops, outs)
            tops, outs = [], []
        s = nxt


def attend_bwd(seq, most, length, qkv, qaug, kaug, mixed, lse, gm, qq, kk, vv, oo, dq, dkv, dqkv, hp):
    n = seq // TR
    def prep(i, _):
        r = slice(i * TR, i * TR + TR)
        low = lane((TR, 128)) < HS
        spot = lane((TR, 128)) % HS
        q, k, v = (qkv[hp, r, 128 * c:128 * c + 128] for c in range(3))
        g = gm[hp, r, :]
        dx = half_sums(g.astype(f32) * mixed[hp, r, :].astype(f32), True)
        def put(base, x):
            hi, mid, lo = split3(x)
            z = jnp.where(spot == 8, hi, base)
            z = jnp.where(spot == 9, mid, z)
            return jnp.where(spot == 10, lo, z)
        zero = jnp.zeros((TR, 128), bf16)
        qa = put(qaug[r, :], lse[hp, r, :])
        oa = put(zero, dx)
        ka = kaug[r, :]
        va = jnp.where((spot >= 8) & (spot < 11), -jnp.ones_like(zero), zero)
        for ref, x, a in ((qq, q, qa), (kk, k, ka), (vv, v, va), (oo, g, oa)):
            ref[0, r, :] = jnp.where(low, x, a)
            ref[1, r, :] = jnp.where(low, a, x)
        if (i + 1) * TR > LEAST:
            q, k, v, g = (x.astype(f32) for x in (q, k, v, g))
            padf = ((lax.broadcasted_iota(jnp.int32, (TR, 1), 0) + i * TR) >= length).astype(f32)
            ls = pltpu.roll(lse[hp, r, :], HS, 1)
            d = pltpu.roll(dx, HS, 1)
            pf = jnp.exp2(jnp.minimum(half_sums(q * k) - ls, 1.0)) * padf
            ds = (pf * (half_sums(g * v) - d)).astype(bf16).astype(f32)
            pf = pf.astype(bf16).astype(f32)
            dkv[2, 0, r, :] = ds
            dkv[2, 1, r, :] = pf
        return 0
    for i in range(n):
        prep(i, 0)
    lo, hi = window(0, seq, most)
    if hi < seq:
        dq[:, hi:seq, :] = jnp.zeros((2, seq - hi, 128), f32)

    def score(i, h):
        lo, hi = window(i, seq, most)
        r = slice(i * TR, i * TR + TR)
        return nt_dot(kk[h, r, :], qq[h, lo:hi, :]), nt_dot(vv[h, r, :], oo[h, lo:hi, :])

    def rest(i, h, st, dpt):
        lo, hi = window(i, seq, most)
        r = slice(i * TR, i * TR + TR)
        pt = jnp.exp2(st)
        dst = (pt * dpt).astype(bf16)
        dkv[h, 0, r, :] = nn_dot(dst, qq[h, lo:hi, :])
        dkv[h, 1, r, :] = nn_dot(pt.astype(bf16), oo[h, lo:hi, :])
        x = tn_dot(dst, kk[h, r, :])
        if i == 0:
            dq[h, lo:hi, :] = x
        else:
            dq[h, lo:hi, :] += x

    units = [(i, h) for i in range(n) for h in range(2)]
    s = score(*units[0])
    for u, (i, h) in enumerate(units):
        nxt = score(*units[u + 1]) if u + 1 < len(units) else None
        rest(i, h, *s)
        s = nxt

    for i in range(n):
        r = slice(i * TR, i * TR + TR)
        low = lane((TR, 128)) < HS
        gq = jnp.where(low, dq[0, r, :], dq[1, r, :])
        gk = jnp.where(low, dkv[0, 0, r, :], dkv[1, 0, r, :])
        gv = jnp.where(low, dkv[0, 1, r, :], dkv[1, 1, r, :])
        if (i + 1) * TR > LEAST:
            ds, pf = dkv[2, 0, r, :], dkv[2, 1, r, :]
            gq = gq + ds * qkv[hp, r, 128:256].astype(f32)
            gk = gk + ds * qkv[hp, r, 0:128].astype(f32)
            gv = gv + pf * gm[hp, r, :].astype(f32)
        dqkv[r, 0:128] = (gq * SCALE).astype(bf16)
        dqkv[r, 128:256] = (gk * LN2).astype(bf16)
        dqkv[r, 256:384] = gv.astype(bf16)


MESH = pl.DeviceIdType.MESH


class Plain:
    def __init__(self, wq, wo, w2, dwq, dwo, dw2, vec):
        self.wq, self.wo, self.w2 = wq, wo, w2
        self.dwq, self.dwo, self.dw2, self.vec = dwq, dwo, dw2, vec

    def getq(self, p):
        return self.wq[p]

    def geto(self):
        return jnp.concatenate([self.wo[p] for p in range(self.wo.shape[0])], axis=1)

    def getu(self, f):
        return self.w2[f, 0]

    def getd(self, f):
        return self.w2[f, 1]

    def putq(self, p, i, x):
        self.dwq[p, i, :] = x

    def puto(self, p, i, x):
        self.dwo[p, i, :] = x

    def put2(self, f, k, i, x):
        self.dw2[f, k, i, :] = x

    def order(self, j):
        return j

    def order_back(self, j):
        return j

    def hook(self, *_):
        pass

    def early(self, rows):
        for k, x in enumerate(rows):
            self.vec[k:k + 1, :] = x

    def late(self, rows):
        for k, x in enumerate(rows):
            self.vec[8 + k:9 + k, :] = x


class Linked:
    def __init__(self, ng, nt, bufs, sems):
        self.ng, self.nt = ng, nt
        self.__dict__.update(bufs)
        self.sem = sems
        d, self.t = lax.axis_index("dp"), lax.axis_index("tensor")
        self.d, self.g, self.c = d, d // 2, d % 2
        self.sent = []

    def dev(self, kind, k):
        if kind == "core":
            return (2 * self.g + 1 - self.c, self.t)
        if kind == "plane":
            return (2 * (self.g ^ k) + self.c, self.t)
        if kind == "dp":
            return (self.d ^ k, self.t)
        return (self.d, self.t ^ k)

    def copy(self, name, at, kind, k, src, dst):
        s, r = self.sem[name]
        for i in at:
            s, r = s.at[i], r.at[i]
        return pltpu.make_async_remote_copy(
            src_ref=src, dst_ref=dst, send_sem=s, recv_sem=r,
            device_id=self.dev(kind, k), device_id_type=MESH)

    def getq(self, p):
        x = self.WQ[p]
        return x.reshape(-1, x.shape[-1])

    def geto(self):
        return jnp.concatenate([self.WO[p].reshape(-1, 128) for p in range(self.nt)], axis=1)

    def getu(self, f):
        x = self.W2[f, 0]
        return x.reshape(-1, x.shape[-1])

    def getd(self, f):
        x = self.W2[f, 1]
        return x.reshape(-1, x.shape[-1])

    def blocks(self, ref, i):
        rows = ref.shape[-2]
        m = (i.stop - i.start) // (2 * rows)
        return slice(i.start // (2 * rows), i.stop // (2 * rows)), (m, 2, rows, ref.shape[-1])

    def putq(self, p, i, x):
        b, shape = self.blocks(self.DQ, i)
        self.DQ[p, b] = x.reshape(shape)

    def puto(self, p, i, x):
        b, shape = self.blocks(self.DO, i)
        self.DO[p, b] = x.reshape(shape)

    def put2(self, f, k, i, x):
        b, shape = self.blocks(self.D2, i)
        self.D2[f, k, b] = x.reshape(shape)

    def order(self, j):
        return self.t ^ j

    def order_back(self, j):
        return self.t ^ (self.nt - 1 - j)

    def enter(self):
        bar = pltpu.get_barrier_semaphore()
        peers = [("dp", k) for k in range(1, 2 * self.ng)] + [("z", k) for k in range(1, self.nt)]
        for kind, k in peers:
            pl.semaphore_signal(bar, inc=1, device_id=self.dev(kind, k), device_id_type=MESH)
        pl.semaphore_wait(bar, len(peers))

    def q_plane(self, x, k, incoming=False):
        g, c, p = self.g, self.c, self.t ^ x
        return self.copy("gq_plane", (x, k), "plane", k, self.WQ.at[p, g, c], self.WQ.at[p, g ^ k if incoming else g, c])

    def q_z(self, k, incoming=False):
        g, c, t = self.g, self.c, self.t
        return self.copy("gq_z", (k,), "z", k, self.WQ.at[t, g, c], self.WQ.at[t ^ k if incoming else t, g, c])

    def q_core(self, k):
        c, t = self.c, self.t
        return self.copy("gq_core", (k,), "core", 0, self.WQ.at[t ^ k, :, c], self.WQ.at[t ^ k, :, c])

    def q_core_in(self, k):
        c, t = self.c, self.t
        return self.copy("gq_core", (k,), "core", 0, self.WQ.at[t ^ k, :, c], self.WQ.at[t ^ k, :, 1 - c])

    def o_z(self, k, incoming=False):
        g, c, t = self.g, self.c, self.t
        return self.copy("go_z", (k,), "z", k, self.WO.at[t, g, c], self.WO.at[t ^ k if incoming else t, g, c])

    def f_z(self, k, incoming=False):
        g, c, t = self.g, self.c, self.t
        return self.copy("g2_z", (k,), "z", k, self.W2.at[t, :, g, c], self.W2.at[t ^ k if incoming else t, :, g, c])

    def o_plane(self, k, incoming=False):
        g, c = self.g, self.c
        return self.copy("go_plane", (k,), "plane", k, self.WO.at[:, g, c], self.WO.at[:, g ^ k if incoming else g, c])

    def o_core(self, incoming=False):
        c = self.c
        return self.copy("go_core", (), "core", 0, self.WO.at[:, :, c], self.WO.at[:, :, 1 - c if incoming else c])

    def f_plane(self, j, k, incoming=False):
        g, c, f = self.g, self.c, self.t ^ j
        return self.copy("g2_plane", (j, k), "plane", k, self.W2.at[f, :, g, c], self.W2.at[f, :, g ^ k if incoming else g, c])

    def f_core(self, j, incoming=False):
        c, f = self.c, self.t ^ j
        return self.copy("g2_core", (j,), "core", 0, self.W2.at[f, :, :, c], self.W2.at[f, :, :, 1 - c if incoming else c])

    def rq(self, stage, x, k=0, incoming=False):
        g, c, p = self.g, self.c, self.t ^ x
        if stage == "core":
            return self.copy("rq_core", (x,), "core", 0, self.DQ.at[p, :, 1 - c], self.CQ.at[x])
        if stage == "plane":
            return self.copy("rq_plane", (x, k), "plane", k, self.DQ.at[p, g ^ k, c], self.XQ.at[x, k])
        return self.copy("rq_z", (x,), "z", x, self.DQ.at[p, g, c], self.ZQ.at[x])

    def r2(self, stage, x, k=0):
        g, c, p = self.g, self.c, self.t ^ x
        if stage == "core":
            return self.copy("r2_core", (x,), "core", 0, self.D2.at[p, :, :, 1 - c], self.C2.at[x])
        if stage == "plane":
            return self.copy("r2_plane", (x, k), "plane", k, self.D2.at[p, :, g ^ k, c], self.X2.at[x, k])
        return self.copy("r2_z", (x,), "z", x, self.D2.at[p, :, g, c], self.Z2.at[x])

    def ro(self, stage, k=0):
        g, c, t = self.g, self.c, self.t
        if stage == "core":
            return self.copy("ro_core", (), "core", 0, self.DO.at[:, :, 1 - c], self.CO)
        if stage == "plane":
            return self.copy("ro_plane", (k,), "plane", k, self.DO.at[:, g ^ k, c], self.XO.at[k])
        return self.copy("ro_z", (k,), "z", k, self.DO.at[t ^ k, g, c], self.ZO.at[k])

    def q_after_core(self, x):
        p, c = self.t ^ x, self.c
        self.rq("core", x).wait_recv()
        self.DQ[p, :, c] = (self.DQ[p, :, c].astype(f32) + self.CQ[x].astype(f32)).astype(bf16)
        for k in range(1, self.ng):
            self.rq("plane", x, k).start()

    def q_after_plane(self, x):
        p, c, g = self.t ^ x, self.c, self.g
        acc = self.DQ[p, g, c].astype(f32)
        for k in range(1, self.ng):
            self.rq("plane", x, k).wait_recv()
            acc = acc + self.XQ[x, k].astype(f32)
        self.DQ[p, g, c] = acc.astype(bf16)

    def f_after_core(self, x):
        p, c = self.t ^ x, self.c
        self.r2("core", x).wait_recv()
        for u in range(2):
            def step(i, _):
                self.D2[p, u, i, c] = (self.D2[p, u, i, c].astype(f32) + self.C2[x, u, i].astype(f32)).astype(bf16)
                return 0
            lax.fori_loop(0, self.ng, step, 0)
        for k in range(1, self.ng):
            self.r2("plane", x, k).start()

    def f_after_plane(self, x):
        p, c, g = self.t ^ x, self.c, self.g
        for k in range(1, self.ng):
            self.r2("plane", x, k).wait_recv()
        for u in range(2):
            acc = self.D2[p, u, g, c].astype(f32)
            for k in range(1, self.ng):
                acc = acc + self.X2[x, k, u].astype(f32)
            self.D2[p, u, g, c] = acc.astype(bf16)

    def hook(self, place, j=None):
        ng, nt, t, g, c = self.ng, self.nt, self.t, self.g, self.c
        if place == "start":
            rq = self.w_qkv.shape[1]
            for k in range(3):
                self.WQ[t, g, c, :, 128 * k:128 * k + 128] = self.w_qkv[k].astype(bf16)
            self.WO[t, g, c] = self.w_out[...].astype(bf16)
            self.W2[t, 0, g, c] = self.w_up[...].astype(bf16)
            self.W2[t, 1, g, c] = self.w_down[...].astype(bf16)
            for x in (self.E[1], self.L[1]):
                x[self.d] = jnp.zeros(x.shape[1:], f32)
            self.enter()
            for k in range(1, ng):
                self.q_plane(0, k).start()
            for k in range(1, nt):
                self.q_z(k).start()
                self.o_z(k).start()
        elif place == "normed":
            for k in range(1, ng):
                self.q_plane(0, k, True).wait_recv()
            self.q_core(0).start()
            for k in range(1, nt):
                self.f_z(k).start()
        elif place == "pair":
            self.q_core_in(j).wait_recv()
        elif place == "pair_proj":
            @pl.when(j == 0)
            def _():
                for x in range(1, nt):
                    self.q_z(x, True).wait_recv()
                    for k in range(1, ng):
                        self.q_plane(x, k).start()
                for x in range(1, nt):
                    self.o_z(x, True).wait_recv()
                for k in range(1, ng):
                    self.o_plane(k).start()
                for k in range(1, ng):
                    self.f_plane(0, k).start()
        elif place == "pair_half":
            @pl.when(j < nt - 1)
            def _():
                for k in range(1, ng):
                    self.q_plane(j + 1, k, True).wait_recv()
                self.q_core(j + 1).start()
            @pl.when(j == nt - 2)
            def _():
                for k in range(1, ng):
                    self.o_plane(k, True).wait_recv()
                self.o_core().start()
            @pl.when(j == nt - 1)
            def _():
                for k in range(1, ng):
                    self.f_plane(0, k, True).wait_recv()
                self.f_core(0).start()
        elif place == "pair_mid":
            @pl.when(j < nt - 1)
            def _():
                self.f_z(j + 1, True).wait_recv()
                for k in range(1, ng):
                    self.f_plane(j + 1, k).start()
        elif place == "mixed":
            self.o_core(True).wait_recv()
        elif place == "chunk":
            self.f_core(j, True).wait_recv()
        elif place == "chunk_mid":
            @pl.when(j < nt - 1)
            def _():
                for k in range(1, ng):
                    self.f_plane(j + 1, k, True).wait_recv()
                self.f_core(j + 1).start()
            @pl.when(j >= 1)
            def _():
                self.f_after_core(j - 1)
        elif place == "chunk_end":
            self.r2("core", j).start()
        elif place == "ffn_done":
            self.f_after_core(nt - 1)
        elif place == "out_grad":
            self.ro("core").start()
        elif place == "back_mid":
            self.f_after_plane(j)
            @pl.when(j >= 1)
            def _():
                self.r2("z", j).start()
                self.q_after_core(nt - j)
            @pl.when(j == 0)
            def _():
                self.ro("core").wait_recv()
                for p in range(nt):
                    self.DO[p, :, c] = (self.DO[p, :, c].astype(f32) + self.CO[p].astype(f32)).astype(bf16)
                for k in range(1, ng):
                    self.ro("plane", k).start()
                self.v_mid("E", self.ne)
            @pl.when(j == 1)
            def _():
                for k in range(1, ng):
                    self.ro("plane", k).wait_recv()
                for p in range(nt):
                    acc = self.DO[p, g, c].astype(f32)
                    for k in range(1, ng):
                        acc = acc + self.XO[k, p].astype(f32)
                    self.DO[p, g, c] = acc.astype(bf16)
                for k in range(1, nt):
                    self.ro("z", k).start()
            @pl.when(j >= 2)
            def _():
                self.q_after_plane(nt - j + 1)
                self.rq("z", nt - j + 1).start()
        elif place == "back_end":
            self.rq("core", nt - 1 - j).start()
        elif place == "back_done":
            self.q_after_core(0)
            self.q_after_plane(1)
            self.rq("z", 1).start()
        elif place == "finish":
            for x in range(1, nt):
                self.r2("z", x).wait_recv()
                self.ro("z", x).wait_recv()
            for u, o in enumerate((self.o_up, self.o_down)):
                acc = self.D2[t, u, g, c].astype(f32)
                for x in range(1, nt):
                    acc = acc + self.Z2[x, u].astype(f32)
                o[...] = acc
            acc = self.DO[t, g, c].astype(f32)
            for x in range(1, nt):
                acc = acc + self.ZO[x].astype(f32)
            self.o_out[...] = acc
        elif place == "finish_q":
            acc = self.DQ[t, g, c].astype(f32)
            for k in range(1, ng):
                self.rq("plane", 0, k).wait_recv()
                acc = acc + self.XQ[0, k].astype(f32)
            for x in range(1, nt):
                self.rq("z", x).wait_recv()
                acc = acc + self.ZQ[x].astype(f32)
            for k in range(3):
                self.o_qkv[k] = acc[:, 128 * k:128 * k + 128]
        elif place == "leave":
            for k in range(1, ng):
                self.o_plane(k).wait_send()
                self.ro("plane", k).wait_send()
                for x in range(nt):
                    self.q_plane(x, k).wait_send()
                    self.f_plane(x, k).wait_send()
                    self.r2("plane", x, k).wait_send()
                    self.rq("plane", x, k).wait_send()
            for k in range(nt):
                self.q_core(k).wait_send()
                self.f_core(k).wait_send()
                self.r2("core", k).wait_send()
                self.rq("core", k).wait_send()
            self.o_core().wait_send()
            self.ro("core").wait_send()
            for k in range(1, nt):
                self.q_z(k).wait_send()
                self.o_z(k).wait_send()
                self.f_z(k).wait_send()
                self.r2("z", k).wait_send()
                self.rq("z", k).wait_send()
                self.ro("z", k).wait_send()

    def v(self, name, stage, k, incoming=False):
        Z, X = getattr(self, name)
        if stage == "z":
            return self.copy(name + "_z", (k,), "z", k, Z.at[self.t], Z.at[self.t ^ k if incoming else self.t])
        return self.copy(name + "_dp", (k,), "dp", k, X.at[self.d], X.at[self.d ^ k if incoming else self.d])

    def v_start(self, name, rows):
        Z = getattr(self, name)[0]
        for k, x in enumerate(rows):
            Z[self.t, k:k + 1, :] = x
        for k in range(1, self.nt):
            self.v(name, "z", k).start()

    def v_mid(self, name, m):
        Z, X = getattr(self, name)
        nt = self.nt
        for k in range(1, nt):
            self.v(name, "z", k, True).wait_recv()
        for k in range(nt):
            X[self.d, k:k + 1, :] = Z[k, 0:1, :]
        s = Z[0, 1:m, :]
        for k in range(1, nt):
            s = s + Z[k, 1:m, :]
        X[self.d, 8:8 + m - 1, :] = s
        for k in range(1, 2 * self.ng):
            self.v(name, "dp", k).start()

    def v_done(self, name, m):
        X = getattr(self, name)[1]
        nd = 2 * self.ng
        for k in range(1, nd):
            self.v(name, "dp", k, True).wait_recv()
        s = X[0, 8:8 + m - 1, :]
        for k in range(1, nd):
            s = s + X[k, 8:8 + m - 1, :]
        return jnp.concatenate([X[k, 0:8, :] for k in range(nd)], axis=0), s

    def v_leave(self, name):
        for k in range(1, self.nt):
            self.v(name, "z", k).wait_send()
        for k in range(1, 2 * self.ng):
            self.v(name, "dp", k).wait_send()


TILE = dict(ln1=256, proj=1024, ln2=512, tile=512, wgrad=512, ln2b=256, gmix=1024, gwo=512, qgrad=512, back=1024, ln1b=256)
UNROLL = {"proj", "ln2", "tile", "wgrad", "gmix", "gwo", "qgrad", "back"}


def loop(name, total, body, init):
    n = TILE[name]
    if name in UNROLL or total == n:
        for i in range(total // n):
            init = body(slice(i * n, i * n + n), init)
        return init
    return lax.fori_loop(0, total // n, lambda i, x: body(pl.ds(pl.multiple_of(i * n, n), n), x), init)


def layer(cm, T, most, length, t, tok, cot, seg, wt, btime, g1, b1, g2, b2, bdown, bup, out, gtok, sc):
    tp, n1, qkv, qaug, kaug, mixed, lse, qq, kk, vv, oo, dq, dkv, dqkv, mid, n2, ffn, gn, act, gu, gm, xT, xT2, bsum = sc
    seq, D = tok.shape
    P = qkv.shape[0]
    NF, F = bsum.shape[0], bsum.shape[2]
    n = seq // TR
    cm.hook("start")
    cm.hook("row_in")
    half = D // 2
    ang = t * jnp.exp(-math.log(10000.0) * lax.broadcasted_iota(jnp.int32, (8, half), 1).astype(f32) / half)
    emb = jnp.concatenate([jnp.sin(ang), jnp.cos(ang)], axis=1)
    tp[...] = jnp.dot(emb, wt[...], precision=lax.Precision.HIGHEST, preferred_element_type=f32)[0:1, :] + btime[...]

    def ln1(r, _):
        xh, _r = normed(tok[r, :].astype(f32) + tp[...])
        n1[r, :] = (xh * g1[...] + b1[...]).astype(bf16)
        return 0

    loop("ln1", seq, ln1, 0)
    cm.hook("normed")
    srow = seg[pl.ds(T, 1), :].astype(f32)
    for b in range(seq // 128):
        col = jnp.broadcast_to(srow[:, 128 * b:128 * b + 128], (128, 128)).T
        spot = lane((128, 128)) % HS
        pos = lax.broadcasted_iota(jnp.int32, (128, 128), 0) + 128 * b
        same = col == spot.astype(f32)
        r = slice(128 * b, 128 * b + 128)
        qaug[r, :] = jnp.where(same & (spot < 8), 1.0, 0.0).astype(bf16)
        ka = jnp.where(same & (pos < length), 0.0, -BIG)
        kaug[r, :] = jnp.where(spot < 8, ka, jnp.where(spot < 11, -1.0, 0.0)).astype(bf16)

    def pair_fwd(j, _):
        hp = cm.order(j)
        cm.hook("pair", j)

        def proj(r, _):
            x = nn_dot(n1[r, :], cm.getq(hp))
            s = jnp.where(lane((1, 384)) < 128, SCALE * LOG2E, 1.0)
            qkv[hp, r, :] = (x * s).astype(bf16)
            return 0

        loop("proj", seq, proj, 0)
        cm.hook("pair_proj", j)
        attend_fwd(seq, most, length, qkv, qaug, kaug, mixed, lse, qq, kk, vv, hp, lambda: cm.hook("pair_half", j))
        cm.hook("pair_mid", j)
        return 0

    lax.fori_loop(0, P, pair_fwd, 0)
    cm.hook("mixed")

    def ln2(r, _):
        mx = jnp.concatenate([mixed[p, r, :] for p in range(P)], axis=1)
        x = tok[r, :].astype(f32) + tp[...] + nt_dot(mx, cm.geto())
        mid[r, :] = x
        xh, _r = normed(x)
        n2[r, :] = (xh * g2[...] + b2[...]).astype(bf16)
        ffn[r, :] = jnp.zeros((TILE["ln2"], D), f32)
        gn[r, :] = jnp.zeros((TILE["ln2"], D), f32)
        return 0

    loop("ln2", seq, ln2, 0)
    cm.hook("cot_in")
    transpose_into(xT, cot, seq)
    transpose_into(xT2, n2, seq)

    def chunk(j, _):
        f = cm.order(j)
        cm.hook("chunk", j)

        def tile(r, acc):
            u = nn_dot(n2[r, :], cm.getu(f)) + bup[f]
            a, ga = gelu_parts(u)
            a = a.astype(bf16)
            g = (nn_dot(cot[r, :], cm.getd(f)) * ga).astype(bf16)
            act[r, :] = a
            gu[r, :] = g
            ffn[r, :] += nt_dot(a, cm.getd(f))
            gn[r, :] += nt_dot(g, cm.getu(f))
            return acc + colsum(g.astype(f32))

        bsum[f] = loop("tile", seq, tile, jnp.zeros((1, F), f32))
        cm.hook("chunk_mid", j)

        def wgrad(r, _):
            cm.put2(f, 1, r, nn_dot(xT[r, :], act[...]).astype(bf16))
            cm.put2(f, 0, r, nn_dot(xT2[r, :], gu[...]).astype(bf16))
            return 0

        loop("wgrad", D, wgrad, 0)
        cm.hook("chunk_end", j)
        return 0

    lax.fori_loop(0, NF, chunk, 0)

    def ln2b(r, acc):
        c = cot[r, :].astype(f32)
        x = mid[r, :]
        out[r, :] = (x + ffn[r, :] + bdown[...]).astype(bf16)
        xh, rr = normed(x)
        gy = gn[r, :]
        gmid = c + norm_back(xh, rr, g2[...], gy)
        mid[r, :] = gmid
        n2[r, :] = gmid.astype(bf16)
        gn[r, :] = jnp.zeros((TILE["ln2b"], D), f32)
        return acc[0] + colsum(gy * xh), acc[1] + colsum(gy), acc[2] + colsum(c)

    z = jnp.zeros((1, D), f32)
    a = loop("ln2b", seq, ln2b, (z, z, z))
    cm.hook("row_out")
    cm.early([emb[0:1, :], *a] + [bsum[f] for f in range(NF)])
    cm.hook("ffn_done")
    transpose_into(xT2, n2, seq)

    def gmix(r, _):
        x = nn_dot(n2[r, :], cm.geto()).astype(bf16)
        for p in range(P):
            gm[p, r, :] = x[:, 128 * p:128 * p + 128]
        return 0

    loop("gmix", seq, gmix, 0)

    def gwo(r, _):
        m = jnp.concatenate([mixed[p] for p in range(P)], axis=1)
        x = nn_dot(xT2[r, :], m).astype(bf16)
        for p in range(P):
            cm.puto(p, r, x[:, 128 * p:128 * p + 128])
        return 0

    loop("gwo", D, gwo, 0)
    cm.hook("out_grad")
    transpose_into(xT, n1, seq)

    def pair_bwd(j, _):
        hp = cm.order_back(j)
        attend_bwd(seq, most, length, qkv, qaug, kaug, mixed, lse, gm, qq, kk, vv, oo, dq, dkv, dqkv, hp)
        cm.hook("back_mid", j)

        def wgrad(r, _):
            cm.putq(hp, r, nn_dot(xT[r, :], dqkv[...]).astype(bf16))
            return 0

        loop("qgrad", D, wgrad, 0)
        cm.hook("back_end", j)

        def back(r, _):
            gn[r, :] += nt_dot(dqkv[r, :], cm.getq(hp))
            return 0

        loop("back", seq, back, 0)
        return 0

    lax.fori_loop(0, P, pair_bwd, 0)
    cm.hook("back_done")

    def ln1b(r, acc):
        xh, rr = normed(tok[r, :].astype(f32) + tp[...])
        gy = gn[r, :]
        gt = mid[r, :] + norm_back(xh, rr, g1[...], gy)
        gtok[r, :] = gt
        return acc[0] + colsum(gt), acc[1] + colsum(gy * xh), acc[2] + colsum(gy)

    a = loop("ln1b", seq, ln1b, (z, z, z))
    cm.late(list(a))


def layer_scratch(seq, D, P, NF, F):
    V = pltpu.VMEM
    return [V((1, D), f32), V((seq, D), bf16), V((P, seq, 384), bf16), V((seq, 128), bf16), V((seq, 128), bf16),
        V((P, seq, 128), bf16), V((P, seq, 128), f32)] + [V((2, seq, 128), bf16)] * 4 + [V((2, seq, 128), f32),
        V((3, 2, seq, 128), f32), V((seq, 384), bf16), V((seq, D), f32), V((seq, D), bf16), V((seq, D), f32), V((seq, D), f32),
        V((seq, F), bf16), V((seq, F), bf16), V((P, seq, 128), bf16), V((D, seq), bf16), V((D, seq), bf16), V((NF, 1, F), f32)]


def plain_kernel(most, n_sc, *refs):
    len_ref, ts_ref, tok, cot, seg, wq, wo, w2, wt, btime, g1, b1, g2, b2, bdown, bup, out, gtok, dwq, dwo, dw2, vec = refs[:22]
    T = lax.axis_index("tensor")
    cm = Plain(wq, wo, w2, dwq, dwo, dw2, vec)
    layer(cm, T, most, len_ref[T], ts_ref[0].astype(f32), tok, cot, seg, wt, btime, g1, b1, g2, b2, bdown, bup, out, gtok, refs[22:])


def run_plain(most, length, ts, tok, cot, seg, wq, wo, w2, wt, vecs, bup):
    seq, D = tok.shape
    P, NF, F = wq.shape[0], w2.shape[0], w2.shape[-1]
    S = jax.ShapeDtypeStruct
    vm = pl.BlockSpec(memory_space=pltpu.VMEM)
    sm = pl.BlockSpec(memory_space=pltpu.SMEM)
    return pl.pallas_call(
        functools.partial(plain_kernel, most, 0),
        out_shape=(S((seq, D), bf16), S((seq, D), f32), S(wq.shape, bf16), S(wo.shape, bf16), S(w2.shape, bf16), S((16, D), f32)),
        in_specs=[sm, sm] + [vm] * 14, out_specs=[vm] * 6,
        scratch_shapes=layer_scratch(seq, D, P, NF, F),
        compiler_params=pltpu.CompilerParams(vmem_limit_bytes=60 << 20),
    )(length, ts, tok, cot, seg, wq, wo, w2, wt, *[v[None] for v in vecs], bup)


def linked_kernel(most, ng, nt, names, semnames, n_layer, *refs):
    len_ref, ts_ref, tok_h, cot_h, seg, w_qkv, w_out, w_up, w_down, wt_h, btime, g1, b1, g2, b2, bdown, bup = refs[:17]
    out_h, gtok_h, o_qkv, o_out, o_up, o_down, embs, grads, vec = refs[17:26]
    sc = refs[26:26 + n_layer]
    rest = refs[26 + n_layer:]
    bufs = dict(zip(names, rest[:len(names)]))
    sr = rest[len(names):]
    sems = {nm: (sr[2 * i], sr[2 * i + 1]) for i, nm in enumerate(semnames)}
    local = sr[-1]
    tok, cot, wt, out, gtok = (bufs.pop(k) for k in ("tok", "cot", "wt", "out", "gtok"))
    bufs.update(w_qkv=w_qkv, w_out=w_out, w_up=w_up, w_down=w_down, o_qkv=o_qkv, o_out=o_out, o_up=o_up, o_down=o_down)
    bufs["E"] = bufs.pop("EZ"), bufs.pop("EX")
    bufs["L"] = bufs.pop("LZ"), bufs.pop("LX")
    cm = Linked(ng, nt, bufs, sems)
    T = cm.t
    cm.ne = 4 + bup.shape[0]
    cm.early = lambda rows: cm.v_start("E", rows)
    cm.late = lambda rows: cm.v_start("L", rows)
    pairs = ((tok_h, tok), (wt_h, wt), (cot_h, cot), (out, out_h), (gtok, gtok_h))
    moves = [pltpu.make_async_copy(a, b, local.at[i]) for i, (a, b) in enumerate(pairs)]
    for x in moves[:3]:
        x.start()
    plain_hook = cm.hook

    def hook(place, j=None):
        if place == "row_in":
            moves[0].wait()
            moves[1].wait()
        elif place == "cot_in":
            moves[2].wait()
        elif place == "row_out":
            moves[3].start()
        else:
            plain_hook(place, j)

    cm.hook = hook
    layer(cm, T, most, len_ref[T], ts_ref[0].astype(f32), tok, cot, seg, wt, btime, g1, b1, g2, b2, bdown, bup, out, gtok, sc)
    moves[4].start()
    cm.hook("finish")
    cm.v_mid("L", 3)
    kept, sums = cm.v_done("E", cm.ne)
    embs[...] = kept
    vec[4:4 + cm.ne - 1, :] = sums
    cm.hook("finish_q")
    kept, late = cm.v_done("L", 3)
    grads[...] = kept
    vec[2:4, :] = late
    cm.hook("leave")
    cm.v_leave("E")
    cm.v_leave("L")
    moves[3].wait()
    moves[4].wait()


def run_linked(most, nd, nt, length, ts, tok, cot, seg, w_qkv, w_out, w_up, w_down, wt, vecs, bup):
    seq, D = tok.shape
    ng = nd // 2
    r, F = w_up.shape
    P, NF = nt, nt
    S, V = jax.ShapeDtypeStruct, pltpu.VMEM
    DMA = pltpu.SemaphoreType.DMA
    bufs = dict(
        WQ=V((nt, ng, 2, r, 384), bf16), WO=V((nt, ng, 2, r, 128), bf16), W2=V((nt, 2, ng, 2, r, F), bf16),
        DQ=V((nt, ng, 2, r, 384), bf16), DO=V((nt, ng, 2, r, 128), bf16), D2=V((nt, 2, ng, 2, r, F), bf16),
        CQ=V((nt, ng, r, 384), bf16), XQ=V((nt, ng, r, 384), bf16), ZQ=V((nt, r, 384), bf16),
        CO=V((nt, ng, r, 128), bf16), XO=V((ng, nt, r, 128), bf16), ZO=V((nt, r, 128), bf16),
        C2=V((nt, 2, ng, r, F), bf16), X2=V((nt, ng, 2, r, F), bf16), Z2=V((nt, 2, r, F), bf16),
        EZ=V((nt, 8, D), f32), EX=V((nd, 16, D), f32), LZ=V((nt, 8, D), f32), LX=V((nd, 16, D), f32),
        tok=V((seq, D), bf16), cot=V((seq, D), bf16), wt=V((D, D), f32), out=V((seq, D), bf16), gtok=V((seq, D), f32),
    )
    sems = dict(gq_plane=(nt, ng), gq_z=(nt,), gq_core=(nt,), go_z=(nt,), g2_z=(nt,), go_plane=(ng,), go_core=(), g2_plane=(nt, ng), g2_core=(nt,),
        rq_core=(nt,), rq_plane=(nt, ng), rq_z=(nt,), r2_core=(nt,), r2_plane=(nt, ng), r2_z=(nt,), ro_core=(), ro_plane=(ng,), ro_z=(nt,),
        E_z=(nt,), E_dp=(nd,), L_z=(nt,), L_dp=(nd,))
    ls = layer_scratch(seq, D, P, NF, F)
    scratch = ls + list(bufs.values())
    for s in sems.values():
        scratch += [DMA(s), DMA(s)]
    scratch.append(DMA((5,)))
    vm = pl.BlockSpec(memory_space=pltpu.VMEM)
    sm = pl.BlockSpec(memory_space=pltpu.SMEM)
    hb = pl.BlockSpec(memory_space=pltpu.HBM)
    return pl.pallas_call(
        functools.partial(linked_kernel, most, ng, nt, tuple(bufs), tuple(sems), len(ls)),
        out_shape=(S((seq, D), bf16), S((seq, D), f32), S(w_qkv.shape, f32), S(w_out.shape, f32), S(w_up.shape, f32), S(w_down.shape, f32),
            S((8 * nd, D), f32), S((8 * nd, D), f32), S((16, D), f32)),
        in_specs=[sm, sm, hb, hb] + [vm] * 5 + [hb] + [vm] * 7, out_specs=[hb, hb] + [vm] * 7,
        scratch_shapes=scratch,
        compiler_params=pltpu.CompilerParams(vmem_limit_bytes=62 << 20, collective_id=0, has_side_effects=True),
    )(length, ts, tok, cot, seg, w_qkv, w_out, w_up, w_down, wt, *[v[None] for v in vecs], bup)


def emit_kernel(nb, *refs):
    big, outs, gwt, small, bufs = refs[:9], refs[9:15], refs[15], refs[16:23], refs[23:32]
    sem_in, sem_out = refs[32:]
    ins = [pltpu.make_async_copy(a, b, sem_in.at[i]) for i, (a, b) in enumerate(zip(big, bufs))]
    ups = [pltpu.make_async_copy(a, b, sem_out.at[i]) for i, (a, b) in enumerate(zip(bufs[3:], outs))]
    for x in ins:
        x.start()
    for x in ins[:3]:
        x.wait()
    embs, grads, vec = (b[...] for b in bufs[:3])
    gwt[...] = lax.dot_general(embs, grads, (((0,), (0,)), ((), ())), precision=lax.Precision.HIGHEST, preferred_element_type=f32)
    small[0][...] = jnp.sum(grads, axis=0)
    for k, o in enumerate(small[1:-1]):
        o[...] = vec[2 + k, :]
    n = vec.shape[1]
    for k in range(nb):
        small[-1][pl.ds(k * n, n)] = vec[7 + k, :]
    for x, y in zip(ins[3:], ups):
        x.wait()
        y.start()
    for y in ups:
        y.wait()


def emit(nb, *big):
    S = jax.ShapeDtypeStruct
    D = big[2].shape[1]
    vm = pl.BlockSpec(memory_space=pltpu.VMEM)
    hb = pl.BlockSpec(memory_space=pltpu.HBM)
    return pl.pallas_call(
        functools.partial(emit_kernel, nb),
        out_shape=tuple(S(x.shape, x.dtype) for x in big[3:]) + (S((D, D), f32),) + tuple(S((D,), f32) for _ in range(6)) + (S((nb * D,), f32),),
        in_specs=[hb] * 9, out_specs=[hb] * 6 + [vm] * 8,
        scratch_shapes=[pltpu.VMEM(x.shape, x.dtype) for x in big] + [pltpu.SemaphoreType.DMA((9,)), pltpu.SemaphoreType.DMA((6,))],
        compiler_params=pltpu.CompilerParams(vmem_limit_bytes=60 << 20),
    )(*big)


def shards(
    tokens,
    timestep,
    segment_ids,
    span_lengths,
    w_qkv,
    w_out_t,
    w_up,
    w_down_t,
    w_time,
    b_time,
    ln1_gain,
    ln1_bias,
    ln2_gain,
    ln2_bias,
    b_up,
    b_down,
    cotangent,
):
    seq, D = tokens.shape[1:]
    nd, nt = lax.axis_size("dp"), lax.axis_size("tensor")
    vecs = (b_time, ln1_gain, ln1_bias, ln2_gain, ln2_bias, b_down)
    F = w_up.shape[1]
    bup = b_up.reshape(nt, 1, F)
    if w_up.shape[0] % 16 == 0:
        out, gtok, *g, embs, lines, vec = run_linked(
            DOC, nd, nt, span_lengths, timestep, tokens[0], cotangent[0], segment_ids,
            w_qkv, w_out_t, w_up, w_down_t, w_time, vecs, bup)
        gq, go, gu, gd, out, gtok, gwt, *v = emit(nt, embs, lines, vec, *g, out, gtok)
        return (out[None], gtok[None], gq, go, gu, gd, gwt, v[0], v[1], v[2], v[3], v[4], v[6], v[5])
    HB = w_qkv.shape[2]

    def whole(w):
        return lax.all_gather(lax.all_gather(w.astype(bf16), "dp", axis=w.ndim - 2, tiled=True), "tensor", axis=0)

    def part(g, dim):
        g = lax.psum_scatter(g, "dp", scatter_dimension=dim, tiled=True)
        return lax.psum_scatter(g, "tensor", scatter_dimension=0, tiled=True)[0].astype(f32)

    wq = whole(jnp.transpose(w_qkv, (1, 0, 2)).reshape(w_qkv.shape[1], 3 * HB))
    out, gtok, dwq, dwo, dw2, vec = run_plain(
        DOC, span_lengths, timestep, tokens[0], cotangent[0], segment_ids,
        wq, whole(w_out_t), whole(jnp.stack([w_up, w_down_t])), w_time, vecs, bup)
    lines = lax.all_gather(jnp.stack([vec[0], vec[8]]), ("dp", "tensor"), axis=1, tiled=False)
    gwt = jnp.dot(lines[0].T, lines[1], precision=lax.Precision.HIGHEST)
    small = lax.psum(vec, ("dp", "tensor"))
    gq, g2 = part(dwq, 1), part(dw2, 2)
    return (
        out[None], gtok[None], jnp.transpose(gq.reshape(gq.shape[0], 3, HB), (1, 0, 2)), part(dwo, 1), g2[0], g2[1],
        gwt, small[8], small[9], small[10], small[1], small[2], small[4:4 + nt].reshape(-1), small[3])


def solution(mesh):
    return jax.shard_map(
        shards,
        mesh=mesh,
        in_specs=(
            P_(("dp", "tensor"), None, None),
            P_(("dp", "tensor")),
            P_("dp", None),
            P_("dp"),
            P_(None, "dp", "tensor"),
            P_("dp", "tensor"),
            P_("dp", "tensor"),
            P_("dp", "tensor"),
            P_(),
            P_(),
            P_(),
            P_(),
            P_(),
            P_(),
            P_(),
            P_(),
            P_(("dp", "tensor"), None, None),
        ),
        out_specs=(
            P_(("dp", "tensor"), None, None),
            P_(("dp", "tensor"), None, None),
            P_(None, "dp", "tensor"),
            P_("dp", "tensor"),
            P_("dp", "tensor"),
            P_("dp", "tensor"),
            P_(),
            P_(),
            P_(),
            P_(),
            P_(),
            P_(),
            P_(),
            P_(),
        ),
        check_vma=False,
    )
```

```python
import functools
import math

import jax
import jax.numpy as jnp
from jax import lax
from jax.experimental import pallas as pl
from jax.experimental.pallas import tpu as pltpu
from jax.sharding import PartitionSpec as P_

f32, bf16 = jnp.float32, jnp.bfloat16
HS = 64
TR = 256
BIG = 1e30
EPS = 1e-5
DOC = 512
LEAST = 512
LOG2E = math.log2(math.e)
LN2 = math.log(2.0)
SCALE = 1.0 / math.sqrt(HS)


def nt_dot(a, b):
    return lax.dot_general(a, b, (((1,), (1,)), ((), ())), preferred_element_type=f32)


def tn_dot(a, b):
    return lax.dot_general(a, b, (((0,), (0,)), ((), ())), preferred_element_type=f32)


def nn_dot(a, b):
    return jnp.dot(a, b, preferred_element_type=f32)


def lane(shape):
    return lax.broadcasted_iota(jnp.int32, shape, len(shape) - 1)


def rows_of(i, n=TR):
    return pl.ds(pl.multiple_of(i * n, n), n)


def normed(x):
    mean = jnp.mean(x, axis=-1, keepdims=True)
    c = x - mean
    var = jnp.mean(c * c, axis=-1, keepdims=True)
    r = lax.rsqrt(var + EPS)
    return c * r, r


def norm_back(xhat, r, gain, gy):
    gh = gy * gain
    a = jnp.mean(gh, axis=-1, keepdims=True)
    b = jnp.mean(gh * xhat, axis=-1, keepdims=True)
    return r * (gh - a - xhat * b)


def colsum(x):
    return jnp.sum(x, axis=0, keepdims=True)


def halves(prod):
    low = lane(prod.shape) < HS
    s0 = jnp.sum(jnp.where(low, prod, 0.0), axis=-1, keepdims=True)
    s1 = jnp.sum(jnp.where(low, 0.0, prod), axis=-1, keepdims=True)
    return s0, s1


def split3(x):
    hi = x.astype(bf16)
    rest = x - hi.astype(f32)
    mid = rest.astype(bf16)
    lo = (rest - mid.astype(f32)).astype(bf16)
    return hi, mid, lo


def window(i, seq, most):
    lo = max(0, (i * TR - most + 1) // 128 * 128)
    hi = min(seq, -(-(i * TR + TR - 1 + most) // 128) * 128)
    return lo, hi


def gelu_parts(u):
    c0, c1 = 0.7978845608028654, 0.044715
    u2 = u * u
    th = jnp.tanh(u * (c0 + (c0 * c1) * u2))
    half = 0.5 + 0.5 * th
    act = u * half
    grad = half + (0.5 * u) * (1.0 - th * th) * (c0 + (3.0 * c0 * c1) * u2)
    return act, grad


def transpose_into(dst, src, seq):
    def step(i, _):
        r = rows_of(i)
        dst[:, r] = src[r, :].T
        return 0
    for i in range(seq // TR):
        r = slice(i * TR, i * TR + TR)
        dst[:, r] = src[r, :].T


def half_sums(prod, swap=False):
    hi = prod.astype(bf16)
    lo = (prod - hi.astype(f32)).astype(bf16)
    a = lax.broadcasted_iota(jnp.int32, (256, 128), 0) // HS % 2
    b = lax.broadcasted_iota(jnp.int32, (256, 128), 1) // HS
    w = jnp.where((a != b) if swap else (a == b), 1.0, 0.0).astype(bf16)
    return nn_dot(jnp.concatenate([hi, lo], axis=1), w)


def attend_fwd(seq, most, length, qkv, qaug, kaug, mixed, lse, qq, kk, vv, hp, half):
    n = seq // TR
    def prep(i, _):
        r = rows_of(i)
        low = lane((TR, 128)) < HS
        q, k, v = (qkv[hp, r, 128 * c:128 * c + 128] for c in range(3))
        qa, ka = qaug[r, :], kaug[r, :]
        one = jnp.ones_like(v)
        qq[0, r, :] = jnp.where(low, q, qa)
        qq[1, r, :] = jnp.where(low, qa, q)
        kk[0, r, :] = jnp.where(low, k, ka)
        kk[1, r, :] = jnp.where(low, ka, k)
        vv[0, r, :] = jnp.where(low, v, one)
        vv[1, r, :] = jnp.where(low, one, v)
        return 0
    for i in range(n):
        prep(i, 0)

    def score(i, h):
        lo, hi = window(i, seq, most)
        return nt_dot(qq[h, i * TR:i * TR + TR, :], kk[h, lo:hi, :])

    def soft(i, s, own):
        m = jnp.max(s, axis=-1, keepdims=True)
        if own is not None:
            pad = (lax.broadcasted_iota(jnp.int32, (TR, 1), 0) + i * TR) >= length
            m = jnp.where(pad, jnp.maximum(m, own), m)
        return m, jnp.exp2(s - m).astype(bf16)

    def finish(i, own, tops, outs):
        r = slice(i * TR, i * TR + TR)
        low = lane((TR, 128)) < HS
        num = jnp.where(low, outs[0], outs[1])
        den_x = jnp.where(low, outs[1], outs[0])
        if own[0] is not None:
            padf = ((lax.broadcasted_iota(jnp.int32, (TR, 1), 0) + i * TR) >= length).astype(f32)
            e0 = jnp.exp2(jnp.minimum(own[0] - tops[0], 0.0)).astype(bf16).astype(f32) * padf
            e1 = jnp.exp2(jnp.minimum(own[1] - tops[1], 0.0)).astype(bf16).astype(f32) * padf
            num = num + jnp.where(low, e0, e1) * qkv[hp, r, 256:384].astype(f32)
            den_x = den_x + jnp.where(low, e1, e0)
        mixed[hp, r, :] = (num / pltpu.roll(den_x, HS, 1)).astype(bf16)
        lse[hp, r, :] = jnp.where(low, tops[1], tops[0]) + jnp.log2(den_x)

    def selfs(i):
        if (i + 1) * TR <= LEAST:
            return (None, None)
        r = slice(i * TR, i * TR + TR)
        return halves(qkv[hp, r, 0:128].astype(f32) * qkv[hp, r, 128:256].astype(f32))

    units = [(i, h) for i in range(n) for h in range(2)]
    s = score(*units[0])
    tops, outs = [], []
    for u, (i, h) in enumerate(units):
        if (i, h) == (n // 2, 0):
            half()
        nxt = score(*units[u + 1]) if u + 1 < len(units) else None
        if h == 0:
            own = selfs(i)
        lo, hi = window(i, seq, most)
        m, p = soft(i, s, own[h])
        tops.append(m)
        outs.append(nn_dot(p, vv[h, lo:hi, :]))
        if h == 1:
            finish(i, own, tops, outs)
            tops, outs = [], []
        s = nxt


def attend_bwd(seq, most, length, qkv, qaug, kaug, mixed, lse, gm, qq, kk, vv, oo, dq, dkv, dqkv, hp):
    n = seq // TR
    def prep(i, _):
        r = slice(i * TR, i * TR + TR)
        low = lane((TR, 128)) < HS
        spot = lane((TR, 128)) % HS
        q, k, v = (qkv[hp, r, 128 * c:128 * c + 128] for c in range(3))
        g = gm[hp, r, :]
        dx = half_sums(g.astype(f32) * mixed[hp, r, :].astype(f32), True)
        def put(base, x):
            hi, mid, lo = split3(x)
            z = jnp.where(spot == 8, hi, base)
            z = jnp.where(spot == 9, mid, z)
            return jnp.where(spot == 10, lo, z)
        zero = jnp.zeros((TR, 128), bf16)
        qa = put(qaug[r, :], lse[hp, r, :])
        oa = put(zero, dx)
        ka = kaug[r, :]
        va = jnp.where((spot >= 8) & (spot < 11), -jnp.ones_like(zero), zero)
        for ref, x, a in ((qq, q, qa), (kk, k, ka), (vv, v, va), (oo, g, oa)):
            ref[0, r, :] = jnp.where(low, x, a)
            ref[1, r, :] = jnp.where(low, a, x)
        if (i + 1) * TR > LEAST:
            q, k, v, g = (x.astype(f32) for x in (q, k, v, g))
            padf = ((lax.broadcasted_iota(jnp.int32, (TR, 1), 0) + i * TR) >= length).astype(f32)
            ls = pltpu.roll(lse[hp, r, :], HS, 1)
            d = pltpu.roll(dx, HS, 1)
            pf = jnp.exp2(jnp.minimum(half_sums(q * k) - ls, 1.0)) * padf
            ds = (pf * (half_sums(g * v) - d)).astype(bf16).astype(f32)
            pf = pf.astype(bf16).astype(f32)
            dkv[2, 0, r, :] = ds
            dkv[2, 1, r, :] = pf
        return 0
    for i in range(n):
        prep(i, 0)
    lo, hi = window(0, seq, most)
    if hi < seq:
        dq[:, hi:seq, :] = jnp.zeros((2, seq - hi, 128), f32)

    def score(i, h):
        lo, hi = window(i, seq, most)
        r = slice(i * TR, i * TR + TR)
        return nt_dot(kk[h, r, :], qq[h, lo:hi, :]), nt_dot(vv[h, r, :], oo[h, lo:hi, :])

    def rest(i, h, st, dpt):
        lo, hi = window(i, seq, most)
        r = slice(i * TR, i * TR + TR)
        pt = jnp.exp2(st)
        dst = (pt * dpt).astype(bf16)
        dkv[h, 0, r, :] = nn_dot(dst, qq[h, lo:hi, :])
        dkv[h, 1, r, :] = nn_dot(pt.astype(bf16), oo[h, lo:hi, :])
        x = tn_dot(dst, kk[h, r, :])
        if i == 0:
            dq[h, lo:hi, :] = x
        else:
            dq[h, lo:hi, :] += x

    units = [(i, h) for i in range(n) for h in range(2)]
    s = score(*units[0])
    for u, (i, h) in enumerate(units):
        nxt = score(*units[u + 1]) if u + 1 < len(units) else None
        rest(i, h, *s)
        s = nxt

    for i in range(n):
        r = slice(i * TR, i * TR + TR)
        low = lane((TR, 128)) < HS
        gq = jnp.where(low, dq[0, r, :], dq[1, r, :])
        gk = jnp.where(low, dkv[0, 0, r, :], dkv[1, 0, r, :])
        gv = jnp.where(low, dkv[0, 1, r, :], dkv[1, 1, r, :])
        if (i + 1) * TR > LEAST:
            ds, pf = dkv[2, 0, r, :], dkv[2, 1, r, :]
            gq = gq + ds * qkv[hp, r, 128:256].astype(f32)
            gk = gk + ds * qkv[hp, r, 0:128].astype(f32)
            gv = gv + pf * gm[hp, r, :].astype(f32)
        dqkv[r, 0:128] = (gq * SCALE).astype(bf16)
        dqkv[r, 128:256] = (gk * LN2).astype(bf16)
        dqkv[r, 256:384] = gv.astype(bf16)


MESH = pl.DeviceIdType.MESH


class Plain:
    def __init__(self, wq, wo, w2, dwq, dwo, dw2, vec):
        self.wq, self.wo, self.w2 = wq, wo, w2
        self.dwq, self.dwo, self.dw2, self.vec = dwq, dwo, dw2, vec

    def getq(self, p):
        return self.wq[p]

    def geto(self):
        return jnp.concatenate([self.wo[p] for p in range(self.wo.shape[0])], axis=1)

    def getu(self, f):
        return self.w2[f, 0]

    def getd(self, f):
        return self.w2[f, 1]

    def putq(self, p, i, x):
        self.dwq[p, i, :] = x

    def puto(self, p, i, x):
        self.dwo[p, i, :] = x

    def put2(self, f, k, i, x):
        self.dw2[f, k, i, :] = x

    def order(self, j):
        return j

    def order_back(self, j):
        return j

    def hook(self, *_):
        pass

    def early(self, rows):
        for k, x in enumerate(rows):
            self.vec[k:k + 1, :] = x

    def late(self, rows):
        for k, x in enumerate(rows):
            self.vec[8 + k:9 + k, :] = x


class Linked:
    def __init__(self, ng, nt, bufs, sems):
        self.ng, self.nt = ng, nt
        self.__dict__.update(bufs)
        self.sem = sems
        d, self.t = lax.axis_index("dp"), lax.axis_index("tensor")
        self.d, self.g, self.c = d, d // 2, d % 2
        self.sent = []

    def dev(self, kind, k):
        if kind == "core":
            return (2 * self.g + 1 - self.c, self.t)
        if kind == "plane":
            return (2 * (self.g ^ k) + self.c, self.t)
        if kind == "dp":
            return (self.d ^ k, self.t)
        return (self.d, self.t ^ k)

    def copy(self, name, at, kind, k, src, dst):
        s, r = self.sem[name]
        for i in at:
            s, r = s.at[i], r.at[i]
        return pltpu.make_async_remote_copy(
            src_ref=src, dst_ref=dst, send_sem=s, recv_sem=r,
            device_id=self.dev(kind, k), device_id_type=MESH)

    def getq(self, p):
        x = self.WQ[p]
        return x.reshape(-1, x.shape[-1])

    def geto(self):
        return jnp.concatenate([self.WO[p].reshape(-1, 128) for p in range(self.nt)], axis=1)

    def getu(self, f):
        x = self.W2[f, 0]
        return x.reshape(-1, x.shape[-1])

    def getd(self, f):
        x = self.W2[f, 1]
        return x.reshape(-1, x.shape[-1])

    def blocks(self, ref, i):
        rows = ref.shape[-2]
        m = (i.stop - i.start) // (2 * rows)
        return slice(i.start // (2 * rows), i.stop // (2 * rows)), (m, 2, rows, ref.shape[-1])

    def putq(self, p, i, x):
        b, shape = self.blocks(self.DQ, i)
        self.DQ[p, b] = x.reshape(shape)

    def puto(self, p, i, x):
        b, shape = self.blocks(self.DO, i)
        self.DO[p, b] = x.reshape(shape)

    def put2(self, f, k, i, x):
        b, shape = self.blocks(self.D2, i)
        self.D2[f, k, b] = x.reshape(shape)

    def order(self, j):
        return self.t ^ j

    def order_back(self, j):
        return self.t ^ (self.nt - 1 - j)

    def peers(self):
        return [("dp", k) for k in range(1, 2 * self.ng)] + [("z", k) for k in range(1, self.nt)]

    def greet(self):
        bar = pltpu.get_barrier_semaphore()
        for kind, k in self.peers():
            pl.semaphore_signal(bar, inc=1, device_id=self.dev(kind, k), device_id_type=MESH)

    def enter(self):
        pl.semaphore_wait(pltpu.get_barrier_semaphore(), len(self.peers()))

    def q_plane(self, x, k, incoming=False):
        g, c, p = self.g, self.c, self.t ^ x
        return self.copy("gq_plane", (x, k), "plane", k, self.WQ.at[p, g, c], self.WQ.at[p, g ^ k if incoming else g, c])

    def q_z(self, k, incoming=False):
        g, c, t = self.g, self.c, self.t
        return self.copy("gq_z", (k,), "z", k, self.WQ.at[t, g, c], self.WQ.at[t ^ k if incoming else t, g, c])

    def q_core(self, k):
        c, t = self.c, self.t
        return self.copy("gq_core", (k,), "core", 0, self.WQ.at[t ^ k, :, c], self.WQ.at[t ^ k, :, c])

    def q_core_in(self, k):
        c, t = self.c, self.t
        return self.copy("gq_core", (k,), "core", 0, self.WQ.at[t ^ k, :, c], self.WQ.at[t ^ k, :, 1 - c])

    def o_z(self, k, incoming=False):
        g, c, t = self.g, self.c, self.t
        return self.copy("go_z", (k,), "z", k, self.WO.at[t, g, c], self.WO.at[t ^ k if incoming else t, g, c])

    def f_z(self, k, incoming=False):
        g, c, t = self.g, self.c, self.t
        return self.copy("g2_z", (k,), "z", k, self.W2.at[t, :, g, c], self.W2.at[t ^ k if incoming else t, :, g, c])

    def o_plane(self, k, incoming=False):
        g, c = self.g, self.c
        return self.copy("go_plane", (k,), "plane", k, self.WO.at[:, g, c], self.WO.at[:, g ^ k if incoming else g, c])

    def o_core(self, incoming=False):
        c = self.c
        return self.copy("go_core", (), "core", 0, self.WO.at[:, :, c], self.WO.at[:, :, 1 - c if incoming else c])

    def f_plane(self, j, k, u, incoming=False):
        g, c, f = self.g, self.c, self.t ^ j
        return self.copy("g2_plane", (j, u, k), "plane", k, self.W2.at[f, u, g, c], self.W2.at[f, u, g ^ k if incoming else g, c])

    def f_on(self, x):
        self.f_z(x, True).wait_recv()
        for u in range(2):
            for k in range(1, self.ng):
                self.f_plane(x, k, u).start()

    def f_pass(self, x):
        for u in range(2):
            for k in range(1, self.ng):
                self.f_plane(x, k, u, True).wait_recv()
        self.f_core(x).start()

    def f_core(self, j, incoming=False):
        c, f = self.c, self.t ^ j
        return self.copy("g2_core", (j,), "core", 0, self.W2.at[f, :, :, c], self.W2.at[f, :, :, 1 - c if incoming else c])

    def rq(self, stage, x, k=0, incoming=False):
        g, c, p = self.g, self.c, self.t ^ x
        if stage == "core":
            return self.copy("rq_core", (x,), "core", 0, self.DQ.at[p, :, 1 - c], self.CQ.at[x])
        if stage == "plane":
            return self.copy("rq_plane", (x, k), "plane", k, self.DQ.at[p, g ^ k, c], self.XQ.at[x, k])
        return self.copy("rq_z", (x,), "z", x, self.DQ.at[p, g, c], self.ZQ.at[x])

    def r2(self, stage, x, k=0):
        g, c, p = self.g, self.c, self.t ^ x
        if stage == "core":
            return self.copy("r2_core", (x,), "core", 0, self.D2.at[p, :, :, 1 - c], self.C2.at[x])
        if stage == "plane":
            return self.copy("r2_plane", (x, k), "plane", k, self.D2.at[p, :, g ^ k, c], self.X2.at[x, k])
        return self.copy("r2_z", (x,), "z", x, self.D2.at[p, :, g, c], self.Z2.at[x])

    def r2_near(self):
        c, t = self.c, self.t
        return self.copy("r2_near", (), "z", 1, self.D2.at[t ^ 1, :, :, c], self.Y2)

    def ro(self, stage, k=0):
        g, c, t = self.g, self.c, self.t
        if stage == "core":
            return self.copy("ro_core", (), "core", 0, self.DO.at[:, :, 1 - c], self.CO)
        if stage == "plane":
            return self.copy("ro_plane", (k,), "plane", k, self.DO.at[:, g ^ k, c], self.XO.at[k])
        return self.copy("ro_z", (k,), "z", k, self.DO.at[t ^ k, g, c], self.ZO.at[k])

    def q_after_core(self, x):
        p, c = self.t ^ x, self.c
        self.rq("core", x).wait_recv()
        self.DQ[p, :, c] = (self.DQ[p, :, c].astype(f32) + self.CQ[x].astype(f32)).astype(bf16)
        for k in range(1, self.ng):
            self.rq("plane", x, k).start()

    def q_after_plane(self, x):
        p, c, g = self.t ^ x, self.c, self.g
        acc = self.DQ[p, g, c].astype(f32)
        for k in range(1, self.ng):
            self.rq("plane", x, k).wait_recv()
            acc = acc + self.XQ[x, k].astype(f32)
        self.DQ[p, g, c] = acc.astype(bf16)

    def f_after_core(self, x):
        p, c = self.t ^ x, self.c
        self.r2("core", x).wait_recv()
        for u in range(2):
            def step(i, _):
                self.D2[p, u, i, c] = (self.D2[p, u, i, c].astype(f32) + self.C2[x, u, i].astype(f32)).astype(bf16)
                return 0
            lax.fori_loop(0, self.ng, step, 0)

    def f_after_plane(self, x):
        p, c, g = self.t ^ x, self.c, self.g
        for k in range(1, self.ng):
            self.r2("plane", x, k).wait_recv()
        for u in range(2):
            acc = self.D2[p, u, g, c].astype(f32)
            for k in range(1, self.ng):
                acc = acc + self.X2[x, k, u].astype(f32)
            self.D2[p, u, g, c] = acc.astype(bf16)

    def hook(self, place, j=None):
        ng, nt, t, g, c = self.ng, self.nt, self.t, self.g, self.c
        planes = range(1, ng)

        def begin(*copies):
            for x in copies:
                x.start()

        def await_in(*copies):
            for x in copies:
                x.wait_recv()

        if place == "greet":
            self.greet()
        elif place == "start":
            for k in range(3):
                self.WQ[t, g, c, :, 128 * k:128 * k + 128] = self.w_qkv[k].astype(bf16)
            self.WO[t, g, c] = self.w_out[...].astype(bf16)
            self.W2[t, 0, g, c] = self.w_up[...].astype(bf16)
            self.W2[t, 1, g, c] = self.w_down[...].astype(bf16)
            for x in (self.E[1], self.L[1]):
                x[self.d] = jnp.zeros(x.shape[1:], f32)
            self.enter()
            begin(*[self.q_plane(0, k) for k in planes], self.q_z(1))
        elif place == "normed":
            begin(self.q_z(2), self.q_z(3))
        elif place == "masked":
            await_in(self.q_z(1, True))
            begin(*[self.q_plane(1, k) for k in planes])
            await_in(*[self.q_plane(0, k, True) for k in planes])
            begin(self.q_core(0))
        elif place == "pair":
            await_in(self.q_core_in(j))
        elif place == "pair_proj":
            @pl.when(j == 0)
            def _():
                begin(*[self.o_z(k) for k in range(1, nt)])
                begin(*[self.f_plane(0, k, 0) for k in planes])
        elif place == "pair_half":
            @pl.when(j == 0)
            def _():
                await_in(*[self.q_plane(1, k, True) for k in planes])
                begin(self.q_core(1))
                await_in(self.q_z(2, True))
                begin(*[self.q_plane(2, k) for k in planes])
            @pl.when(j == 1)
            def _():
                begin(self.f_z(2), self.f_z(3))
                begin(*[self.f_plane(0, k, 1) for k in planes])
            @pl.when(j == 2)
            def _():
                await_in(*[self.q_plane(3, k, True) for k in planes])
                begin(self.q_core(3))
            @pl.when(j == 3)
            def _():
                await_in(*[self.o_plane(k, True) for k in planes])
                begin(self.o_core())
        elif place == "pair_mid":
            @pl.when(j == 0)
            def _():
                await_in(self.q_z(3, True))
                begin(*[self.q_plane(3, k) for k in planes])
                begin(self.f_z(1))
            @pl.when(j == 1)
            def _():
                await_in(*[self.o_z(k, True) for k in range(1, nt)])
                begin(*[self.o_plane(k) for k in planes])
                await_in(*[self.q_plane(2, k, True) for k in planes])
                begin(self.q_core(2))
            @pl.when(j == 2)
            def _():
                self.f_on(1)
            @pl.when(j == 3)
            def _():
                self.f_on(2)
        elif place == "mixed":
            await_in(self.o_core(True))
        elif place == "second":
            self.f_pass(0)
            self.f_on(3)
        elif place == "chunk":
            await_in(self.f_core(j, True))
        elif place == "chunk_mid":
            @pl.when(j < nt - 1)
            def _():
                self.f_pass(j + 1)
            @pl.when(j >= 1)
            def _():
                self.f_after_core(j - 1)
            @pl.when(j == 2)
            def _():
                begin(self.r2_near())
            @pl.when(j == 3)
            def _():
                begin(*[self.r2("plane", 2, k) for k in planes])
        elif place == "chunk_end":
            begin(self.r2("core", j))
        elif place == "ffn_done":
            self.f_after_core(nt - 1)
            begin(*[self.r2("plane", 3, k) for k in planes])
        elif place == "out_grad":
            begin(self.ro("core"))
        elif place == "back_mid":
            @pl.when(j >= 1)
            def _():
                self.q_after_core(nt - j)
            @pl.when(j == 0)
            def _():
                await_in(self.ro("core"))
                for p in range(nt):
                    self.DO[p, :, c] = (self.DO[p, :, c].astype(f32) + self.CO[p].astype(f32)).astype(bf16)
                begin(*[self.ro("plane", k) for k in planes])
                self.v_mid("E", self.ne)
                await_in(self.r2_near())
                for u in range(2):
                    def step(i, _):
                        self.D2[t, u, i, c] = (self.D2[t, u, i, c].astype(f32) + self.Y2[u, i].astype(f32)).astype(bf16)
                        return 0
                    lax.fori_loop(0, ng, step, 0)
                begin(*[self.r2("plane", 0, k) for k in planes])
            @pl.when(j == 1)
            def _():
                self.f_after_plane(2)
                begin(self.r2("z", 2))
            @pl.when(j == 2)
            def _():
                await_in(*[self.ro("plane", k) for k in planes])
                for p in range(nt):
                    acc = self.DO[p, g, c].astype(f32)
                    for k in planes:
                        acc = acc + self.XO[k, p].astype(f32)
                    self.DO[p, g, c] = acc.astype(bf16)
                begin(*[self.ro("z", k) for k in range(1, nt)])
                self.f_after_plane(3)
                begin(self.r2("z", 3))
            @pl.when(j == 3)
            def _():
                self.f_after_plane(0)
            @pl.when(j >= 2)
            def _():
                self.q_after_plane(nt - j + 1)
                begin(self.rq("z", nt - j + 1))
        elif place == "back_end":
            self.rq("core", nt - 1 - j).start()
        elif place == "back_done":
            self.q_after_core(0)
            self.q_after_plane(1)
            self.rq("z", 1).start()
        elif place == "finish":
            for x in range(1, nt):
                if x > 1:
                    self.r2("z", x).wait_recv()
                self.ro("z", x).wait_recv()
            for u, o in enumerate((self.o_up, self.o_down)):
                acc = self.D2[t, u, g, c].astype(f32)
                for x in range(2, nt):
                    acc = acc + self.Z2[x, u].astype(f32)
                o[...] = acc
            acc = self.DO[t, g, c].astype(f32)
            for x in range(1, nt):
                acc = acc + self.ZO[x].astype(f32)
            self.o_out[...] = acc
        elif place == "finish_q":
            acc = self.DQ[t, g, c].astype(f32)
            for k in range(1, ng):
                self.rq("plane", 0, k).wait_recv()
                acc = acc + self.XQ[0, k].astype(f32)
            for x in range(1, nt):
                self.rq("z", x).wait_recv()
                acc = acc + self.ZQ[x].astype(f32)
            for k in range(3):
                self.o_qkv[k] = acc[:, 128 * k:128 * k + 128]
        elif place == "leave":
            for k in planes:
                self.o_plane(k).wait_send()
                self.ro("plane", k).wait_send()
                for x in range(nt):
                    self.q_plane(x, k).wait_send()
                    for u in range(2):
                        self.f_plane(x, k, u).wait_send()
                    if x != 1:
                        self.r2("plane", x, k).wait_send()
                    self.rq("plane", x, k).wait_send()
            for k in range(nt):
                self.q_core(k).wait_send()
                self.f_core(k).wait_send()
                self.r2("core", k).wait_send()
                self.rq("core", k).wait_send()
            self.o_core().wait_send()
            self.ro("core").wait_send()
            self.r2_near().wait_send()
            for k in range(1, nt):
                self.q_z(k).wait_send()
                self.o_z(k).wait_send()
                self.f_z(k).wait_send()
                if k > 1:
                    self.r2("z", k).wait_send()
                self.rq("z", k).wait_send()
                self.ro("z", k).wait_send()

    def v(self, name, stage, k, incoming=False):
        Z, X = getattr(self, name)
        if stage == "z":
            return self.copy(name + "_z", (k,), "z", k, Z.at[self.t], Z.at[self.t ^ k if incoming else self.t])
        return self.copy(name + "_dp", (k,), "dp", k, X.at[self.d], X.at[self.d ^ k if incoming else self.d])

    def v_start(self, name, rows):
        Z = getattr(self, name)[0]
        for k, x in enumerate(rows):
            Z[self.t, k:k + 1, :] = x
        for k in range(1, self.nt):
            self.v(name, "z", k).start()

    def v_mid(self, name, m):
        Z, X = getattr(self, name)
        nt = self.nt
        for k in range(1, nt):
            self.v(name, "z", k, True).wait_recv()
        for k in range(nt):
            X[self.d, k:k + 1, :] = Z[k, 0:1, :]
        s = Z[0, 1:m, :]
        for k in range(1, nt):
            s = s + Z[k, 1:m, :]
        X[self.d, 8:8 + m - 1, :] = s
        for k in range(1, 2 * self.ng):
            self.v(name, "dp", k).start()

    def v_done(self, name, m):
        X = getattr(self, name)[1]
        nd = 2 * self.ng
        for k in range(1, nd):
            self.v(name, "dp", k, True).wait_recv()
        s = X[0, 8:8 + m - 1, :]
        for k in range(1, nd):
            s = s + X[k, 8:8 + m - 1, :]
        return jnp.concatenate([X[k, 0:8, :] for k in range(nd)], axis=0), s

    def v_leave(self, name):
        for k in range(1, self.nt):
            self.v(name, "z", k).wait_send()
        for k in range(1, 2 * self.ng):
            self.v(name, "dp", k).wait_send()


TILE = dict(ln1=256, proj=1024, ln2=512, tile=512, wgrad=512, ln2b=256, gmix=1024, gwo=512, qgrad=512, back=1024, ln1b=256)
UNROLL = {"proj", "ln2", "tile", "wgrad", "gmix", "gwo", "qgrad", "back"}


def loop(name, total, body, init):
    n = TILE[name]
    if name in UNROLL or total == n:
        for i in range(total // n):
            init = body(slice(i * n, i * n + n), init)
        return init
    return lax.fori_loop(0, total // n, lambda i, x: body(pl.ds(pl.multiple_of(i * n, n), n), x), init)


def layer(cm, T, most, length, t, tok, cot, seg, wt, btime, g1, b1, g2, b2, bdown, bup, out, gtok, sc):
    tp, n1, qkv, qaug, kaug, mixed, lse, qq, kk, vv, oo, dq, dkv, dqkv, mid, n2, ffn, gn, act, gu, gm, xT, xT2, xT3, bsum = sc
    seq, D = tok.shape
    P = qkv.shape[0]
    NF, F = bsum.shape[0], bsum.shape[2]
    n = seq // TR
    cm.hook("greet")
    cm.hook("start")
    cm.hook("row_in")
    half = D // 2
    ang = t * jnp.exp(-math.log(10000.0) * lax.broadcasted_iota(jnp.int32, (8, half), 1).astype(f32) / half)
    emb = jnp.concatenate([jnp.sin(ang), jnp.cos(ang)], axis=1)
    tp[...] = jnp.dot(emb, wt[...], precision=lax.Precision.HIGHEST, preferred_element_type=f32)[0:1, :] + btime[...]

    def ln1(r, _):
        xh, _r = normed(tok[r, :].astype(f32) + tp[...])
        n1[r, :] = (xh * g1[...] + b1[...]).astype(bf16)
        return 0

    loop("ln1", seq, ln1, 0)
    cm.hook("normed")
    srow = seg[pl.ds(T, 1), :].astype(f32)
    for b in range(seq // 128):
        col = jnp.broadcast_to(srow[:, 128 * b:128 * b + 128], (128, 128)).T
        spot = lane((128, 128)) % HS
        pos = lax.broadcasted_iota(jnp.int32, (128, 128), 0) + 128 * b
        same = col == spot.astype(f32)
        r = slice(128 * b, 128 * b + 128)
        qaug[r, :] = jnp.where(same & (spot < 8), 1.0, 0.0).astype(bf16)
        ka = jnp.where(same & (pos < length), 0.0, -BIG)
        kaug[r, :] = jnp.where(spot < 8, ka, jnp.where(spot < 11, -1.0, 0.0)).astype(bf16)

    cm.hook("cot_in")
    transpose_into(xT, cot, seq)
    cm.hook("masked")
    transpose_into(xT3, n1, seq)

    def pair_fwd(j, _):
        hp = cm.order(j)
        cm.hook("pair", j)

        def proj(r, _):
            x = nn_dot(n1[r, :], cm.getq(hp))
            s = jnp.where(lane((1, 384)) < 128, SCALE * LOG2E, 1.0)
            qkv[hp, r, :] = (x * s).astype(bf16)
            return 0

        loop("proj", seq, proj, 0)
        cm.hook("pair_proj", j)
        attend_fwd(seq, most, length, qkv, qaug, kaug, mixed, lse, qq, kk, vv, hp, lambda: cm.hook("pair_half", j))
        cm.hook("pair_mid", j)
        return 0

    lax.fori_loop(0, P, pair_fwd, 0)
    cm.hook("mixed")

    def ln2(r, _):
        mx = jnp.concatenate([mixed[p, r, :] for p in range(P)], axis=1)
        x = tok[r, :].astype(f32) + tp[...] + nt_dot(mx, cm.geto())
        mid[r, :] = x
        xh, _r = normed(x)
        n2[r, :] = (xh * g2[...] + b2[...]).astype(bf16)
        ffn[r, :] = jnp.zeros((TILE["ln2"], D), f32)
        gn[r, :] = jnp.zeros((TILE["ln2"], D), f32)
        return 0

    loop("ln2", seq, ln2, 0)
    cm.hook("second")
    transpose_into(xT2, n2, seq)

    def chunk(j, _):
        f = cm.order(j)
        cm.hook("chunk", j)

        def tile(r, acc):
            u = nn_dot(n2[r, :], cm.getu(f)) + bup[f]
            a, ga = gelu_parts(u)
            a = a.astype(bf16)
            g = (nn_dot(cot[r, :], cm.getd(f)) * ga).astype(bf16)
            act[r, :] = a
            gu[r, :] = g
            ffn[r, :] += nt_dot(a, cm.getd(f))
            gn[r, :] += nt_dot(g, cm.getu(f))
            return acc + colsum(g.astype(f32))

        bsum[f] = loop("tile", seq, tile, jnp.zeros((1, F), f32))
        cm.hook("chunk_mid", j)

        def wgrad(r, _):
            cm.put2(f, 1, r, nn_dot(xT[r, :], act[...]).astype(bf16))
            cm.put2(f, 0, r, nn_dot(xT2[r, :], gu[...]).astype(bf16))
            return 0

        loop("wgrad", D, wgrad, 0)
        cm.hook("chunk_end", j)
        return 0

    lax.fori_loop(0, NF, chunk, 0)

    def ln2b(r, acc):
        c = cot[r, :].astype(f32)
        x = mid[r, :]
        out[r, :] = (x + ffn[r, :] + bdown[...]).astype(bf16)
        xh, rr = normed(x)
        gy = gn[r, :]
        gmid = c + norm_back(xh, rr, g2[...], gy)
        mid[r, :] = gmid
        n2[r, :] = gmid.astype(bf16)
        gn[r, :] = jnp.zeros((TILE["ln2b"], D), f32)
        return acc[0] + colsum(gy * xh), acc[1] + colsum(gy), acc[2] + colsum(c)

    z = jnp.zeros((1, D), f32)
    a = loop("ln2b", seq, ln2b, (z, z, z))
    cm.early([emb[0:1, :], *a] + [bsum[f] for f in range(NF)])
    cm.hook("ffn_done")
    transpose_into(xT2, n2, seq)

    def gmix(r, _):
        x = nn_dot(n2[r, :], cm.geto()).astype(bf16)
        for p in range(P):
            gm[p, r, :] = x[:, 128 * p:128 * p + 128]
        return 0

    loop("gmix", seq, gmix, 0)

    def gwo(r, _):
        m = jnp.concatenate([mixed[p] for p in range(P)], axis=1)
        x = nn_dot(xT2[r, :], m).astype(bf16)
        for p in range(P):
            cm.puto(p, r, x[:, 128 * p:128 * p + 128])
        return 0

    loop("gwo", D, gwo, 0)
    cm.hook("out_grad")
    def pair_bwd(j, _):
        hp = cm.order_back(j)
        attend_bwd(seq, most, length, qkv, qaug, kaug, mixed, lse, gm, qq, kk, vv, oo, dq, dkv, dqkv, hp)
        cm.hook("back_mid", j)

        def wgrad(r, _):
            cm.putq(hp, r, nn_dot(xT3[r, :], dqkv[...]).astype(bf16))
            return 0

        loop("qgrad", D, wgrad, 0)
        cm.hook("back_end", j)

        def back(r, _):
            gn[r, :] += nt_dot(dqkv[r, :], cm.getq(hp))
            return 0

        loop("back", seq, back, 0)
        return 0

    lax.fori_loop(0, P, pair_bwd, 0)
    cm.hook("back_done")

    def ln1b(r, acc):
        xh, rr = normed(tok[r, :].astype(f32) + tp[...])
        gy = gn[r, :]
        gt = mid[r, :] + norm_back(xh, rr, g1[...], gy)
        gtok[r, :] = gt
        return acc[0] + colsum(gt), acc[1] + colsum(gy * xh), acc[2] + colsum(gy)

    a = loop("ln1b", seq, ln1b, (z, z, z))
    cm.late(list(a))


def layer_scratch(seq, D, P, NF, F):
    V = pltpu.VMEM
    return [V((1, D), f32), V((seq, D), bf16), V((P, seq, 384), bf16), V((seq, 128), bf16), V((seq, 128), bf16),
        V((P, seq, 128), bf16), V((P, seq, 128), f32)] + [V((2, seq, 128), bf16)] * 4 + [V((2, seq, 128), f32),
        V((3, 2, seq, 128), f32), V((seq, 384), bf16), V((seq, D), f32), V((seq, D), bf16), V((seq, D), f32), V((seq, D), f32),
        V((seq, F), bf16), V((seq, F), bf16), V((P, seq, 128), bf16), V((D, seq), bf16), V((D, seq), bf16), V((D, seq), bf16), V((NF, 1, F), f32)]


def plain_kernel(most, n_sc, *refs):
    len_ref, ts_ref, tok, cot, seg, wq, wo, w2, wt, btime, g1, b1, g2, b2, bdown, bup, out, gtok, dwq, dwo, dw2, vec = refs[:22]
    T = lax.axis_index("tensor")
    cm = Plain(wq, wo, w2, dwq, dwo, dw2, vec)
    layer(cm, T, most, len_ref[T], ts_ref[0].astype(f32), tok, cot, seg, wt, btime, g1, b1, g2, b2, bdown, bup, out, gtok, refs[22:])


def run_plain(most, length, ts, tok, cot, seg, wq, wo, w2, wt, vecs, bup):
    seq, D = tok.shape
    P, NF, F = wq.shape[0], w2.shape[0], w2.shape[-1]
    S = jax.ShapeDtypeStruct
    vm = pl.BlockSpec(memory_space=pltpu.VMEM)
    sm = pl.BlockSpec(memory_space=pltpu.SMEM)
    return pl.pallas_call(
        functools.partial(plain_kernel, most, 0),
        out_shape=(S((seq, D), bf16), S((seq, D), f32), S(wq.shape, bf16), S(wo.shape, bf16), S(w2.shape, bf16), S((16, D), f32)),
        in_specs=[sm, sm] + [vm] * 14, out_specs=[vm] * 6,
        scratch_shapes=layer_scratch(seq, D, P, NF, F),
        compiler_params=pltpu.CompilerParams(vmem_limit_bytes=60 << 20),
    )(length, ts, tok, cot, seg, wq, wo, w2, wt, *[v[None] for v in vecs], bup)


def linked_kernel(most, ng, nt, names, semnames, n_layer, *refs):
    len_ref, ts_ref, tok_h, cot_h, seg, w_qkv, w_out, w_up, w_down, wt_h, btime, g1, b1, g2, b2, bdown, bup = refs[:17]
    out, gtok, o_qkv, o_out, o_up, o_down, embs, grads, vec = refs[17:26]
    sc = refs[26:26 + n_layer]
    rest = refs[26 + n_layer:]
    bufs = dict(zip(names, rest[:len(names)]))
    sr = rest[len(names):]
    sems = {nm: (sr[2 * i], sr[2 * i + 1]) for i, nm in enumerate(semnames)}
    local = sr[-1]
    tok, cot, wt = (bufs.pop(k) for k in ("tok", "cot", "wt"))
    bufs.update(w_qkv=w_qkv, w_out=w_out, w_up=w_up, w_down=w_down, o_qkv=o_qkv, o_out=o_out, o_up=o_up, o_down=o_down)
    bufs["E"] = bufs.pop("EZ"), bufs.pop("EX")
    bufs["L"] = bufs.pop("LZ"), bufs.pop("LX")
    cm = Linked(ng, nt, bufs, sems)
    T = cm.t
    cm.ne = 4 + bup.shape[0]
    cm.early = lambda rows: cm.v_start("E", rows)
    cm.late = lambda rows: cm.v_start("L", rows)
    pairs = ((tok_h, tok), (wt_h, wt), (cot_h, cot))
    moves = [pltpu.make_async_copy(a, b, local.at[i]) for i, (a, b) in enumerate(pairs)]
    plain_hook = cm.hook

    def hook(place, j=None):
        if place == "greet":
            plain_hook(place)
            for x in moves:
                x.start()
        elif place == "row_in":
            moves[0].wait()
            moves[1].wait()
        elif place == "cot_in":
            moves[2].wait()
        else:
            plain_hook(place, j)

    cm.hook = hook
    layer(cm, T, most, len_ref[T], ts_ref[0].astype(f32), tok, cot, seg, wt, btime, g1, b1, g2, b2, bdown, bup, out, gtok, sc)
    cm.hook("finish")
    cm.v_mid("L", 3)
    kept, sums = cm.v_done("E", cm.ne)
    embs[...] = kept
    vec[4:4 + cm.ne - 1, :] = sums
    cm.hook("finish_q")
    kept, late = cm.v_done("L", 3)
    grads[...] = kept
    vec[2:4, :] = late
    cm.hook("leave")
    cm.v_leave("E")
    cm.v_leave("L")


def run_linked(most, nd, nt, length, ts, tok, cot, seg, w_qkv, w_out, w_up, w_down, wt, vecs, bup):
    seq, D = tok.shape
    ng = nd // 2
    r, F = w_up.shape
    P, NF = nt, nt
    S, V = jax.ShapeDtypeStruct, pltpu.VMEM
    DMA = pltpu.SemaphoreType.DMA
    bufs = dict(
        WQ=V((nt, ng, 2, r, 384), bf16), WO=V((nt, ng, 2, r, 128), bf16), W2=V((nt, 2, ng, 2, r, F), bf16),
        DQ=V((nt, ng, 2, r, 384), bf16), DO=V((nt, ng, 2, r, 128), bf16), D2=V((nt, 2, ng, 2, r, F), bf16),
        CQ=V((nt, ng, r, 384), bf16), XQ=V((nt, ng, r, 384), bf16), ZQ=V((nt, r, 384), bf16),
        CO=V((nt, ng, r, 128), bf16), XO=V((ng, nt, r, 128), bf16), ZO=V((nt, r, 128), bf16),
        C2=V((nt, 2, ng, r, F), bf16), X2=V((nt, ng, 2, r, F), bf16), Z2=V((nt, 2, r, F), bf16), Y2=V((2, ng, r, F), bf16),
        EZ=V((nt, 8, D), f32), EX=V((nd, 16, D), f32), LZ=V((nt, 8, D), f32), LX=V((nd, 16, D), f32),
        tok=V((seq, D), bf16), cot=V((seq, D), bf16), wt=V((D, D), f32),
    )
    sems = dict(gq_plane=(nt, ng), gq_z=(nt,), gq_core=(nt,), go_z=(nt,), g2_z=(nt,), go_plane=(ng,), go_core=(), g2_plane=(nt, 2, ng), g2_core=(nt,),
        rq_core=(nt,), rq_plane=(nt, ng), rq_z=(nt,), r2_core=(nt,), r2_plane=(nt, ng), r2_z=(nt,), r2_near=(), ro_core=(), ro_plane=(ng,), ro_z=(nt,),
        E_z=(nt,), E_dp=(nd,), L_z=(nt,), L_dp=(nd,))
    ls = layer_scratch(seq, D, P, NF, F)
    scratch = ls + list(bufs.values())
    for s in sems.values():
        scratch += [DMA(s), DMA(s)]
    scratch.append(DMA((3,)))
    vm = pl.BlockSpec(memory_space=pltpu.VMEM)
    sm = pl.BlockSpec(memory_space=pltpu.SMEM)
    hb = pl.BlockSpec(memory_space=pltpu.HBM)
    an = pl.BlockSpec(memory_space=pl.ANY)
    return pl.pallas_call(
        functools.partial(linked_kernel, most, ng, nt, tuple(bufs), tuple(sems), len(ls)),
        out_shape=(V((seq, D), bf16), V((seq, D), f32), V(w_qkv.shape, f32), V(w_out.shape, f32), V(w_up.shape, f32), V(w_down.shape, f32),
            V((8 * nd, D), f32), V((8 * nd, D), f32), V((16, D), f32)),
        in_specs=[sm, sm, hb, hb] + [vm] * 5 + [hb] + [vm] * 7, out_specs=[vm] * 9,
        scratch_shapes=scratch,
        compiler_params=pltpu.CompilerParams(vmem_limit_bytes=56 << 20, collective_id=0, has_side_effects=True),
    )(length, ts, tok, cot, seg, w_qkv, w_out, w_up, w_down, wt, *[v[None] for v in vecs], bup)


def emit_kernel(nb, *refs):
    big, outs, gwt, small, sem = refs[:9], refs[9:15], refs[15], refs[16:23], refs[23]
    ups = [pltpu.make_async_copy(a, b, sem.at[i]) for i, (a, b) in enumerate(zip(big[3:], outs))]
    for x in ups:
        x.start()
    embs, grads, vec = (b[...] for b in big[:3])
    gwt[...] = lax.dot_general(embs, grads, (((0,), (0,)), ((), ())), precision=lax.Precision.HIGHEST, preferred_element_type=f32)
    small[0][...] = jnp.sum(grads, axis=0)
    for k, o in enumerate(small[1:-1]):
        o[...] = vec[2 + k, :]
    n = vec.shape[1]
    for k in range(nb):
        small[-1][pl.ds(k * n, n)] = vec[7 + k, :]
    for y in ups:
        y.wait()


def emit(nb, *big):
    S = jax.ShapeDtypeStruct
    D = big[2].shape[1]
    vm = pl.BlockSpec(memory_space=pltpu.VMEM)
    an = pl.BlockSpec(memory_space=pl.ANY)
    hb = pl.BlockSpec(memory_space=pltpu.HBM)
    return pl.pallas_call(
        functools.partial(emit_kernel, nb),
        out_shape=tuple(S(x.shape, x.dtype) for x in big[3:]) + (S((D, D), f32),) + tuple(S((D,), f32) for _ in range(6)) + (S((nb * D,), f32),),
        in_specs=[vm] * 3 + [an] * 6, out_specs=[hb] * 6 + [vm] * 8,
        scratch_shapes=[pltpu.SemaphoreType.DMA((6,))],
        compiler_params=pltpu.CompilerParams(vmem_limit_bytes=16 << 20),
    )(*big)


def shards(
    tokens,
    timestep,
    segment_ids,
    span_lengths,
    w_qkv,
    w_out_t,
    w_up,
    w_down_t,
    w_time,
    b_time,
    ln1_gain,
    ln1_bias,
    ln2_gain,
    ln2_bias,
    b_up,
    b_down,
    cotangent,
):
    seq, D = tokens.shape[1:]
    nd, nt = lax.axis_size("dp"), lax.axis_size("tensor")
    vecs = (b_time, ln1_gain, ln1_bias, ln2_gain, ln2_bias, b_down)
    F = w_up.shape[1]
    bup = b_up.reshape(nt, 1, F)
    if w_up.shape[0] % 16 == 0 and (nd, nt) == (8, 4):
        out, gtok, *g, embs, lines, vec = run_linked(
            DOC, nd, nt, span_lengths, timestep, tokens[0], cotangent[0], segment_ids,
            w_qkv, w_out_t, w_up, w_down_t, w_time, vecs, bup)
        gq, go, gu, gd, out, gtok, gwt, *v = emit(nt, embs, lines, vec, *g, out, gtok)
        return (out[None], gtok[None], gq, go, gu, gd, gwt, v[0], v[1], v[2], v[3], v[4], v[6], v[5])
    HB = w_qkv.shape[2]

    def whole(w):
        return lax.all_gather(lax.all_gather(w.astype(bf16), "dp", axis=w.ndim - 2, tiled=True), "tensor", axis=0)

    def part(g, dim):
        g = lax.psum_scatter(g, "dp", scatter_dimension=dim, tiled=True)
        return lax.psum_scatter(g, "tensor", scatter_dimension=0, tiled=True)[0].astype(f32)

    wq = whole(jnp.transpose(w_qkv, (1, 0, 2)).reshape(w_qkv.shape[1], 3 * HB))
    out, gtok, dwq, dwo, dw2, vec = run_plain(
        DOC, span_lengths, timestep, tokens[0], cotangent[0], segment_ids,
        wq, whole(w_out_t), whole(jnp.stack([w_up, w_down_t])), w_time, vecs, bup)
    lines = lax.all_gather(jnp.stack([vec[0], vec[8]]), ("dp", "tensor"), axis=1, tiled=False)
    gwt = jnp.dot(lines[0].T, lines[1], precision=lax.Precision.HIGHEST)
    small = lax.psum(vec, ("dp", "tensor"))
    gq, g2 = part(dwq, 1), part(dw2, 2)
    return (
        out[None], gtok[None], jnp.transpose(gq.reshape(gq.shape[0], 3, HB), (1, 0, 2)), part(dwo, 1), g2[0], g2[1],
        gwt, small[8], small[9], small[10], small[1], small[2], small[4:4 + nt].reshape(-1), small[3])


def solution(mesh):
    return jax.shard_map(
        shards,
        mesh=mesh,
        in_specs=(
            P_(("dp", "tensor"), None, None),
            P_(("dp", "tensor")),
            P_("dp", None),
            P_("dp"),
            P_(None, "dp", "tensor"),
            P_("dp", "tensor"),
            P_("dp", "tensor"),
            P_("dp", "tensor"),
            P_(),
            P_(),
            P_(),
            P_(),
            P_(),
            P_(),
            P_(),
            P_(),
            P_(("dp", "tensor"), None, None),
        ),
        out_specs=(
            P_(("dp", "tensor"), None, None),
            P_(("dp", "tensor"), None, None),
            P_(None, "dp", "tensor"),
            P_("dp", "tensor"),
            P_("dp", "tensor"),
            P_("dp", "tensor"),
            P_(),
            P_(),
            P_(),
            P_(),
            P_(),
            P_(),
            P_(),
            P_(),
        ),
        check_vma=False,
    )
```

```python
import functools
import math

import jax
import jax.numpy as jnp
from jax import lax
from jax.experimental import pallas as pl
from jax.experimental.pallas import tpu as pltpu
from jax.sharding import PartitionSpec as P_

f32, bf16 = jnp.float32, jnp.bfloat16
HS = 64
TR = 256
TB = 256
BIG = 1e30
EPS = 1e-5
DOC = 512
LEAST = 512
LOG2E = math.log2(math.e)
LN2 = math.log(2.0)
SCALE = 1.0 / math.sqrt(HS)


def nt_dot(a, b):
    return lax.dot_general(a, b, (((1,), (1,)), ((), ())), preferred_element_type=f32)


def tn_dot(a, b):
    return lax.dot_general(a, b, (((0,), (0,)), ((), ())), preferred_element_type=f32)


def nn_dot(a, b):
    return jnp.dot(a, b, preferred_element_type=f32)


def lane(shape):
    return lax.broadcasted_iota(jnp.int32, shape, len(shape) - 1)


def rows_of(i, n=TR):
    return pl.ds(pl.multiple_of(i * n, n), n)


def normed(x):
    mean = jnp.mean(x, axis=-1, keepdims=True)
    c = x - mean
    var = jnp.mean(c * c, axis=-1, keepdims=True)
    r = lax.rsqrt(var + EPS)
    return c * r, r


def norm_back(xhat, r, gain, gy):
    gh = gy * gain
    a = jnp.mean(gh, axis=-1, keepdims=True)
    b = jnp.mean(gh * xhat, axis=-1, keepdims=True)
    return r * (gh - a - xhat * b)


def colsum(x):
    return jnp.sum(x, axis=0, keepdims=True)


def halves(prod):
    low = lane(prod.shape) < HS
    s0 = jnp.sum(jnp.where(low, prod, 0.0), axis=-1, keepdims=True)
    s1 = jnp.sum(jnp.where(low, 0.0, prod), axis=-1, keepdims=True)
    return s0, s1


def split3(x):
    hi = x.astype(bf16)
    rest = x - hi.astype(f32)
    mid = rest.astype(bf16)
    lo = (rest - mid.astype(f32)).astype(bf16)
    return hi, mid, lo


def window(i, seq, most, tr):
    lo = max(0, (i * tr - most + 1) // 128 * 128)
    hi = min(seq, -(-(i * tr + tr - 1 + most) // 128) * 128)
    return lo, hi


def gelu_parts(u):
    c0, c1 = 0.7978845608028654, 0.044715
    u2 = u * u
    th = jnp.tanh(u * (c0 + (c0 * c1) * u2))
    half = 0.5 + 0.5 * th
    act = u * half
    grad = half + (0.5 * u) * (1.0 - th * th) * (c0 + (3.0 * c0 * c1) * u2)
    return act, grad


def transpose_into(dst, src, seq):
    def step(i, _):
        r = rows_of(i)
        dst[:, r] = src[r, :].T
        return 0
    for i in range(seq // TR):
        r = slice(i * TR, i * TR + TR)
        dst[:, r] = src[r, :].T


def half_sums(prod, swap=False):
    hi = prod.astype(bf16)
    lo = (prod - hi.astype(f32)).astype(bf16)
    a = lax.broadcasted_iota(jnp.int32, (256, 128), 0) // HS % 2
    b = lax.broadcasted_iota(jnp.int32, (256, 128), 1) // HS
    w = jnp.where((a != b) if swap else (a == b), 1.0, 0.0).astype(bf16)
    return nn_dot(jnp.concatenate([hi, lo], axis=1), w)


def attend_fwd(seq, most, length, qkv, qaug, kaug, mixed, lse, qq, kk, vv, hp, half):
    n = seq // TR
    def prep(i, _):
        r = rows_of(i)
        low = lane((TR, 128)) < HS
        q, k, v = (qkv[hp, r, 128 * c:128 * c + 128] for c in range(3))
        qa, ka = qaug[r, :], kaug[r, :]
        one = jnp.ones_like(v)
        qq[0, r, :] = jnp.where(low, q, qa)
        qq[1, r, :] = jnp.where(low, qa, q)
        kk[0, r, :] = jnp.where(low, k, ka)
        kk[1, r, :] = jnp.where(low, ka, k)
        vv[0, r, :] = jnp.where(low, v, one)
        vv[1, r, :] = jnp.where(low, one, v)
        return 0
    for i in range(n):
        prep(i, 0)

    def score(i, h):
        lo, hi = window(i, seq, most, TR)
        return nt_dot(qq[h, i * TR:i * TR + TR, :], kk[h, lo:hi, :])

    def soft(i, s, own):
        m = jnp.max(s, axis=-1, keepdims=True)
        if own is not None:
            pad = (lax.broadcasted_iota(jnp.int32, (TR, 1), 0) + i * TR) >= length
            m = jnp.where(pad, jnp.maximum(m, own), m)
        return m, jnp.exp2(s - m).astype(bf16)

    def finish(i, own, tops, outs):
        r = slice(i * TR, i * TR + TR)
        low = lane((TR, 128)) < HS
        num = jnp.where(low, outs[0], outs[1])
        den_x = jnp.where(low, outs[1], outs[0])
        if own[0] is not None:
            padf = ((lax.broadcasted_iota(jnp.int32, (TR, 1), 0) + i * TR) >= length).astype(f32)
            e0 = jnp.exp2(jnp.minimum(own[0] - tops[0], 0.0)).astype(bf16).astype(f32) * padf
            e1 = jnp.exp2(jnp.minimum(own[1] - tops[1], 0.0)).astype(bf16).astype(f32) * padf
            num = num + jnp.where(low, e0, e1) * qkv[hp, r, 256:384].astype(f32)
            den_x = den_x + jnp.where(low, e1, e0)
        mixed[hp, r, :] = (num / pltpu.roll(den_x, HS, 1)).astype(bf16)
        lse[hp, r, :] = jnp.where(low, tops[1], tops[0]) + jnp.log2(den_x)

    def selfs(i):
        if (i + 1) * TR <= LEAST:
            return (None, None)
        r = slice(i * TR, i * TR + TR)
        return halves(qkv[hp, r, 0:128].astype(f32) * qkv[hp, r, 128:256].astype(f32))

    units = [(i, h) for i in range(n) for h in range(2)]
    s = score(*units[0])
    tops, outs = [], []
    for u, (i, h) in enumerate(units):
        if (i, h) == (n // 2, 0):
            half()
        nxt = score(*units[u + 1]) if u + 1 < len(units) else None
        if h == 0:
            own = selfs(i)
        lo, hi = window(i, seq, most, TR)
        m, p = soft(i, s, own[h])
        tops.append(m)
        outs.append(nn_dot(p, vv[h, lo:hi, :]))
        if h == 1:
            finish(i, own, tops, outs)
            tops, outs = [], []
        s = nxt


def attend_bwd(seq, most, length, qkv, qaug, kaug, mixed, lse, gm, qq, kk, vv, oo, dq, dkv, dqkv, hp):
    n = seq // TB
    def prep(i, _):
        r = slice(i * TB, i * TB + TB)
        low = lane((TB, 128)) < HS
        spot = lane((TB, 128)) % HS
        q, k, v = (qkv[hp, r, 128 * c:128 * c + 128] for c in range(3))
        g = gm[hp, r, :]
        dx = half_sums(g.astype(f32) * mixed[hp, r, :].astype(f32), True)
        def put(base, x):
            hi, mid, lo = split3(x)
            z = jnp.where(spot == 8, hi, base)
            z = jnp.where(spot == 9, mid, z)
            return jnp.where(spot == 10, lo, z)
        zero = jnp.zeros((TB, 128), bf16)
        qa = put(qaug[r, :], lse[hp, r, :])
        oa = put(zero, dx)
        ka = kaug[r, :]
        va = jnp.where((spot >= 8) & (spot < 11), -jnp.ones_like(zero), zero)
        for ref, x, a in ((qq, q, qa), (kk, k, ka), (vv, v, va), (oo, g, oa)):
            ref[0, r, :] = jnp.where(low, x, a)
            ref[1, r, :] = jnp.where(low, a, x)
        if (i + 1) * TB > LEAST:
            q, k, v, g = (x.astype(f32) for x in (q, k, v, g))
            padf = ((lax.broadcasted_iota(jnp.int32, (TB, 1), 0) + i * TB) >= length).astype(f32)
            ls = pltpu.roll(lse[hp, r, :], HS, 1)
            d = pltpu.roll(dx, HS, 1)
            pf = jnp.exp2(jnp.minimum(half_sums(q * k) - ls, 1.0)) * padf
            ds = (pf * (half_sums(g * v) - d)).astype(bf16).astype(f32)
            pf = pf.astype(bf16).astype(f32)
            dkv[2, 0, r, :] = ds
            dkv[2, 1, r, :] = pf
        return 0
    for i in range(n):
        prep(i, 0)
    hi = window(0, seq, most, TB)[1]
    if hi < seq:
        dq[:, hi:seq, :] = jnp.zeros((2, seq - hi, 128), f32)

    def score(i, h):
        lo, hi = window(i, seq, most, TB)
        r = slice(i * TB, i * TB + TB)
        return nt_dot(kk[h, r, :], qq[h, lo:hi, :]), nt_dot(vv[h, r, :], oo[h, lo:hi, :])

    def rest(i, h, st, dpt):
        lo, hi = window(i, seq, most, TB)
        r = slice(i * TB, i * TB + TB)
        pt = jnp.exp2(st)
        dst = (pt * dpt).astype(bf16)
        dkv[h, 0, r, :] = nn_dot(dst, qq[h, lo:hi, :])
        dkv[h, 1, r, :] = nn_dot(pt.astype(bf16), oo[h, lo:hi, :])
        x = tn_dot(dst, kk[h, r, :])
        if i == 0:
            dq[h, lo:hi, :] = x
        else:
            dq[h, lo:hi, :] += x

    units = [(i, h) for i in range(n) for h in range(2)]
    s = score(*units[0])
    for u, (i, h) in enumerate(units):
        nxt = score(*units[u + 1]) if u + 1 < len(units) else None
        rest(i, h, *s)
        s = nxt

    for i in range(n):
        r = slice(i * TB, i * TB + TB)
        low = lane((TB, 128)) < HS
        gq = jnp.where(low, dq[0, r, :], dq[1, r, :])
        gk = jnp.where(low, dkv[0, 0, r, :], dkv[1, 0, r, :])
        gv = jnp.where(low, dkv[0, 1, r, :], dkv[1, 1, r, :])
        if (i + 1) * TB > LEAST:
            ds, pf = dkv[2, 0, r, :], dkv[2, 1, r, :]
            gq = gq + ds * qkv[hp, r, 128:256].astype(f32)
            gk = gk + ds * qkv[hp, r, 0:128].astype(f32)
            gv = gv + pf * gm[hp, r, :].astype(f32)
        dqkv[r, 0:128] = (gq * SCALE).astype(bf16)
        dqkv[r, 128:256] = (gk * LN2).astype(bf16)
        dqkv[r, 256:384] = gv.astype(bf16)


MESH = pl.DeviceIdType.MESH


class Plain:
    def __init__(self, wq, wo, w2, dwq, dwo, dw2, vec):
        self.wq, self.wo, self.w2 = wq, wo, w2
        self.dwq, self.dwo, self.dw2, self.vec = dwq, dwo, dw2, vec

    def getq(self, p):
        return self.wq[p]

    def geto(self):
        return jnp.concatenate([self.wo[p] for p in range(self.wo.shape[0])], axis=1)

    def getu(self, f):
        return self.w2[f, 0]

    def getd(self, f):
        return self.w2[f, 1]

    def putq(self, p, i, x):
        self.dwq[p, i, :] = x

    def puto(self, p, i, x):
        self.dwo[p, i, :] = x

    def put2(self, f, k, i, x):
        self.dw2[f, k, i, :] = x

    def order(self, j):
        return j

    def order_back(self, j):
        return j

    def order_ffn(self, j):
        return j

    def hook(self, *_):
        pass

    def early(self, rows):
        for k, x in enumerate(rows):
            self.vec[k:k + 1, :] = x

    def late(self, rows):
        for k, x in enumerate(rows):
            self.vec[8 + k:9 + k, :] = x


class Linked:
    def __init__(self, ng, nt, bufs, sems):
        self.ng, self.nt = ng, nt
        self.__dict__.update(bufs)
        self.sem = sems
        d, self.t = lax.axis_index("dp"), lax.axis_index("tensor")
        self.d, self.g, self.c = d, d // 2, d % 2
        self.sent = []

    def dev(self, kind, k):
        if kind == "core":
            return (2 * self.g + 1 - self.c, self.t)
        if kind == "plane":
            return (2 * (self.g ^ k) + self.c, self.t)
        if kind == "dp":
            return (self.d ^ k, self.t)
        return (self.d, self.t ^ k)

    def copy(self, name, at, kind, k, src, dst):
        s, r = self.sem[name]
        for i in at:
            s, r = s.at[i], r.at[i]
        return pltpu.make_async_remote_copy(
            src_ref=src, dst_ref=dst, send_sem=s, recv_sem=r,
            device_id=self.dev(kind, k), device_id_type=MESH)

    def getq(self, p):
        x = self.WQ[p]
        return x.reshape(-1, x.shape[-1])

    def geto(self):
        return jnp.concatenate([self.WO[p].reshape(-1, 128) for p in range(self.nt)], axis=1)

    def getu(self, f):
        x = self.W2[f, 0]
        return x.reshape(-1, x.shape[-1])

    def getd(self, f):
        x = self.W2[f, 1]
        return x.reshape(-1, x.shape[-1])

    def blocks(self, ref, i):
        rows = ref.shape[-2]
        m = (i.stop - i.start) // (2 * rows)
        return slice(i.start // (2 * rows), i.stop // (2 * rows)), (m, 2, rows, ref.shape[-1])

    def putq(self, p, i, x):
        b, shape = self.blocks(self.DQ, i)
        self.DQ[p, b] = x.reshape(shape)

    def puto(self, p, i, x):
        b, shape = self.blocks(self.DO, i)
        self.DO[p, b] = x.reshape(shape)

    def put2(self, f, k, i, x):
        b, shape = self.blocks(self.D2, i)
        self.D2[f, k, b] = x.reshape(shape)

    def order(self, j):
        return self.t ^ j

    def order_back(self, j):
        return self.t ^ (self.nt - 1 - j)

    def turn(self, j):
        return (2 * j) ^ (7 * (j // 2))

    def order_ffn(self, j):
        return self.t ^ self.turn(j)

    def peers(self):
        return [("dp", k) for k in range(1, 2 * self.ng)] + [("z", k) for k in range(1, self.nt)]

    def greet(self):
        bar = pltpu.get_barrier_semaphore()
        for kind, k in self.peers():
            pl.semaphore_signal(bar, inc=1, device_id=self.dev(kind, k), device_id_type=MESH)

    def enter(self):
        pl.semaphore_wait(pltpu.get_barrier_semaphore(), len(self.peers()))

    def q_plane(self, x, k, incoming=False):
        g, c, p = self.g, self.c, self.t ^ x
        return self.copy("gq_plane", (x, k), "plane", k, self.WQ.at[p, g, c], self.WQ.at[p, g ^ k if incoming else g, c])

    def q_z(self, k, incoming=False):
        g, c, t = self.g, self.c, self.t
        return self.copy("gq_z", (k,), "z", k, self.WQ.at[t, g, c], self.WQ.at[t ^ k if incoming else t, g, c])

    def q_core(self, k):
        c, t = self.c, self.t
        return self.copy("gq_core", (k,), "core", 0, self.WQ.at[t ^ k, :, c], self.WQ.at[t ^ k, :, c])

    def q_core_in(self, k):
        c, t = self.c, self.t
        return self.copy("gq_core", (k,), "core", 0, self.WQ.at[t ^ k, :, c], self.WQ.at[t ^ k, :, 1 - c])

    def o_z(self, k, incoming=False):
        g, c, t = self.g, self.c, self.t
        return self.copy("go_z", (k,), "z", k, self.WO.at[t, g, c], self.WO.at[t ^ k if incoming else t, g, c])

    def f_z(self, k, incoming=False):
        g, c, t = self.g, self.c, self.t
        return self.copy("g2_z", (k,), "z", k, self.W2.at[t, :, g, c], self.W2.at[t ^ k if incoming else t, :, g, c])

    def o_plane(self, k, incoming=False):
        g, c = self.g, self.c
        return self.copy("go_plane", (k,), "plane", k, self.WO.at[:, g, c], self.WO.at[:, g ^ k if incoming else g, c])

    def o_core(self, incoming=False):
        c = self.c
        return self.copy("go_core", (), "core", 0, self.WO.at[:, :, c], self.WO.at[:, :, 1 - c if incoming else c])

    def f_plane(self, j, k, u, incoming=False):
        g, c, f = self.g, self.c, self.t ^ j
        return self.copy("g2_plane", (j, u, k), "plane", k, self.W2.at[f, u, g, c], self.W2.at[f, u, g ^ k if incoming else g, c])

    def f_near(self, u, incoming=False):
        c, t = self.c, self.t
        return self.copy("g2_near", (u,), "z", 1, self.W2.at[t, u, :, c], self.W2.at[t ^ 1 if incoming else t, u, :, c])

    def f_on(self, x):
        self.f_z(x, True).wait_recv()
        for u in range(2):
            for k in range(1, self.ng):
                self.f_plane(x, k, u).start()

    def f_pass(self, x):
        for u in range(2):
            for k in range(1, self.ng):
                self.f_plane(x, k, u, True).wait_recv()
        self.f_core(x).start()

    def f_core(self, j, incoming=False):
        c, f = self.c, self.t ^ j
        return self.copy("g2_core", (j,), "core", 0, self.W2.at[f, :, :, c], self.W2.at[f, :, :, 1 - c if incoming else c])

    def rq(self, stage, x, k=0, incoming=False):
        g, c, p = self.g, self.c, self.t ^ x
        if stage == "core":
            return self.copy("rq_core", (x,), "core", 0, self.DQ.at[p, :, 1 - c], self.CQ.at[x])
        if stage == "plane":
            return self.copy("rq_plane", (x, k), "plane", k, self.DQ.at[p, g ^ k, c], self.XQ.at[x, k])
        return self.copy("rq_z", (x,), "z", x, self.DQ.at[p, g, c], self.ZQ.at[x])

    def r2(self, stage, x, k=0):
        g, c, p = self.g, self.c, self.t ^ x
        if stage == "core":
            return self.copy("r2_core", (x,), "core", 0, self.D2.at[p, :, :, 1 - c], self.C2.at[x])
        if stage == "plane":
            return self.copy("r2_plane", (x, k), "plane", k, self.D2.at[p, :, g ^ k, c], self.X2.at[x, k])
        return self.copy("r2_z", (x,), "z", x, self.D2.at[p, :, g, c], self.Z2.at[x])

    def r2_near(self):
        c, t = self.c, self.t
        return self.copy("r2_near", (), "z", 1, self.D2.at[t ^ 1, :, :, c], self.Y2)

    def ro(self, stage, k=0):
        g, c, t = self.g, self.c, self.t
        if stage == "core":
            return self.copy("ro_core", (), "core", 0, self.DO.at[:, :, 1 - c], self.CO)
        if stage == "plane":
            return self.copy("ro_plane", (k,), "plane", k, self.DO.at[:, g ^ k, c], self.XO.at[k])
        return self.copy("ro_z", (k,), "z", k, self.DO.at[t ^ k, g, c], self.ZO.at[k])

    def q_after_core(self, x):
        p, c = self.t ^ x, self.c
        self.rq("core", x).wait_recv()
        self.DQ[p, :, c] = self.DQ[p, :, c] + self.CQ[x]

    def q_after_plane(self, x):
        p, c, g = self.t ^ x, self.c, self.g
        acc = self.DQ[p, g, c].astype(f32)
        for k in range(1, self.ng):
            self.rq("plane", x, k).wait_recv()
            acc = acc + self.XQ[x, k].astype(f32)
        self.DQ[p, g, c] = acc.astype(bf16)

    def f_after_core(self, x):
        p, c = self.t ^ x, self.c
        self.r2("core", x).wait_recv()
        for u in range(2):
            def step(i, _):
                self.D2[p, u, i, c] = self.D2[p, u, i, c] + self.C2[x, u, i]
                return 0
            lax.fori_loop(0, self.ng, step, 0)

    def f_after_plane(self, x):
        p, c, g = self.t ^ x, self.c, self.g
        for k in range(1, self.ng):
            self.r2("plane", x, k).wait_recv()
        for u in range(2):
            acc = self.D2[p, u, g, c].astype(f32)
            for k in range(1, self.ng):
                acc = acc + self.X2[x, k, u].astype(f32)
            self.D2[p, u, g, c] = acc.astype(bf16)

    def hook(self, place, j=None):
        ng, nt, t, g, c = self.ng, self.nt, self.t, self.g, self.c
        planes = range(1, ng)

        def begin(*copies):
            for x in copies:
                x.start()

        def await_in(*copies):
            for x in copies:
                x.wait_recv()

        if place == "greet":
            self.greet()
        elif place == "start":
            for k in range(3):
                self.WQ[t, g, c, :, 128 * k:128 * k + 128] = self.w_qkv[k].astype(bf16)
            self.WO[t, g, c] = self.w_out[...].astype(bf16)
            self.W2[t, 0, g, c] = self.w_up[...].astype(bf16)
            self.W2[t, 1, g, c] = self.w_down[...].astype(bf16)
            self.enter()
            begin(*[self.q_plane(0, k) for k in planes], self.q_z(1))
        elif place == "normed":
            begin(self.q_z(2), self.q_z(3))
        elif place == "masked":
            await_in(self.q_z(1, True))
            begin(*[self.q_plane(1, k) for k in planes])
            await_in(*[self.q_plane(0, k, True) for k in planes])
            begin(self.q_core(0))
        elif place == "pair":
            await_in(self.q_core_in(j))
        elif place == "pair_proj":
            @pl.when(j == 0)
            def _():
                begin(*[self.o_z(k) for k in range(1, nt)])
                begin(self.f_z(2))
                begin(*[self.f_plane(0, k, 0) for k in planes])
        elif place == "pair_half":
            @pl.when(j == 0)
            def _():
                await_in(*[self.q_plane(1, k, True) for k in planes])
                begin(self.q_core(1))
                await_in(self.q_z(2, True))
                begin(*[self.q_plane(2, k) for k in planes])
            @pl.when(j == 1)
            def _():
                begin(*[self.f_plane(0, k, 1) for k in planes])
            @pl.when(j == 2)
            def _():
                await_in(*[self.q_plane(3, k, True) for k in planes])
                begin(self.q_core(3))
                await_in(*[self.f_plane(0, k, 0, True) for k in planes])
                begin(self.f_near(0))
            @pl.when(j == 3)
            def _():
                await_in(*[self.o_plane(k, True) for k in planes])
                begin(self.o_core())
                await_in(*[self.f_plane(0, k, 1, True) for k in planes])
                begin(self.f_near(1), self.f_core(0))
        elif place == "pair_mid":
            @pl.when(j == 0)
            def _():
                await_in(self.q_z(3, True))
                begin(*[self.q_plane(3, k) for k in planes])
                begin(self.f_z(3))
            @pl.when(j == 1)
            def _():
                await_in(*[self.o_z(k, True) for k in range(1, nt)])
                begin(*[self.o_plane(k) for k in planes])
                await_in(*[self.q_plane(2, k, True) for k in planes])
                begin(self.q_core(2))
            @pl.when(j == 2)
            def _():
                self.f_on(2)
            @pl.when(j == 3)
            def _():
                self.f_on(3)
        elif place == "mixed":
            await_in(self.o_core(True))
        elif place == "chunk":
            await_in(self.f_core(self.turn(j), True))
        elif place == "chunk_mid":
            @pl.when(j < 2)
            def _():
                self.f_pass(j + 2)
            @pl.when(j == 2)
            def _():
                await_in(self.f_near(0, True), self.f_near(1, True))
                begin(self.f_core(1))
            @pl.when(j >= 1)
            def _():
                x = self.turn(j - 1)
                self.f_after_core(x)
                @pl.when(j >= 2)
                def _():
                    begin(*[self.r2("plane", x, k) for k in planes])
        elif place == "chunk_end":
            begin(self.r2("core", self.turn(j)))
        elif place == "ffn_done":
            self.f_after_core(1)
            begin(self.r2_near())
        elif place == "out_grad":
            begin(self.ro("core"))
        elif place == "back_mid":
            @pl.when(j >= 1)
            def _():
                self.q_after_core(nt - j)
                begin(*[self.rq("plane", nt - j, k) for k in planes])
            @pl.when(j == 0)
            def _():
                await_in(self.ro("core"))
                for p in range(nt):
                    self.DO[p, :, c] = self.DO[p, :, c] + self.CO[p]
                begin(*[self.ro("plane", k) for k in planes])
                self.v_mid("E", self.ne)
            @pl.when(j == 1)
            def _():
                await_in(self.r2_near())
                for u in range(2):
                    def step(i, _):
                        self.D2[t, u, i, c] = self.D2[t, u, i, c] + self.Y2[u, i]
                        return 0
                    lax.fori_loop(0, ng, step, 0)
                begin(*[self.r2("plane", 0, k) for k in planes])
                self.f_after_plane(2)
                begin(self.r2("z", 2))
            @pl.when(j == 2)
            def _():
                await_in(*[self.ro("plane", k) for k in planes])
                for p in range(nt):
                    acc = self.DO[p, g, c].astype(f32)
                    for k in planes:
                        acc = acc + self.XO[k, p].astype(f32)
                    self.DO[p, g, c] = acc.astype(bf16)
                begin(*[self.ro("z", k) for k in range(1, nt)])
                self.f_after_plane(3)
                begin(self.r2("z", 3))
            @pl.when(j >= 2)
            def _():
                self.q_after_plane(nt - j + 1)
                begin(self.rq("z", nt - j + 1))
        elif place == "back_end":
            self.rq("core", nt - 1 - j).start()
        elif place == "finish":
            self.q_after_core(0)
            begin(*[self.rq("plane", 0, k) for k in planes])
            for x in range(1, nt):
                if x > 1:
                    self.r2("z", x).wait_recv()
                self.ro("z", x).wait_recv()
            await_in(*[self.r2("plane", 0, k) for k in planes])
            for u, o in enumerate((self.o_up, self.o_down)):
                acc = self.D2[t, u, g, c].astype(f32)
                for k in planes:
                    acc = acc + self.X2[0, k, u].astype(f32)
                for x in range(2, nt):
                    acc = acc + self.Z2[x, u].astype(f32)
                o[...] = acc
            acc = self.DO[t, g, c].astype(f32)
            for x in range(1, nt):
                acc = acc + self.ZO[x].astype(f32)
            self.o_out[...] = acc
        elif place == "finish_z":
            self.q_after_plane(1)
            begin(self.rq("z", 1))
        elif place == "finish_q":
            acc = self.DQ[t, g, c].astype(f32)
            for k in range(1, ng):
                self.rq("plane", 0, k).wait_recv()
                acc = acc + self.XQ[0, k].astype(f32)
            for x in range(1, nt):
                self.rq("z", x).wait_recv()
                acc = acc + self.ZQ[x].astype(f32)
            for k in range(3):
                self.o_qkv[k] = acc[:, 128 * k:128 * k + 128]
        elif place == "leave":
            for k in planes:
                self.o_plane(k).wait_send()
                self.ro("plane", k).wait_send()
                for x in range(nt):
                    self.q_plane(x, k).wait_send()
                    if x != 1:
                        for u in range(2):
                            self.f_plane(x, k, u).wait_send()
                    if x != 1:
                        self.r2("plane", x, k).wait_send()
                    self.rq("plane", x, k).wait_send()
            for k in range(nt):
                self.q_core(k).wait_send()
                self.f_core(k).wait_send()
                self.r2("core", k).wait_send()
                self.rq("core", k).wait_send()
            self.o_core().wait_send()
            self.ro("core").wait_send()
            self.r2_near().wait_send()
            self.f_near(0).wait_send()
            self.f_near(1).wait_send()
            for k in range(1, nt):
                self.q_z(k).wait_send()
                self.o_z(k).wait_send()
                if k > 1:
                    self.f_z(k).wait_send()
                    self.r2("z", k).wait_send()
                self.rq("z", k).wait_send()
                self.ro("z", k).wait_send()

    def v(self, name, stage, k, incoming=False):
        Z, X = getattr(self, name)
        if stage == "z":
            return self.copy(name + "_z", (k,), "z", k, Z.at[self.t], Z.at[self.t ^ k if incoming else self.t])
        return self.copy(name + "_dp", (k,), "dp", k, X.at[self.d], X.at[self.d ^ k if incoming else self.d])

    def v_start(self, name, rows):
        Z = getattr(self, name)[0]
        n = rows[0].shape[1]
        for k, x in enumerate(rows):
            Z[self.t, :, k * n:k * n + n] = x
        for k in range(1, self.nt):
            self.v(name, "z", k).start()

    def v_mid(self, name, m):
        Z, X = getattr(self, name)
        nt, n = self.nt, Z.shape[2] // m
        for k in range(1, nt):
            self.v(name, "z", k, True).wait_recv()
        for k in range(nt):
            X[self.d, :, k * n:k * n + n] = Z[k, :, 0:n]
        s = Z[0, :, n:m * n]
        for k in range(1, nt):
            s = s + Z[k, :, n:m * n]
        X[self.d, :, nt * n:(nt + m - 1) * n] = s
        for k in range(1, 2 * self.ng):
            self.v(name, "dp", k).start()

    def v_done(self, name, m, kept, sums, at):
        Z, X = getattr(self, name)
        nd, nt, n = 2 * self.ng, self.nt, Z.shape[2] // m
        for k in range(1, nd):
            self.v(name, "dp", k, True).wait_recv()
        for k in range(nd):
            for i in range(nt):
                kept[k * nt + i:k * nt + i + 1, :] = X[k, :, i * n:i * n + n]
        s = X[0, :, nt * n:(nt + m - 1) * n]
        for k in range(1, nd):
            s = s + X[k, :, nt * n:(nt + m - 1) * n]
        for i in range(m - 1):
            sums[at + i:at + i + 1, :] = s[:, i * n:i * n + n]

    def v_leave(self, name):
        for k in range(1, self.nt):
            self.v(name, "z", k).wait_send()
        for k in range(1, 2 * self.ng):
            self.v(name, "dp", k).wait_send()


TILE = dict(ln1=256, proj=1024, ln2=512, tile=512, wgrad=512, ln2b=256, gmix=1024, gwo=512, qgrad=512, back=1024, ln1b=256)
UNROLL = {"proj", "ln2", "tile", "wgrad", "gmix", "gwo", "qgrad", "back"}


def loop(name, total, body, init):
    n = TILE[name]
    if name in UNROLL or total == n:
        for i in range(total // n):
            init = body(slice(i * n, i * n + n), init)
        return init
    return lax.fori_loop(0, total // n, lambda i, x: body(pl.ds(pl.multiple_of(i * n, n), n), x), init)


def layer(cm, T, most, length, t, tok, cot, seg, wt, btime, g1, b1, g2, b2, bdown, bup, out, gtok, sc):
    tp, n1, qkv, qaug, kaug, mixed, lse, qq, kk, vv, oo, dq, dkv, dqkv, mid, n2, ffn, gn, act, gu, gm, xT, xT3, bsum = sc
    seq, D = tok.shape
    P = qkv.shape[0]
    NF, F = bsum.shape[0], bsum.shape[2]
    n = seq // TR
    cm.hook("greet")
    cm.hook("start")
    cm.hook("row_in")
    half = D // 2
    ang = t * jnp.exp(-math.log(10000.0) * lax.broadcasted_iota(jnp.int32, (8, half), 1).astype(f32) / half)
    emb = jnp.concatenate([jnp.sin(ang), jnp.cos(ang)], axis=1)
    tp[...] = jnp.dot(emb, wt[...], precision=lax.Precision.HIGHEST, preferred_element_type=f32)[0:1, :] + btime[...]

    def ln1(r, _):
        xh, _r = normed(tok[r, :].astype(f32) + tp[...])
        n1[r, :] = (xh * g1[...] + b1[...]).astype(bf16)
        return 0

    loop("ln1", seq, ln1, 0)
    cm.hook("normed")
    srow = seg[pl.ds(T, 1), :].astype(f32)
    for b in range(seq // 128):
        col = jnp.broadcast_to(srow[:, 128 * b:128 * b + 128], (128, 128)).T
        spot = lane((128, 128)) % HS
        pos = lax.broadcasted_iota(jnp.int32, (128, 128), 0) + 128 * b
        same = col == spot.astype(f32)
        r = slice(128 * b, 128 * b + 128)
        qaug[r, :] = jnp.where(same & (spot < 8), 1.0, 0.0).astype(bf16)
        ka = jnp.where(same & (pos < length), 0.0, -BIG)
        kaug[r, :] = jnp.where(spot < 8, ka, jnp.where(spot < 11, -1.0, 0.0)).astype(bf16)

    cm.hook("cot_in")
    transpose_into(xT, cot, seq)
    cm.hook("masked")
    transpose_into(xT3, n1, seq)

    def pair_fwd(j, _):
        hp = cm.order(j)
        cm.hook("pair", j)

        def proj(r, _):
            x = nn_dot(n1[r, :], cm.getq(hp))
            s = jnp.where(lane((1, 384)) < 128, SCALE * LOG2E, 1.0)
            qkv[hp, r, :] = (x * s).astype(bf16)
            return 0

        loop("proj", seq, proj, 0)
        cm.hook("pair_proj", j)
        attend_fwd(seq, most, length, qkv, qaug, kaug, mixed, lse, qq, kk, vv, hp, lambda: cm.hook("pair_half", j))
        cm.hook("pair_mid", j)
        return 0

    lax.fori_loop(0, P, pair_fwd, 0)
    cm.hook("mixed")

    def ln2(r, _):
        mx = jnp.concatenate([mixed[p, r, :] for p in range(P)], axis=1)
        x = tok[r, :].astype(f32) + tp[...] + nt_dot(mx, cm.geto())
        mid[r, :] = x
        xh, _r = normed(x)
        n2[r, :] = (xh * g2[...] + b2[...]).astype(bf16)
        ffn[r, :] = jnp.zeros((TILE["ln2"], D), f32)
        gn[r, :] = jnp.zeros((TILE["ln2"], D), f32)
        return 0

    loop("ln2", seq, ln2, 0)
    cm.hook("second")

    def chunk(j, _):
        f = cm.order_ffn(j)
        cm.hook("chunk", j)

        def tile(r, acc):
            u = nn_dot(n2[r, :], cm.getu(f)) + bup[f]
            a, ga = gelu_parts(u)
            a = a.astype(bf16)
            g = (nn_dot(cot[r, :], cm.getd(f)) * ga).astype(bf16)
            act[r, :] = a
            gu[r, :] = g
            ffn[r, :] += nt_dot(a, cm.getd(f))
            gn[r, :] += nt_dot(g, cm.getu(f))
            return acc + colsum(g.astype(f32))

        bsum[f] = loop("tile", seq, tile, jnp.zeros((1, F), f32))
        cm.hook("chunk_mid", j)

        def wgrad(r, _):
            cm.put2(f, 1, r, nn_dot(xT[r, :], act[...]).astype(bf16))
            cm.put2(f, 0, r, tn_dot(n2[:, r], gu[...]).astype(bf16))
            return 0

        loop("wgrad", D, wgrad, 0)
        cm.hook("chunk_end", j)
        return 0

    lax.fori_loop(0, NF, chunk, 0)

    def ln2b(r, acc):
        c = cot[r, :].astype(f32)
        x = mid[r, :]
        out[r, :] = (x + ffn[r, :] + bdown[...]).astype(bf16)
        xh, rr = normed(x)
        gy = gn[r, :]
        gmid = c + norm_back(xh, rr, g2[...], gy)
        mid[r, :] = gmid
        n2[r, :] = gmid.astype(bf16)
        gn[r, :] = jnp.zeros((TILE["ln2b"], D), f32)
        return acc[0] + colsum(gy * xh), acc[1] + colsum(gy), acc[2] + colsum(c)

    z = jnp.zeros((1, D), f32)
    a = loop("ln2b", seq, ln2b, (z, z, z))
    cm.early([emb[0:1, :], *a] + [bsum[f] for f in range(NF)])
    cm.hook("ffn_done")

    def gmix(r, _):
        x = nn_dot(n2[r, :], cm.geto()).astype(bf16)
        for p in range(P):
            gm[p, r, :] = x[:, 128 * p:128 * p + 128]
        return 0

    loop("gmix", seq, gmix, 0)

    def gwo(r, _):
        m = jnp.concatenate([mixed[p] for p in range(P)], axis=1)
        x = tn_dot(n2[:, r], m).astype(bf16)
        for p in range(P):
            cm.puto(p, r, x[:, 128 * p:128 * p + 128])
        return 0

    loop("gwo", D, gwo, 0)
    cm.hook("out_grad")
    def pair_bwd(j, _):
        hp = cm.order_back(j)
        attend_bwd(seq, most, length, qkv, qaug, kaug, mixed, lse, gm, qq, kk, vv, oo, dq, dkv, dqkv, hp)
        cm.hook("back_mid", j)

        def wgrad(r, _):
            cm.putq(hp, r, nn_dot(xT3[r, :], dqkv[...]).astype(bf16))
            return 0

        loop("qgrad", D, wgrad, 0)
        cm.hook("back_end", j)

        def back(r, _):
            gn[r, :] += nt_dot(dqkv[r, :], cm.getq(hp))
            return 0

        loop("back", seq, back, 0)
        return 0

    lax.fori_loop(0, P, pair_bwd, 0)

    def ln1b(r, acc):
        xh, rr = normed(tok[r, :].astype(f32) + tp[...])
        gy = gn[r, :]
        gt = mid[r, :] + norm_back(xh, rr, g1[...], gy)
        gtok[r, :] = gt
        return acc[0] + colsum(gt), acc[1] + colsum(gy * xh), acc[2] + colsum(gy)

    a = loop("ln1b", seq, ln1b, (z, z, z))
    cm.late(list(a))


def layer_scratch(seq, D, P, NF, F):
    V = pltpu.VMEM
    return [V((1, D), f32), V((seq, D), bf16), V((P, seq, 384), bf16), V((seq, 128), bf16), V((seq, 128), bf16),
        V((P, seq, 128), bf16), V((P, seq, 128), f32)] + [V((2, seq, 128), bf16)] * 4 + [V((2, seq, 128), f32),
        V((3, 2, seq, 128), f32), V((seq, 384), bf16), V((seq, D), f32), V((seq, D), bf16), V((seq, D), f32), V((seq, D), f32),
        V((seq, F), bf16), V((seq, F), bf16), V((P, seq, 128), bf16), V((D, seq), bf16), V((D, seq), bf16), V((NF, 1, F), f32)]


def plain_kernel(most, n_sc, *refs):
    len_ref, ts_ref, tok, cot, seg, wq, wo, w2, wt, btime, g1, b1, g2, b2, bdown, bup, out, gtok, dwq, dwo, dw2, vec = refs[:22]
    T = lax.axis_index("tensor")
    cm = Plain(wq, wo, w2, dwq, dwo, dw2, vec)
    layer(cm, T, most, len_ref[T], ts_ref[0].astype(f32), tok, cot, seg, wt, btime, g1, b1, g2, b2, bdown, bup, out, gtok, refs[22:])


def run_plain(most, length, ts, tok, cot, seg, wq, wo, w2, wt, vecs, bup):
    seq, D = tok.shape
    P, NF, F = wq.shape[0], w2.shape[0], w2.shape[-1]
    S = jax.ShapeDtypeStruct
    vm = pl.BlockSpec(memory_space=pltpu.VMEM)
    sm = pl.BlockSpec(memory_space=pltpu.SMEM)
    return pl.pallas_call(
        functools.partial(plain_kernel, most, 0),
        out_shape=(S((seq, D), bf16), S((seq, D), f32), S(wq.shape, bf16), S(wo.shape, bf16), S(w2.shape, bf16), S((16, D), f32)),
        in_specs=[sm, sm] + [vm] * 14, out_specs=[vm] * 6,
        scratch_shapes=layer_scratch(seq, D, P, NF, F),
        compiler_params=pltpu.CompilerParams(vmem_limit_bytes=60 << 20),
    )(length, ts, tok, cot, seg, wq, wo, w2, wt, *[v[None] for v in vecs], bup)


def linked_kernel(most, ng, nt, names, semnames, n_layer, *refs):
    len_ref, ts_ref = refs[:2]
    held = refs[2:17]
    out, gtok, o_qkv, o_out, o_up, o_down, embs, grads, vec = refs[17:26]
    sc = refs[26:26 + n_layer]
    rest = refs[26 + n_layer:]
    bufs = dict(zip(names, rest[:len(names)]))
    sr = rest[len(names):]
    sems = {nm: (sr[2 * i], sr[2 * i + 1]) for i, nm in enumerate(semnames)}
    local = sr[-1]
    here = [bufs.pop("in%d" % i) for i in range(15)]
    tok, cot, seg, w_qkv, w_out, w_up, w_down, wt, btime, g1, b1, g2, b2, bdown, bup = here
    bufs.update(w_qkv=w_qkv, w_out=w_out, w_up=w_up, w_down=w_down, o_qkv=o_qkv, o_out=o_out, o_up=o_up, o_down=o_down)
    bufs["E"] = bufs.pop("EZ"), bufs.pop("EX")
    bufs["L"] = bufs.pop("LZ"), bufs.pop("LX")
    cm = Linked(ng, nt, bufs, sems)
    T = cm.t
    cm.ne = 4 + bup.shape[0]
    cm.early = lambda rows: cm.v_start("E", rows)
    cm.late = lambda rows: cm.v_start("L", rows)
    moves = [pltpu.make_async_copy(a, b, local.at[i]) for i, (a, b) in enumerate(zip(held, here))]
    plain_hook = cm.hook

    def hook(place, j=None):
        if place == "greet":
            plain_hook(place)
            for i in (3, 4, 5, 6, 0, 7, 2, *range(8, 15), 1):
                moves[i].start()
            for i in range(3, 7):
                moves[i].wait()
        elif place == "row_in":
            for i in (0, 7, 2, *range(8, 15)):
                moves[i].wait()
        elif place == "cot_in":
            moves[1].wait()
        else:
            plain_hook(place, j)

    cm.hook = hook
    layer(cm, T, most, len_ref[T], ts_ref[0].astype(f32), tok, cot, seg, wt, btime, g1, b1, g2, b2, bdown, bup, out, gtok, sc)
    cm.hook("finish")
    cm.v_mid("L", 3)
    cm.hook("finish_z")
    cm.v_done("E", cm.ne, embs, vec, 4)
    cm.hook("finish_q")
    cm.v_done("L", 3, grads, vec, 2)
    cm.hook("leave")
    cm.v_leave("E")
    cm.v_leave("L")


def run_linked(most, nd, nt, length, ts, tok, cot, seg, w_qkv, w_out, w_up, w_down, wt, vecs, bup):
    seq, D = tok.shape
    ng = nd // 2
    r, F = w_up.shape
    P, NF, ne = nt, nt, 4 + nt
    S, V = jax.ShapeDtypeStruct, pltpu.VMEM
    DMA = pltpu.SemaphoreType.DMA
    bufs = dict(
        WQ=V((nt, ng, 2, r, 384), bf16), WO=V((nt, ng, 2, r, 128), bf16), W2=V((nt, 2, ng, 2, r, F), bf16),
        DQ=V((nt, ng, 2, r, 384), bf16), DO=V((nt, ng, 2, r, 128), bf16), D2=V((nt, 2, ng, 2, r, F), bf16),
        CQ=V((nt, ng, r, 384), bf16), XQ=V((nt, ng, r, 384), bf16), ZQ=V((nt, r, 384), bf16),
        CO=V((nt, ng, r, 128), bf16), XO=V((ng, nt, r, 128), bf16), ZO=V((nt, r, 128), bf16),
        C2=V((nt, 2, ng, r, F), bf16), X2=V((nt, ng, 2, r, F), bf16), Z2=V((nt, 2, r, F), bf16), Y2=V((2, ng, r, F), bf16),
        EZ=V((nt, 1, ne * D), f32), EX=V((nd, 1, (nt + ne - 1) * D), f32), LZ=V((nt, 1, 3 * D), f32), LX=V((nd, 1, (nt + 2) * D), f32),
    )
    held = (tok, cot, seg, w_qkv, w_out, w_up, w_down, wt, *[v[None] for v in vecs], bup)
    for i, x in enumerate(held):
        bufs["in%d" % i] = V(x.shape, x.dtype)
    sems = dict(gq_plane=(nt, ng), gq_z=(nt,), gq_core=(nt,), go_z=(nt,), g2_z=(nt,), go_plane=(ng,), go_core=(), g2_plane=(nt, 2, ng), g2_core=(nt,), g2_near=(2,),
        rq_core=(nt,), rq_plane=(nt, ng), rq_z=(nt,), r2_core=(nt,), r2_plane=(nt, ng), r2_z=(nt,), r2_near=(), ro_core=(), ro_plane=(ng,), ro_z=(nt,),
        E_z=(nt,), E_dp=(nd,), L_z=(nt,), L_dp=(nd,))
    ls = layer_scratch(seq, D, P, NF, F)
    scratch = ls + list(bufs.values())
    for s in sems.values():
        scratch += [DMA(s), DMA(s)]
    scratch.append(DMA((15,)))
    vm = pl.BlockSpec(memory_space=pltpu.VMEM)
    sm = pl.BlockSpec(memory_space=pltpu.SMEM)
    hb = pl.BlockSpec(memory_space=pltpu.HBM)
    an = pl.BlockSpec(memory_space=pl.ANY)
    return pl.pallas_call(
        functools.partial(linked_kernel, most, ng, nt, tuple(bufs), tuple(sems), len(ls)),
        out_shape=(V((seq, D), bf16), V((seq, D), f32), V(w_qkv.shape, f32), V(w_out.shape, f32), V(w_up.shape, f32), V(w_down.shape, f32),
            V((nd * nt, D), f32), V((nd * nt, D), f32), V((16, D), f32)),
        in_specs=[sm, sm] + [hb] * 15, out_specs=[vm] * 9,
        scratch_shapes=scratch,
        compiler_params=pltpu.CompilerParams(vmem_limit_bytes=56 << 20, collective_id=0, has_side_effects=True),
    )(length, ts, *held)


def emit_kernel(nb, *refs):
    big, outs, gwt, small, sem = refs[:9], refs[9:15], refs[15], refs[16:23], refs[23]
    ups = [pltpu.make_async_copy(a, b, sem.at[i]) for i, (a, b) in enumerate(zip(big[3:], outs))]
    for x in ups:
        x.start()
    embs, grads, vec = (b[...] for b in big[:3])
    gwt[...] = lax.dot_general(embs, grads, (((0,), (0,)), ((), ())), precision=lax.Precision.HIGHEST, preferred_element_type=f32)
    small[0][...] = jnp.sum(grads, axis=0)
    for k, o in enumerate(small[1:-1]):
        o[...] = vec[2 + k, :]
    n = vec.shape[1]
    for k in range(nb):
        small[-1][pl.ds(k * n, n)] = vec[7 + k, :]
    for y in ups:
        y.wait()


def emit(nb, *big):
    S = jax.ShapeDtypeStruct
    D = big[2].shape[1]
    vm = pl.BlockSpec(memory_space=pltpu.VMEM)
    an = pl.BlockSpec(memory_space=pl.ANY)
    hb = pl.BlockSpec(memory_space=pltpu.HBM)
    return pl.pallas_call(
        functools.partial(emit_kernel, nb),
        out_shape=tuple(S(x.shape, x.dtype) for x in big[3:]) + (S((D, D), f32),) + tuple(S((D,), f32) for _ in range(6)) + (S((nb * D,), f32),),
        in_specs=[vm] * 3 + [an] * 6, out_specs=[hb] * 6 + [vm] * 8,
        scratch_shapes=[pltpu.SemaphoreType.DMA((6,))],
        compiler_params=pltpu.CompilerParams(vmem_limit_bytes=16 << 20),
    )(*big)


def shards(
    tokens,
    timestep,
    segment_ids,
    span_lengths,
    w_qkv,
    w_out_t,
    w_up,
    w_down_t,
    w_time,
    b_time,
    ln1_gain,
    ln1_bias,
    ln2_gain,
    ln2_bias,
    b_up,
    b_down,
    cotangent,
):
    seq, D = tokens.shape[1:]
    nd, nt = lax.axis_size("dp"), lax.axis_size("tensor")
    vecs = (b_time, ln1_gain, ln1_bias, ln2_gain, ln2_bias, b_down)
    F = w_up.shape[1]
    bup = b_up.reshape(nt, 1, F)
    if w_up.shape[0] % 16 == 0 and (nd, nt) == (8, 4):
        out, gtok, *g, embs, lines, vec = run_linked(
            DOC, nd, nt, span_lengths, timestep, tokens[0], cotangent[0], segment_ids,
            w_qkv, w_out_t, w_up, w_down_t, w_time, vecs, bup)
        gq, go, gu, gd, out, gtok, gwt, *v = emit(nt, embs, lines, vec, *g, out, gtok)
        return (out[None], gtok[None], gq, go, gu, gd, gwt, v[0], v[1], v[2], v[3], v[4], v[6], v[5])
    HB = w_qkv.shape[2]

    def whole(w):
        return lax.all_gather(lax.all_gather(w.astype(bf16), "dp", axis=w.ndim - 2, tiled=True), "tensor", axis=0)

    def part(g, dim):
        g = lax.psum_scatter(g, "dp", scatter_dimension=dim, tiled=True)
        return lax.psum_scatter(g, "tensor", scatter_dimension=0, tiled=True)[0].astype(f32)

    wq = whole(jnp.transpose(w_qkv, (1, 0, 2)).reshape(w_qkv.shape[1], 3 * HB))
    out, gtok, dwq, dwo, dw2, vec = run_plain(
        DOC, span_lengths, timestep, tokens[0], cotangent[0], segment_ids,
        wq, whole(w_out_t), whole(jnp.stack([w_up, w_down_t])), w_time, vecs, bup)
    lines = lax.all_gather(jnp.stack([vec[0], vec[8]]), ("dp", "tensor"), axis=1, tiled=False)
    gwt = jnp.dot(lines[0].T, lines[1], precision=lax.Precision.HIGHEST)
    small = lax.psum(vec, ("dp", "tensor"))
    gq, g2 = part(dwq, 1), part(dw2, 2)
    return (
        out[None], gtok[None], jnp.transpose(gq.reshape(gq.shape[0], 3, HB), (1, 0, 2)), part(dwo, 1), g2[0], g2[1],
        gwt, small[8], small[9], small[10], small[1], small[2], small[4:4 + nt].reshape(-1), small[3])


def solution(mesh):
    return jax.shard_map(
        shards,
        mesh=mesh,
        in_specs=(
            P_(("dp", "tensor"), None, None),
            P_(("dp", "tensor")),
            P_("dp", None),
            P_("dp"),
            P_(None, "dp", "tensor"),
            P_("dp", "tensor"),
            P_("dp", "tensor"),
            P_("dp", "tensor"),
            P_(),
            P_(),
            P_(),
            P_(),
            P_(),
            P_(),
            P_(),
            P_(),
            P_(("dp", "tensor"), None, None),
        ),
        out_specs=(
            P_(("dp", "tensor"), None, None),
            P_(("dp", "tensor"), None, None),
            P_(None, "dp", "tensor"),
            P_("dp", "tensor"),
            P_("dp", "tensor"),
            P_("dp", "tensor"),
            P_(),
            P_(),
            P_(),
            P_(),
            P_(),
            P_(),
            P_(),
            P_(),
        ),
        check_vma=False,
    )
```

```python
import functools
import math

import jax
import jax.numpy as jnp
from jax import lax
from jax.experimental import pallas as pl
from jax.experimental.pallas import tpu as pltpu
from jax.sharding import PartitionSpec as P_

f32, bf16 = jnp.float32, jnp.bfloat16
HS = 64
TR = 256
TB = 256
BIG = 1e30
EPS = 1e-5
DOC = 512
LEAST = 512
LOG2E = math.log2(math.e)
LN2 = math.log(2.0)
SCALE = 1.0 / math.sqrt(HS)


def nt_dot(a, b):
    return lax.dot_general(a, b, (((1,), (1,)), ((), ())), preferred_element_type=f32)


def tn_dot(a, b):
    return lax.dot_general(a, b, (((0,), (0,)), ((), ())), preferred_element_type=f32)


def nn_dot(a, b):
    return jnp.dot(a, b, preferred_element_type=f32)


def lane(shape):
    return lax.broadcasted_iota(jnp.int32, shape, len(shape) - 1)


def rows_of(i, n=TR):
    return pl.ds(pl.multiple_of(i * n, n), n)


def normed_keep(x, stats, r):
    mean = jnp.mean(x, axis=-1, keepdims=True)
    c = x - mean
    var = jnp.mean(c * c, axis=-1, keepdims=True)
    f = lax.rsqrt(var + EPS)
    stats[0, r, :] = jnp.broadcast_to(mean, (x.shape[0], 128))
    stats[1, r, :] = jnp.broadcast_to(f, (x.shape[0], 128))
    return c * f


def normed_again(x, stats, r):
    n = x.shape[1] // 128
    f = jnp.concatenate([stats[1, r, :]] * n, axis=1)
    return (x - jnp.concatenate([stats[0, r, :]] * n, axis=1)) * f, f


def norm_back(gyx, xhat, r, gain, gy):
    gh = gy * gain
    a = jnp.mean(gh, axis=-1, keepdims=True)
    b = jnp.mean(gyx * gain, axis=-1, keepdims=True)
    return r * (gh - a - xhat * b)


def colsum(x):
    return jnp.sum(x, axis=0, keepdims=True)


def halves(prod):
    low = lane(prod.shape) < HS
    s0 = jnp.sum(jnp.where(low, prod, 0.0), axis=-1, keepdims=True)
    s1 = jnp.sum(jnp.where(low, 0.0, prod), axis=-1, keepdims=True)
    return s0, s1


def split3(x):
    hi = x.astype(bf16)
    rest = x - hi.astype(f32)
    mid = rest.astype(bf16)
    lo = (rest - mid.astype(f32)).astype(bf16)
    return hi, mid, lo


def window(i, seq, most, tr):
    lo = max(0, (i * tr - most + 1) // 128 * 128)
    hi = min(seq, -(-(i * tr + tr - 1 + most) // 128) * 128)
    return lo, hi


def gelu_parts(u):
    c0, c1 = 0.7978845608028654, 0.044715
    u2 = u * u
    th = jnp.tanh(u * (c0 + (c0 * c1) * u2))
    half = 0.5 + 0.5 * th
    act = u * half
    grad = half + (0.5 * u) * (1.0 - th * th) * (c0 + (3.0 * c0 * c1) * u2)
    return act, grad


def transpose_into(dst, src, seq):
    def step(i, _):
        r = rows_of(i)
        dst[:, r] = src[r, :].T
        return 0
    for i in range(seq // TR):
        r = slice(i * TR, i * TR + TR)
        dst[:, r] = src[r, :].T


def half_sums(prod, swap=False):
    hi = prod.astype(bf16)
    lo = (prod - hi.astype(f32)).astype(bf16)
    a = lax.broadcasted_iota(jnp.int32, (256, 128), 0) // HS % 2
    b = lax.broadcasted_iota(jnp.int32, (256, 128), 1) // HS
    w = jnp.where((a != b) if swap else (a == b), 1.0, 0.0).astype(bf16)
    return nn_dot(jnp.concatenate([hi, lo], axis=1), w)


def attend_fwd(seq, most, length, qkv, qaug, kaug, mixed, lse, qq, kk, vv, hp, half):
    n = seq // TR
    def prep(i, _):
        r = rows_of(i)
        low = lane((TR, 128)) < HS
        q, k, v = (qkv[hp, r, 128 * c:128 * c + 128] for c in range(3))
        qa, ka = qaug[r, :], kaug[r, :]
        one = jnp.ones_like(v)
        qq[0, r, :] = jnp.where(low, q, qa)
        qq[1, r, :] = jnp.where(low, qa, q)
        kk[0, r, :] = jnp.where(low, k, ka)
        kk[1, r, :] = jnp.where(low, ka, k)
        vv[0, r, :] = jnp.where(low, v, one)
        vv[1, r, :] = jnp.where(low, one, v)
        return 0
    for i in range(n):
        prep(i, 0)

    def score(i, h):
        lo, hi = window(i, seq, most, TR)
        return nt_dot(qq[h, i * TR:i * TR + TR, :], kk[h, lo:hi, :])

    def soft(i, s, own):
        m = jnp.max(s, axis=-1, keepdims=True)
        if own is not None:
            pad = (lax.broadcasted_iota(jnp.int32, (TR, 1), 0) + i * TR) >= length
            m = jnp.where(pad, jnp.maximum(m, own), m)
        return m, jnp.exp2(s - m).astype(bf16)

    def finish(i, own, tops, outs):
        r = slice(i * TR, i * TR + TR)
        low = lane((TR, 128)) < HS
        num = jnp.where(low, outs[0], outs[1])
        den_x = jnp.where(low, outs[1], outs[0])
        if own[0] is not None:
            padf = ((lax.broadcasted_iota(jnp.int32, (TR, 1), 0) + i * TR) >= length).astype(f32)
            e0 = jnp.exp2(jnp.minimum(own[0] - tops[0], 0.0)).astype(bf16).astype(f32) * padf
            e1 = jnp.exp2(jnp.minimum(own[1] - tops[1], 0.0)).astype(bf16).astype(f32) * padf
            num = num + jnp.where(low, e0, e1) * qkv[hp, r, 256:384].astype(f32)
            den_x = den_x + jnp.where(low, e1, e0)
        mixed[hp, r, :] = (num / pltpu.roll(den_x, HS, 1)).astype(bf16)
        lse[hp, r, :] = jnp.where(low, tops[1], tops[0]) + jnp.log2(den_x)

    def selfs(i):
        if (i + 1) * TR <= LEAST:
            return (None, None)
        r = slice(i * TR, i * TR + TR)
        return halves(qkv[hp, r, 0:128].astype(f32) * qkv[hp, r, 128:256].astype(f32))

    units = [(i, h) for i in range(n) for h in range(2)]
    s = score(*units[0])
    tops, outs = [], []
    for u, (i, h) in enumerate(units):
        if (i, h) == (n // 2, 0):
            half()
        nxt = score(*units[u + 1]) if u + 1 < len(units) else None
        if h == 0:
            own = selfs(i)
        lo, hi = window(i, seq, most, TR)
        m, p = soft(i, s, own[h])
        tops.append(m)
        outs.append(nn_dot(p, vv[h, lo:hi, :]))
        if h == 1:
            finish(i, own, tops, outs)
            tops, outs = [], []
        s = nxt


def attend_bwd(seq, most, length, qkv, qaug, kaug, mixed, lse, gm, qq, kk, vv, oo, dq, dkv, dqkv, hp):
    n = seq // TB
    def prep(i, _):
        r = slice(i * TB, i * TB + TB)
        low = lane((TB, 128)) < HS
        spot = lane((TB, 128)) % HS
        q, k, v = (qkv[hp, r, 128 * c:128 * c + 128] for c in range(3))
        g = gm[hp, r, :]
        dx = half_sums(g.astype(f32) * mixed[hp, r, :].astype(f32), True)
        def put(base, x):
            hi, mid, lo = split3(x)
            z = jnp.where(spot == 8, hi, base)
            z = jnp.where(spot == 9, mid, z)
            return jnp.where(spot == 10, lo, z)
        zero = jnp.zeros((TB, 128), bf16)
        qa = put(qaug[r, :], lse[hp, r, :])
        oa = put(zero, dx)
        ka = kaug[r, :]
        va = jnp.where((spot >= 8) & (spot < 11), -jnp.ones_like(zero), zero)
        for ref, x, a in ((qq, q, qa), (kk, k, ka), (vv, v, va), (oo, g, oa)):
            ref[0, r, :] = jnp.where(low, x, a)
            ref[1, r, :] = jnp.where(low, a, x)
        if (i + 1) * TB > LEAST:
            q, k, v, g = (x.astype(f32) for x in (q, k, v, g))
            padf = ((lax.broadcasted_iota(jnp.int32, (TB, 1), 0) + i * TB) >= length).astype(f32)
            ls = pltpu.roll(lse[hp, r, :], HS, 1)
            d = pltpu.roll(dx, HS, 1)
            pf = jnp.exp2(jnp.minimum(half_sums(q * k) - ls, 1.0)) * padf
            ds = (pf * (half_sums(g * v) - d)).astype(bf16).astype(f32)
            pf = pf.astype(bf16).astype(f32)
            dkv[2, 0, r, :] = ds
            dkv[2, 1, r, :] = pf
        return 0
    for i in range(n):
        prep(i, 0)
    hi = window(0, seq, most, TB)[1]
    if hi < seq:
        dq[:, hi:seq, :] = jnp.zeros((2, seq - hi, 128), f32)

    def score(i, h):
        lo, hi = window(i, seq, most, TB)
        r = slice(i * TB, i * TB + TB)
        return nt_dot(kk[h, r, :], qq[h, lo:hi, :]), nt_dot(vv[h, r, :], oo[h, lo:hi, :])

    def rest(i, h, st, dpt):
        lo, hi = window(i, seq, most, TB)
        r = slice(i * TB, i * TB + TB)
        pt = jnp.exp2(st)
        dst = (pt * dpt).astype(bf16)
        dkv[h, 0, r, :] = nn_dot(dst, qq[h, lo:hi, :])
        dkv[h, 1, r, :] = nn_dot(pt.astype(bf16), oo[h, lo:hi, :])
        x = tn_dot(dst, kk[h, r, :])
        if i == 0:
            dq[h, lo:hi, :] = x
        else:
            dq[h, lo:hi, :] += x

    units = [(i, h) for i in range(n) for h in range(2)]
    s = score(*units[0])
    for u, (i, h) in enumerate(units):
        nxt = score(*units[u + 1]) if u + 1 < len(units) else None
        rest(i, h, *s)
        s = nxt

    for i in range(n):
        r = slice(i * TB, i * TB + TB)
        low = lane((TB, 128)) < HS
        gq = jnp.where(low, dq[0, r, :], dq[1, r, :])
        gk = jnp.where(low, dkv[0, 0, r, :], dkv[1, 0, r, :])
        gv = jnp.where(low, dkv[0, 1, r, :], dkv[1, 1, r, :])
        if (i + 1) * TB > LEAST:
            ds, pf = dkv[2, 0, r, :], dkv[2, 1, r, :]
            gq = gq + ds * qkv[hp, r, 128:256].astype(f32)
            gk = gk + ds * qkv[hp, r, 0:128].astype(f32)
            gv = gv + pf * gm[hp, r, :].astype(f32)
        dqkv[r, 0:128] = (gq * SCALE).astype(bf16)
        dqkv[r, 128:256] = (gk * LN2).astype(bf16)
        dqkv[r, 256:384] = gv.astype(bf16)


MESH = pl.DeviceIdType.MESH


class Plain:
    def __init__(self, wq, wo, w2, dwq, dwo, dw2, vec):
        self.wq, self.wo, self.w2 = wq, wo, w2
        self.dwq, self.dwo, self.dw2, self.vec = dwq, dwo, dw2, vec

    def getq(self, p):
        return self.wq[p]

    def geto(self):
        return jnp.concatenate([self.wo[p] for p in range(self.wo.shape[0])], axis=1)

    def getu(self, f):
        return self.w2[f, 0]

    def getd(self, f):
        return self.w2[f, 1]

    def putq(self, p, i, x):
        self.dwq[p, i, :] = x

    def puto(self, p, i, x):
        self.dwo[p, i, :] = x

    def put2(self, f, k, i, x):
        self.dw2[f, k, i, :] = x

    def order(self, j):
        return j

    def order_back(self, j):
        return j

    def order_ffn(self, j):
        return j

    def hook(self, *_):
        pass

    def early(self, rows):
        for k, x in enumerate(rows):
            self.vec[k:k + 1, :] = x

    def late(self, rows):
        for k, x in enumerate(rows):
            self.vec[8 + k:9 + k, :] = x


class Linked:
    def __init__(self, ng, nt, bufs, sems):
        self.ng, self.nt = ng, nt
        self.__dict__.update(bufs)
        self.sem = sems
        d, self.t = lax.axis_index("dp"), lax.axis_index("tensor")
        self.d, self.g, self.c = d, d // 2, d % 2
        self.sent = []

    def dev(self, kind, k):
        if kind == "core":
            return (2 * self.g + 1 - self.c, self.t)
        if kind == "plane":
            return (2 * (self.g ^ k) + self.c, self.t)
        if kind == "dp":
            return (self.d ^ k, self.t)
        return (self.d, self.t ^ k)

    def copy(self, name, at, kind, k, src, dst):
        s, r = self.sem[name]
        for i in at:
            s, r = s.at[i], r.at[i]
        return pltpu.make_async_remote_copy(
            src_ref=src, dst_ref=dst, send_sem=s, recv_sem=r,
            device_id=self.dev(kind, k), device_id_type=MESH)

    def getq(self, p):
        x = self.WQ[p]
        return x.reshape(-1, x.shape[-1])

    def geto(self):
        return jnp.concatenate([self.WO[p].reshape(-1, 128) for p in range(self.nt)], axis=1)

    def getu(self, f):
        x = self.W2[f, 0]
        return x.reshape(-1, x.shape[-1])

    def getd(self, f):
        x = self.W2[f, 1]
        return x.reshape(-1, x.shape[-1])

    def blocks(self, ref, i):
        rows = ref.shape[-2]
        m = (i.stop - i.start) // (2 * rows)
        return slice(i.start // (2 * rows), i.stop // (2 * rows)), (m, 2, rows, ref.shape[-1])

    def putq(self, p, i, x):
        b, shape = self.blocks(self.DQ, i)
        self.DQ[p, b] = x.reshape(shape)

    def puto(self, p, i, x):
        b, shape = self.blocks(self.DO, i)
        self.DO[p, b] = x.reshape(shape)

    def put2(self, f, k, i, x):
        b, shape = self.blocks(self.D2, i)
        self.D2[f, k, b] = x.reshape(shape)

    def order(self, j):
        return self.t ^ j

    def order_back(self, j):
        return self.t ^ (self.nt - 1 - j)

    def turn(self, j):
        return (2 * j) ^ (7 * (j // 2))

    def order_ffn(self, j):
        return self.t ^ self.turn(j)

    def peers(self):
        return [("dp", k) for k in range(1, 2 * self.ng)] + [("z", k) for k in range(1, self.nt)]

    def greet(self):
        bar = pltpu.get_barrier_semaphore()
        for kind, k in self.peers():
            pl.semaphore_signal(bar, inc=1, device_id=self.dev(kind, k), device_id_type=MESH)

    def enter(self):
        pl.semaphore_wait(pltpu.get_barrier_semaphore(), len(self.peers()))

    def q_plane(self, x, k, incoming=False):
        g, c, p = self.g, self.c, self.t ^ x
        return self.copy("gq_plane", (x, k), "plane", k, self.WQ.at[p, g, c], self.WQ.at[p, g ^ k if incoming else g, c])

    def q_z(self, k, incoming=False):
        g, c, t = self.g, self.c, self.t
        return self.copy("gq_z", (k,), "z", k, self.WQ.at[t, g, c], self.WQ.at[t ^ k if incoming else t, g, c])

    def q_core(self, k):
        c, t = self.c, self.t
        return self.copy("gq_core", (k,), "core", 0, self.WQ.at[t ^ k, :, c], self.WQ.at[t ^ k, :, c])

    def q_core_in(self, k):
        c, t = self.c, self.t
        return self.copy("gq_core", (k,), "core", 0, self.WQ.at[t ^ k, :, c], self.WQ.at[t ^ k, :, 1 - c])

    def o_z(self, k, incoming=False):
        g, c, t = self.g, self.c, self.t
        return self.copy("go_z", (k,), "z", k, self.WO.at[t, g, c], self.WO.at[t ^ k if incoming else t, g, c])

    def f_z(self, k, incoming=False):
        g, c, t = self.g, self.c, self.t
        return self.copy("g2_z", (k,), "z", k, self.W2.at[t, :, g, c], self.W2.at[t ^ k if incoming else t, :, g, c])

    def o_plane(self, k, incoming=False):
        g, c = self.g, self.c
        return self.copy("go_plane", (k,), "plane", k, self.WO.at[:, g, c], self.WO.at[:, g ^ k if incoming else g, c])

    def o_core(self, incoming=False):
        c = self.c
        return self.copy("go_core", (), "core", 0, self.WO.at[:, :, c], self.WO.at[:, :, 1 - c if incoming else c])

    def f_plane(self, j, k, u, incoming=False):
        g, c, f = self.g, self.c, self.t ^ j
        return self.copy("g2_plane", (j, u, k), "plane", k, self.W2.at[f, u, g, c], self.W2.at[f, u, g ^ k if incoming else g, c])

    def f_near(self, u, incoming=False):
        c, t = self.c, self.t
        return self.copy("g2_near", (u,), "z", 1, self.W2.at[t, u, :, c], self.W2.at[t ^ 1 if incoming else t, u, :, c])

    def f_on(self, x):
        self.f_z(x, True).wait_recv()
        for u in range(2):
            for k in range(1, self.ng):
                self.f_plane(x, k, u).start()

    def f_pass(self, x):
        for u in range(2):
            for k in range(1, self.ng):
                self.f_plane(x, k, u, True).wait_recv()
        self.f_core(x).start()

    def f_core(self, j, incoming=False):
        c, f = self.c, self.t ^ j
        return self.copy("g2_core", (j,), "core", 0, self.W2.at[f, :, :, c], self.W2.at[f, :, :, 1 - c if incoming else c])

    def rq(self, stage, x, k=0, incoming=False):
        g, c, p = self.g, self.c, self.t ^ x
        if stage == "core":
            return self.copy("rq_core", (x,), "core", 0, self.DQ.at[p, :, 1 - c], self.CQ.at[x])
        if stage == "plane":
            return self.copy("rq_plane", (x, k), "plane", k, self.DQ.at[p, g ^ k, c], self.XQ.at[x, k])
        return self.copy("rq_z", (x,), "z", x, self.DQ.at[p, g, c], self.ZQ.at[x])

    def r2(self, stage, x, k=0):
        g, c, p = self.g, self.c, self.t ^ x
        if stage == "core":
            return self.copy("r2_core", (x,), "core", 0, self.D2.at[p, :, :, 1 - c], self.C2.at[x])
        if stage == "plane":
            return self.copy("r2_plane", (x, k), "plane", k, self.D2.at[p, :, g ^ k, c], self.X2.at[x, k])
        return self.copy("r2_z", (x,), "z", x, self.D2.at[p, :, g, c], self.Z2.at[x])

    def r2_near(self):
        c, t = self.c, self.t
        return self.copy("r2_near", (), "z", 1, self.D2.at[t ^ 1, :, :, c], self.Y2)

    def ro(self, stage, k=0):
        g, c, t = self.g, self.c, self.t
        if stage == "core":
            return self.copy("ro_core", (), "core", 0, self.DO.at[:, :, 1 - c], self.CO)
        if stage == "plane":
            return self.copy("ro_plane", (k,), "plane", k, self.DO.at[:, g ^ k, c], self.XO.at[k])
        return self.copy("ro_z", (k,), "z", k, self.DO.at[t ^ k, g, c], self.ZO.at[k])

    def q_after_core(self, x):
        p, c = self.t ^ x, self.c
        self.rq("core", x).wait_recv()
        self.DQ[p, :, c] = self.DQ[p, :, c] + self.CQ[x]

    def q_after_plane(self, x):
        p, c, g = self.t ^ x, self.c, self.g
        acc = self.DQ[p, g, c].astype(f32)
        for k in range(1, self.ng):
            self.rq("plane", x, k).wait_recv()
            acc = acc + self.XQ[x, k].astype(f32)
        self.DQ[p, g, c] = acc.astype(bf16)

    def f_after_core(self, x):
        p, c = self.t ^ x, self.c
        self.r2("core", x).wait_recv()
        for u in range(2):
            def step(i, _):
                self.D2[p, u, i, c] = self.D2[p, u, i, c] + self.C2[x, u, i]
                return 0
            for i in range(self.ng):
                step(i, 0)

    def f_after_plane(self, x):
        p, c, g = self.t ^ x, self.c, self.g
        for k in range(1, self.ng):
            self.r2("plane", x, k).wait_recv()
        for u in range(2):
            acc = self.D2[p, u, g, c].astype(f32)
            for k in range(1, self.ng):
                acc = acc + self.X2[x, k, u].astype(f32)
            self.D2[p, u, g, c] = acc.astype(bf16)

    def hook(self, place, j=None):
        ng, nt, t, g, c = self.ng, self.nt, self.t, self.g, self.c
        planes = range(1, ng)

        def begin(*copies):
            for x in copies:
                x.start()

        def await_in(*copies):
            for x in copies:
                x.wait_recv()

        if place == "greet":
            self.greet()
        elif place == "start":
            for k in range(3):
                self.WQ[t, g, c, :, 128 * k:128 * k + 128] = self.w_qkv[k].astype(bf16)
            self.WO[t, g, c] = self.w_out[...].astype(bf16)
            self.W2[t, 0, g, c] = self.w_up[...].astype(bf16)
            self.W2[t, 1, g, c] = self.w_down[...].astype(bf16)
            self.enter()
            begin(*[self.q_plane(0, k) for k in planes], self.q_z(1))
        elif place == "normed":
            begin(self.q_z(2))
        elif place == "masked":
            await_in(self.q_z(1, True))
            begin(*[self.q_plane(1, k) for k in planes])
            begin(self.q_z(3))
            await_in(*[self.q_plane(0, k, True) for k in planes])
            begin(self.q_core(0))
        elif place == "pair":
            await_in(self.q_core_in(j))
        elif place == "pair_proj":
            @pl.when(j == 0)
            def _():
                await_in(self.q_z(2, True))
                begin(*[self.q_plane(2, k) for k in planes])
                begin(*[self.o_z(k) for k in range(1, nt)])
                begin(self.f_z(2))
        elif place == "pair_half":
            @pl.when(j == 0)
            def _():
                await_in(*[self.q_plane(1, k, True) for k in planes])
                begin(self.q_core(1))
                begin(*[self.f_plane(0, k, 0) for k in planes])
            @pl.when(j == 1)
            def _():
                await_in(*[self.q_plane(2, k, True) for k in planes])
                begin(self.q_core(2))
                begin(*[self.f_plane(0, k, 1) for k in planes])
            @pl.when(j == 2)
            def _():
                await_in(*[self.q_plane(3, k, True) for k in planes])
                begin(self.q_core(3))
                await_in(*[self.f_plane(0, k, 0, True) for k in planes])
                begin(self.f_near(0))
            @pl.when(j == 3)
            def _():
                await_in(*[self.o_plane(k, True) for k in planes])
                begin(self.o_core())
                await_in(*[self.f_plane(0, k, 1, True) for k in planes])
                begin(self.f_near(1), self.f_core(0))
        elif place == "pair_mid":
            @pl.when(j == 0)
            def _():
                await_in(self.q_z(3, True))
                begin(*[self.q_plane(3, k) for k in planes])
                begin(self.f_z(3))
            @pl.when(j == 1)
            def _():
                await_in(*[self.o_z(k, True) for k in range(1, nt)])
                begin(*[self.o_plane(k) for k in planes])
            @pl.when(j == 2)
            def _():
                self.f_on(2)
            @pl.when(j == 3)
            def _():
                self.f_on(3)
        elif place == "mixed":
            await_in(self.o_core(True))
        elif place == "chunk":
            await_in(self.f_core(self.turn(j), True))
        elif place == "chunk_mid":
            @pl.when(j < 2)
            def _():
                self.f_pass(j + 2)
            @pl.when(j == 2)
            def _():
                await_in(self.f_near(0, True), self.f_near(1, True))
                begin(self.f_core(1))
            @pl.when(j >= 1)
            def _():
                x = self.turn(j - 1)
                self.f_after_core(x)
                @pl.when(j >= 2)
                def _():
                    begin(*[self.r2("plane", x, k) for k in planes])
        elif place == "chunk_end":
            begin(self.r2("core", self.turn(j)))
        elif place == "ffn_done":
            self.f_after_core(1)
            begin(self.r2_near())
        elif place == "out_grad":
            begin(self.ro("core"))
        elif place == "back_mid":
            @pl.when(j >= 1)
            def _():
                self.q_after_core(nt - j)
                begin(*[self.rq("plane", nt - j, k) for k in planes])
            @pl.when(j == 0)
            def _():
                await_in(self.ro("core"))
                for p in range(nt):
                    self.DO[p, :, c] = self.DO[p, :, c] + self.CO[p]
                begin(*[self.ro("plane", k) for k in planes])
                self.v_mid("E", self.ne)
            @pl.when(j == 1)
            def _():
                await_in(self.r2_near())
                for u in range(2):
                    def step(i, _):
                        self.D2[t, u, i, c] = self.D2[t, u, i, c] + self.Y2[u, i]
                        return 0
                    for i in range(ng):
                        step(i, 0)
                begin(*[self.r2("plane", 0, k) for k in planes])
                self.f_after_plane(2)
                begin(self.r2("z", 2))
            @pl.when(j == 2)
            def _():
                await_in(*[self.ro("plane", k) for k in planes])
                for p in range(nt):
                    acc = self.DO[p, g, c].astype(f32)
                    for k in planes:
                        acc = acc + self.XO[k, p].astype(f32)
                    self.DO[p, g, c] = acc.astype(bf16)
                begin(*[self.ro("z", k) for k in range(1, nt)])
                self.f_after_plane(3)
                begin(self.r2("z", 3))
            @pl.when(j >= 2)
            def _():
                self.q_after_plane(nt - j + 1)
                begin(self.rq("z", nt - j + 1))
        elif place == "back_end":
            self.rq("core", nt - 1 - j).start()
        elif place == "finish":
            self.q_after_core(0)
            begin(*[self.rq("plane", 0, k) for k in planes])
            for x in range(1, nt):
                if x > 1:
                    self.r2("z", x).wait_recv()
                self.ro("z", x).wait_recv()
            await_in(*[self.r2("plane", 0, k) for k in planes])
            for u, o in enumerate((self.o_up, self.o_down)):
                acc = self.D2[t, u, g, c].astype(f32)
                for k in planes:
                    acc = acc + self.X2[0, k, u].astype(f32)
                for x in range(2, nt):
                    acc = acc + self.Z2[x, u].astype(f32)
                o[...] = acc
            acc = self.DO[t, g, c].astype(f32)
            for x in range(1, nt):
                acc = acc + self.ZO[x].astype(f32)
            self.o_out[...] = acc
        elif place == "finish_z":
            self.q_after_plane(1)
            begin(self.rq("z", 1))
        elif place == "finish_q":
            acc = self.DQ[t, g, c].astype(f32)
            for k in range(1, ng):
                self.rq("plane", 0, k).wait_recv()
                acc = acc + self.XQ[0, k].astype(f32)
            for x in range(1, nt):
                self.rq("z", x).wait_recv()
                acc = acc + self.ZQ[x].astype(f32)
            for k in range(3):
                self.o_qkv[k] = acc[:, 128 * k:128 * k + 128]
        elif place == "leave":
            for k in planes:
                self.o_plane(k).wait_send()
                self.ro("plane", k).wait_send()
                for x in range(nt):
                    self.q_plane(x, k).wait_send()
                    if x != 1:
                        for u in range(2):
                            self.f_plane(x, k, u).wait_send()
                    if x != 1:
                        self.r2("plane", x, k).wait_send()
                    self.rq("plane", x, k).wait_send()
            for k in range(nt):
                self.q_core(k).wait_send()
                self.f_core(k).wait_send()
                self.r2("core", k).wait_send()
                self.rq("core", k).wait_send()
            self.o_core().wait_send()
            self.ro("core").wait_send()
            self.r2_near().wait_send()
            self.f_near(0).wait_send()
            self.f_near(1).wait_send()
            for k in range(1, nt):
                self.q_z(k).wait_send()
                self.o_z(k).wait_send()
                if k > 1:
                    self.f_z(k).wait_send()
                    self.r2("z", k).wait_send()
                self.rq("z", k).wait_send()
                self.ro("z", k).wait_send()

    def v(self, name, stage, k, incoming=False):
        Z, X = getattr(self, name)
        if stage == "z":
            return self.copy(name + "_z", (k,), "z", k, Z.at[self.t], Z.at[self.t ^ k if incoming else self.t])
        return self.copy(name + "_dp", (k,), "dp", k, X.at[self.d], X.at[self.d ^ k if incoming else self.d])

    def v_start(self, name, rows):
        Z = getattr(self, name)[0]
        n = rows[0].shape[1]
        for k, x in enumerate(rows):
            Z[self.t, :, k * n:k * n + n] = x
        for k in range(1, self.nt):
            self.v(name, "z", k).start()

    def v_mid(self, name, m):
        Z, X = getattr(self, name)
        nt, n = self.nt, Z.shape[2] // m
        for k in range(1, nt):
            self.v(name, "z", k, True).wait_recv()
        for k in range(nt):
            X[self.d, :, k * n:k * n + n] = Z[k, :, 0:n]
        s = Z[0, :, n:m * n]
        for k in range(1, nt):
            s = s + Z[k, :, n:m * n]
        X[self.d, :, nt * n:(nt + m - 1) * n] = s
        for k in range(1, 2 * self.ng):
            self.v(name, "dp", k).start()

    def v_done(self, name, m, kept, sums, at):
        Z, X = getattr(self, name)
        nd, nt, n = 2 * self.ng, self.nt, Z.shape[2] // m
        for k in range(1, nd):
            self.v(name, "dp", k, True).wait_recv()
        for k in range(nd):
            for i in range(nt):
                kept[k * nt + i:k * nt + i + 1, :] = X[k, :, i * n:i * n + n]
        s = X[0, :, nt * n:(nt + m - 1) * n]
        for k in range(1, nd):
            s = s + X[k, :, nt * n:(nt + m - 1) * n]
        for i in range(m - 1):
            sums[at + i:at + i + 1, :] = s[:, i * n:i * n + n]

    def v_leave(self, name):
        for k in range(1, self.nt):
            self.v(name, "z", k).wait_send()
        for k in range(1, 2 * self.ng):
            self.v(name, "dp", k).wait_send()


TILE = dict(ln1=256, proj=1024, ln2=512, tile=512, wgrad=512, ln2b=256, gmix=1024, gwo=512, qgrad=512, back=1024, ln1b=256)
UNROLL = {"ln1", "ln1b", "ln2b", "proj", "ln2", "tile", "wgrad", "gmix", "gwo", "qgrad", "back"}


def loop(name, total, body, init):
    n = TILE[name]
    if name in UNROLL or total == n:
        for i in range(total // n):
            init = body(slice(i * n, i * n + n), init)
        return init
    return lax.fori_loop(0, total // n, lambda i, x: body(pl.ds(pl.multiple_of(i * n, n), n), x), init)


def layer(cm, T, most, length, t, tok, cot, seg, wt, btime, g1, b1, g2, b2, bdown, bup, out, gtok, sc):
    tp, n1, qkv, qaug, kaug, mixed, lse, qq, kk, vv, oo, dq, dkv, dqkv, mid, n2, ffn, gn, act, gu, gm, xT, xT3, bsum, stat1, stat2 = sc
    seq, D = tok.shape
    P = qkv.shape[0]
    NF, F = bsum.shape[0], bsum.shape[2]
    n = seq // TR
    cm.hook("greet")
    cm.hook("start")
    cm.hook("row_in")
    half = D // 2
    ang = t * jnp.exp(-math.log(10000.0) * lax.broadcasted_iota(jnp.int32, (8, half), 1).astype(f32) / half)
    emb = jnp.concatenate([jnp.sin(ang), jnp.cos(ang)], axis=1)
    tp[...] = jnp.dot(emb, wt[...], precision=lax.Precision.HIGHEST, preferred_element_type=f32)[0:1, :] + btime[...]

    def ln1(r, _):
        xh = normed_keep(tok[r, :].astype(f32) + tp[...], stat1, r)
        n1[r, :] = (xh * g1[...] + b1[...]).astype(bf16)
        return 0

    loop("ln1", seq, ln1, 0)
    cm.hook("normed")
    srow = seg[pl.ds(T, 1), :].astype(f32)
    for b in range(seq // 128):
        col = jnp.broadcast_to(srow[:, 128 * b:128 * b + 128], (128, 128)).T
        spot = lane((128, 128)) % HS
        pos = lax.broadcasted_iota(jnp.int32, (128, 128), 0) + 128 * b
        same = col == spot.astype(f32)
        r = slice(128 * b, 128 * b + 128)
        qaug[r, :] = jnp.where(same & (spot < 8), 1.0, 0.0).astype(bf16)
        ka = jnp.where(same & (pos < length), 0.0, -BIG)
        kaug[r, :] = jnp.where(spot < 8, ka, jnp.where(spot < 11, -1.0, 0.0)).astype(bf16)

    cm.hook("cot_in")
    transpose_into(xT, cot, seq)
    cm.hook("masked")
    transpose_into(xT3, n1, seq)

    def pair_fwd(j, _):
        hp = cm.order(j)
        cm.hook("pair", j)

        def proj(r, _):
            x = nn_dot(n1[r, :], cm.getq(hp))
            s = jnp.where(lane((1, 384)) < 128, SCALE * LOG2E, 1.0)
            qkv[hp, r, :] = (x * s).astype(bf16)
            return 0

        loop("proj", seq, proj, 0)
        cm.hook("pair_proj", j)
        attend_fwd(seq, most, length, qkv, qaug, kaug, mixed, lse, qq, kk, vv, hp, lambda: cm.hook("pair_half", j))
        cm.hook("pair_mid", j)
        return 0

    lax.fori_loop(0, P, pair_fwd, 0)
    cm.hook("mixed")

    def ln2(r, _):
        mx = jnp.concatenate([mixed[p, r, :] for p in range(P)], axis=1)
        x = tok[r, :].astype(f32) + tp[...] + nt_dot(mx, cm.geto())
        mid[r, :] = x
        xh = normed_keep(x, stat2, r)
        n2[r, :] = (xh * g2[...] + b2[...]).astype(bf16)
        ffn[r, :] = jnp.zeros((TILE["ln2"], D), f32)
        gn[r, :] = jnp.zeros((TILE["ln2"], D), f32)
        return 0

    loop("ln2", seq, ln2, 0)
    cm.hook("second")

    def chunk(j, _):
        f = cm.order_ffn(j)
        cm.hook("chunk", j)

        def tile(r, acc):
            u = nn_dot(n2[r, :], cm.getu(f)) + bup[f]
            a, ga = gelu_parts(u)
            a = a.astype(bf16)
            g = (nn_dot(cot[r, :], cm.getd(f)) * ga).astype(bf16)
            act[r, :] = a
            gu[r, :] = g
            ffn[r, :] += nt_dot(a, cm.getd(f))
            gn[r, :] += nt_dot(g, cm.getu(f))
            return acc + colsum(g.astype(f32))

        bsum[f] = loop("tile", seq, tile, jnp.zeros((1, F), f32))
        cm.hook("chunk_mid", j)

        def wgrad(r, _):
            cm.put2(f, 1, r, nn_dot(xT[r, :], act[...]).astype(bf16))
            cm.put2(f, 0, r, tn_dot(n2[:, r], gu[...]).astype(bf16))
            return 0

        loop("wgrad", D, wgrad, 0)
        cm.hook("chunk_end", j)
        return 0

    lax.fori_loop(0, NF, chunk, 0)

    def ln2b(r, acc):
        c = cot[r, :].astype(f32)
        x = mid[r, :]
        out[r, :] = (x + ffn[r, :] + bdown[...]).astype(bf16)
        xh, rr = normed_again(x, stat2, r)
        gy = gn[r, :]
        gyx = gy * xh
        gmid = c + norm_back(gyx, xh, rr, g2[...], gy)
        mid[r, :] = gmid
        n2[r, :] = gmid.astype(bf16)
        gn[r, :] = jnp.zeros((TILE["ln2b"], D), f32)
        return acc[0] + colsum(gyx), acc[1] + colsum(gy), acc[2] + colsum(c)

    z = jnp.zeros((1, D), f32)
    a = loop("ln2b", seq, ln2b, (z, z, z))
    cm.early([emb[0:1, :], *a] + [bsum[f] for f in range(NF)])
    cm.hook("ffn_done")

    def gmix(r, _):
        x = nn_dot(n2[r, :], cm.geto()).astype(bf16)
        for p in range(P):
            gm[p, r, :] = x[:, 128 * p:128 * p + 128]
        return 0

    loop("gmix", seq, gmix, 0)

    def gwo(r, _):
        m = jnp.concatenate([mixed[p] for p in range(P)], axis=1)
        x = tn_dot(n2[:, r], m).astype(bf16)
        for p in range(P):
            cm.puto(p, r, x[:, 128 * p:128 * p + 128])
        return 0

    loop("gwo", D, gwo, 0)
    cm.hook("out_grad")
    def pair_bwd(j, _):
        hp = cm.order_back(j)
        attend_bwd(seq, most, length, qkv, qaug, kaug, mixed, lse, gm, qq, kk, vv, oo, dq, dkv, dqkv, hp)
        cm.hook("back_mid", j)

        def wgrad(r, _):
            cm.putq(hp, r, nn_dot(xT3[r, :], dqkv[...]).astype(bf16))
            return 0

        loop("qgrad", D, wgrad, 0)
        cm.hook("back_end", j)

        def back(r, _):
            gn[r, :] += nt_dot(dqkv[r, :], cm.getq(hp))
            return 0

        loop("back", seq, back, 0)
        return 0

    lax.fori_loop(0, P, pair_bwd, 0)

    def ln1b(r, acc):
        xh, rr = normed_again(tok[r, :].astype(f32) + tp[...], stat1, r)
        gy = gn[r, :]
        gyx = gy * xh
        gt = mid[r, :] + norm_back(gyx, xh, rr, g1[...], gy)
        gtok[r, :] = gt
        return acc[0] + colsum(gt), acc[1] + colsum(gyx), acc[2] + colsum(gy)

    a = loop("ln1b", seq, ln1b, (z, z, z))
    cm.late(list(a))


def layer_scratch(seq, D, P, NF, F):
    V = pltpu.VMEM
    return [V((1, D), f32), V((seq, D), bf16), V((P, seq, 384), bf16), V((seq, 128), bf16), V((seq, 128), bf16),
        V((P, seq, 128), bf16), V((P, seq, 128), f32)] + [V((2, seq, 128), bf16)] * 4 + [V((2, seq, 128), f32),
        V((3, 2, seq, 128), f32), V((seq, 384), bf16), V((seq, D), f32), V((seq, D), bf16), V((seq, D), f32), V((seq, D), f32),
        V((seq, F), bf16), V((seq, F), bf16), V((P, seq, 128), bf16), V((D, seq), bf16), V((D, seq), bf16), V((NF, 1, F), f32), V((2, seq, 128), f32), V((2, seq, 128), f32)]


def plain_kernel(most, n_sc, *refs):
    len_ref, ts_ref, tok, cot, seg, wq, wo, w2, wt, btime, g1, b1, g2, b2, bdown, bup, out, gtok, dwq, dwo, dw2, vec = refs[:22]
    T = lax.axis_index("tensor")
    cm = Plain(wq, wo, w2, dwq, dwo, dw2, vec)
    layer(cm, T, most, len_ref[T], ts_ref[0].astype(f32), tok, cot, seg, wt, btime, g1, b1, g2, b2, bdown, bup, out, gtok, refs[22:])


def run_plain(most, length, ts, tok, cot, seg, wq, wo, w2, wt, vecs, bup):
    seq, D = tok.shape
    P, NF, F = wq.shape[0], w2.shape[0], w2.shape[-1]
    S = jax.ShapeDtypeStruct
    vm = pl.BlockSpec(memory_space=pltpu.VMEM)
    sm = pl.BlockSpec(memory_space=pltpu.SMEM)
    return pl.pallas_call(
        functools.partial(plain_kernel, most, 0),
        out_shape=(S((seq, D), bf16), S((seq, D), f32), S(wq.shape, bf16), S(wo.shape, bf16), S(w2.shape, bf16), S((16, D), f32)),
        in_specs=[sm, sm] + [vm] * 14, out_specs=[vm] * 6,
        scratch_shapes=layer_scratch(seq, D, P, NF, F),
        compiler_params=pltpu.CompilerParams(vmem_limit_bytes=60 << 20),
    )(length, ts, tok, cot, seg, wq, wo, w2, wt, *[v[None] for v in vecs], bup)


def linked_kernel(most, ng, nt, names, semnames, n_layer, *refs):
    len_ref, ts_ref = refs[:2]
    held = refs[2:17]
    out, gtok, o_qkv, o_out, o_up, o_down, embs, grads, vec = refs[17:26]
    sc = refs[26:26 + n_layer]
    rest = refs[26 + n_layer:]
    bufs = dict(zip(names, rest[:len(names)]))
    sr = rest[len(names):]
    sems = {nm: (sr[2 * i], sr[2 * i + 1]) for i, nm in enumerate(semnames)}
    local = sr[-1]
    here = [bufs.pop("in%d" % i) for i in range(15)]
    tok, cot, seg, w_qkv, w_out, w_up, w_down, wt, btime, g1, b1, g2, b2, bdown, bup = here
    bufs.update(w_qkv=w_qkv, w_out=w_out, w_up=w_up, w_down=w_down, o_qkv=o_qkv, o_out=o_out, o_up=o_up, o_down=o_down)
    bufs["E"] = bufs.pop("EZ"), bufs.pop("EX")
    bufs["L"] = bufs.pop("LZ"), bufs.pop("LX")
    cm = Linked(ng, nt, bufs, sems)
    T = cm.t
    cm.ne = 4 + bup.shape[0]
    cm.early = lambda rows: cm.v_start("E", rows)
    cm.late = lambda rows: cm.v_start("L", rows)
    moves = [pltpu.make_async_copy(a, b, local.at[i]) for i, (a, b) in enumerate(zip(held, here))]
    plain_hook = cm.hook

    def hook(place, j=None):
        if place == "greet":
            plain_hook(place)
            for i in (3, 4, 5, 6, 0, 7, 2, *range(8, 15), 1):
                moves[i].start()
            for i in range(3, 7):
                moves[i].wait()
        elif place == "row_in":
            for i in (0, 7, 2, *range(8, 15)):
                moves[i].wait()
        elif place == "cot_in":
            moves[1].wait()
        else:
            plain_hook(place, j)

    cm.hook = hook
    layer(cm, T, most, len_ref[T], ts_ref[0].astype(f32), tok, cot, seg, wt, btime, g1, b1, g2, b2, bdown, bup, out, gtok, sc)
    cm.hook("finish")
    cm.v_mid("L", 3)
    cm.hook("finish_z")
    cm.v_done("E", cm.ne, embs, vec, 4)
    cm.hook("finish_q")
    cm.v_done("L", 3, grads, vec, 2)
    cm.hook("leave")
    cm.v_leave("E")
    cm.v_leave("L")


def run_linked(most, nd, nt, length, ts, tok, cot, seg, w_qkv, w_out, w_up, w_down, wt, vecs, bup):
    seq, D = tok.shape
    ng = nd // 2
    r, F = w_up.shape
    P, NF, ne = nt, nt, 4 + nt
    S, V = jax.ShapeDtypeStruct, pltpu.VMEM
    DMA = pltpu.SemaphoreType.DMA
    bufs = dict(
        WQ=V((nt, ng, 2, r, 384), bf16), WO=V((nt, ng, 2, r, 128), bf16), W2=V((nt, 2, ng, 2, r, F), bf16),
        DQ=V((nt, ng, 2, r, 384), bf16), DO=V((nt, ng, 2, r, 128), bf16), D2=V((nt, 2, ng, 2, r, F), bf16),
        CQ=V((nt, ng, r, 384), bf16), XQ=V((nt, ng, r, 384), bf16), ZQ=V((nt, r, 384), bf16),
        CO=V((nt, ng, r, 128), bf16), XO=V((ng, nt, r, 128), bf16), ZO=V((nt, r, 128), bf16),
        C2=V((nt, 2, ng, r, F), bf16), X2=V((nt, ng, 2, r, F), bf16), Z2=V((nt, 2, r, F), bf16), Y2=V((2, ng, r, F), bf16),
        EZ=V((nt, 1, ne * D), f32), EX=V((nd, 1, (nt + ne - 1) * D), f32), LZ=V((nt, 1, 3 * D), f32), LX=V((nd, 1, (nt + 2) * D), f32),
    )
    held = (tok, cot, seg, w_qkv, w_out, w_up, w_down, wt, *[v[None] for v in vecs], bup)
    for i, x in enumerate(held):
        bufs["in%d" % i] = V(x.shape, x.dtype)
    sems = dict(gq_plane=(nt, ng), gq_z=(nt,), gq_core=(nt,), go_z=(nt,), g2_z=(nt,), go_plane=(ng,), go_core=(), g2_plane=(nt, 2, ng), g2_core=(nt,), g2_near=(2,),
        rq_core=(nt,), rq_plane=(nt, ng), rq_z=(nt,), r2_core=(nt,), r2_plane=(nt, ng), r2_z=(nt,), r2_near=(), ro_core=(), ro_plane=(ng,), ro_z=(nt,),
        E_z=(nt,), E_dp=(nd,), L_z=(nt,), L_dp=(nd,))
    ls = layer_scratch(seq, D, P, NF, F)
    scratch = ls + list(bufs.values())
    for s in sems.values():
        scratch += [DMA(s), DMA(s)]
    scratch.append(DMA((15,)))
    vm = pl.BlockSpec(memory_space=pltpu.VMEM)
    sm = pl.BlockSpec(memory_space=pltpu.SMEM)
    hb = pl.BlockSpec(memory_space=pltpu.HBM)
    an = pl.BlockSpec(memory_space=pl.ANY)
    return pl.pallas_call(
        functools.partial(linked_kernel, most, ng, nt, tuple(bufs), tuple(sems), len(ls)),
        out_shape=(V((seq, D), bf16), V((seq, D), f32), V(w_qkv.shape, f32), V(w_out.shape, f32), V(w_up.shape, f32), V(w_down.shape, f32),
            V((nd * nt, D), f32), V((nd * nt, D), f32), V((16, D), f32)),
        in_specs=[sm, sm] + [hb] * 15, out_specs=[vm] * 9,
        scratch_shapes=scratch,
        compiler_params=pltpu.CompilerParams(vmem_limit_bytes=56 << 20, collective_id=0, has_side_effects=True),
    )(length, ts, *held)


def emit_kernel(nb, *refs):
    big, outs, gwt, small, sem = refs[:9], refs[9:15], refs[15], refs[16:23], refs[23]
    ups = [pltpu.make_async_copy(a, b, sem.at[i]) for i, (a, b) in enumerate(zip(big[3:], outs))]
    for x in ups:
        x.start()
    embs, grads, vec = (b[...] for b in big[:3])
    gwt[...] = lax.dot_general(embs, grads, (((0,), (0,)), ((), ())), precision=lax.Precision.HIGHEST, preferred_element_type=f32)
    small[0][...] = jnp.sum(grads, axis=0)
    for k, o in enumerate(small[1:-1]):
        o[...] = vec[2 + k, :]
    n = vec.shape[1]
    for k in range(nb):
        small[-1][pl.ds(k * n, n)] = vec[7 + k, :]
    for y in ups:
        y.wait()


def emit(nb, *big):
    S = jax.ShapeDtypeStruct
    D = big[2].shape[1]
    vm = pl.BlockSpec(memory_space=pltpu.VMEM)
    an = pl.BlockSpec(memory_space=pl.ANY)
    hb = pl.BlockSpec(memory_space=pltpu.HBM)
    return pl.pallas_call(
        functools.partial(emit_kernel, nb),
        out_shape=tuple(S(x.shape, x.dtype) for x in big[3:]) + (S((D, D), f32),) + tuple(S((D,), f32) for _ in range(6)) + (S((nb * D,), f32),),
        in_specs=[vm] * 3 + [an] * 6, out_specs=[hb] * 6 + [vm] * 8,
        scratch_shapes=[pltpu.SemaphoreType.DMA((6,))],
        compiler_params=pltpu.CompilerParams(vmem_limit_bytes=16 << 20),
    )(*big)


def shards(
    tokens,
    timestep,
    segment_ids,
    span_lengths,
    w_qkv,
    w_out_t,
    w_up,
    w_down_t,
    w_time,
    b_time,
    ln1_gain,
    ln1_bias,
    ln2_gain,
    ln2_bias,
    b_up,
    b_down,
    cotangent,
):
    seq, D = tokens.shape[1:]
    nd, nt = lax.axis_size("dp"), lax.axis_size("tensor")
    vecs = (b_time, ln1_gain, ln1_bias, ln2_gain, ln2_bias, b_down)
    F = w_up.shape[1]
    bup = b_up.reshape(nt, 1, F)
    if w_up.shape[0] % 16 == 0 and (nd, nt) == (8, 4):
        out, gtok, *g, embs, lines, vec = run_linked(
            DOC, nd, nt, span_lengths, timestep, tokens[0], cotangent[0], segment_ids,
            w_qkv, w_out_t, w_up, w_down_t, w_time, vecs, bup)
        gq, go, gu, gd, out, gtok, gwt, *v = emit(nt, embs, lines, vec, *g, out, gtok)
        return (out[None], gtok[None], gq, go, gu, gd, gwt, v[0], v[1], v[2], v[3], v[4], v[6], v[5])
    HB = w_qkv.shape[2]

    def whole(w):
        return lax.all_gather(lax.all_gather(w.astype(bf16), "dp", axis=w.ndim - 2, tiled=True), "tensor", axis=0)

    def part(g, dim):
        g = lax.psum_scatter(g, "dp", scatter_dimension=dim, tiled=True)
        return lax.psum_scatter(g, "tensor", scatter_dimension=0, tiled=True)[0].astype(f32)

    wq = whole(jnp.transpose(w_qkv, (1, 0, 2)).reshape(w_qkv.shape[1], 3 * HB))
    out, gtok, dwq, dwo, dw2, vec = run_plain(
        DOC, span_lengths, timestep, tokens[0], cotangent[0], segment_ids,
        wq, whole(w_out_t), whole(jnp.stack([w_up, w_down_t])), w_time, vecs, bup)
    lines = lax.all_gather(jnp.stack([vec[0], vec[8]]), ("dp", "tensor"), axis=1, tiled=False)
    gwt = jnp.dot(lines[0].T, lines[1], precision=lax.Precision.HIGHEST)
    small = lax.psum(vec, ("dp", "tensor"))
    gq, g2 = part(dwq, 1), part(dw2, 2)
    return (
        out[None], gtok[None], jnp.transpose(gq.reshape(gq.shape[0], 3, HB), (1, 0, 2)), part(dwo, 1), g2[0], g2[1],
        gwt, small[8], small[9], small[10], small[1], small[2], small[4:4 + nt].reshape(-1), small[3])


def solution(mesh):
    return jax.shard_map(
        shards,
        mesh=mesh,
        in_specs=(
            P_(("dp", "tensor"), None, None),
            P_(("dp", "tensor")),
            P_("dp", None),
            P_("dp"),
            P_(None, "dp", "tensor"),
            P_("dp", "tensor"),
            P_("dp", "tensor"),
            P_("dp", "tensor"),
            P_(),
            P_(),
            P_(),
            P_(),
            P_(),
            P_(),
            P_(),
            P_(),
            P_(("dp", "tensor"), None, None),
        ),
        out_specs=(
            P_(("dp", "tensor"), None, None),
            P_(("dp", "tensor"), None, None),
            P_(None, "dp", "tensor"),
            P_("dp", "tensor"),
            P_("dp", "tensor"),
            P_("dp", "tensor"),
            P_(),
            P_(),
            P_(),
            P_(),
            P_(),
            P_(),
            P_(),
            P_(),
        ),
        check_vma=False,
    )
```

```python
import functools
import math

import jax
import jax.numpy as jnp
from jax import lax
from jax.experimental import pallas as pl
from jax.experimental.pallas import tpu as pltpu
from jax.sharding import PartitionSpec as P_

f32, bf16 = jnp.float32, jnp.bfloat16
HS = 64
TR = 256
TB = 128
BIG = 1e30
EPS = 1e-5
DOC = 512
LEAST = 512
LOG2E = math.log2(math.e)
LN2 = math.log(2.0)
SCALE = 1.0 / math.sqrt(HS)


def nt_dot(a, b):
    return lax.dot_general(a, b, (((1,), (1,)), ((), ())), preferred_element_type=f32)


def tn_dot(a, b):
    return lax.dot_general(a, b, (((0,), (0,)), ((), ())), preferred_element_type=f32)


def nn_dot(a, b):
    return jnp.dot(a, b, preferred_element_type=f32)


def lane(shape):
    return lax.broadcasted_iota(jnp.int32, shape, len(shape) - 1)


def rows_of(i, n=TR):
    return pl.ds(pl.multiple_of(i * n, n), n)


def normed_keep(x, stats, r):
    mean = jnp.mean(x, axis=-1, keepdims=True)
    c = x - mean
    var = jnp.mean(c * c, axis=-1, keepdims=True)
    f = lax.rsqrt(var + EPS)
    stats[0, r, :] = jnp.broadcast_to(mean, (x.shape[0], 128))
    stats[1, r, :] = jnp.broadcast_to(f, (x.shape[0], 128))
    return c * f


def normed_again(x, stats, r):
    n = x.shape[1] // 128
    f = jnp.concatenate([stats[1, r, :]] * n, axis=1)
    return (x - jnp.concatenate([stats[0, r, :]] * n, axis=1)) * f, f


def norm_back(gyx, xhat, r, gain, gy):
    gh = gy * gain
    a = jnp.mean(gh, axis=-1, keepdims=True)
    b = jnp.mean(gyx * gain, axis=-1, keepdims=True)
    return r * (gh - a - xhat * b)


def colsum(x):
    return jnp.sum(x, axis=0, keepdims=True)


def halves(prod):
    low = lane(prod.shape) < HS
    s0 = jnp.sum(jnp.where(low, prod, 0.0), axis=-1, keepdims=True)
    s1 = jnp.sum(jnp.where(low, 0.0, prod), axis=-1, keepdims=True)
    return s0, s1


def split3(x):
    hi = x.astype(bf16)
    rest = x - hi.astype(f32)
    mid = rest.astype(bf16)
    lo = (rest - mid.astype(f32)).astype(bf16)
    return hi, mid, lo


def window(i, seq, most, tr):
    lo = max(0, (i * tr - most + 1) // 128 * 128)
    hi = min(seq, -(-(i * tr + tr - 1 + most) // 128) * 128)
    return lo, hi


def gelu_parts(u):
    c0, c1 = 0.7978845608028654, 0.044715
    u2 = u * u
    th = jnp.tanh(u * (c0 + (c0 * c1) * u2))
    half = 0.5 + 0.5 * th
    act = u * half
    grad = half + (0.5 * u) * (1.0 - th * th) * (c0 + (3.0 * c0 * c1) * u2)
    return act, grad


def transpose_into(dst, src, seq):
    def step(i, _):
        r = rows_of(i)
        dst[:, r] = src[r, :].T
        return 0
    for i in range(seq // TR):
        r = slice(i * TR, i * TR + TR)
        dst[:, r] = src[r, :].T


def half_sums(prod, swap=False):
    hi = prod.astype(bf16)
    lo = (prod - hi.astype(f32)).astype(bf16)
    a = lax.broadcasted_iota(jnp.int32, (256, 128), 0) // HS % 2
    b = lax.broadcasted_iota(jnp.int32, (256, 128), 1) // HS
    w = jnp.where((a != b) if swap else (a == b), 1.0, 0.0).astype(bf16)
    return nn_dot(jnp.concatenate([hi, lo], axis=1), w)


def attend_fwd(seq, most, length, qkv, qaug, kaug, mixed, lse, qq, kk, vv, hp, half):
    n = seq // TR
    def prep(i, _):
        r = rows_of(i)
        low = lane((TR, 128)) < HS
        q, k, v = (qkv[hp, r, 128 * c:128 * c + 128] for c in range(3))
        qa, ka = qaug[r, :], kaug[r, :]
        one = jnp.ones_like(v)
        qq[0, r, :] = jnp.where(low, q, qa)
        qq[1, r, :] = jnp.where(low, qa, q)
        kk[0, r, :] = jnp.where(low, k, ka)
        kk[1, r, :] = jnp.where(low, ka, k)
        vv[0, r, :] = jnp.where(low, v, one)
        vv[1, r, :] = jnp.where(low, one, v)
        return 0
    for i in range(n):
        prep(i, 0)

    def score(i, h):
        lo, hi = window(i, seq, most, TR)
        return nt_dot(qq[h, i * TR:i * TR + TR, :], kk[h, lo:hi, :])

    def soft(i, s, own):
        m = jnp.max(s, axis=-1, keepdims=True)
        if own is not None:
            pad = (lax.broadcasted_iota(jnp.int32, (TR, 1), 0) + i * TR) >= length
            m = jnp.where(pad, jnp.maximum(m, own), m)
        return m, jnp.exp2(s - m).astype(bf16)

    def finish(i, own, tops, outs):
        r = slice(i * TR, i * TR + TR)
        low = lane((TR, 128)) < HS
        num = jnp.where(low, outs[0], outs[1])
        den_x = jnp.where(low, outs[1], outs[0])
        if own[0] is not None:
            padf = ((lax.broadcasted_iota(jnp.int32, (TR, 1), 0) + i * TR) >= length).astype(f32)
            e0 = jnp.exp2(jnp.minimum(own[0] - tops[0], 0.0)).astype(bf16).astype(f32) * padf
            e1 = jnp.exp2(jnp.minimum(own[1] - tops[1], 0.0)).astype(bf16).astype(f32) * padf
            num = num + jnp.where(low, e0, e1) * qkv[hp, r, 256:384].astype(f32)
            den_x = den_x + jnp.where(low, e1, e0)
        mixed[hp, r, :] = (num / pltpu.roll(den_x, HS, 1)).astype(bf16)
        lse[hp, r, :] = jnp.where(low, tops[1], tops[0]) + jnp.log2(den_x)

    def selfs(i):
        if (i + 1) * TR <= LEAST:
            return (None, None)
        r = slice(i * TR, i * TR + TR)
        return halves(qkv[hp, r, 0:128].astype(f32) * qkv[hp, r, 128:256].astype(f32))

    units = [(i, h) for i in range(n) for h in range(2)]
    s = score(*units[0])
    tops, outs = [], []
    for u, (i, h) in enumerate(units):
        if (i, h) == (n // 2, 0):
            half()
        nxt = score(*units[u + 1]) if u + 1 < len(units) else None
        if h == 0:
            own = selfs(i)
        lo, hi = window(i, seq, most, TR)
        m, p = soft(i, s, own[h])
        tops.append(m)
        outs.append(nn_dot(p, vv[h, lo:hi, :]))
        if h == 1:
            finish(i, own, tops, outs)
            tops, outs = [], []
        s = nxt


def attend_bwd(seq, most, length, qkv, qaug, kaug, mixed, lse, gm, qq, kk, vv, oo, dq, dkv, dqkv, hp):
    n = seq // TB
    def prep(i, _):
        r = slice(i * TB, i * TB + TB)
        low = lane((TB, 128)) < HS
        spot = lane((TB, 128)) % HS
        q, k, v = (qkv[hp, r, 128 * c:128 * c + 128] for c in range(3))
        g = gm[hp, r, :]
        dx = half_sums(g.astype(f32) * mixed[hp, r, :].astype(f32), True)
        def put(base, x):
            hi, mid, lo = split3(x)
            z = jnp.where(spot == 8, hi, base)
            z = jnp.where(spot == 9, mid, z)
            return jnp.where(spot == 10, lo, z)
        zero = jnp.zeros((TB, 128), bf16)
        qa = put(qaug[r, :], lse[hp, r, :])
        oa = put(zero, dx)
        ka = kaug[r, :]
        va = jnp.where((spot >= 8) & (spot < 11), -jnp.ones_like(zero), zero)
        for ref, x, a in ((qq, q, qa), (kk, k, ka), (vv, v, va), (oo, g, oa)):
            ref[0, r, :] = jnp.where(low, x, a)
            ref[1, r, :] = jnp.where(low, a, x)
        if (i + 1) * TB > LEAST:
            q, k, v, g = (x.astype(f32) for x in (q, k, v, g))
            padf = ((lax.broadcasted_iota(jnp.int32, (TB, 1), 0) + i * TB) >= length).astype(f32)
            ls = pltpu.roll(lse[hp, r, :], HS, 1)
            d = pltpu.roll(dx, HS, 1)
            pf = jnp.exp2(jnp.minimum(half_sums(q * k) - ls, 1.0)) * padf
            ds = (pf * (half_sums(g * v) - d)).astype(bf16).astype(f32)
            pf = pf.astype(bf16).astype(f32)
            dkv[2, 0, r, :] = ds
            dkv[2, 1, r, :] = pf
        return 0
    for i in range(n):
        prep(i, 0)
    hi = window(0, seq, most, TB)[1]
    if hi < seq:
        dq[:, hi:seq, :] = jnp.zeros((2, seq - hi, 128), f32)

    def score(i, h):
        lo, hi = window(i, seq, most, TB)
        r = slice(i * TB, i * TB + TB)
        return nt_dot(kk[h, r, :], qq[h, lo:hi, :]), nt_dot(vv[h, r, :], oo[h, lo:hi, :])

    def rest(i, h, st, dpt):
        lo, hi = window(i, seq, most, TB)
        r = slice(i * TB, i * TB + TB)
        pt = jnp.exp2(st)
        dst = (pt * dpt).astype(bf16)
        dkv[h, 0, r, :] = nn_dot(dst, qq[h, lo:hi, :])
        dkv[h, 1, r, :] = nn_dot(pt.astype(bf16), oo[h, lo:hi, :])
        x = tn_dot(dst, kk[h, r, :])
        if i == 0:
            dq[h, lo:hi, :] = x
        else:
            dq[h, lo:hi, :] += x

    units = [(i, h) for i in range(n) for h in range(2)]
    s = score(*units[0])
    for u, (i, h) in enumerate(units):
        nxt = score(*units[u + 1]) if u + 1 < len(units) else None
        rest(i, h, *s)
        s = nxt

    for i in range(n):
        r = slice(i * TB, i * TB + TB)
        low = lane((TB, 128)) < HS
        gq = jnp.where(low, dq[0, r, :], dq[1, r, :])
        gk = jnp.where(low, dkv[0, 0, r, :], dkv[1, 0, r, :])
        gv = jnp.where(low, dkv[0, 1, r, :], dkv[1, 1, r, :])
        if (i + 1) * TB > LEAST:
            ds, pf = dkv[2, 0, r, :], dkv[2, 1, r, :]
            gq = gq + ds * qkv[hp, r, 128:256].astype(f32)
            gk = gk + ds * qkv[hp, r, 0:128].astype(f32)
            gv = gv + pf * gm[hp, r, :].astype(f32)
        dqkv[r, 0:128] = (gq * SCALE).astype(bf16)
        dqkv[r, 128:256] = (gk * LN2).astype(bf16)
        dqkv[r, 256:384] = gv.astype(bf16)


MESH = pl.DeviceIdType.MESH


class Plain:
    def __init__(self, wq, wo, w2, dwq, dwo, dw2, vec):
        self.wq, self.wo, self.w2 = wq, wo, w2
        self.dwq, self.dwo, self.dw2, self.vec = dwq, dwo, dw2, vec

    def getq(self, p):
        return self.wq[p]

    def geto(self):
        return jnp.concatenate([self.wo[p] for p in range(self.wo.shape[0])], axis=1)

    def getu(self, f):
        return self.w2[f, 0]

    def getd(self, f):
        return self.w2[f, 1]

    def putq(self, p, i, x):
        self.dwq[p, i, :] = x

    def puto(self, p, i, x):
        self.dwo[p, i, :] = x

    def put2(self, f, k, i, x):
        self.dw2[f, k, i, :] = x

    def order(self, j):
        return j

    def order_back(self, j):
        return j

    def order_ffn(self, j):
        return j

    def hook(self, *_):
        pass

    def early(self, rows):
        for k, x in enumerate(rows):
            self.vec[k:k + 1, :] = x

    def late(self, rows):
        for k, x in enumerate(rows):
            self.vec[8 + k:9 + k, :] = x


class Linked:
    def __init__(self, ng, nt, bufs, sems):
        self.ng, self.nt = ng, nt
        self.__dict__.update(bufs)
        self.sem = sems
        d, self.t = lax.axis_index("dp"), lax.axis_index("tensor")
        self.d, self.g, self.c = d, d // 2, d % 2
        self.sent = []

    def dev(self, kind, k):
        if kind == "core":
            return (2 * self.g + 1 - self.c, self.t)
        if kind == "plane":
            return (2 * (self.g ^ k) + self.c, self.t)
        if kind == "dp":
            return (self.d ^ k, self.t)
        return (self.d, self.t ^ k)

    def copy(self, name, at, kind, k, src, dst):
        s, r = self.sem[name]
        for i in at:
            s, r = s.at[i], r.at[i]
        return pltpu.make_async_remote_copy(
            src_ref=src, dst_ref=dst, send_sem=s, recv_sem=r,
            device_id=self.dev(kind, k), device_id_type=MESH)

    def getq(self, p):
        x = self.WQ[p]
        return x.reshape(-1, x.shape[-1])

    def geto(self):
        return jnp.concatenate([self.WO[p].reshape(-1, 128) for p in range(self.nt)], axis=1)

    def getu(self, f):
        x = self.W2[f, 0]
        return x.reshape(-1, x.shape[-1])

    def getd(self, f):
        x = self.W2[f, 1]
        return x.reshape(-1, x.shape[-1])

    def blocks(self, ref, i):
        rows = ref.shape[-2]
        m = (i.stop - i.start) // (2 * rows)
        return slice(i.start // (2 * rows), i.stop // (2 * rows)), (m, 2, rows, ref.shape[-1])

    def putq(self, p, i, x):
        b, shape = self.blocks(self.DQ, i)
        self.DQ[p, b] = x.reshape(shape)

    def puto(self, p, i, x):
        b, shape = self.blocks(self.DO, i)
        self.DO[p, b] = x.reshape(shape)

    def put2(self, f, k, i, x):
        b, shape = self.blocks(self.D2, i)
        self.D2[f, k, b] = x.reshape(shape)

    def order(self, j):
        return self.t ^ j

    def order_back(self, j):
        return self.t ^ (self.nt - 1 - j)

    def turn(self, j):
        return (2 * j) ^ (7 * (j // 2))

    def order_ffn(self, j):
        return self.t ^ self.turn(j)

    def peers(self):
        return [("dp", k) for k in range(1, 2 * self.ng)] + [("z", k) for k in range(1, self.nt)]

    def greet(self):
        bar = pltpu.get_barrier_semaphore()
        for kind, k in self.peers():
            pl.semaphore_signal(bar, inc=1, device_id=self.dev(kind, k), device_id_type=MESH)

    def enter(self):
        pl.semaphore_wait(pltpu.get_barrier_semaphore(), len(self.peers()))

    def q_plane(self, x, k, incoming=False):
        g, c, p = self.g, self.c, self.t ^ x
        return self.copy("gq_plane", (x, k), "plane", k, self.WQ.at[p, g, c], self.WQ.at[p, g ^ k if incoming else g, c])

    def q_z(self, k, incoming=False):
        g, c, t = self.g, self.c, self.t
        return self.copy("gq_z", (k,), "z", k, self.WQ.at[t, g, c], self.WQ.at[t ^ k if incoming else t, g, c])

    def q_core(self, k):
        c, t = self.c, self.t
        return self.copy("gq_core", (k,), "core", 0, self.WQ.at[t ^ k, :, c], self.WQ.at[t ^ k, :, c])

    def q_core_in(self, k):
        c, t = self.c, self.t
        return self.copy("gq_core", (k,), "core", 0, self.WQ.at[t ^ k, :, c], self.WQ.at[t ^ k, :, 1 - c])

    def o_z(self, k, incoming=False):
        g, c, t = self.g, self.c, self.t
        return self.copy("go_z", (k,), "z", k, self.WO.at[t, g, c], self.WO.at[t ^ k if incoming else t, g, c])

    def f_z(self, k, incoming=False):
        g, c, t = self.g, self.c, self.t
        return self.copy("g2_z", (k,), "z", k, self.W2.at[t, :, g, c], self.W2.at[t ^ k if incoming else t, :, g, c])

    def o_plane(self, k, incoming=False):
        g, c = self.g, self.c
        return self.copy("go_plane", (k,), "plane", k, self.WO.at[:, g, c], self.WO.at[:, g ^ k if incoming else g, c])

    def o_core(self, incoming=False):
        c = self.c
        return self.copy("go_core", (), "core", 0, self.WO.at[:, :, c], self.WO.at[:, :, 1 - c if incoming else c])

    def f_plane(self, j, k, u, incoming=False):
        g, c, f = self.g, self.c, self.t ^ j
        return self.copy("g2_plane", (j, u, k), "plane", k, self.W2.at[f, u, g, c], self.W2.at[f, u, g ^ k if incoming else g, c])

    def f_near(self, u, incoming=False):
        c, t = self.c, self.t
        return self.copy("g2_near", (u,), "z", 1, self.W2.at[t, u, :, c], self.W2.at[t ^ 1 if incoming else t, u, :, c])

    def f_on(self, x):
        self.f_z(x, True).wait_recv()
        for u in range(2):
            for k in range(1, self.ng):
                self.f_plane(x, k, u).start()

    def f_pass(self, x):
        for u in range(2):
            for k in range(1, self.ng):
                self.f_plane(x, k, u, True).wait_recv()
        self.f_core(x).start()

    def f_core(self, j, incoming=False):
        c, f = self.c, self.t ^ j
        return self.copy("g2_core", (j,), "core", 0, self.W2.at[f, :, :, c], self.W2.at[f, :, :, 1 - c if incoming else c])

    def rq(self, stage, x, k=0, incoming=False):
        g, c, p = self.g, self.c, self.t ^ x
        if stage == "core":
            return self.copy("rq_core", (x,), "core", 0, self.DQ.at[p, :, 1 - c], self.CQ.at[x])
        if stage == "plane":
            return self.copy("rq_plane", (x, k), "plane", k, self.DQ.at[p, g ^ k, c], self.XQ.at[x, k])
        return self.copy("rq_z", (x,), "z", x, self.DQ.at[p, g, c], self.ZQ.at[x])

    def r2(self, stage, x, k=0):
        g, c, p = self.g, self.c, self.t ^ x
        if stage == "core":
            return self.copy("r2_core", (x,), "core", 0, self.D2.at[p, :, :, 1 - c], self.C2.at[x])
        if stage == "plane":
            return self.copy("r2_plane", (x, k), "plane", k, self.D2.at[p, :, g ^ k, c], self.X2.at[x, k])
        return self.copy("r2_z", (x,), "z", x, self.D2.at[p, :, g, c], self.Z2.at[x])

    def r2_near(self):
        c, t = self.c, self.t
        return self.copy("r2_near", (), "z", 1, self.D2.at[t ^ 1, :, :, c], self.Y2)

    def ro(self, stage, k=0):
        g, c, t = self.g, self.c, self.t
        if stage == "core":
            return self.copy("ro_core", (), "core", 0, self.DO.at[:, :, 1 - c], self.CO)
        if stage == "plane":
            return self.copy("ro_plane", (k,), "plane", k, self.DO.at[:, g ^ k, c], self.XO.at[k])
        return self.copy("ro_z", (k,), "z", k, self.DO.at[t ^ k, g, c], self.ZO.at[k])

    def q_after_core(self, x):
        p, c = self.t ^ x, self.c
        self.rq("core", x).wait_recv()
        self.DQ[p, :, c] = self.DQ[p, :, c] + self.CQ[x]

    def q_after_plane(self, x):
        p, c, g = self.t ^ x, self.c, self.g
        acc = self.DQ[p, g, c].astype(f32)
        for k in range(1, self.ng):
            self.rq("plane", x, k).wait_recv()
            acc = acc + self.XQ[x, k].astype(f32)
        self.DQ[p, g, c] = acc.astype(bf16)

    def f_after_core(self, x):
        p, c = self.t ^ x, self.c
        self.r2("core", x).wait_recv()
        for u in range(2):
            def step(i, _):
                self.D2[p, u, i, c] = self.D2[p, u, i, c] + self.C2[x, u, i]
                return 0
            for i in range(self.ng):
                step(i, 0)

    def f_after_plane(self, x):
        p, c, g = self.t ^ x, self.c, self.g
        for k in range(1, self.ng):
            self.r2("plane", x, k).wait_recv()
        for u in range(2):
            acc = self.D2[p, u, g, c].astype(f32)
            for k in range(1, self.ng):
                acc = acc + self.X2[x, k, u].astype(f32)
            self.D2[p, u, g, c] = acc.astype(bf16)

    def hook(self, place, j=None):
        ng, nt, t, g, c = self.ng, self.nt, self.t, self.g, self.c
        planes = range(1, ng)

        def begin(*copies):
            for x in copies:
                x.start()

        def await_in(*copies):
            for x in copies:
                x.wait_recv()

        if place == "greet":
            self.greet()
        elif place == "start":
            for k in range(3):
                self.WQ[t, g, c, :, 128 * k:128 * k + 128] = self.w_qkv[k].astype(bf16)
            self.WO[t, g, c] = self.w_out[...].astype(bf16)
            self.W2[t, 0, g, c] = self.w_up[...].astype(bf16)
            self.W2[t, 1, g, c] = self.w_down[...].astype(bf16)
            self.enter()
            begin(*[self.q_plane(0, k) for k in planes], self.q_z(1))
        elif place == "normed":
            begin(self.q_z(2))
        elif place == "masked":
            await_in(self.q_z(1, True))
            begin(*[self.q_plane(1, k) for k in planes])
            begin(self.q_z(3))
            await_in(*[self.q_plane(0, k, True) for k in planes])
            begin(self.q_core(0))
        elif place == "pair":
            await_in(self.q_core_in(j))
        elif place == "pair_proj":
            @pl.when(j == 0)
            def _():
                await_in(self.q_z(2, True))
                begin(*[self.q_plane(2, k) for k in planes])
                begin(*[self.o_z(k) for k in range(1, nt)])
                begin(self.f_z(2))
        elif place == "pair_half":
            @pl.when(j == 0)
            def _():
                await_in(*[self.q_plane(1, k, True) for k in planes])
                begin(self.q_core(1))
                begin(*[self.f_plane(0, k, 0) for k in planes])
            @pl.when(j == 1)
            def _():
                await_in(*[self.q_plane(2, k, True) for k in planes])
                begin(self.q_core(2))
                begin(*[self.f_plane(0, k, 1) for k in planes])
            @pl.when(j == 2)
            def _():
                await_in(*[self.q_plane(3, k, True) for k in planes])
                begin(self.q_core(3))
                await_in(*[self.f_plane(0, k, 0, True) for k in planes])
                begin(self.f_near(0))
            @pl.when(j == 3)
            def _():
                await_in(*[self.o_plane(k, True) for k in planes])
                begin(self.o_core())
                await_in(*[self.f_plane(0, k, 1, True) for k in planes])
                begin(self.f_near(1), self.f_core(0))
        elif place == "pair_mid":
            @pl.when(j == 0)
            def _():
                await_in(self.q_z(3, True))
                begin(*[self.q_plane(3, k) for k in planes])
                begin(self.f_z(3))
            @pl.when(j == 1)
            def _():
                await_in(*[self.o_z(k, True) for k in range(1, nt)])
                begin(*[self.o_plane(k) for k in planes])
            @pl.when(j == 2)
            def _():
                self.f_on(2)
            @pl.when(j == 3)
            def _():
                self.f_on(3)
        elif place == "mixed":
            await_in(self.o_core(True))
        elif place == "chunk":
            await_in(self.f_core(self.turn(j), True))
        elif place == "chunk_mid":
            @pl.when(j < 2)
            def _():
                self.f_pass(j + 2)
            @pl.when(j == 2)
            def _():
                await_in(self.f_near(0, True), self.f_near(1, True))
                begin(self.f_core(1))
            @pl.when(j >= 1)
            def _():
                x = self.turn(j - 1)
                self.f_after_core(x)
                @pl.when(j >= 2)
                def _():
                    begin(*[self.r2("plane", x, k) for k in planes])
        elif place == "chunk_end":
            begin(self.r2("core", self.turn(j)))
        elif place == "ffn_done":
            self.f_after_core(1)
            begin(self.r2_near())
        elif place == "out_grad":
            begin(self.ro("core"))
        elif place == "back_mid":
            @pl.when(j >= 1)
            def _():
                self.q_after_core(nt - j)
                begin(*[self.rq("plane", nt - j, k) for k in planes])
            @pl.when(j == 0)
            def _():
                await_in(self.ro("core"))
                for p in range(nt):
                    self.DO[p, :, c] = self.DO[p, :, c] + self.CO[p]
                begin(*[self.ro("plane", k) for k in planes])
                self.v_mid("E", self.ne)
            @pl.when(j == 1)
            def _():
                await_in(self.r2_near())
                for u in range(2):
                    def step(i, _):
                        self.D2[t, u, i, c] = self.D2[t, u, i, c] + self.Y2[u, i]
                        return 0
                    for i in range(ng):
                        step(i, 0)
                begin(*[self.r2("plane", 0, k) for k in planes])
                self.f_after_plane(2)
                begin(self.r2("z", 2))
            @pl.when(j == 2)
            def _():
                await_in(*[self.ro("plane", k) for k in planes])
                for p in range(nt):
                    acc = self.DO[p, g, c].astype(f32)
                    for k in planes:
                        acc = acc + self.XO[k, p].astype(f32)
                    self.DO[p, g, c] = acc.astype(bf16)
                begin(*[self.ro("z", k) for k in range(1, nt)])
                self.f_after_plane(3)
                begin(self.r2("z", 3))
            @pl.when(j >= 2)
            def _():
                self.q_after_plane(nt - j + 1)
                begin(self.rq("z", nt - j + 1))
        elif place == "back_end":
            self.rq("core", nt - 1 - j).start()
        elif place == "finish":
            self.q_after_core(0)
            begin(*[self.rq("plane", 0, k) for k in planes])
            for x in range(1, nt):
                if x > 1:
                    self.r2("z", x).wait_recv()
                self.ro("z", x).wait_recv()
            await_in(*[self.r2("plane", 0, k) for k in planes])
            for u, o in enumerate((self.o_up, self.o_down)):
                acc = self.D2[t, u, g, c].astype(f32)
                for k in planes:
                    acc = acc + self.X2[0, k, u].astype(f32)
                for x in range(2, nt):
                    acc = acc + self.Z2[x, u].astype(f32)
                o[...] = acc
            acc = self.DO[t, g, c].astype(f32)
            for x in range(1, nt):
                acc = acc + self.ZO[x].astype(f32)
            self.o_out[...] = acc
        elif place == "finish_z":
            self.q_after_plane(1)
            begin(self.rq("z", 1))
        elif place == "finish_q":
            acc = self.DQ[t, g, c].astype(f32)
            for k in range(1, ng):
                self.rq("plane", 0, k).wait_recv()
                acc = acc + self.XQ[0, k].astype(f32)
            for x in range(1, nt):
                self.rq("z", x).wait_recv()
                acc = acc + self.ZQ[x].astype(f32)
            for k in range(3):
                self.o_qkv[k] = acc[:, 128 * k:128 * k + 128]
        elif place == "leave":
            for k in planes:
                self.o_plane(k).wait_send()
                self.ro("plane", k).wait_send()
                for x in range(nt):
                    self.q_plane(x, k).wait_send()
                    if x != 1:
                        for u in range(2):
                            self.f_plane(x, k, u).wait_send()
                    if x != 1:
                        self.r2("plane", x, k).wait_send()
                    self.rq("plane", x, k).wait_send()
            for k in range(nt):
                self.q_core(k).wait_send()
                self.f_core(k).wait_send()
                self.r2("core", k).wait_send()
                self.rq("core", k).wait_send()
            self.o_core().wait_send()
            self.ro("core").wait_send()
            self.r2_near().wait_send()
            self.f_near(0).wait_send()
            self.f_near(1).wait_send()
            for k in range(1, nt):
                self.q_z(k).wait_send()
                self.o_z(k).wait_send()
                if k > 1:
                    self.f_z(k).wait_send()
                    self.r2("z", k).wait_send()
                self.rq("z", k).wait_send()
                self.ro("z", k).wait_send()

    def v(self, name, stage, k, incoming=False):
        Z, X = getattr(self, name)
        if stage == "z":
            return self.copy(name + "_z", (k,), "z", k, Z.at[self.t], Z.at[self.t ^ k if incoming else self.t])
        return self.copy(name + "_dp", (k,), "dp", k, X.at[self.d], X.at[self.d ^ k if incoming else self.d])

    def v_start(self, name, rows):
        Z = getattr(self, name)[0]
        n = rows[0].shape[1]
        for k, x in enumerate(rows):
            Z[self.t, :, k * n:k * n + n] = x
        for k in range(1, self.nt):
            self.v(name, "z", k).start()

    def v_mid(self, name, m):
        Z, X = getattr(self, name)
        nt, n = self.nt, Z.shape[2] // m
        for k in range(1, nt):
            self.v(name, "z", k, True).wait_recv()
        for k in range(nt):
            X[self.d, :, k * n:k * n + n] = Z[k, :, 0:n]
        s = Z[0, :, n:m * n]
        for k in range(1, nt):
            s = s + Z[k, :, n:m * n]
        X[self.d, :, nt * n:(nt + m - 1) * n] = s
        for k in range(1, 2 * self.ng):
            self.v(name, "dp", k).start()

    def v_done(self, name, m, kept, sums, at):
        Z, X = getattr(self, name)
        nd, nt, n = 2 * self.ng, self.nt, Z.shape[2] // m
        for k in range(1, nd):
            self.v(name, "dp", k, True).wait_recv()
        for k in range(nd):
            for i in range(nt):
                kept[k * nt + i:k * nt + i + 1, :] = X[k, :, i * n:i * n + n]
        s = X[0, :, nt * n:(nt + m - 1) * n]
        for k in range(1, nd):
            s = s + X[k, :, nt * n:(nt + m - 1) * n]
        for i in range(m - 1):
            sums[at + i:at + i + 1, :] = s[:, i * n:i * n + n]

    def v_leave(self, name):
        for k in range(1, self.nt):
            self.v(name, "z", k).wait_send()
        for k in range(1, 2 * self.ng):
            self.v(name, "dp", k).wait_send()


TILE = dict(ln1=256, proj=1024, ln2=512, tile=512, wgrad=512, ln2b=256, gmix=1024, gwo=512, qgrad=512, back=1024, ln1b=256)
UNROLL = {"ln1", "ln1b", "ln2b", "proj", "ln2", "tile", "wgrad", "gmix", "gwo", "qgrad", "back"}


def loop(name, total, body, init):
    n = TILE[name]
    if name in UNROLL or total == n:
        for i in range(total // n):
            init = body(slice(i * n, i * n + n), init)
        return init
    return lax.fori_loop(0, total // n, lambda i, x: body(pl.ds(pl.multiple_of(i * n, n), n), x), init)


def layer(cm, T, most, length, t, tok, cot, seg, wt, btime, g1, b1, g2, b2, bdown, bup, out, gtok, sc):
    tp, n1, qkv, qaug, kaug, mixed, lse, qq, kk, vv, oo, dq, dkv, dqkv, mid, n2, ffn, gn, act, gu, gm, xT, xT3, bsum, stat1, stat2 = sc
    seq, D = tok.shape
    P = qkv.shape[0]
    NF, F = bsum.shape[0], bsum.shape[2]
    n = seq // TR
    cm.hook("greet")
    cm.hook("start")
    cm.hook("row_in")
    half = D // 2
    ang = t * jnp.exp(-math.log(10000.0) * lax.broadcasted_iota(jnp.int32, (8, half), 1).astype(f32) / half)
    emb = jnp.concatenate([jnp.sin(ang), jnp.cos(ang)], axis=1)
    tp[...] = jnp.dot(emb, wt[...], precision=lax.Precision.HIGHEST, preferred_element_type=f32)[0:1, :] + btime[...]

    def ln1(r, _):
        xh = normed_keep(tok[r, :].astype(f32) + tp[...], stat1, r)
        n1[r, :] = (xh * g1[...] + b1[...]).astype(bf16)
        return 0

    loop("ln1", seq, ln1, 0)
    cm.hook("normed")
    srow = seg[pl.ds(T, 1), :].astype(f32)
    for b in range(seq // 128):
        col = jnp.broadcast_to(srow[:, 128 * b:128 * b + 128], (128, 128)).T
        spot = lane((128, 128)) % HS
        pos = lax.broadcasted_iota(jnp.int32, (128, 128), 0) + 128 * b
        same = col == spot.astype(f32)
        r = slice(128 * b, 128 * b + 128)
        qaug[r, :] = jnp.where(same & (spot < 8), 1.0, 0.0).astype(bf16)
        ka = jnp.where(same & (pos < length), 0.0, -BIG)
        kaug[r, :] = jnp.where(spot < 8, ka, jnp.where(spot < 11, -1.0, 0.0)).astype(bf16)

    cm.hook("cot_in")
    transpose_into(xT, cot, seq)
    cm.hook("masked")
    transpose_into(xT3, n1, seq)

    def pair_fwd(j, _):
        hp = cm.order(j)
        cm.hook("pair", j)

        def proj(r, _):
            x = nn_dot(n1[r, :], cm.getq(hp))
            s = jnp.where(lane((1, 384)) < 128, SCALE * LOG2E, 1.0)
            qkv[hp, r, :] = (x * s).astype(bf16)
            return 0

        loop("proj", seq, proj, 0)
        cm.hook("pair_proj", j)
        attend_fwd(seq, most, length, qkv, qaug, kaug, mixed, lse, qq, kk, vv, hp, lambda: cm.hook("pair_half", j))
        cm.hook("pair_mid", j)
        return 0

    lax.fori_loop(0, P, pair_fwd, 0)
    cm.hook("mixed")

    def ln2(r, _):
        mx = jnp.concatenate([mixed[p, r, :] for p in range(P)], axis=1)
        x = tok[r, :].astype(f32) + tp[...] + nt_dot(mx, cm.geto())
        mid[r, :] = x
        xh = normed_keep(x, stat2, r)
        n2[r, :] = (xh * g2[...] + b2[...]).astype(bf16)
        ffn[r, :] = jnp.zeros((TILE["ln2"], D), f32)
        gn[r, :] = jnp.zeros((TILE["ln2"], D), f32)
        return 0

    loop("ln2", seq, ln2, 0)
    cm.hook("second")

    def chunk(j, _):
        f = cm.order_ffn(j)
        cm.hook("chunk", j)

        n = TILE["tile"]
        spans = [slice(i * n, i * n + n) for i in range(seq // n)]

        def lead(r):
            return nn_dot(n2[r, :], cm.getu(f)) + bup[f], nn_dot(cot[r, :], cm.getd(f))

        acc = jnp.zeros((1, F), f32)
        ready = lead(spans[0])
        for i, r in enumerate(spans):
            ahead = lead(spans[i + 1]) if i + 1 < len(spans) else None
            a, ga = gelu_parts(ready[0])
            a = a.astype(bf16)
            g = (ready[1] * ga).astype(bf16)
            act[r, :] = a
            gu[r, :] = g
            ffn[r, :] += nt_dot(a, cm.getd(f))
            gn[r, :] += nt_dot(g, cm.getu(f))
            acc = acc + colsum(g.astype(f32))
            ready = ahead
        bsum[f] = acc
        cm.hook("chunk_mid", j)

        def wgrad(r, _):
            cm.put2(f, 1, r, nn_dot(xT[r, :], act[...]).astype(bf16))
            cm.put2(f, 0, r, tn_dot(n2[:, r], gu[...]).astype(bf16))
            return 0

        loop("wgrad", D, wgrad, 0)
        cm.hook("chunk_end", j)
        return 0

    lax.fori_loop(0, NF, chunk, 0)

    def ln2b(r, acc):
        c = cot[r, :].astype(f32)
        x = mid[r, :]
        out[r, :] = (x + ffn[r, :] + bdown[...]).astype(bf16)
        xh, rr = normed_again(x, stat2, r)
        gy = gn[r, :]
        gyx = gy * xh
        gmid = c + norm_back(gyx, xh, rr, g2[...], gy)
        mid[r, :] = gmid
        n2[r, :] = gmid.astype(bf16)
        gn[r, :] = jnp.zeros((TILE["ln2b"], D), f32)
        return acc[0] + colsum(gyx), acc[1] + colsum(gy), acc[2] + colsum(c)

    z = jnp.zeros((1, D), f32)
    a = loop("ln2b", seq, ln2b, (z, z, z))
    cm.early([emb[0:1, :], *a] + [bsum[f] for f in range(NF)])
    cm.hook("ffn_done")

    def gmix(r, _):
        x = nn_dot(n2[r, :], cm.geto()).astype(bf16)
        for p in range(P):
            gm[p, r, :] = x[:, 128 * p:128 * p + 128]
        return 0

    loop("gmix", seq, gmix, 0)

    def gwo(r, _):
        m = jnp.concatenate([mixed[p] for p in range(P)], axis=1)
        x = tn_dot(n2[:, r], m).astype(bf16)
        for p in range(P):
            cm.puto(p, r, x[:, 128 * p:128 * p + 128])
        return 0

    loop("gwo", D, gwo, 0)
    cm.hook("out_grad")
    def pair_bwd(j, _):
        hp = cm.order_back(j)
        attend_bwd(seq, most, length, qkv, qaug, kaug, mixed, lse, gm, qq, kk, vv, oo, dq, dkv, dqkv, hp)
        cm.hook("back_mid", j)

        def wgrad(r, _):
            cm.putq(hp, r, nn_dot(xT3[r, :], dqkv[...]).astype(bf16))
            return 0

        loop("qgrad", D, wgrad, 0)
        cm.hook("back_end", j)

        def back(r, _):
            gn[r, :] += nt_dot(dqkv[r, :], cm.getq(hp))
            return 0

        loop("back", seq, back, 0)
        return 0

    lax.fori_loop(0, P, pair_bwd, 0)

    def ln1b(r, acc):
        xh, rr = normed_again(tok[r, :].astype(f32) + tp[...], stat1, r)
        gy = gn[r, :]
        gyx = gy * xh
        gt = mid[r, :] + norm_back(gyx, xh, rr, g1[...], gy)
        gtok[r, :] = gt
        return acc[0] + colsum(gt), acc[1] + colsum(gyx), acc[2] + colsum(gy)

    a = loop("ln1b", seq, ln1b, (z, z, z))
    cm.late(list(a))


def layer_scratch(seq, D, P, NF, F):
    V = pltpu.VMEM
    return [V((1, D), f32), V((seq, D), bf16), V((P, seq, 384), bf16), V((seq, 128), bf16), V((seq, 128), bf16),
        V((P, seq, 128), bf16), V((P, seq, 128), f32)] + [V((2, seq, 128), bf16)] * 4 + [V((2, seq, 128), f32),
        V((3, 2, seq, 128), f32), V((seq, 384), bf16), V((seq, D), f32), V((seq, D), bf16), V((seq, D), f32), V((seq, D), f32),
        V((seq, F), bf16), V((seq, F), bf16), V((P, seq, 128), bf16), V((D, seq), bf16), V((D, seq), bf16), V((NF, 1, F), f32), V((2, seq, 128), f32), V((2, seq, 128), f32)]


def plain_kernel(most, n_sc, *refs):
    len_ref, ts_ref, tok, cot, seg, wq, wo, w2, wt, btime, g1, b1, g2, b2, bdown, bup, out, gtok, dwq, dwo, dw2, vec = refs[:22]
    T = lax.axis_index("tensor")
    cm = Plain(wq, wo, w2, dwq, dwo, dw2, vec)
    layer(cm, T, most, len_ref[T], ts_ref[0].astype(f32), tok, cot, seg, wt, btime, g1, b1, g2, b2, bdown, bup, out, gtok, refs[22:])


def run_plain(most, length, ts, tok, cot, seg, wq, wo, w2, wt, vecs, bup):
    seq, D = tok.shape
    P, NF, F = wq.shape[0], w2.shape[0], w2.shape[-1]
    S = jax.ShapeDtypeStruct
    vm = pl.BlockSpec(memory_space=pltpu.VMEM)
    sm = pl.BlockSpec(memory_space=pltpu.SMEM)
    return pl.pallas_call(
        functools.partial(plain_kernel, most, 0),
        out_shape=(S((seq, D), bf16), S((seq, D), f32), S(wq.shape, bf16), S(wo.shape, bf16), S(w2.shape, bf16), S((16, D), f32)),
        in_specs=[sm, sm] + [vm] * 14, out_specs=[vm] * 6,
        scratch_shapes=layer_scratch(seq, D, P, NF, F),
        compiler_params=pltpu.CompilerParams(vmem_limit_bytes=60 << 20),
    )(length, ts, tok, cot, seg, wq, wo, w2, wt, *[v[None] for v in vecs], bup)


def linked_kernel(most, ng, nt, names, semnames, n_layer, *refs):
    len_ref, ts_ref = refs[:2]
    held = refs[2:17]
    out, gtok, o_qkv, o_out, o_up, o_down, embs, grads, vec = refs[17:26]
    sc = refs[26:26 + n_layer]
    rest = refs[26 + n_layer:]
    bufs = dict(zip(names, rest[:len(names)]))
    sr = rest[len(names):]
    sems = {nm: (sr[2 * i], sr[2 * i + 1]) for i, nm in enumerate(semnames)}
    local = sr[-1]
    here = [bufs.pop("in%d" % i) for i in range(15)]
    tok, cot, seg, w_qkv, w_out, w_up, w_down, wt, btime, g1, b1, g2, b2, bdown, bup = here
    bufs.update(w_qkv=w_qkv, w_out=w_out, w_up=w_up, w_down=w_down, o_qkv=o_qkv, o_out=o_out, o_up=o_up, o_down=o_down)
    bufs["E"] = bufs.pop("EZ"), bufs.pop("EX")
    bufs["L"] = bufs.pop("LZ"), bufs.pop("LX")
    cm = Linked(ng, nt, bufs, sems)
    T = cm.t
    cm.ne = 4 + bup.shape[0]
    cm.early = lambda rows: cm.v_start("E", rows)
    cm.late = lambda rows: cm.v_start("L", rows)
    moves = [pltpu.make_async_copy(a, b, local.at[i]) for i, (a, b) in enumerate(zip(held, here))]
    plain_hook = cm.hook

    def hook(place, j=None):
        if place == "greet":
            plain_hook(place)
            for i in (3, 4, 5, 6, 0, 7, 2, *range(8, 15), 1):
                moves[i].start()
            for i in range(3, 7):
                moves[i].wait()
        elif place == "row_in":
            for i in (0, 7, 2, *range(8, 15)):
                moves[i].wait()
        elif place == "cot_in":
            moves[1].wait()
        else:
            plain_hook(place, j)

    cm.hook = hook
    layer(cm, T, most, len_ref[T], ts_ref[0].astype(f32), tok, cot, seg, wt, btime, g1, b1, g2, b2, bdown, bup, out, gtok, sc)
    cm.hook("finish")
    cm.v_mid("L", 3)
    cm.hook("finish_z")
    cm.v_done("E", cm.ne, embs, vec, 4)
    cm.hook("finish_q")
    cm.v_done("L", 3, grads, vec, 2)
    cm.hook("leave")
    cm.v_leave("E")
    cm.v_leave("L")


def run_linked(most, nd, nt, length, ts, tok, cot, seg, w_qkv, w_out, w_up, w_down, wt, vecs, bup):
    seq, D = tok.shape
    ng = nd // 2
    r, F = w_up.shape
    P, NF, ne = nt, nt, 4 + nt
    S, V = jax.ShapeDtypeStruct, pltpu.VMEM
    DMA = pltpu.SemaphoreType.DMA
    bufs = dict(
        WQ=V((nt, ng, 2, r, 384), bf16), WO=V((nt, ng, 2, r, 128), bf16), W2=V((nt, 2, ng, 2, r, F), bf16),
        DQ=V((nt, ng, 2, r, 384), bf16), DO=V((nt, ng, 2, r, 128), bf16), D2=V((nt, 2, ng, 2, r, F), bf16),
        CQ=V((nt, ng, r, 384), bf16), XQ=V((nt, ng, r, 384), bf16), ZQ=V((nt, r, 384), bf16),
        CO=V((nt, ng, r, 128), bf16), XO=V((ng, nt, r, 128), bf16), ZO=V((nt, r, 128), bf16),
        C2=V((nt, 2, ng, r, F), bf16), X2=V((nt, ng, 2, r, F), bf16), Z2=V((nt, 2, r, F), bf16), Y2=V((2, ng, r, F), bf16),
        EZ=V((nt, 1, ne * D), f32), EX=V((nd, 1, (nt + ne - 1) * D), f32), LZ=V((nt, 1, 3 * D), f32), LX=V((nd, 1, (nt + 2) * D), f32),
    )
    held = (tok, cot, seg, w_qkv, w_out, w_up, w_down, wt, *[v[None] for v in vecs], bup)
    for i, x in enumerate(held):
        bufs["in%d" % i] = V(x.shape, x.dtype)
    sems = dict(gq_plane=(nt, ng), gq_z=(nt,), gq_core=(nt,), go_z=(nt,), g2_z=(nt,), go_plane=(ng,), go_core=(), g2_plane=(nt, 2, ng), g2_core=(nt,), g2_near=(2,),
        rq_core=(nt,), rq_plane=(nt, ng), rq_z=(nt,), r2_core=(nt,), r2_plane=(nt, ng), r2_z=(nt,), r2_near=(), ro_core=(), ro_plane=(ng,), ro_z=(nt,),
        E_z=(nt,), E_dp=(nd,), L_z=(nt,), L_dp=(nd,))
    ls = layer_scratch(seq, D, P, NF, F)
    scratch = ls + list(bufs.values())
    for s in sems.values():
        scratch += [DMA(s), DMA(s)]
    scratch.append(DMA((15,)))
    vm = pl.BlockSpec(memory_space=pltpu.VMEM)
    sm = pl.BlockSpec(memory_space=pltpu.SMEM)
    hb = pl.BlockSpec(memory_space=pltpu.HBM)
    an = pl.BlockSpec(memory_space=pl.ANY)
    return pl.pallas_call(
        functools.partial(linked_kernel, most, ng, nt, tuple(bufs), tuple(sems), len(ls)),
        out_shape=(V((seq, D), bf16), V((seq, D), f32), V(w_qkv.shape, f32), V(w_out.shape, f32), V(w_up.shape, f32), V(w_down.shape, f32),
            V((nd * nt, D), f32), V((nd * nt, D), f32), V((16, D), f32)),
        in_specs=[sm, sm] + [hb] * 15, out_specs=[vm] * 9,
        scratch_shapes=scratch,
        compiler_params=pltpu.CompilerParams(vmem_limit_bytes=56 << 20, collective_id=0, has_side_effects=True),
    )(length, ts, *held)


def emit_kernel(nb, *refs):
    big, outs, gwt, small, sem = refs[:9], refs[9:15], refs[15], refs[16:23], refs[23]
    ups = [pltpu.make_async_copy(a, b, sem.at[i]) for i, (a, b) in enumerate(zip(big[3:], outs))]
    for x in ups:
        x.start()
    embs, grads, vec = (b[...] for b in big[:3])
    gwt[...] = lax.dot_general(embs, grads, (((0,), (0,)), ((), ())), precision=lax.Precision.HIGHEST, preferred_element_type=f32)
    small[0][...] = jnp.sum(grads, axis=0)
    for k, o in enumerate(small[1:-1]):
        o[...] = vec[2 + k, :]
    n = vec.shape[1]
    for k in range(nb):
        small[-1][pl.ds(k * n, n)] = vec[7 + k, :]
    for y in ups:
        y.wait()


def emit(nb, *big):
    S = jax.ShapeDtypeStruct
    D = big[2].shape[1]
    vm = pl.BlockSpec(memory_space=pltpu.VMEM)
    an = pl.BlockSpec(memory_space=pl.ANY)
    hb = pl.BlockSpec(memory_space=pltpu.HBM)
    return pl.pallas_call(
        functools.partial(emit_kernel, nb),
        out_shape=tuple(S(x.shape, x.dtype) for x in big[3:]) + (S((D, D), f32),) + tuple(S((D,), f32) for _ in range(6)) + (S((nb * D,), f32),),
        in_specs=[vm] * 3 + [an] * 6, out_specs=[hb] * 6 + [vm] * 8,
        scratch_shapes=[pltpu.SemaphoreType.DMA((6,))],
        compiler_params=pltpu.CompilerParams(vmem_limit_bytes=16 << 20),
    )(*big)


def shards(
    tokens,
    timestep,
    segment_ids,
    span_lengths,
    w_qkv,
    w_out_t,
    w_up,
    w_down_t,
    w_time,
    b_time,
    ln1_gain,
    ln1_bias,
    ln2_gain,
    ln2_bias,
    b_up,
    b_down,
    cotangent,
):
    seq, D = tokens.shape[1:]
    nd, nt = lax.axis_size("dp"), lax.axis_size("tensor")
    vecs = (b_time, ln1_gain, ln1_bias, ln2_gain, ln2_bias, b_down)
    F = w_up.shape[1]
    bup = b_up.reshape(nt, 1, F)
    if w_up.shape[0] % 16 == 0 and (nd, nt) == (8, 4):
        out, gtok, *g, embs, lines, vec = run_linked(
            DOC, nd, nt, span_lengths, timestep, tokens[0], cotangent[0], segment_ids,
            w_qkv, w_out_t, w_up, w_down_t, w_time, vecs, bup)
        gq, go, gu, gd, out, gtok, gwt, *v = emit(nt, embs, lines, vec, *g, out, gtok)
        return (out[None], gtok[None], gq, go, gu, gd, gwt, v[0], v[1], v[2], v[3], v[4], v[6], v[5])
    HB = w_qkv.shape[2]

    def whole(w):
        return lax.all_gather(lax.all_gather(w.astype(bf16), "dp", axis=w.ndim - 2, tiled=True), "tensor", axis=0)

    def part(g, dim):
        g = lax.psum_scatter(g, "dp", scatter_dimension=dim, tiled=True)
        return lax.psum_scatter(g, "tensor", scatter_dimension=0, tiled=True)[0].astype(f32)

    wq = whole(jnp.transpose(w_qkv, (1, 0, 2)).reshape(w_qkv.shape[1], 3 * HB))
    out, gtok, dwq, dwo, dw2, vec = run_plain(
        DOC, span_lengths, timestep, tokens[0], cotangent[0], segment_ids,
        wq, whole(w_out_t), whole(jnp.stack([w_up, w_down_t])), w_time, vecs, bup)
    lines = lax.all_gather(jnp.stack([vec[0], vec[8]]), ("dp", "tensor"), axis=1, tiled=False)
    gwt = jnp.dot(lines[0].T, lines[1], precision=lax.Precision.HIGHEST)
    small = lax.psum(vec, ("dp", "tensor"))
    gq, g2 = part(dwq, 1), part(dw2, 2)
    return (
        out[None], gtok[None], jnp.transpose(gq.reshape(gq.shape[0], 3, HB), (1, 0, 2)), part(dwo, 1), g2[0], g2[1],
        gwt, small[8], small[9], small[10], small[1], small[2], small[4:4 + nt].reshape(-1), small[3])


def solution(mesh):
    return jax.shard_map(
        shards,
        mesh=mesh,
        in_specs=(
            P_(("dp", "tensor"), None, None),
            P_(("dp", "tensor")),
            P_("dp", None),
            P_("dp"),
            P_(None, "dp", "tensor"),
            P_("dp", "tensor"),
            P_("dp", "tensor"),
            P_("dp", "tensor"),
            P_(),
            P_(),
            P_(),
            P_(),
            P_(),
            P_(),
            P_(),
            P_(),
            P_(("dp", "tensor"), None, None),
        ),
        out_specs=(
            P_(("dp", "tensor"), None, None),
            P_(("dp", "tensor"), None, None),
            P_(None, "dp", "tensor"),
            P_("dp", "tensor"),
            P_("dp", "tensor"),
            P_("dp", "tensor"),
            P_(),
            P_(),
            P_(),
            P_(),
            P_(),
            P_(),
            P_(),
            P_(),
        ),
        check_vma=False,
    )
```

```python
import functools
import math

import jax
import jax.numpy as jnp
from jax import lax
from jax.experimental import pallas as pl
from jax.experimental.pallas import tpu as pltpu
from jax.sharding import PartitionSpec as P_

f32, bf16 = jnp.float32, jnp.bfloat16
HS = 64
TR = 256
TB = 128
BIG = 1e30
EPS = 1e-5
DOC = 512
LEAST = 512
LOG2E = math.log2(math.e)
LN2 = math.log(2.0)
SCALE = 1.0 / math.sqrt(HS)


def nt_dot(a, b):
    return lax.dot_general(a, b, (((1,), (1,)), ((), ())), preferred_element_type=f32)


def tn_dot(a, b):
    return lax.dot_general(a, b, (((0,), (0,)), ((), ())), preferred_element_type=f32)


def nn_dot(a, b):
    return jnp.dot(a, b, preferred_element_type=f32)


def lane(shape):
    return lax.broadcasted_iota(jnp.int32, shape, len(shape) - 1)


def rows_of(i, n=TR):
    return pl.ds(pl.multiple_of(i * n, n), n)


def normed_keep(x, stats, r):
    mean = jnp.mean(x, axis=-1, keepdims=True)
    c = x - mean
    var = jnp.mean(c * c, axis=-1, keepdims=True)
    f = lax.rsqrt(var + EPS)
    stats[0, r, :] = jnp.broadcast_to(mean, (x.shape[0], 128))
    stats[1, r, :] = jnp.broadcast_to(f, (x.shape[0], 128))
    return c * f


def normed_again(x, stats, r):
    n = x.shape[1] // 128
    f = jnp.concatenate([stats[1, r, :]] * n, axis=1)
    return (x - jnp.concatenate([stats[0, r, :]] * n, axis=1)) * f, f


def norm_back(gyx, xhat, r, gain, gy):
    gh = gy * gain
    a = jnp.mean(gh, axis=-1, keepdims=True)
    b = jnp.mean(gyx * gain, axis=-1, keepdims=True)
    return r * (gh - a - xhat * b)


def colsum(x):
    return jnp.sum(x, axis=0, keepdims=True)


def halves(prod):
    low = lane(prod.shape) < HS
    s0 = jnp.sum(jnp.where(low, prod, 0.0), axis=-1, keepdims=True)
    s1 = jnp.sum(jnp.where(low, 0.0, prod), axis=-1, keepdims=True)
    return s0, s1


def split3(x):
    hi = x.astype(bf16)
    rest = x - hi.astype(f32)
    mid = rest.astype(bf16)
    lo = (rest - mid.astype(f32)).astype(bf16)
    return hi, mid, lo


def window(i, seq, most, tr):
    lo = max(0, (i * tr - most + 1) // 128 * 128)
    hi = min(seq, -(-(i * tr + tr - 1 + most) // 128) * 128)
    return lo, hi


def gelu_parts(u):
    c0, c1 = 0.7978845608028654, 0.044715
    u2 = u * u
    th = jnp.tanh(u * (c0 + (c0 * c1) * u2))
    half = 0.5 + 0.5 * th
    act = u * half
    grad = half + (0.5 * u) * (1.0 - th * th) * (c0 + (3.0 * c0 * c1) * u2)
    return act, grad


def transpose_into(dst, src, seq):
    def step(i, _):
        r = rows_of(i)
        dst[:, r] = src[r, :].T
        return 0
    for i in range(seq // TR):
        r = slice(i * TR, i * TR + TR)
        dst[:, r] = src[r, :].T


def half_sums(prod, swap=False):
    hi = prod.astype(bf16)
    lo = (prod - hi.astype(f32)).astype(bf16)
    a = lax.broadcasted_iota(jnp.int32, (256, 128), 0) // HS % 2
    b = lax.broadcasted_iota(jnp.int32, (256, 128), 1) // HS
    w = jnp.where((a != b) if swap else (a == b), 1.0, 0.0).astype(bf16)
    return nn_dot(jnp.concatenate([hi, lo], axis=1), w)


def attend_fwd(seq, most, length, qkv, qaug, kaug, mixed, lse, qq, kk, vv, hp, half):
    n = seq // TR
    def prep(i, _):
        r = rows_of(i)
        low = lane((TR, 128)) < HS
        q, k, v = (qkv[hp, r, 128 * c:128 * c + 128] for c in range(3))
        qa, ka = qaug[r, :], kaug[r, :]
        one = jnp.ones_like(v)
        qq[0, r, :] = jnp.where(low, q, qa)
        qq[1, r, :] = jnp.where(low, qa, q)
        kk[0, r, :] = jnp.where(low, k, ka)
        kk[1, r, :] = jnp.where(low, ka, k)
        vv[0, r, :] = jnp.where(low, v, one)
        vv[1, r, :] = jnp.where(low, one, v)
        return 0
    for i in range(n):
        prep(i, 0)

    def score(i, h):
        lo, hi = window(i, seq, most, TR)
        return nt_dot(qq[h, i * TR:i * TR + TR, :], kk[h, lo:hi, :])

    def soft(i, s, own):
        m = jnp.max(s, axis=-1, keepdims=True)
        if own is not None:
            pad = (lax.broadcasted_iota(jnp.int32, (TR, 1), 0) + i * TR) >= length
            m = jnp.where(pad, jnp.maximum(m, own), m)
        return m, jnp.exp2(s - m).astype(bf16)

    def finish(i, own, tops, outs):
        r = slice(i * TR, i * TR + TR)
        low = lane((TR, 128)) < HS
        num = jnp.where(low, outs[0], outs[1])
        den_x = jnp.where(low, outs[1], outs[0])
        if own[0] is not None:
            padf = ((lax.broadcasted_iota(jnp.int32, (TR, 1), 0) + i * TR) >= length).astype(f32)
            e0 = jnp.exp2(jnp.minimum(own[0] - tops[0], 0.0)).astype(bf16).astype(f32) * padf
            e1 = jnp.exp2(jnp.minimum(own[1] - tops[1], 0.0)).astype(bf16).astype(f32) * padf
            num = num + jnp.where(low, e0, e1) * qkv[hp, r, 256:384].astype(f32)
            den_x = den_x + jnp.where(low, e1, e0)
        mixed[hp, r, :] = (num / pltpu.roll(den_x, HS, 1)).astype(bf16)
        lse[hp, r, :] = jnp.where(low, tops[1], tops[0]) + jnp.log2(den_x)

    def selfs(i):
        if (i + 1) * TR <= LEAST:
            return (None, None)
        r = slice(i * TR, i * TR + TR)
        return halves(qkv[hp, r, 0:128].astype(f32) * qkv[hp, r, 128:256].astype(f32))

    units = [(i, h) for i in range(n) for h in range(2)]
    s = score(*units[0])
    tops, outs = [], []
    for u, (i, h) in enumerate(units):
        if (i, h) == (n // 2, 0):
            half()
        nxt = score(*units[u + 1]) if u + 1 < len(units) else None
        if h == 0:
            own = selfs(i)
        lo, hi = window(i, seq, most, TR)
        m, p = soft(i, s, own[h])
        tops.append(m)
        outs.append(nn_dot(p, vv[h, lo:hi, :]))
        if h == 1:
            finish(i, own, tops, outs)
            tops, outs = [], []
        s = nxt


def attend_bwd(seq, most, length, qkv, qaug, kaug, mixed, lse, gm, qq, kk, vv, oo, dq, dkv, dqkv, hp):
    n = seq // TB
    def prep(i, _):
        r = slice(i * TB, i * TB + TB)
        low = lane((TB, 128)) < HS
        spot = lane((TB, 128)) % HS
        q, k, v = (qkv[hp, r, 128 * c:128 * c + 128] for c in range(3))
        g = gm[hp, r, :]
        dx = half_sums(g.astype(f32) * mixed[hp, r, :].astype(f32), True)
        def put(base, x):
            hi, mid, lo = split3(x)
            z = jnp.where(spot == 8, hi, base)
            z = jnp.where(spot == 9, mid, z)
            return jnp.where(spot == 10, lo, z)
        zero = jnp.zeros((TB, 128), bf16)
        qa = put(qaug[r, :], lse[hp, r, :])
        oa = put(zero, dx)
        ka = kaug[r, :]
        va = jnp.where((spot >= 8) & (spot < 11), -jnp.ones_like(zero), zero)
        for ref, x, a in ((qq, q, qa), (kk, k, ka), (vv, v, va), (oo, g, oa)):
            ref[0, r, :] = jnp.where(low, x, a)
            ref[1, r, :] = jnp.where(low, a, x)
        if (i + 1) * TB > LEAST:
            q, k, v, g = (x.astype(f32) for x in (q, k, v, g))
            padf = ((lax.broadcasted_iota(jnp.int32, (TB, 1), 0) + i * TB) >= length).astype(f32)
            ls = pltpu.roll(lse[hp, r, :], HS, 1)
            d = pltpu.roll(dx, HS, 1)
            pf = jnp.exp2(jnp.minimum(half_sums(q * k) - ls, 1.0)) * padf
            ds = (pf * (half_sums(g * v) - d)).astype(bf16).astype(f32)
            pf = pf.astype(bf16).astype(f32)
            dkv[2, 0, r, :] = ds
            dkv[2, 1, r, :] = pf
        return 0
    for i in range(n):
        prep(i, 0)
    hi = window(0, seq, most, TB)[1]
    if hi < seq:
        dq[:, hi:seq, :] = jnp.zeros((2, seq - hi, 128), f32)

    def score(i, h):
        lo, hi = window(i, seq, most, TB)
        r = slice(i * TB, i * TB + TB)
        return nt_dot(kk[h, r, :], qq[h, lo:hi, :]), nt_dot(vv[h, r, :], oo[h, lo:hi, :])

    def rest(i, h, st, dpt):
        lo, hi = window(i, seq, most, TB)
        r = slice(i * TB, i * TB + TB)
        pt = jnp.exp2(st)
        dst = (pt * dpt).astype(bf16)
        dkv[h, 0, r, :] = nn_dot(dst, qq[h, lo:hi, :])
        dkv[h, 1, r, :] = nn_dot(pt.astype(bf16), oo[h, lo:hi, :])
        x = tn_dot(dst, kk[h, r, :])
        if i == 0:
            dq[h, lo:hi, :] = x
        else:
            dq[h, lo:hi, :] += x

    units = [(i, h) for i in range(n) for h in range(2)]
    s = score(*units[0])
    for u, (i, h) in enumerate(units):
        nxt = score(*units[u + 1]) if u + 1 < len(units) else None
        rest(i, h, *s)
        s = nxt

    for i in range(n):
        r = slice(i * TB, i * TB + TB)
        low = lane((TB, 128)) < HS
        gq = jnp.where(low, dq[0, r, :], dq[1, r, :])
        gk = jnp.where(low, dkv[0, 0, r, :], dkv[1, 0, r, :])
        gv = jnp.where(low, dkv[0, 1, r, :], dkv[1, 1, r, :])
        if (i + 1) * TB > LEAST:
            ds, pf = dkv[2, 0, r, :], dkv[2, 1, r, :]
            gq = gq + ds * qkv[hp, r, 128:256].astype(f32)
            gk = gk + ds * qkv[hp, r, 0:128].astype(f32)
            gv = gv + pf * gm[hp, r, :].astype(f32)
        dqkv[r, 0:128] = (gq * SCALE).astype(bf16)
        dqkv[r, 128:256] = (gk * LN2).astype(bf16)
        dqkv[r, 256:384] = gv.astype(bf16)


MESH = pl.DeviceIdType.MESH


class Plain:
    def __init__(self, wq, wo, w2, dwq, dwo, dw2, vec):
        self.wq, self.wo, self.w2 = wq, wo, w2
        self.dwq, self.dwo, self.dw2, self.vec = dwq, dwo, dw2, vec

    def getq(self, p):
        return self.wq[p]

    def geto(self):
        return jnp.concatenate([self.wo[p] for p in range(self.wo.shape[0])], axis=1)

    def getu(self, f):
        return self.w2[f, 0]

    def getd(self, f):
        return self.w2[f, 1]

    def putq(self, p, i, x):
        self.dwq[p, i, :] = x

    def puto(self, p, i, x):
        self.dwo[p, i, :] = x

    def put2(self, f, k, i, x):
        self.dw2[f, k, i, :] = x

    def order(self, j):
        return j

    def order_back(self, j):
        return j

    def order_ffn(self, j):
        return j

    def hook(self, *_):
        pass

    def early(self, rows):
        for k, x in enumerate(rows):
            self.vec[k:k + 1, :] = x

    def late(self, rows):
        for k, x in enumerate(rows):
            self.vec[8 + k:9 + k, :] = x


class Linked:
    def __init__(self, ng, nt, bufs, sems):
        self.ng, self.nt = ng, nt
        self.__dict__.update(bufs)
        self.sem = sems
        d, self.t = lax.axis_index("dp"), lax.axis_index("tensor")
        self.d, self.g, self.c = d, d // 2, d % 2
        self.sent = []

    def dev(self, kind, k):
        if kind == "core":
            return (2 * self.g + 1 - self.c, self.t)
        if kind == "plane":
            return (2 * (self.g ^ k) + self.c, self.t)
        if kind == "dp":
            return (self.d ^ k, self.t)
        return (self.d, self.t ^ k)

    def copy(self, name, at, kind, k, src, dst):
        s, r = self.sem[name]
        for i in at:
            s, r = s.at[i], r.at[i]
        return pltpu.make_async_remote_copy(
            src_ref=src, dst_ref=dst, send_sem=s, recv_sem=r,
            device_id=self.dev(kind, k), device_id_type=MESH)

    def getq(self, p):
        x = self.WQ[p]
        return x.reshape(-1, x.shape[-1])

    def geto(self):
        return jnp.concatenate([self.WO[p].reshape(-1, 128) for p in range(self.nt)], axis=1)

    def getu(self, f):
        x = self.W2[f, 0]
        return x.reshape(-1, x.shape[-1])

    def getd(self, f):
        x = self.W2[f, 1]
        return x.reshape(-1, x.shape[-1])

    def blocks(self, ref, i):
        rows = ref.shape[-2]
        m = (i.stop - i.start) // (2 * rows)
        return slice(i.start // (2 * rows), i.stop // (2 * rows)), (m, 2, rows, ref.shape[-1])

    def putq(self, p, i, x):
        b, shape = self.blocks(self.DQ, i)
        self.DQ[p, b] = x.reshape(shape)

    def puto(self, p, i, x):
        b, shape = self.blocks(self.DO, i)
        self.DO[p, b] = x.reshape(shape)

    def put2(self, f, k, i, x):
        b, shape = self.blocks(self.D2, i)
        self.D2[f, k, b] = x.reshape(shape)

    def order(self, j):
        return self.t ^ j

    def order_back(self, j):
        return self.t ^ (self.nt - 1 - j)

    def turn(self, j):
        return (2 * j) ^ (7 * (j // 2))

    def order_ffn(self, j):
        return self.t ^ self.turn(j)

    def peers(self):
        return [("dp", k) for k in range(1, 2 * self.ng)] + [("z", k) for k in range(1, self.nt)]

    def greet(self):
        bar = pltpu.get_barrier_semaphore()
        for kind, k in self.peers():
            pl.semaphore_signal(bar, inc=1, device_id=self.dev(kind, k), device_id_type=MESH)

    def enter(self):
        pl.semaphore_wait(pltpu.get_barrier_semaphore(), len(self.peers()))

    def q_plane(self, x, k, incoming=False):
        g, c, p = self.g, self.c, self.t ^ x
        return self.copy("gq_plane", (x, k), "plane", k, self.WQ.at[p, g, c], self.WQ.at[p, g ^ k if incoming else g, c])

    def q_z(self, k, incoming=False):
        g, c, t = self.g, self.c, self.t
        return self.copy("gq_z", (k,), "z", k, self.WQ.at[t, g, c], self.WQ.at[t ^ k if incoming else t, g, c])

    def q_core(self, k):
        c, t = self.c, self.t
        return self.copy("gq_core", (k,), "core", 0, self.WQ.at[t ^ k, :, c], self.WQ.at[t ^ k, :, c])

    def q_core_in(self, k):
        c, t = self.c, self.t
        return self.copy("gq_core", (k,), "core", 0, self.WQ.at[t ^ k, :, c], self.WQ.at[t ^ k, :, 1 - c])

    def o_z(self, k, incoming=False):
        g, c, t = self.g, self.c, self.t
        return self.copy("go_z", (k,), "z", k, self.WO.at[t, g, c], self.WO.at[t ^ k if incoming else t, g, c])

    def f_z(self, k, incoming=False):
        g, c, t = self.g, self.c, self.t
        return self.copy("g2_z", (k,), "z", k, self.W2.at[t, :, g, c], self.W2.at[t ^ k if incoming else t, :, g, c])

    def o_plane(self, k, incoming=False):
        g, c = self.g, self.c
        return self.copy("go_plane", (k,), "plane", k, self.WO.at[:, g, c], self.WO.at[:, g ^ k if incoming else g, c])

    def o_core(self, incoming=False):
        c = self.c
        return self.copy("go_core", (), "core", 0, self.WO.at[:, :, c], self.WO.at[:, :, 1 - c if incoming else c])

    def f_plane(self, j, k, u, incoming=False):
        g, c, f = self.g, self.c, self.t ^ j
        return self.copy("g2_plane", (j, u, k), "plane", k, self.W2.at[f, u, g, c], self.W2.at[f, u, g ^ k if incoming else g, c])

    def f_near(self, u, incoming=False):
        c, t = self.c, self.t
        return self.copy("g2_near", (u,), "z", 1, self.W2.at[t, u, :, c], self.W2.at[t ^ 1 if incoming else t, u, :, c])

    def f_on(self, x):
        self.f_z(x, True).wait_recv()
        for u in range(2):
            for k in range(1, self.ng):
                self.f_plane(x, k, u).start()

    def f_pass(self, x):
        for u in range(2):
            for k in range(1, self.ng):
                self.f_plane(x, k, u, True).wait_recv()
        self.f_core(x).start()

    def f_core(self, j, incoming=False):
        c, f = self.c, self.t ^ j
        return self.copy("g2_core", (j,), "core", 0, self.W2.at[f, :, :, c], self.W2.at[f, :, :, 1 - c if incoming else c])

    def rq(self, stage, x, k=0, incoming=False):
        g, c, p = self.g, self.c, self.t ^ x
        if stage == "core":
            return self.copy("rq_core", (x,), "core", 0, self.DQ.at[p, :, 1 - c], self.CQ.at[x])
        if stage == "plane":
            return self.copy("rq_plane", (x, k), "plane", k, self.DQ.at[p, g ^ k, c], self.XQ.at[x, k])
        return self.copy("rq_z", (x,), "z", x, self.DQ.at[p, g, c], self.ZQ.at[x])

    def r2(self, stage, x, k=0):
        g, c, p = self.g, self.c, self.t ^ x
        if stage == "core":
            return self.copy("r2_core", (x,), "core", 0, self.D2.at[p, :, :, 1 - c], self.C2.at[x])
        if stage == "plane":
            return self.copy("r2_plane", (x, k), "plane", k, self.D2.at[p, :, g ^ k, c], self.X2.at[x, k])
        return self.copy("r2_z", (x,), "z", x, self.D2.at[p, :, g, c], self.Z2.at[x])

    def r2_near(self):
        c, t = self.c, self.t
        return self.copy("r2_near", (), "z", 1, self.D2.at[t ^ 1, :, :, c], self.Y2)

    def ro(self, stage, k=0):
        g, c, t = self.g, self.c, self.t
        if stage == "core":
            return self.copy("ro_core", (), "core", 0, self.DO.at[:, :, 1 - c], self.CO)
        if stage == "plane":
            return self.copy("ro_plane", (k,), "plane", k, self.DO.at[:, g ^ k, c], self.XO.at[k])
        return self.copy("ro_z", (k,), "z", k, self.DO.at[t ^ k, g, c], self.ZO.at[k])

    def q_after_core(self, x):
        p, c = self.t ^ x, self.c
        self.rq("core", x).wait_recv()
        self.DQ[p, :, c] = self.DQ[p, :, c] + self.CQ[x]

    def q_after_plane(self, x):
        p, c, g = self.t ^ x, self.c, self.g
        acc = self.DQ[p, g, c].astype(f32)
        for k in range(1, self.ng):
            self.rq("plane", x, k).wait_recv()
            acc = acc + self.XQ[x, k].astype(f32)
        self.DQ[p, g, c] = acc.astype(bf16)

    def f_after_core(self, x):
        p, c = self.t ^ x, self.c
        self.r2("core", x).wait_recv()
        for u in range(2):
            def step(i, _):
                self.D2[p, u, i, c] = self.D2[p, u, i, c] + self.C2[x, u, i]
                return 0
            for i in range(self.ng):
                step(i, 0)

    def f_after_plane(self, x):
        p, c, g = self.t ^ x, self.c, self.g
        for k in range(1, self.ng):
            self.r2("plane", x, k).wait_recv()
        for u in range(2):
            acc = self.D2[p, u, g, c].astype(f32)
            for k in range(1, self.ng):
                acc = acc + self.X2[x, k, u].astype(f32)
            self.D2[p, u, g, c] = acc.astype(bf16)

    def hook(self, place, j=None):
        ng, nt, t, g, c = self.ng, self.nt, self.t, self.g, self.c
        planes = range(1, ng)

        def begin(*copies):
            for x in copies:
                x.start()

        def await_in(*copies):
            for x in copies:
                x.wait_recv()

        if place == "greet":
            self.greet()
        elif place == "start":
            for k in range(3):
                self.WQ[t, g, c, :, 128 * k:128 * k + 128] = self.w_qkv[k].astype(bf16)
            self.enter()
            begin(*[self.q_plane(0, k) for k in planes], self.q_z(1))
        elif place == "shards":
            self.WO[t, g, c] = self.w_out[...].astype(bf16)
            self.W2[t, 0, g, c] = self.w_up[...].astype(bf16)
            self.W2[t, 1, g, c] = self.w_down[...].astype(bf16)
        elif place == "normed":
            begin(self.q_z(2))
        elif place == "masked":
            await_in(self.q_z(1, True))
            begin(*[self.q_plane(1, k) for k in planes])
            begin(self.q_z(3))
            await_in(*[self.q_plane(0, k, True) for k in planes])
            begin(self.q_core(0))
        elif place == "pair":
            await_in(self.q_core_in(j))
        elif place == "pair_proj":
            @pl.when(j == 0)
            def _():
                await_in(self.q_z(2, True))
                begin(*[self.q_plane(2, k) for k in planes])
                begin(*[self.o_z(k) for k in range(1, nt)])
                begin(self.f_z(2))
        elif place == "pair_half":
            @pl.when(j == 0)
            def _():
                await_in(*[self.q_plane(1, k, True) for k in planes])
                begin(self.q_core(1))
                begin(*[self.f_plane(0, k, 0) for k in planes])
            @pl.when(j == 1)
            def _():
                await_in(*[self.q_plane(2, k, True) for k in planes])
                begin(self.q_core(2))
                begin(*[self.f_plane(0, k, 1) for k in planes])
            @pl.when(j == 2)
            def _():
                await_in(*[self.q_plane(3, k, True) for k in planes])
                begin(self.q_core(3))
                await_in(*[self.f_plane(0, k, 0, True) for k in planes])
                begin(self.f_near(0))
            @pl.when(j == 3)
            def _():
                await_in(*[self.o_plane(k, True) for k in planes])
                begin(self.o_core())
                await_in(*[self.f_plane(0, k, 1, True) for k in planes])
                begin(self.f_near(1), self.f_core(0))
        elif place == "pair_mid":
            @pl.when(j == 0)
            def _():
                await_in(self.q_z(3, True))
                begin(*[self.q_plane(3, k) for k in planes])
                begin(self.f_z(3))
            @pl.when(j == 1)
            def _():
                await_in(*[self.o_z(k, True) for k in range(1, nt)])
                begin(*[self.o_plane(k) for k in planes])
            @pl.when(j == 2)
            def _():
                self.f_on(2)
            @pl.when(j == 3)
            def _():
                self.f_on(3)
        elif place == "mixed":
            await_in(self.o_core(True))
        elif place == "chunk":
            await_in(self.f_core(self.turn(j), True))
        elif place == "chunk_mid":
            @pl.when(j < 2)
            def _():
                self.f_pass(j + 2)
            @pl.when(j == 2)
            def _():
                await_in(self.f_near(0, True), self.f_near(1, True))
                begin(self.f_core(1))
            @pl.when(j >= 1)
            def _():
                x = self.turn(j - 1)
                self.f_after_core(x)
                @pl.when(j >= 2)
                def _():
                    begin(*[self.r2("plane", x, k) for k in planes])
        elif place == "chunk_end":
            begin(self.r2("core", self.turn(j)))
        elif place == "ffn_done":
            self.f_after_core(1)
            begin(self.r2_near())
        elif place == "out_grad":
            begin(self.ro("core"))
        elif place == "back_mid":
            @pl.when(j >= 1)
            def _():
                self.q_after_core(nt - j)
                begin(*[self.rq("plane", nt - j, k) for k in planes])
            @pl.when(j == 0)
            def _():
                await_in(self.ro("core"))
                for p in range(nt):
                    self.DO[p, :, c] = self.DO[p, :, c] + self.CO[p]
                begin(*[self.ro("plane", k) for k in planes])
                self.v_mid("E", self.ne)
            @pl.when(j == 1)
            def _():
                await_in(self.r2_near())
                for u in range(2):
                    def step(i, _):
                        self.D2[t, u, i, c] = self.D2[t, u, i, c] + self.Y2[u, i]
                        return 0
                    for i in range(ng):
                        step(i, 0)
                begin(*[self.r2("plane", 0, k) for k in planes])
                self.f_after_plane(2)
                begin(self.r2("z", 2))
            @pl.when(j == 2)
            def _():
                await_in(*[self.ro("plane", k) for k in planes])
                for p in range(nt):
                    acc = self.DO[p, g, c].astype(f32)
                    for k in planes:
                        acc = acc + self.XO[k, p].astype(f32)
                    self.DO[p, g, c] = acc.astype(bf16)
                begin(*[self.ro("z", k) for k in range(1, nt)])
                self.f_after_plane(3)
                begin(self.r2("z", 3))
            @pl.when(j >= 2)
            def _():
                self.q_after_plane(nt - j + 1)
                begin(self.rq("z", nt - j + 1))
        elif place == "back_end":
            self.rq("core", nt - 1 - j).start()
        elif place == "finish":
            self.q_after_core(0)
            begin(*[self.rq("plane", 0, k) for k in planes])
            for x in range(1, nt):
                if x > 1:
                    self.r2("z", x).wait_recv()
                self.ro("z", x).wait_recv()
            await_in(*[self.r2("plane", 0, k) for k in planes])
            for u, o in enumerate((self.o_up, self.o_down)):
                acc = self.D2[t, u, g, c].astype(f32)
                for k in planes:
                    acc = acc + self.X2[0, k, u].astype(f32)
                for x in range(2, nt):
                    acc = acc + self.Z2[x, u].astype(f32)
                o[...] = acc
            acc = self.DO[t, g, c].astype(f32)
            for x in range(1, nt):
                acc = acc + self.ZO[x].astype(f32)
            self.o_out[...] = acc
        elif place == "finish_z":
            self.q_after_plane(1)
            begin(self.rq("z", 1))
        elif place == "finish_q":
            acc = self.DQ[t, g, c].astype(f32)
            for k in range(1, ng):
                self.rq("plane", 0, k).wait_recv()
                acc = acc + self.XQ[0, k].astype(f32)
            for x in range(1, nt):
                self.rq("z", x).wait_recv()
                acc = acc + self.ZQ[x].astype(f32)
            for k in range(3):
                self.o_qkv[k] = acc[:, 128 * k:128 * k + 128]
        elif place == "leave":
            for k in planes:
                self.o_plane(k).wait_send()
                self.ro("plane", k).wait_send()
                for x in range(nt):
                    self.q_plane(x, k).wait_send()
                    if x != 1:
                        for u in range(2):
                            self.f_plane(x, k, u).wait_send()
                    if x != 1:
                        self.r2("plane", x, k).wait_send()
                    self.rq("plane", x, k).wait_send()
            for k in range(nt):
                self.q_core(k).wait_send()
                self.f_core(k).wait_send()
                self.r2("core", k).wait_send()
                self.rq("core", k).wait_send()
            self.o_core().wait_send()
            self.ro("core").wait_send()
            self.r2_near().wait_send()
            self.f_near(0).wait_send()
            self.f_near(1).wait_send()
            for k in range(1, nt):
                self.q_z(k).wait_send()
                self.o_z(k).wait_send()
                if k > 1:
                    self.f_z(k).wait_send()
                    self.r2("z", k).wait_send()
                self.rq("z", k).wait_send()
                self.ro("z", k).wait_send()

    def v(self, name, stage, k, incoming=False):
        Z, X = getattr(self, name)
        if stage == "z":
            return self.copy(name + "_z", (k,), "z", k, Z.at[self.t], Z.at[self.t ^ k if incoming else self.t])
        return self.copy(name + "_dp", (k,), "dp", k, X.at[self.d], X.at[self.d ^ k if incoming else self.d])

    def v_start(self, name, rows):
        Z = getattr(self, name)[0]
        n = rows[0].shape[1]
        for k, x in enumerate(rows):
            Z[self.t, :, k * n:k * n + n] = x
        for k in range(1, self.nt):
            self.v(name, "z", k).start()

    def v_mid(self, name, m):
        Z, X = getattr(self, name)
        nt, n = self.nt, Z.shape[2] // m
        for k in range(1, nt):
            self.v(name, "z", k, True).wait_recv()
        for k in range(nt):
            X[self.d, :, k * n:k * n + n] = Z[k, :, 0:n]
        s = Z[0, :, n:m * n]
        for k in range(1, nt):
            s = s + Z[k, :, n:m * n]
        X[self.d, :, nt * n:(nt + m - 1) * n] = s
        for k in range(1, 2 * self.ng):
            self.v(name, "dp", k).start()

    def v_done(self, name, m, kept, sums, at):
        Z, X = getattr(self, name)
        nd, nt, n = 2 * self.ng, self.nt, Z.shape[2] // m
        for k in range(1, nd):
            self.v(name, "dp", k, True).wait_recv()
        for k in range(nd):
            for i in range(nt):
                kept[k * nt + i:k * nt + i + 1, :] = X[k, :, i * n:i * n + n]
        s = X[0, :, nt * n:(nt + m - 1) * n]
        for k in range(1, nd):
            s = s + X[k, :, nt * n:(nt + m - 1) * n]
        for i in range(m - 1):
            sums[at + i:at + i + 1, :] = s[:, i * n:i * n + n]

    def v_leave(self, name):
        for k in range(1, self.nt):
            self.v(name, "z", k).wait_send()
        for k in range(1, 2 * self.ng):
            self.v(name, "dp", k).wait_send()


TILE = dict(ln1=256, proj=1024, ln2=512, tile=512, wgrad=512, ln2b=256, gmix=1024, gwo=512, qgrad=512, back=1024, ln1b=256)
UNROLL = {"ln1", "ln1b", "ln2b", "proj", "ln2", "tile", "wgrad", "gmix", "gwo", "qgrad", "back"}


def loop(name, total, body, init):
    n = TILE[name]
    if name in UNROLL or total == n:
        for i in range(total // n):
            init = body(slice(i * n, i * n + n), init)
        return init
    return lax.fori_loop(0, total // n, lambda i, x: body(pl.ds(pl.multiple_of(i * n, n), n), x), init)


def layer(cm, T, most, length, t, tok, cot, seg, wt, btime, g1, b1, g2, b2, bdown, bup, out, gtok, sc):
    tp, n1, qkv, qaug, kaug, mixed, lse, qq, kk, vv, oo, dq, dkv, dqkv, mid, n2, ffn, gn, act, gu, gm, xT, xT3, bsum, stat1, stat2 = sc
    seq, D = tok.shape
    P = qkv.shape[0]
    NF, F = bsum.shape[0], bsum.shape[2]
    n = seq // TR
    cm.hook("greet")
    cm.hook("start")
    cm.hook("row_in")
    half = D // 2
    ang = t * jnp.exp(-math.log(10000.0) * lax.broadcasted_iota(jnp.int32, (8, half), 1).astype(f32) / half)
    emb = jnp.concatenate([jnp.sin(ang), jnp.cos(ang)], axis=1)
    tp[...] = jnp.dot(emb, wt[...], precision=lax.Precision.HIGHEST, preferred_element_type=f32)[0:1, :] + btime[...]

    def ln1(r, _):
        xh = normed_keep(tok[r, :].astype(f32) + tp[...], stat1, r)
        n1[r, :] = (xh * g1[...] + b1[...]).astype(bf16)
        return 0

    loop("ln1", seq, ln1, 0)
    cm.hook("normed")
    srow = seg[pl.ds(T, 1), :].astype(f32)
    for b in range(seq // 128):
        col = jnp.broadcast_to(srow[:, 128 * b:128 * b + 128], (128, 128)).T
        spot = lane((128, 128)) % HS
        pos = lax.broadcasted_iota(jnp.int32, (128, 128), 0) + 128 * b
        same = col == spot.astype(f32)
        r = slice(128 * b, 128 * b + 128)
        qaug[r, :] = jnp.where(same & (spot < 8), 1.0, 0.0).astype(bf16)
        ka = jnp.where(same & (pos < length), 0.0, -BIG)
        kaug[r, :] = jnp.where(spot < 8, ka, jnp.where(spot < 11, -1.0, 0.0)).astype(bf16)

    cm.hook("cot_in")
    transpose_into(xT, cot, seq)
    cm.hook("masked")
    transpose_into(xT3, n1, seq)

    def pair_fwd(j, _):
        hp = cm.order(j)
        cm.hook("pair", j)

        def proj(r, _):
            x = nn_dot(n1[r, :], cm.getq(hp))
            s = jnp.where(lane((1, 384)) < 128, SCALE * LOG2E, 1.0)
            qkv[hp, r, :] = (x * s).astype(bf16)
            return 0

        loop("proj", seq, proj, 0)
        cm.hook("pair_proj", j)
        attend_fwd(seq, most, length, qkv, qaug, kaug, mixed, lse, qq, kk, vv, hp, lambda: cm.hook("pair_half", j))
        cm.hook("pair_mid", j)
        return 0

    lax.fori_loop(0, P, pair_fwd, 0)
    cm.hook("mixed")

    def ln2(r, _):
        mx = jnp.concatenate([mixed[p, r, :] for p in range(P)], axis=1)
        x = tok[r, :].astype(f32) + tp[...] + nt_dot(mx, cm.geto())
        mid[r, :] = x
        xh = normed_keep(x, stat2, r)
        n2[r, :] = (xh * g2[...] + b2[...]).astype(bf16)
        ffn[r, :] = jnp.zeros((TILE["ln2"], D), f32)
        gn[r, :] = jnp.zeros((TILE["ln2"], D), f32)
        return 0

    loop("ln2", seq, ln2, 0)
    cm.hook("second")

    def chunk(j, _):
        f = cm.order_ffn(j)
        cm.hook("chunk", j)

        n = TILE["tile"]
        spans = [slice(i * n, i * n + n) for i in range(seq // n)]

        def lead(r):
            return nn_dot(n2[r, :], cm.getu(f)) + bup[f], nn_dot(cot[r, :], cm.getd(f))

        acc = jnp.zeros((1, F), f32)
        ready = lead(spans[0])
        for i, r in enumerate(spans):
            ahead = lead(spans[i + 1]) if i + 1 < len(spans) else None
            a, ga = gelu_parts(ready[0])
            a = a.astype(bf16)
            g = (ready[1] * ga).astype(bf16)
            act[r, :] = a
            gu[r, :] = g
            ffn[r, :] += nt_dot(a, cm.getd(f))
            gn[r, :] += nt_dot(g, cm.getu(f))
            acc = acc + colsum(g.astype(f32))
            ready = ahead
        bsum[f] = acc
        cm.hook("chunk_mid", j)

        def wgrad(r, _):
            cm.put2(f, 1, r, nn_dot(xT[r, :], act[...]).astype(bf16))
            cm.put2(f, 0, r, tn_dot(n2[:, r], gu[...]).astype(bf16))
            return 0

        loop("wgrad", D, wgrad, 0)
        cm.hook("chunk_end", j)
        return 0

    lax.fori_loop(0, NF, chunk, 0)

    def ln2b(r, acc):
        c = cot[r, :].astype(f32)
        x = mid[r, :]
        out[r, :] = (x + ffn[r, :] + bdown[...]).astype(bf16)
        xh, rr = normed_again(x, stat2, r)
        gy = gn[r, :]
        gyx = gy * xh
        gmid = c + norm_back(gyx, xh, rr, g2[...], gy)
        mid[r, :] = gmid
        n2[r, :] = gmid.astype(bf16)
        gn[r, :] = jnp.zeros((TILE["ln2b"], D), f32)
        return acc[0] + colsum(gyx), acc[1] + colsum(gy), acc[2] + colsum(c)

    z = jnp.zeros((1, D), f32)
    a = loop("ln2b", seq, ln2b, (z, z, z))
    cm.early([emb[0:1, :], *a] + [bsum[f] for f in range(NF)])
    cm.hook("ffn_done")

    def gmix(r, _):
        x = nn_dot(n2[r, :], cm.geto()).astype(bf16)
        for p in range(P):
            gm[p, r, :] = x[:, 128 * p:128 * p + 128]
        return 0

    loop("gmix", seq, gmix, 0)

    def gwo(r, _):
        m = jnp.concatenate([mixed[p] for p in range(P)], axis=1)
        x = tn_dot(n2[:, r], m).astype(bf16)
        for p in range(P):
            cm.puto(p, r, x[:, 128 * p:128 * p + 128])
        return 0

    loop("gwo", D, gwo, 0)
    cm.hook("out_grad")
    def pair_bwd(j, _):
        hp = cm.order_back(j)
        attend_bwd(seq, most, length, qkv, qaug, kaug, mixed, lse, gm, qq, kk, vv, oo, dq, dkv, dqkv, hp)
        cm.hook("back_mid", j)

        def wgrad(r, _):
            cm.putq(hp, r, nn_dot(xT3[r, :], dqkv[...]).astype(bf16))
            return 0

        loop("qgrad", D, wgrad, 0)
        cm.hook("back_end", j)

        def back(r, _):
            gn[r, :] += nt_dot(dqkv[r, :], cm.getq(hp))
            return 0

        loop("back", seq, back, 0)
        return 0

    lax.fori_loop(0, P, pair_bwd, 0)

    def ln1b(r, acc):
        xh, rr = normed_again(tok[r, :].astype(f32) + tp[...], stat1, r)
        gy = gn[r, :]
        gyx = gy * xh
        gt = mid[r, :] + norm_back(gyx, xh, rr, g1[...], gy)
        gtok[r, :] = gt
        return acc[0] + colsum(gt), acc[1] + colsum(gyx), acc[2] + colsum(gy)

    a = loop("ln1b", seq, ln1b, (z, z, z))
    cm.late(list(a))


def layer_scratch(seq, D, P, NF, F):
    V = pltpu.VMEM
    return [V((1, D), f32), V((seq, D), bf16), V((P, seq, 384), bf16), V((seq, 128), bf16), V((seq, 128), bf16),
        V((P, seq, 128), bf16), V((P, seq, 128), f32)] + [V((2, seq, 128), bf16)] * 4 + [V((2, seq, 128), f32),
        V((3, 2, seq, 128), f32), V((seq, 384), bf16), V((seq, D), f32), V((seq, D), bf16), V((seq, D), f32), V((seq, D), f32),
        V((seq, F), bf16), V((seq, F), bf16), V((P, seq, 128), bf16), V((D, seq), bf16), V((D, seq), bf16), V((NF, 1, F), f32), V((2, seq, 128), f32), V((2, seq, 128), f32)]


def plain_kernel(most, n_sc, *refs):
    len_ref, ts_ref, tok, cot, seg, wq, wo, w2, wt, btime, g1, b1, g2, b2, bdown, bup, out, gtok, dwq, dwo, dw2, vec = refs[:22]
    T = lax.axis_index("tensor")
    cm = Plain(wq, wo, w2, dwq, dwo, dw2, vec)
    layer(cm, T, most, len_ref[T], ts_ref[0].astype(f32), tok, cot, seg, wt, btime, g1, b1, g2, b2, bdown, bup, out, gtok, refs[22:])


def run_plain(most, length, ts, tok, cot, seg, wq, wo, w2, wt, vecs, bup):
    seq, D = tok.shape
    P, NF, F = wq.shape[0], w2.shape[0], w2.shape[-1]
    S = jax.ShapeDtypeStruct
    vm = pl.BlockSpec(memory_space=pltpu.VMEM)
    sm = pl.BlockSpec(memory_space=pltpu.SMEM)
    return pl.pallas_call(
        functools.partial(plain_kernel, most, 0),
        out_shape=(S((seq, D), bf16), S((seq, D), f32), S(wq.shape, bf16), S(wo.shape, bf16), S(w2.shape, bf16), S((16, D), f32)),
        in_specs=[sm, sm] + [vm] * 14, out_specs=[vm] * 6,
        scratch_shapes=layer_scratch(seq, D, P, NF, F),
        compiler_params=pltpu.CompilerParams(vmem_limit_bytes=60 << 20),
    )(length, ts, tok, cot, seg, wq, wo, w2, wt, *[v[None] for v in vecs], bup)


def linked_kernel(most, ng, nt, names, semnames, n_layer, *refs):
    len_ref, ts_ref = refs[:2]
    held = refs[2:17]
    out, gtok, o_qkv, o_out, o_up, o_down, embs, grads, vec = refs[17:26]
    sc = refs[26:26 + n_layer]
    rest = refs[26 + n_layer:]
    bufs = dict(zip(names, rest[:len(names)]))
    sr = rest[len(names):]
    sems = {nm: (sr[2 * i], sr[2 * i + 1]) for i, nm in enumerate(semnames)}
    local = sr[-1]
    here = [bufs.pop("in%d" % i) for i in range(15)]
    tok, cot, seg, w_qkv, w_out, w_up, w_down, wt, btime, g1, b1, g2, b2, bdown, bup = here
    bufs.update(w_qkv=w_qkv, w_out=w_out, w_up=w_up, w_down=w_down, o_qkv=o_qkv, o_out=o_out, o_up=o_up, o_down=o_down)
    bufs["E"] = bufs.pop("EZ"), bufs.pop("EX")
    bufs["L"] = bufs.pop("LZ"), bufs.pop("LX")
    cm = Linked(ng, nt, bufs, sems)
    T = cm.t
    cm.ne = 4 + bup.shape[0]
    cm.early = lambda rows: cm.v_start("E", rows)
    cm.late = lambda rows: cm.v_start("L", rows)
    moves = [pltpu.make_async_copy(a, b, local.at[i]) for i, (a, b) in enumerate(zip(held, here))]
    plain_hook = cm.hook

    def hook(place, j=None):
        if place == "greet":
            plain_hook(place)
            for i in (3, 4, 5, 6, 0, 7, 2, *range(8, 15), 1):
                moves[i].start()
            moves[3].wait()
        elif place == "row_in":
            for i in range(4, 7):
                moves[i].wait()
            plain_hook("shards")
            for i in (0, 7, 2, *range(8, 15)):
                moves[i].wait()
        elif place == "cot_in":
            moves[1].wait()
        else:
            plain_hook(place, j)

    cm.hook = hook
    layer(cm, T, most, len_ref[T], ts_ref[0].astype(f32), tok, cot, seg, wt, btime, g1, b1, g2, b2, bdown, bup, out, gtok, sc)
    cm.hook("finish")
    cm.v_mid("L", 3)
    cm.hook("finish_z")
    cm.v_done("E", cm.ne, embs, vec, 4)
    cm.hook("finish_q")
    cm.v_done("L", 3, grads, vec, 2)
    cm.hook("leave")
    cm.v_leave("E")
    cm.v_leave("L")


def run_linked(most, nd, nt, length, ts, tok, cot, seg, w_qkv, w_out, w_up, w_down, wt, vecs, bup):
    seq, D = tok.shape
    ng = nd // 2
    r, F = w_up.shape
    P, NF, ne = nt, nt, 4 + nt
    S, V = jax.ShapeDtypeStruct, pltpu.VMEM
    DMA = pltpu.SemaphoreType.DMA
    bufs = dict(
        WQ=V((nt, ng, 2, r, 384), bf16), WO=V((nt, ng, 2, r, 128), bf16), W2=V((nt, 2, ng, 2, r, F), bf16),
        DQ=V((nt, ng, 2, r, 384), bf16), DO=V((nt, ng, 2, r, 128), bf16), D2=V((nt, 2, ng, 2, r, F), bf16),
        CQ=V((nt, ng, r, 384), bf16), XQ=V((nt, ng, r, 384), bf16), ZQ=V((nt, r, 384), bf16),
        CO=V((nt, ng, r, 128), bf16), XO=V((ng, nt, r, 128), bf16), ZO=V((nt, r, 128), bf16),
        C2=V((nt, 2, ng, r, F), bf16), X2=V((nt, ng, 2, r, F), bf16), Z2=V((nt, 2, r, F), bf16), Y2=V((2, ng, r, F), bf16),
        EZ=V((nt, 1, ne * D), f32), EX=V((nd, 1, (nt + ne - 1) * D), f32), LZ=V((nt, 1, 3 * D), f32), LX=V((nd, 1, (nt + 2) * D), f32),
    )
    held = (tok, cot, seg, w_qkv, w_out, w_up, w_down, wt, *[v[None] for v in vecs], bup)
    for i, x in enumerate(held):
        bufs["in%d" % i] = V(x.shape, x.dtype)
    sems = dict(gq_plane=(nt, ng), gq_z=(nt,), gq_core=(nt,), go_z=(nt,), g2_z=(nt,), go_plane=(ng,), go_core=(), g2_plane=(nt, 2, ng), g2_core=(nt,), g2_near=(2,),
        rq_core=(nt,), rq_plane=(nt, ng), rq_z=(nt,), r2_core=(nt,), r2_plane=(nt, ng), r2_z=(nt,), r2_near=(), ro_core=(), ro_plane=(ng,), ro_z=(nt,),
        E_z=(nt,), E_dp=(nd,), L_z=(nt,), L_dp=(nd,))
    ls = layer_scratch(seq, D, P, NF, F)
    scratch = ls + list(bufs.values())
    for s in sems.values():
        scratch += [DMA(s), DMA(s)]
    scratch.append(DMA((15,)))
    vm = pl.BlockSpec(memory_space=pltpu.VMEM)
    sm = pl.BlockSpec(memory_space=pltpu.SMEM)
    hb = pl.BlockSpec(memory_space=pltpu.HBM)
    an = pl.BlockSpec(memory_space=pl.ANY)
    return pl.pallas_call(
        functools.partial(linked_kernel, most, ng, nt, tuple(bufs), tuple(sems), len(ls)),
        out_shape=(V((seq, D), bf16), V((seq, D), f32), V(w_qkv.shape, f32), V(w_out.shape, f32), V(w_up.shape, f32), V(w_down.shape, f32),
            V((nd * nt, D), f32), V((nd * nt, D), f32), V((16, D), f32)),
        in_specs=[sm, sm] + [hb] * 15, out_specs=[vm] * 9,
        scratch_shapes=scratch,
        compiler_params=pltpu.CompilerParams(vmem_limit_bytes=56 << 20, collective_id=0, has_side_effects=True),
    )(length, ts, *held)


def emit_kernel(nb, *refs):
    big, outs, gwt, small, sem = refs[:9], refs[9:15], refs[15], refs[16:23], refs[23]
    ups = [pltpu.make_async_copy(a, b, sem.at[i]) for i, (a, b) in enumerate(zip(big[3:], outs))]
    for x in ups:
        x.start()
    embs, grads, vec = (b[...] for b in big[:3])
    gwt[...] = lax.dot_general(embs, grads, (((0,), (0,)), ((), ())), precision=lax.Precision.HIGHEST, preferred_element_type=f32)
    small[0][...] = jnp.sum(grads, axis=0)
    for k, o in enumerate(small[1:-1]):
        o[...] = vec[2 + k, :]
    n = vec.shape[1]
    for k in range(nb):
        small[-1][pl.ds(k * n, n)] = vec[7 + k, :]
    for y in ups:
        y.wait()


def emit(nb, *big):
    S = jax.ShapeDtypeStruct
    D = big[2].shape[1]
    vm = pl.BlockSpec(memory_space=pltpu.VMEM)
    an = pl.BlockSpec(memory_space=pl.ANY)
    hb = pl.BlockSpec(memory_space=pltpu.HBM)
    return pl.pallas_call(
        functools.partial(emit_kernel, nb),
        out_shape=tuple(S(x.shape, x.dtype) for x in big[3:]) + (S((D, D), f32),) + tuple(S((D,), f32) for _ in range(6)) + (S((nb * D,), f32),),
        in_specs=[vm] * 3 + [an] * 6, out_specs=[hb] * 6 + [vm] * 8,
        scratch_shapes=[pltpu.SemaphoreType.DMA((6,))],
        compiler_params=pltpu.CompilerParams(vmem_limit_bytes=16 << 20),
    )(*big)


def shards(
    tokens,
    timestep,
    segment_ids,
    span_lengths,
    w_qkv,
    w_out_t,
    w_up,
    w_down_t,
    w_time,
    b_time,
    ln1_gain,
    ln1_bias,
    ln2_gain,
    ln2_bias,
    b_up,
    b_down,
    cotangent,
):
    seq, D = tokens.shape[1:]
    nd, nt = lax.axis_size("dp"), lax.axis_size("tensor")
    vecs = (b_time, ln1_gain, ln1_bias, ln2_gain, ln2_bias, b_down)
    F = w_up.shape[1]
    bup = b_up.reshape(nt, 1, F)
    if w_up.shape[0] % 16 == 0 and (nd, nt) == (8, 4):
        out, gtok, *g, embs, lines, vec = run_linked(
            DOC, nd, nt, span_lengths, timestep, tokens[0], cotangent[0], segment_ids,
            w_qkv, w_out_t, w_up, w_down_t, w_time, vecs, bup)
        gq, go, gu, gd, out, gtok, gwt, *v = emit(nt, embs, lines, vec, *g, out, gtok)
        return (out[None], gtok[None], gq, go, gu, gd, gwt, v[0], v[1], v[2], v[3], v[4], v[6], v[5])
    HB = w_qkv.shape[2]

    def whole(w):
        return lax.all_gather(lax.all_gather(w.astype(bf16), "dp", axis=w.ndim - 2, tiled=True), "tensor", axis=0)

    def part(g, dim):
        g = lax.psum_scatter(g, "dp", scatter_dimension=dim, tiled=True)
        return lax.psum_scatter(g, "tensor", scatter_dimension=0, tiled=True)[0].astype(f32)

    wq = whole(jnp.transpose(w_qkv, (1, 0, 2)).reshape(w_qkv.shape[1], 3 * HB))
    out, gtok, dwq, dwo, dw2, vec = run_plain(
        DOC, span_lengths, timestep, tokens[0], cotangent[0], segment_ids,
        wq, whole(w_out_t), whole(jnp.stack([w_up, w_down_t])), w_time, vecs, bup)
    lines = lax.all_gather(jnp.stack([vec[0], vec[8]]), ("dp", "tensor"), axis=1, tiled=False)
    gwt = jnp.dot(lines[0].T, lines[1], precision=lax.Precision.HIGHEST)
    small = lax.psum(vec, ("dp", "tensor"))
    gq, g2 = part(dwq, 1), part(dw2, 2)
    return (
        out[None], gtok[None], jnp.transpose(gq.reshape(gq.shape[0], 3, HB), (1, 0, 2)), part(dwo, 1), g2[0], g2[1],
        gwt, small[8], small[9], small[10], small[1], small[2], small[4:4 + nt].reshape(-1), small[3])


def solution(mesh):
    return jax.shard_map(
        shards,
        mesh=mesh,
        in_specs=(
            P_(("dp", "tensor"), None, None),
            P_(("dp", "tensor")),
            P_("dp", None),
            P_("dp"),
            P_(None, "dp", "tensor"),
            P_("dp", "tensor"),
            P_("dp", "tensor"),
            P_("dp", "tensor"),
            P_(),
            P_(),
            P_(),
            P_(),
            P_(),
            P_(),
            P_(),
            P_(),
            P_(("dp", "tensor"), None, None),
        ),
        out_specs=(
            P_(("dp", "tensor"), None, None),
            P_(("dp", "tensor"), None, None),
            P_(None, "dp", "tensor"),
            P_("dp", "tensor"),
            P_("dp", "tensor"),
            P_("dp", "tensor"),
            P_(),
            P_(),
            P_(),
            P_(),
            P_(),
            P_(),
            P_(),
            P_(),
        ),
        check_vma=False,
    )
```
